32 devices in a mesh: ctx: 8 (over z, x), tp: 4 (over y, core).
Axes of the slice: x: 2, y: 2, z: 4, core: 2. Of those that a mesh axis runs over, the one named last changes fastest.
Arguments:
- layer_input: bfloat16 [4096, 2048], P('ctx'), may hold values from -6 to 6
- attn_gain: float32 [2048], replicated, may hold values from 0.5 to 1.5
- w_query: bfloat16 [2048, 2048], P(None, 'tp'), may hold values from -0.125 to 0.125
- key_matrix: bfloat16 [2048, 1024], P(None, 'tp'), may hold values from -0.125 to 0.125
- value_matrix: bfloat16 [2048, 1024], P(None, 'tp'), may hold values from -0.125 to 0.125
- w_out: bfloat16 [2048, 2048], P('tp'), may hold values from -1 to 1
- ffn_gain: float32 [2048], replicated, may hold values from 0.5 to 1.5
- w_gate: bfloat16 [2048, 8192], P(None, 'tp'), may hold values from -0.125 to 0.125
- w_up: bfloat16 [2048, 8192], P(None, 'tp'), may hold values from -0.125 to 0.125
- w_down: bfloat16 [8192, 2048], P('tp'), may hold values from -0.125 to 0.125
- cotangent: bfloat16 [4096, 2048], P('ctx'), may hold values from -6 to 6
- block_order: int32 [32], replicated, may hold values from 0 to 31, each once
- cont_prompt: int32 [8], replicated, may hold values from 0 to 0, as said below
Outputs:
- output: bfloat16 [4096, 2048], P('ctx')
- grad_input: bfloat16 [4096, 2048], P('ctx')
- grad_attn_gain: float32 [2048], P(('ctx', 'tp'))
- grad_w_query: float32 [2048, 2048], P('ctx', 'tp')
- grad_w_key: float32 [2048, 1024], P('ctx', 'tp')
- grad_w_value: float32 [2048, 1024], P('ctx', 'tp')
- grad_w_out: float32 [2048, 2048], P('tp', 'ctx')
- grad_ffn_gain: float32 [2048], P(('ctx', 'tp'))
- grad_w_gate: float32 [2048, 8192], P('ctx', 'tp')
- grad_w_up: float32 [2048, 8192], P('ctx', 'tp')
- grad_w_down: float32 [8192, 2048], P('tp', 'ctx')
The draws below stay inside these ranges and needn't reach their ends.
Inputs may be any that keep to these rules, and one draw needn't show every extreme that they name: `block_order`: a permutation: each logical block is stored exactly once. `cont_prompt`: each prompt is named by exactly 8 continuations.
All inputs are finite; a program needn't handle non-finite values.
Results may differ from the reference program's by a relative error of at most 0.028.
Values may be sent and summed in bfloat16 or wider, within the bound.
No kernel may reach another device: no remote copies, remote signals or barrier semaphores. Data moves between devices by JAX's collectives and lax.ppermute only.
A program may use at most 256 MiB of HBM per device.

```python
import math
import jax
import jax.numpy as jnp
from jax import lax

MODEL_WIDTH = 2048
QUERY_HEADS = 16
KEY_VALUE_HEADS = 8
HEAD_SIZE = 128
FF = 8192
PROMPT = 2048
CONT_LEN = 256
CONTS = 8
BLOCK = 128
TOKENS = 4096
GROUPS = 1
NBLOCKS = 32


def draw_cont_prompt(key, part):
    listing = jnp.repeat(jnp.arange(GROUPS, dtype=jnp.int32), CONTS)
    return jax.random.permutation(key, listing)


def shard_levels(key, dims, shards, smallest, largest):
    level, own = 1.0, jax.random.fold_in(key, 6)
    for dim, blocks in shards:
        draws = jnp.exp(jax.random.uniform(jax.random.fold_in(own, dim), (blocks,), jnp.float32, smallest / len(shards), largest / len(shards)))
        level = level * jnp.repeat(draws, dims[dim] // blocks).reshape([-1 if axis == dim else 1 for axis in range(len(dims))])
    return level


def bell_draw(key, shape, scale, bound, split=(), kind=jnp.bfloat16):
    values = scale * jax.random.normal(key, shape, jnp.float32)
    if split:
        values = values * shard_levels(key, shape, split, -0.22, 0.18)
    return jnp.clip(values, -bound, bound).astype(kind)


def setup_inputs(seed: int = 0) -> dict:
    keys = jax.random.split(jax.random.key(seed), 14)
    layer_input = bell_draw(keys[0], (TOKENS, MODEL_WIDTH), 1.0, 6.0, ((0, 8),))
    attn_gain = jnp.clip(1.0 + 0.1 * jax.random.normal(keys[1], (MODEL_WIDTH,), jnp.float32), 0.5, 1.5)
    w_query = bell_draw(keys[2], (MODEL_WIDTH, QUERY_HEADS * HEAD_SIZE), MODEL_WIDTH ** -0.5, 0.125, ((1, 4),))
    key_matrix = bell_draw(keys[3], (MODEL_WIDTH, KEY_VALUE_HEADS * HEAD_SIZE), MODEL_WIDTH ** -0.5, 0.125, ((1, 4),))
    value_matrix = bell_draw(keys[4], (MODEL_WIDTH, KEY_VALUE_HEADS * HEAD_SIZE), MODEL_WIDTH ** -0.5, 0.125, ((1, 4),))
    w_out = bell_draw(keys[5], (QUERY_HEADS * HEAD_SIZE, MODEL_WIDTH), (QUERY_HEADS * HEAD_SIZE // 64) ** -0.5, 1.0, ((0, 4),))
    ffn_gain = jnp.clip(1.0 + 0.1 * jax.random.normal(keys[6], (MODEL_WIDTH,), jnp.float32), 0.5, 1.5)
    w_gate = bell_draw(keys[7], (MODEL_WIDTH, FF), MODEL_WIDTH ** -0.5, 0.125, ((1, 4),))
    w_up = bell_draw(keys[8], (MODEL_WIDTH, FF), MODEL_WIDTH ** -0.5, 0.125, ((1, 4),))
    w_down = bell_draw(keys[9], (FF, MODEL_WIDTH), (FF // 4) ** -0.5, 0.125, ((0, 4),))
    cotangent = bell_draw(keys[10], (TOKENS, MODEL_WIDTH), 1.0, 6.0, ((0, 8),))
    block_order = jax.random.permutation(keys[11], NBLOCKS).astype(jnp.int32)
    cont_prompt = draw_cont_prompt(jax.random.fold_in(keys[13], 71), 0)
    return dict(layer_input=layer_input, attn_gain=attn_gain, w_query=w_query, key_matrix=key_matrix, value_matrix=value_matrix, w_out=w_out, ffn_gain=ffn_gain, w_gate=w_gate, w_up=w_up, w_down=w_down, cotangent=cotangent, block_order=block_order, cont_prompt=cont_prompt)


eps_norm = 1e-05
rope_base = 1000000.0
highest = lax.Precision.HIGHEST

@jax.custom_vjp
def lowered_precision(v):
    return lax.optimization_barrier(v.astype(jnp.bfloat16)).astype(jnp.float32)

@jax.custom_vjp
def lowered_backward(v):
    return v

def low_keep(v):
    return (lowered_precision(v), None)

def low_pass(kept, grad):
    return (grad,)

def back_keep(v):
    return (v, None)

def back_low(kept, grad):
    return (lowered_precision(grad),)
lowered_precision.defvjp(low_keep, low_pass)
lowered_backward.defvjp(back_keep, back_low)

def matrix_product(left, right):
    return jnp.dot(left, right, precision=highest, preferred_element_type=jnp.float32)

def token_meta(row_ids, block_order, cont_prompt):
    count = cont_prompt.shape[0]
    prompt_total = count // CONTS * PROMPT
    logical = jnp.take(block_order, row_ids // BLOCK) * BLOCK + row_ids % BLOCK
    is_prompt = logical < prompt_total
    offset = logical - prompt_total
    which = jnp.clip(offset // CONT_LEN, 0, count - 1)
    group = jnp.where(is_prompt, logical // PROMPT, jnp.take(cont_prompt, which))
    member = jnp.where(is_prompt, 0, which + 1)
    place = jnp.where(is_prompt, logical % PROMPT, PROMPT + offset % CONT_LEN)
    return (group.astype(jnp.int32), member.astype(jnp.int32), place.astype(jnp.int32))

def visible(query_meta, key_meta):
    same = query_meta[0][:, None] == key_meta[0][None, :]
    causal = key_meta[2][None, :] <= query_meta[2][:, None]
    shared = (key_meta[1][None, :] == 0) | (key_meta[1][None, :] == query_meta[1][:, None])
    return same & causal & shared

def rope_tables(place):
    half_dim = HEAD_SIZE // 2
    freq = rope_base ** (-(2.0 * jnp.arange(half_dim, dtype=jnp.float32) / HEAD_SIZE))
    angle = place.astype(jnp.float32)[:, None] * freq[None, :]
    angle = jnp.concatenate([angle, angle], axis=-1)
    return (jnp.cos(angle), jnp.sin(angle))

def rotate(vec, cosine, sine):
    half_dim = vec.shape[-1] // 2
    turned = jnp.concatenate([-vec[..., half_dim:], vec[..., :half_dim]], axis=-1)
    return vec * cosine[:, None, :] + turned * sine[:, None, :]

def rms_norm(vec, gain):
    return vec * lax.rsqrt(lax.optimization_barrier(jnp.mean(vec * vec, axis=-1, keepdims=True)) + eps_norm) * gain

def layer(params, meta, cosine, sine):
    inputs, attn_gain, w_query, key_matrix, value_matrix, w_out, ffn_gain, w_gate, w_up, w_down = params
    row_total_count = inputs.shape[0]
    first_input = lowered_precision(rms_norm(inputs, attn_gain))
    query_lin = lowered_backward(matrix_product(first_input, w_query)).reshape(row_total_count, QUERY_HEADS, HEAD_SIZE)
    key_linear = lowered_backward(matrix_product(first_input, key_matrix)).reshape(row_total_count, KEY_VALUE_HEADS, HEAD_SIZE)
    value_states = lowered_precision(lowered_backward(matrix_product(first_input, value_matrix))).reshape(row_total_count, KEY_VALUE_HEADS, HEAD_SIZE)
    queries = lowered_precision(lowered_backward(rotate(query_lin, cosine, sine)))
    key_states = lowered_precision(lowered_backward(rotate(key_linear, cosine, sine)))
    key_states = jnp.repeat(key_states, QUERY_HEADS // KEY_VALUE_HEADS, axis=1)
    value_states = jnp.repeat(value_states, QUERY_HEADS // KEY_VALUE_HEADS, axis=1)
    block_rows = math.gcd(512, row_total_count)
    blocks = row_total_count // block_rows
    score_scale = 1.0 / math.sqrt(HEAD_SIZE)

    def attend(pieces):
        query_rows, group, member, place = pieces
        scores = jnp.einsum('qhd,khd->hqk', query_rows, key_states, precision=highest) * score_scale
        scores = lowered_backward(scores)
        visible_mask = visible((group, member, place), meta)
        scores = jnp.where(visible_mask[None], scores, -1e+30)
        weights = lowered_precision(jax.nn.softmax(scores, axis=-1))
        mixed = jnp.einsum('hqk,khd->qhd', weights, value_states, precision=highest)
        return lowered_precision(lowered_backward(mixed)).reshape(query_rows.shape[0], QUERY_HEADS * HEAD_SIZE)
    mixed_all = lax.map(jax.checkpoint(attend), (queries.reshape(blocks, block_rows, QUERY_HEADS, HEAD_SIZE), meta[0].reshape(blocks, block_rows), meta[1].reshape(blocks, block_rows), meta[2].reshape(blocks, block_rows)))
    mixed_all = mixed_all.reshape(row_total_count, QUERY_HEADS * HEAD_SIZE)
    middle = inputs + lowered_backward(matrix_product(mixed_all, w_out))
    second_in = lowered_precision(rms_norm(middle, ffn_gain))
    gate = lowered_backward(matrix_product(second_in, w_gate))
    upward = lowered_backward(matrix_product(second_in, w_up))
    hidden = lowered_precision(jax.nn.silu(gate) * upward)
    return middle + lowered_backward(matrix_product(hidden, w_down))

def reference(layer_input, attn_gain, w_query, key_matrix, value_matrix, w_out, ffn_gain, w_gate, w_up, w_down, cotangent, block_order, cont_prompt):
    row_total_count = layer_input.shape[0]
    row_ids = jnp.arange(row_total_count, dtype=jnp.int32)
    meta = token_meta(row_ids, block_order, cont_prompt)
    cosine, sine = rope_tables(meta[2])
    params = tuple((piece.astype(jnp.float32) for piece in (layer_input, attn_gain, w_query, key_matrix, value_matrix, w_out, ffn_gain, w_gate, w_up, w_down)))
    result, pull = jax.vjp(lambda *pieces: layer(pieces, meta, cosine, sine), *params)
    grads = pull(cotangent.astype(jnp.float32))
    return (result.astype(jnp.bfloat16), grads[0].astype(jnp.bfloat16), grads[1], grads[2], grads[3], grads[4], grads[5], grads[6], grads[7], grads[8], grads[9])
```

```python
import functools
import math

import jax
import jax.numpy as jnp
from jax import lax
from jax.experimental import pallas as pl
from jax.experimental.pallas import tpu as pltpu
from jax.sharding import PartitionSpec as P

HEAD_SIZE = 128
PROMPT = 2048
CONT_LEN = 256
CONTS = 8
BLOCK = 128
LOG2E = 1.4426950408889634
NEG = -1e30


eps_norm = 1e-05
rope_base = 1000000.0

def token_meta(row_ids, block_order, cont_prompt):
    count = cont_prompt.shape[0]
    prompt_total = count // CONTS * PROMPT
    logical = jnp.take(block_order, row_ids // BLOCK) * BLOCK + row_ids % BLOCK
    is_prompt = logical < prompt_total
    offset = logical - prompt_total
    which = jnp.clip(offset // CONT_LEN, 0, count - 1)
    group = jnp.where(is_prompt, logical // PROMPT, jnp.take(cont_prompt, which))
    member = jnp.where(is_prompt, 0, which + 1)
    place = jnp.where(is_prompt, logical % PROMPT, PROMPT + offset % CONT_LEN)
    return (group, member, place)


def rope_tables(place):
    half_dim = HEAD_SIZE // 2
    freq = rope_base ** (-(2.0 * jnp.arange(half_dim, dtype=jnp.float32) / HEAD_SIZE))
    angle = place.astype(jnp.float32)[:, None] * freq[None, :]
    angle = jnp.concatenate([angle, angle], axis=-1)
    return (jnp.cos(angle), jnp.sin(angle))


def rotate(vec, cosine, sine):
    half_dim = vec.shape[-1] // 2
    turned = jnp.concatenate([-vec[..., half_dim:], vec[..., :half_dim]], axis=-1)
    return vec * cosine[:, None, :] + turned * sine[:, None, :]


def unrotate(vec, cosine, sine):
    half_dim = vec.shape[-1] // 2
    moved = vec * sine[:, None, :]
    turned = jnp.concatenate([moved[..., half_dim:], -moved[..., :half_dim]], axis=-1)
    return vec * cosine[:, None, :] + turned


def plain_dot(left, right):
    return jnp.dot(left, right, preferred_element_type=jnp.float32)


def left_dot(left, right):
    return lax.dot_general(
        left, right, (((0,), (0,)), ((), ())), preferred_element_type=jnp.float32
    )


def right_dot(left, right):
    return lax.dot_general(
        left, right, (((1,), (1,)), ((), ())), preferred_element_type=jnp.float32
    )


def norm_back(grad_out, normed, inv_scale, gain):
    scaled = grad_out * gain
    inner = jnp.mean(scaled * normed, axis=-1, keepdims=True)
    return (inv_scale * (scaled - normed * inner), jnp.sum(grad_out * normed, axis=0))


def gain_share(grad_full, ctx_count, tp_count):
    width = grad_full.shape[0] // (ctx_count * tp_count)
    shaped = grad_full.reshape(ctx_count, tp_count, width)
    return lax.dynamic_index_in_dim(shaped, lax.axis_index("tp"), 1, keepdims=False)


def block_plan(order_ref, cont_ref, stored):
    per_prompt = PROMPT // BLOCK
    per_cont = CONT_LEN // BLOCK
    count = cont_ref.shape[0]
    prompt_blocks = count // CONTS * per_prompt
    own = order_ref[stored]
    is_prompt = own < prompt_blocks
    offset = own - prompt_blocks
    which = jnp.clip(lax.div(offset, per_cont), 0, count - 1)
    group = jnp.where(is_prompt, lax.div(own, per_prompt), cont_ref[which])
    inner = jnp.where(is_prompt, lax.rem(own, per_prompt), lax.rem(offset, per_cont))
    has_prev = lax.rem(inner, 2)
    pairs = jnp.where(is_prompt, lax.div(inner, 2), per_prompt // 2)
    prev = own - has_prev
    return group * per_prompt, pairs, prev, own, has_prev


def fill_inverse(order_ref, inverse_ref):
    def put(stored, carry):
        inverse_ref[order_ref[stored]] = stored
        return carry

    lax.fori_loop(0, order_ref.shape[0], put, 0)


def key_rows(inverse_ref, logical):
    return pl.ds(pl.multiple_of(inverse_ref[logical] * BLOCK, BLOCK), BLOCK)


def tile_pair(ref, rows_a, rows_b, column):
    cols = pl.ds(column, HEAD_SIZE)
    return jnp.concatenate([ref[rows_a, cols], ref[rows_b, cols]], axis=0)


def own_mask(has_prev, rep):
    shape = (2 * BLOCK, rep * BLOCK)
    row = lax.broadcasted_iota(jnp.int32, shape, 0)
    col = lax.broadcasted_iota(jnp.int32, shape, 1)
    first_row = BLOCK * (1 - has_prev)
    return (row >= first_row) & (row - BLOCK <= lax.rem(col, BLOCK))


def stack_t(ref, rows, column, rep):
    return jnp.concatenate(
        [ref[rows, pl.ds(column + r * HEAD_SIZE, HEAD_SIZE)].T for r in range(rep)], axis=1
    )


def stack_rows(ref, rows, column, rep):
    return jnp.concatenate(
        [ref[rows, pl.ds(column + r * HEAD_SIZE, HEAD_SIZE)] for r in range(rep)], axis=0
    )


def dot(left, right):
    return jnp.dot(left, right, preferred_element_type=jnp.float32)


def forward_kernel(rep, hps, order_ref, cont_ref, first_ref, q_ref, kv_ref, out_ref, lse_ref,
                   inverse_ref, qt_ref, acc_ref):
    fill_inverse(order_ref, inverse_ref)
    q_blocks = q_ref.shape[0] // BLOCK
    factor = LOG2E / math.sqrt(HEAD_SIZE)
    width = rep * HEAD_SIZE

    def one_query_block(qb, carry):
        base, pairs, prev, own, has_prev = block_plan(order_ref, cont_ref, first_ref[0] + qb)
        rows = pl.ds(pl.multiple_of(qb * BLOCK, BLOCK), BLOCK)
        mask = own_mask(has_prev, rep)
        rows_a, rows_b = key_rows(inverse_ref, prev), key_rows(inverse_ref, own)
        state = []
        for h in range(hps):
            qt = stack_t(q_ref, rows, h * width, rep)
            qt_ref[h] = qt
            scores = dot(tile_pair(kv_ref, rows_a, rows_b, 2 * h * HEAD_SIZE), qt) * factor
            scores = jnp.where(mask, scores, NEG)
            best = jnp.max(scores, axis=0, keepdims=True)
            weights = jnp.exp2(scores - best)
            total = jnp.sum(weights, axis=0, keepdims=True)
            values = tile_pair(kv_ref, rows_a, rows_b, (2 * h + 1) * HEAD_SIZE)
            acc_ref[h] = dot(values.T, weights.astype(jnp.bfloat16))
            state += [best, total]

        def one_pair(t, state):
            rows_a = key_rows(inverse_ref, base + 2 * t)
            rows_b = key_rows(inverse_ref, base + 2 * t + 1)
            after = []
            for h in range(hps):
                best, total = state[2 * h], state[2 * h + 1]
                keys = tile_pair(kv_ref, rows_a, rows_b, 2 * h * HEAD_SIZE)
                scores = dot(keys, qt_ref[h]) * factor
                newest = jnp.maximum(best, jnp.max(scores, axis=0, keepdims=True))
                weights = jnp.exp2(scores - newest)
                shrink = jnp.exp2(best - newest)
                total = total * shrink + jnp.sum(weights, axis=0, keepdims=True)
                values = tile_pair(kv_ref, rows_a, rows_b, (2 * h + 1) * HEAD_SIZE)
                acc_ref[h] = acc_ref[h] * shrink + dot(values.T, weights.astype(jnp.bfloat16))
                after += [newest, total]
            return tuple(after)

        state = lax.fori_loop(0, pairs, one_pair, tuple(state))
        for h in range(hps):
            best, total = state[2 * h], state[2 * h + 1]
            mixed = acc_ref[h] * (1.0 / total)
            for r in range(rep):
                part = mixed[:, r * BLOCK : (r + 1) * BLOCK]
                out_ref[rows, pl.ds(h * width + r * HEAD_SIZE, HEAD_SIZE)] = part.T.astype(
                    jnp.bfloat16
                )
            lse_ref[0, h, pl.ds(qb, 1), :] = best + jnp.log2(total)
        return carry

    lax.fori_loop(0, q_blocks, one_query_block, 0)


def backward_kernel(rep, hps, order_ref, cont_ref, first_ref, q_ref, kv_ref, gm_ref, mix_ref,
                    lse_ref, gq_ref, gkv_ref, inverse_ref, qt_ref, gmt_ref, gqt_ref, acc_ref):
    fill_inverse(order_ref, inverse_ref)
    q_blocks = q_ref.shape[0] // BLOCK
    scale = 1.0 / math.sqrt(HEAD_SIZE)
    factor = LOG2E * scale
    width = rep * HEAD_SIZE

    def clear(i, carry):
        acc_ref[pl.ds(pl.multiple_of(i * BLOCK, BLOCK), BLOCK), :] = jnp.zeros(
            (BLOCK, acc_ref.shape[1]), jnp.float32
        )
        return carry

    lax.fori_loop(0, order_ref.shape[0], clear, 0)

    def tile_terms(h, rows_a, rows_b, lse, delta, q_rows, gm_rows, mask):
        kcol, vcol = 2 * h * HEAD_SIZE, (2 * h + 1) * HEAD_SIZE
        keys = tile_pair(kv_ref, rows_a, rows_b, kcol)
        values = tile_pair(kv_ref, rows_a, rows_b, vcol)
        weights = jnp.exp2(dot(keys, qt_ref[h]) * factor - lse)
        if mask is not None:
            weights = jnp.where(mask, weights, 0.0)
        grad_weights = dot(values, gmt_ref[h])
        grad_scores = (weights * (grad_weights - delta)).astype(jnp.bfloat16)
        gv = dot(weights.astype(jnp.bfloat16), gm_rows)
        gk = dot(grad_scores, q_rows)
        acc_ref[rows_a, pl.ds(kcol, HEAD_SIZE)] += gk[:BLOCK]
        acc_ref[rows_b, pl.ds(kcol, HEAD_SIZE)] += gk[BLOCK:]
        acc_ref[rows_a, pl.ds(vcol, HEAD_SIZE)] += gv[:BLOCK]
        acc_ref[rows_b, pl.ds(vcol, HEAD_SIZE)] += gv[BLOCK:]
        return dot(keys.T, grad_scores)

    def one_query_block(qb, carry):
        base, pairs, prev, own, has_prev = block_plan(order_ref, cont_ref, first_ref[0] + qb)
        rows = pl.ds(pl.multiple_of(qb * BLOCK, BLOCK), BLOCK)
        mask = own_mask(has_prev, rep)
        rows_a, rows_b = key_rows(inverse_ref, prev), key_rows(inverse_ref, own)
        deltas, lses, q_stack, gm_stack = [], [], [], []
        for h in range(hps):
            qt_ref[h] = stack_t(q_ref, rows, h * width, rep)
            gmt = stack_t(gm_ref, rows, h * width, rep)
            gmt_ref[h] = gmt
            mixt = stack_t(mix_ref, rows, h * width, rep)
            deltas.append(
                jnp.sum(
                    gmt.astype(jnp.float32) * mixt.astype(jnp.float32), axis=0, keepdims=True
                )
            )
            lses.append(lse_ref[0, h, pl.ds(qb, 1), :])
        for h in range(hps):
            q_rows = stack_rows(q_ref, rows, h * width, rep)
            gm_rows = stack_rows(gm_ref, rows, h * width, rep)
            gqt_ref[h] = tile_terms(
                h, rows_a, rows_b, lses[h], deltas[h], q_rows, gm_rows, mask
            )

        def one_pair(t, carry):
            rows_a = key_rows(inverse_ref, base + 2 * t)
            rows_b = key_rows(inverse_ref, base + 2 * t + 1)
            for h in range(hps):
                q_rows = stack_rows(q_ref, rows, h * width, rep)
                gm_rows = stack_rows(gm_ref, rows, h * width, rep)
                gqt_ref[h] += tile_terms(
                    h, rows_a, rows_b, lses[h], deltas[h], q_rows, gm_rows, None
                )
            return carry

        lax.fori_loop(0, pairs, one_pair, 0)
        for h in range(hps):
            total = gqt_ref[h] * scale
            for r in range(rep):
                part = total[:, r * BLOCK : (r + 1) * BLOCK]
                gq_ref[rows, pl.ds(h * width + r * HEAD_SIZE, HEAD_SIZE)] = part.T.astype(
                    jnp.bfloat16
                )
        return carry

    lax.fori_loop(0, q_blocks, one_query_block, 0)

    def flush(i, carry):
        rows = pl.ds(pl.multiple_of(i * BLOCK, BLOCK), BLOCK)
        for h in range(hps):
            kcols = pl.ds(2 * h * HEAD_SIZE, HEAD_SIZE)
            vcols = pl.ds((2 * h + 1) * HEAD_SIZE, HEAD_SIZE)
            gkv_ref[rows, kcols] = (acc_ref[rows, kcols] * scale).astype(jnp.bfloat16)
            gkv_ref[rows, vcols] = acc_ref[rows, vcols].astype(jnp.bfloat16)
        return carry

    lax.fori_loop(0, order_ref.shape[0], flush, 0)


def attention_sizes(q, kv):
    kv_heads = kv.shape[1] // (2 * HEAD_SIZE)
    rep = q.shape[1] // HEAD_SIZE // kv_heads
    hps = kv_heads if kv.shape[0] <= 8192 else 1
    return kv_heads, rep, hps


def attention_forward(q, kv, order, cont, first):
    kv_heads, rep, hps = attention_sizes(q, kv)
    rows, tokens = q.shape[0], kv.shape[0]
    q_blocks = rows // BLOCK
    wide = hps * rep * HEAD_SIZE
    q_spec = pl.BlockSpec((rows, wide), lambda g, *_: (0, g))
    flops = 4 * rows * (tokens // 2) * q.shape[1]
    return pl.pallas_call(
        functools.partial(forward_kernel, rep, hps),
        out_shape=(
            jax.ShapeDtypeStruct(q.shape, jnp.bfloat16),
            jax.ShapeDtypeStruct((kv_heads // hps, hps, q_blocks, rep * BLOCK), jnp.float32),
        ),
        grid_spec=pltpu.PrefetchScalarGridSpec(
            num_scalar_prefetch=3,
            grid=(kv_heads // hps,),
            in_specs=[
                q_spec,
                pl.BlockSpec((tokens, 2 * hps * HEAD_SIZE), lambda g, *_: (0, g)),
            ],
            out_specs=[
                q_spec,
                pl.BlockSpec((1, hps, q_blocks, rep * BLOCK), lambda g, *_: (g, 0, 0, 0)),
            ],
            scratch_shapes=[
                pltpu.SMEM((order.shape[0],), jnp.int32),
                pltpu.VMEM((hps, HEAD_SIZE, rep * BLOCK), jnp.bfloat16),
                pltpu.VMEM((hps, HEAD_SIZE, rep * BLOCK), jnp.float32),
            ],
        ),
        compiler_params=pltpu.CompilerParams(vmem_limit_bytes=56 << 20),
        cost_estimate=pl.CostEstimate(
            flops=flops, bytes_accessed=2 * (q.size * 2 + kv.size), transcendentals=flops // 512
        ),
        name="attention_forward",
    )(order, cont, first, q, kv)


def attention_backward(q, kv, grad_mixed, mixed, lse, order, cont, first):
    kv_heads, rep, hps = attention_sizes(q, kv)
    rows, tokens = q.shape[0], kv.shape[0]
    q_blocks = rows // BLOCK
    wide = hps * rep * HEAD_SIZE
    q_spec = pl.BlockSpec((rows, wide), lambda g, *_: (0, g))
    kv_spec = pl.BlockSpec((tokens, 2 * hps * HEAD_SIZE), lambda g, *_: (0, g))
    flops = 10 * rows * (tokens // 2) * q.shape[1]
    return pl.pallas_call(
        functools.partial(backward_kernel, rep, hps),
        out_shape=(
            jax.ShapeDtypeStruct(q.shape, jnp.bfloat16),
            jax.ShapeDtypeStruct(kv.shape, jnp.bfloat16),
        ),
        grid_spec=pltpu.PrefetchScalarGridSpec(
            num_scalar_prefetch=3,
            grid=(kv_heads // hps,),
            in_specs=[
                q_spec,
                kv_spec,
                q_spec,
                q_spec,
                pl.BlockSpec((1, hps, q_blocks, rep * BLOCK), lambda g, *_: (g, 0, 0, 0)),
            ],
            out_specs=[q_spec, kv_spec],
            scratch_shapes=[
                pltpu.SMEM((order.shape[0],), jnp.int32),
                pltpu.VMEM((hps, HEAD_SIZE, rep * BLOCK), jnp.bfloat16),
                pltpu.VMEM((hps, HEAD_SIZE, rep * BLOCK), jnp.bfloat16),
                pltpu.VMEM((hps, HEAD_SIZE, rep * BLOCK), jnp.float32),
                pltpu.VMEM((tokens, 2 * hps * HEAD_SIZE), jnp.float32),
            ],
        ),
        compiler_params=pltpu.CompilerParams(vmem_limit_bytes=60 << 20),
        cost_estimate=pl.CostEstimate(
            flops=flops, bytes_accessed=4 * (q.size * 2 + kv.size), transcendentals=flops // 1280
        ),
        name="attention_backward",
    )(order, cont, first, q, kv, grad_mixed, mixed, lse)


def body(
    layer_input,
    attn_gain,
    w_query,
    key_matrix,
    value_matrix,
    w_out,
    ffn_gain,
    w_gate,
    w_up,
    w_down,
    cotangent,
    block_order,
    cont_prompt,
):
    local_rows = layer_input.shape[0]
    ctx_count = lax.axis_size("ctx")
    tp_count = lax.axis_size("tp")
    heads = w_query.shape[1] // HEAD_SIZE
    kv_width = key_matrix.shape[1]
    kv_heads = kv_width // HEAD_SIZE
    row_ids = lax.axis_index("ctx") * local_rows + jnp.arange(local_rows, dtype=jnp.int32)
    query_meta = token_meta(row_ids, block_order, cont_prompt)
    cosine, sine = rope_tables(query_meta[2])
    inputs_full = layer_input.astype(jnp.float32)
    inv_one = lax.rsqrt(jnp.mean(inputs_full * inputs_full, axis=-1, keepdims=True) + eps_norm)
    normed_one = inputs_full * inv_one
    first_input = (normed_one * attn_gain).astype(jnp.bfloat16)
    query_lin = plain_dot(first_input, w_query).reshape(local_rows, heads, HEAD_SIZE)
    key_linear = plain_dot(first_input, key_matrix).reshape(local_rows, kv_heads, HEAD_SIZE)
    value_rows = plain_dot(first_input, value_matrix).astype(jnp.bfloat16)
    query_rot = rotate(query_lin, cosine, sine).astype(jnp.bfloat16)
    key_rot = rotate(key_linear, cosine, sine).astype(jnp.bfloat16)
    kv_local = jnp.concatenate(
        [key_rot, value_rows.reshape(local_rows, kv_heads, HEAD_SIZE)], axis=2
    ).reshape(local_rows, 2 * kv_width)
    queries = query_rot.reshape(local_rows, heads * HEAD_SIZE)
    first = (lax.axis_index("ctx") * (local_rows // BLOCK)).astype(jnp.int32).reshape(1)
    kv_all = lax.all_gather(kv_local, "ctx", axis=0, tiled=True)
    mixed_rows, log_total = attention_forward(queries, kv_all, block_order, cont_prompt, first)
    attn_out = lax.psum(plain_dot(mixed_rows, w_out).astype(jnp.bfloat16), "tp").astype(jnp.float32)
    middle = inputs_full + attn_out
    inv_two = lax.rsqrt(jnp.mean(middle * middle, axis=-1, keepdims=True) + eps_norm)
    normed_two = middle * inv_two
    second_in = (normed_two * ffn_gain).astype(jnp.bfloat16)
    gate = plain_dot(second_in, w_gate)
    upward = plain_dot(second_in, w_up)
    sigma = jax.nn.sigmoid(gate)
    swish = gate * sigma
    hidden = (swish * upward).astype(jnp.bfloat16)
    ffn_out = lax.psum(plain_dot(hidden, w_down).astype(jnp.bfloat16), "tp").astype(jnp.float32)
    output = (middle + ffn_out).astype(jnp.bfloat16)
    grad_down = left_dot(hidden, cotangent)
    grad_hidden = right_dot(cotangent, w_down)
    grad_gate = (grad_hidden * upward * sigma * (1.0 + gate * (1.0 - sigma))).astype(jnp.bfloat16)
    grad_upward = (grad_hidden * swish).astype(jnp.bfloat16)
    grad_w_gate = left_dot(second_in, grad_gate)
    grad_w_up = left_dot(second_in, grad_upward)
    grad_second = lax.psum(
        (right_dot(grad_gate, w_gate) + right_dot(grad_upward, w_up)).astype(jnp.bfloat16), "tp"
    ).astype(jnp.float32)
    grad_norm_two, ffn_gain_full = norm_back(grad_second, normed_two, inv_two, ffn_gain)
    grad_middle = cotangent.astype(jnp.float32) + grad_norm_two
    ffn_gain_share = gain_share(ffn_gain_full, ctx_count, tp_count)
    grad_branch = grad_middle.astype(jnp.bfloat16)
    grad_w_out = left_dot(mixed_rows, grad_branch)
    grad_mixed = right_dot(grad_branch, w_out).astype(jnp.bfloat16)
    grad_query_rot, kv_terms = attention_backward(
        queries, kv_all, grad_mixed, mixed_rows, log_total, block_order, cont_prompt, first
    )
    kv_sums = lax.psum_scatter(
        kv_terms.astype(jnp.bfloat16), "ctx", scatter_dimension=0, tiled=True
    ).astype(jnp.float32)
    kv_sums = kv_sums.reshape(local_rows, kv_heads, 2, HEAD_SIZE)
    grad_key_rot = kv_sums[:, :, 0]
    grad_values = kv_sums[:, :, 1].reshape(local_rows, kv_width).astype(jnp.bfloat16)
    grad_key = (
        unrotate(grad_key_rot, cosine, sine).reshape(local_rows, kv_width).astype(jnp.bfloat16)
    )
    grad_query_rows = grad_query_rot.reshape(local_rows, heads, HEAD_SIZE)
    grad_query = (
        unrotate(grad_query_rows, cosine, sine)
        .reshape(local_rows, heads * HEAD_SIZE)
        .astype(jnp.bfloat16)
    )
    grad_w_query = left_dot(first_input, grad_query)
    grad_w_key = left_dot(first_input, grad_key)
    grad_w_value = left_dot(first_input, grad_values)
    grad_first = lax.psum(
        (
            right_dot(grad_query, w_query)
            + right_dot(grad_key, key_matrix)
            + right_dot(grad_values, value_matrix)
        ).astype(jnp.bfloat16),
        "tp",
    ).astype(jnp.float32)
    grad_norm_one, attn_gain_full = norm_back(grad_first, normed_one, inv_one, attn_gain)
    grad_input = (grad_middle + grad_norm_one).astype(jnp.bfloat16)
    attn_gain_share = gain_share(attn_gain_full, ctx_count, tp_count)
    (
        sum_query,
        sum_key,
        sum_value,
        sum_out,
        sum_attn_gain,
        sum_gate,
        sum_up,
        sum_down,
        sum_ffn_gain,
    ) = (
        lax.psum_scatter(
            grad_w_query.astype(jnp.bfloat16), "ctx", scatter_dimension=0, tiled=True
        ).astype(jnp.float32),
        lax.psum_scatter(
            grad_w_key.astype(jnp.bfloat16), "ctx", scatter_dimension=0, tiled=True
        ).astype(jnp.float32),
        lax.psum_scatter(
            grad_w_value.astype(jnp.bfloat16), "ctx", scatter_dimension=0, tiled=True
        ).astype(jnp.float32),
        lax.psum_scatter(
            grad_w_out.astype(jnp.bfloat16), "ctx", scatter_dimension=1, tiled=True
        ).astype(jnp.float32),
        lax.psum_scatter(
            attn_gain_share.astype(jnp.bfloat16), "ctx", scatter_dimension=0, tiled=True
        ).astype(jnp.float32),
        lax.psum_scatter(
            grad_w_gate.astype(jnp.bfloat16), "ctx", scatter_dimension=0, tiled=True
        ).astype(jnp.float32),
        lax.psum_scatter(
            grad_w_up.astype(jnp.bfloat16), "ctx", scatter_dimension=0, tiled=True
        ).astype(jnp.float32),
        lax.psum_scatter(
            grad_down.astype(jnp.bfloat16), "ctx", scatter_dimension=1, tiled=True
        ).astype(jnp.float32),
        lax.psum_scatter(
            ffn_gain_share.astype(jnp.bfloat16), "ctx", scatter_dimension=0, tiled=True
        ).astype(jnp.float32),
    )
    return (
        output,
        grad_input,
        sum_attn_gain.reshape(-1),
        sum_query,
        sum_key,
        sum_value,
        sum_out,
        sum_ffn_gain.reshape(-1),
        sum_gate,
        sum_up,
        sum_down,
    )


def solution(mesh):
    placed = (
        P("ctx", None),
        P(),
        P(None, "tp"),
        P(None, "tp"),
        P(None, "tp"),
        P("tp", None),
        P(),
        P(None, "tp"),
        P(None, "tp"),
        P("tp", None),
        P("ctx", None),
        P(),
        P(),
    )
    return jax.shard_map(
        body,
        mesh=mesh,
        in_specs=placed,
        out_specs=(
            P("ctx", None),
            P("ctx", None),
            P(("ctx", "tp")),
            P("ctx", "tp"),
            P("ctx", "tp"),
            P("ctx", "tp"),
            P("tp", "ctx"),
            P(("ctx", "tp")),
            P("ctx", "tp"),
            P("ctx", "tp"),
            P("tp", "ctx"),
        ),
        check_vma=False,
    )
```

```python
import functools
import math

import jax
import jax.numpy as jnp
import numpy as np
from jax import lax
from jax.experimental import pallas as pl
from jax.experimental.pallas import tpu as pltpu
from jax.sharding import PartitionSpec as P

HEAD_SIZE = 128
PROMPT = 2048
CONT_LEN = 256
CONTS = 8
BLOCK = 128
PER_PROMPT = PROMPT // BLOCK
PER_CONT = CONT_LEN // BLOCK
LOG2E = 1.4426950408889634
NEG = -1e30
SLOTS = 4

eps_norm = 1e-05
rope_base = 1000000.0

SLOT_XOR = (0, 2, 1, 3)


def plain_dot(left, right):
    return jnp.dot(left, right, preferred_element_type=jnp.float32)


def left_dot(left, right):
    return lax.dot_general(
        left, right, (((0,), (0,)), ((), ())), preferred_element_type=jnp.float32
    )


def right_dot(left, right):
    return lax.dot_general(
        left, right, (((1,), (1,)), ((), ())), preferred_element_type=jnp.float32
    )


def slot_quarter(slot, tensor):
    return ((slot & 1) * 2 + lax.shift_right_logical(slot, 1)) ^ tensor


def stored_block(index, tensor):
    return (index & ~3) + slot_quarter(index & 3, tensor)


def block_plan(order_ref, cont_ref, where_ref, slot):
    count = cont_ref.shape[0]
    prompt_blocks = count // CONTS * PER_PROMPT
    own = order_ref[where_ref[0] * SLOTS + slot_quarter(slot, where_ref[1])]
    is_prompt = own < prompt_blocks
    offset = own - prompt_blocks
    which = jnp.clip(lax.div(offset, PER_CONT), 0, count - 1)
    group = jnp.where(is_prompt, lax.div(own, PER_PROMPT), cont_ref[which])
    inner = jnp.where(is_prompt, lax.rem(own, PER_PROMPT), lax.rem(offset, PER_CONT))
    has_prev = lax.rem(inner, 2)
    pairs = jnp.where(is_prompt, lax.div(inner, 2), PER_PROMPT // 2)
    prev = own - has_prev
    return group * PER_PROMPT, pairs, prev, own, has_prev


def fill_inverse(order_ref, where_ref, inverse_ref):
    def put(index, carry):
        inverse_ref[order_ref[stored_block(index, where_ref[1])]] = index
        return carry

    lax.fori_loop(0, order_ref.shape[0], put, 0)


def rotate(vec, cosine, sine):
    return vec * cosine + pltpu.roll(vec, HEAD_SIZE // 2, 1) * sine


def unrotate(vec, cosine, sine):
    return vec * cosine + pltpu.roll(vec * sine, HEAD_SIZE // 2, 1)


def angle_tables():
    half = HEAD_SIZE // 2
    freq = np.float64(rope_base) ** (-(2.0 * np.arange(half) / HEAD_SIZE))
    freq = np.concatenate([freq, freq])
    starts = np.arange(-(-(PER_PROMPT + PER_CONT) // 8) * 8) * BLOCK
    start = starts[:, None] * freq[None]
    inner = np.arange(BLOCK)[:, None] * freq[None]
    return tuple(
        f(a).astype(np.float32) for a in (start, inner) for f in (np.cos, np.sin)
    )


def key_rows(inverse_ref, logical):
    return pl.ds(pl.multiple_of(inverse_ref[logical] * BLOCK, BLOCK), BLOCK)


def tile_pair(ref, rows_a, rows_b, column):
    cols = pl.ds(column, HEAD_SIZE)
    return jnp.concatenate([ref[rows_a, cols], ref[rows_b, cols]], axis=0)


def own_mask(has_prev, rep):
    shape = (2 * BLOCK, rep * BLOCK)
    row = lax.broadcasted_iota(jnp.int32, shape, 0)
    col = lax.broadcasted_iota(jnp.int32, shape, 1)
    first_row = BLOCK * (1 - has_prev)
    return (row >= first_row) & (row - BLOCK <= lax.rem(col, BLOCK))


def stack_t(ref, rows, column, rep):
    return jnp.concatenate(
        [ref[rows, pl.ds(column + r * HEAD_SIZE, HEAD_SIZE)].T for r in range(rep)], axis=1
    )


def stack_rows(ref, rows, column, rep):
    return jnp.concatenate(
        [ref[rows, pl.ds(column + r * HEAD_SIZE, HEAD_SIZE)] for r in range(rep)], axis=0
    )


def dot(left, right):
    return jnp.dot(left, right, preferred_element_type=jnp.float32)


def forward_kernel(rep, hps, order_ref, cont_ref, where_ref, q_ref, kv_ref, out_ref, lse_ref,
                   inverse_ref, qt_ref, acc_ref):
    fill_inverse(order_ref, where_ref, inverse_ref)
    q_blocks = q_ref.shape[0] // BLOCK
    factor = LOG2E / math.sqrt(HEAD_SIZE)
    width = rep * HEAD_SIZE

    def one_query_block(qb, carry):
        base, pairs, prev, own, has_prev = block_plan(order_ref, cont_ref, where_ref, qb)
        rows = pl.ds(pl.multiple_of(qb * BLOCK, BLOCK), BLOCK)
        mask = own_mask(has_prev, rep)
        rows_a, rows_b = key_rows(inverse_ref, prev), key_rows(inverse_ref, own)
        state = []
        for h in range(hps):
            qt = stack_t(q_ref, rows, h * width, rep)
            qt_ref[h] = qt
            scores = dot(tile_pair(kv_ref, rows_a, rows_b, 2 * h * HEAD_SIZE), qt) * factor
            scores = jnp.where(mask, scores, NEG)
            best = jnp.max(scores, axis=0, keepdims=True)
            weights = jnp.exp2(scores - best)
            total = jnp.sum(weights, axis=0, keepdims=True)
            values = tile_pair(kv_ref, rows_a, rows_b, (2 * h + 1) * HEAD_SIZE)
            acc_ref[h] = dot(values.T, weights.astype(jnp.bfloat16))
            state += [best, total]

        def one_pair(t, state):
            rows_a = key_rows(inverse_ref, base + 2 * t)
            rows_b = key_rows(inverse_ref, base + 2 * t + 1)
            after = []
            for h in range(hps):
                best, total = state[2 * h], state[2 * h + 1]
                keys = tile_pair(kv_ref, rows_a, rows_b, 2 * h * HEAD_SIZE)
                scores = dot(keys, qt_ref[h]) * factor
                newest = jnp.maximum(best, jnp.max(scores, axis=0, keepdims=True))
                weights = jnp.exp2(scores - newest)
                shrink = jnp.exp2(best - newest)
                total = total * shrink + jnp.sum(weights, axis=0, keepdims=True)
                values = tile_pair(kv_ref, rows_a, rows_b, (2 * h + 1) * HEAD_SIZE)
                acc_ref[h] = acc_ref[h] * shrink + dot(values.T, weights.astype(jnp.bfloat16))
                after += [newest, total]
            return tuple(after)

        state = lax.fori_loop(0, pairs, one_pair, tuple(state))
        for h in range(hps):
            best, total = state[2 * h], state[2 * h + 1]
            mixed = acc_ref[h] * (1.0 / total)
            for r in range(rep):
                part = mixed[:, r * BLOCK : (r + 1) * BLOCK]
                out_ref[rows, pl.ds(h * width + r * HEAD_SIZE, HEAD_SIZE)] = part.T.astype(
                    jnp.bfloat16
                )
            lse_ref[0, h, pl.ds(qb, 1), :] = best + jnp.log2(total)
        return carry

    lax.fori_loop(0, q_blocks, one_query_block, 0)


def backward_kernel(rep, hps, order_ref, cont_ref, where_ref, q_ref, kv_ref, gm_ref, mix_ref,
                    lse_ref, cos_ref, sin_ref, gq_ref, keep_ref, send_ref, inverse_ref, qt_ref, gmt_ref, gqt_ref, acc_ref):
    fill_inverse(order_ref, where_ref, inverse_ref)
    q_blocks = q_ref.shape[0] // BLOCK
    scale = 1.0 / math.sqrt(HEAD_SIZE)
    factor = LOG2E * scale
    width = rep * HEAD_SIZE

    def clear(i, carry):
        acc_ref[pl.ds(pl.multiple_of(i * BLOCK, BLOCK), BLOCK), :] = jnp.zeros(
            (BLOCK, acc_ref.shape[1]), jnp.float32
        )
        return carry

    lax.fori_loop(0, order_ref.shape[0], clear, 0)

    def tile_terms(h, rows_a, rows_b, lse, delta, q_rows, gm_rows, mask):
        kcol, vcol = 2 * h * HEAD_SIZE, (2 * h + 1) * HEAD_SIZE
        keys = tile_pair(kv_ref, rows_a, rows_b, kcol)
        values = tile_pair(kv_ref, rows_a, rows_b, vcol)
        weights = jnp.exp2(dot(keys, qt_ref[h]) * factor - lse)
        if mask is not None:
            weights = jnp.where(mask, weights, 0.0)
        grad_weights = dot(values, gmt_ref[h])
        grad_scores = (weights * (grad_weights - delta)).astype(jnp.bfloat16)
        gv = dot(weights.astype(jnp.bfloat16), gm_rows)
        gk = dot(grad_scores, q_rows)
        acc_ref[rows_a, pl.ds(kcol, HEAD_SIZE)] += gk[:BLOCK]
        acc_ref[rows_b, pl.ds(kcol, HEAD_SIZE)] += gk[BLOCK:]
        acc_ref[rows_a, pl.ds(vcol, HEAD_SIZE)] += gv[:BLOCK]
        acc_ref[rows_b, pl.ds(vcol, HEAD_SIZE)] += gv[BLOCK:]
        return dot(keys.T, grad_scores)

    def one_query_block(qb, carry):
        base, pairs, prev, own, has_prev = block_plan(order_ref, cont_ref, where_ref, qb)
        rows = pl.ds(pl.multiple_of(qb * BLOCK, BLOCK), BLOCK)
        mask = own_mask(has_prev, rep)
        rows_a, rows_b = key_rows(inverse_ref, prev), key_rows(inverse_ref, own)
        deltas, lses, q_stack, gm_stack = [], [], [], []
        for h in range(hps):
            qt_ref[h] = stack_t(q_ref, rows, h * width, rep)
            gmt = stack_t(gm_ref, rows, h * width, rep)
            gmt_ref[h] = gmt
            mixt = stack_t(mix_ref, rows, h * width, rep)
            deltas.append(
                jnp.sum(
                    gmt.astype(jnp.float32) * mixt.astype(jnp.float32), axis=0, keepdims=True
                )
            )
            lses.append(lse_ref[0, h, pl.ds(qb, 1), :])
        for h in range(hps):
            q_rows = stack_rows(q_ref, rows, h * width, rep)
            gm_rows = stack_rows(gm_ref, rows, h * width, rep)
            gqt_ref[h] = tile_terms(
                h, rows_a, rows_b, lses[h], deltas[h], q_rows, gm_rows, mask
            )

        def one_pair(t, carry):
            rows_a = key_rows(inverse_ref, base + 2 * t)
            rows_b = key_rows(inverse_ref, base + 2 * t + 1)
            for h in range(hps):
                q_rows = stack_rows(q_ref, rows, h * width, rep)
                gm_rows = stack_rows(gm_ref, rows, h * width, rep)
                gqt_ref[h] += tile_terms(
                    h, rows_a, rows_b, lses[h], deltas[h], q_rows, gm_rows, None
                )
            return carry

        lax.fori_loop(0, pairs, one_pair, 0)
        for h in range(hps):
            total = gqt_ref[h] * scale
            for r in range(rep):
                part = total[:, r * BLOCK : (r + 1) * BLOCK]
                rounded = part.T.astype(jnp.bfloat16).astype(jnp.float32)
                gq_ref[rows, pl.ds(h * width + r * HEAD_SIZE, HEAD_SIZE)] = unrotate(
                    rounded, cos_ref[rows, :], sin_ref[rows, :]
                ).astype(jnp.bfloat16)
        return carry

    lax.fori_loop(0, q_blocks, one_query_block, 0)

    blocks = order_ref.shape[0]
    ctx_count = blocks // SLOTS

    def place(index):
        chunk = lax.div(index, SLOTS) ^ where_ref[0]
        spot = (chunk & 1) * (ctx_count // 2) + (chunk & 2) // 2 * (ctx_count // 4) + (
            lax.shift_right_logical(chunk, 2)
        )
        return spot * SLOTS + (index & 3)

    def flush(i, carry):
        rows = pl.ds(pl.multiple_of(i * BLOCK, BLOCK), BLOCK)
        spot = place(i)
        parts = []
        for h in range(hps):
            parts.append(acc_ref[rows, pl.ds(2 * h * HEAD_SIZE, HEAD_SIZE)] * scale)
            parts.append(acc_ref[rows, pl.ds((2 * h + 1) * HEAD_SIZE, HEAD_SIZE)])
        value = jnp.concatenate(parts, axis=1).astype(jnp.bfloat16)

        @pl.when(spot < blocks // 2)
        def _():
            keep_ref[pl.ds(pl.multiple_of(spot * BLOCK, BLOCK), BLOCK), :] = value

        @pl.when(spot >= blocks // 2)
        def _():
            far = (spot - blocks // 2) * BLOCK
            send_ref[pl.ds(pl.multiple_of(far, BLOCK), BLOCK), :] = value

        return carry

    lax.fori_loop(0, blocks, flush, 0)


def attention_sizes(q, kv):
    kv_heads = kv.shape[1] // (2 * HEAD_SIZE)
    rep = q.shape[1] // HEAD_SIZE // kv_heads
    hps = kv_heads if kv.shape[0] <= 8192 else 1
    return kv_heads, rep, hps


def attention_forward(q, kv, order, cont, where):
    kv_heads, rep, hps = attention_sizes(q, kv)
    rows, tokens = q.shape[0], kv.shape[0]
    q_blocks = rows // BLOCK
    wide = hps * rep * HEAD_SIZE
    q_spec = pl.BlockSpec((rows, wide), lambda g, *_: (0, g))
    flops = 4 * rows * (tokens // 2) * q.shape[1]
    return pl.pallas_call(
        functools.partial(forward_kernel, rep, hps),
        out_shape=(
            jax.ShapeDtypeStruct(q.shape, jnp.bfloat16),
            jax.ShapeDtypeStruct((kv_heads // hps, hps, q_blocks, rep * BLOCK), jnp.float32),
        ),
        grid_spec=pltpu.PrefetchScalarGridSpec(
            num_scalar_prefetch=3,
            grid=(kv_heads // hps,),
            in_specs=[
                q_spec,
                pl.BlockSpec((tokens, 2 * hps * HEAD_SIZE), lambda g, *_: (0, g)),
            ],
            out_specs=[
                q_spec,
                pl.BlockSpec((1, hps, q_blocks, rep * BLOCK), lambda g, *_: (g, 0, 0, 0)),
            ],
            scratch_shapes=[
                pltpu.SMEM((order.shape[0],), jnp.int32),
                pltpu.VMEM((hps, HEAD_SIZE, rep * BLOCK), jnp.bfloat16),
                pltpu.VMEM((hps, HEAD_SIZE, rep * BLOCK), jnp.float32),
            ],
        ),
        compiler_params=pltpu.CompilerParams(vmem_limit_bytes=56 << 20),
        cost_estimate=pl.CostEstimate(
            flops=flops, bytes_accessed=2 * (q.size * 2 + kv.size), transcendentals=flops // 512
        ),
        name="attention_forward",
    )(order, cont, where, q, kv)


def attention_backward(head, q, kv, grad_mixed, mixed, lse, cosine, sine, order, cont, where):
    kv_heads, rep, _ = attention_sizes(q, kv)
    hps_forward = lse.shape[1]
    rows, tokens = q.shape[0], kv.shape[0]
    q_blocks = rows // BLOCK
    wide = rep * HEAD_SIZE
    q_spec = pl.BlockSpec((rows, wide), lambda g, *_: (0, head))
    kv_spec = pl.BlockSpec((tokens, 2 * HEAD_SIZE), lambda g, *_: (0, head))
    lse_spec = pl.BlockSpec(
        (1, 1, q_blocks, rep * BLOCK),
        lambda g, *_: (head // hps_forward, head % hps_forward, 0, 0),
    )
    whole = lambda g, *_: (0, 0)
    table_spec = pl.BlockSpec((rows, HEAD_SIZE), whole)
    half = (tokens // 2, 2 * HEAD_SIZE)
    flops = 10 * rows * (tokens // 2) * wide
    return pl.pallas_call(
        functools.partial(backward_kernel, rep, 1),
        out_shape=(
            jax.ShapeDtypeStruct((rows, wide), jnp.bfloat16),
            jax.ShapeDtypeStruct(half, jnp.bfloat16),
            jax.ShapeDtypeStruct(half, jnp.bfloat16),
        ),
        grid_spec=pltpu.PrefetchScalarGridSpec(
            num_scalar_prefetch=3,
            grid=(1,),
            in_specs=[q_spec, kv_spec, q_spec, q_spec, lse_spec, table_spec, table_spec],
            out_specs=[
                pl.BlockSpec((rows, wide), whole),
                pl.BlockSpec(half, whole),
                pl.BlockSpec(half, whole),
            ],
            scratch_shapes=[
                pltpu.SMEM((order.shape[0],), jnp.int32),
                pltpu.VMEM((1, HEAD_SIZE, rep * BLOCK), jnp.bfloat16),
                pltpu.VMEM((1, HEAD_SIZE, rep * BLOCK), jnp.bfloat16),
                pltpu.VMEM((1, HEAD_SIZE, rep * BLOCK), jnp.float32),
                pltpu.VMEM((tokens, 2 * HEAD_SIZE), jnp.float32),
            ],
        ),
        compiler_params=pltpu.CompilerParams(vmem_limit_bytes=56 << 20),
        cost_estimate=pl.CostEstimate(
            flops=flops,
            bytes_accessed=4 * (rows * wide * 2 + tokens * 2 * HEAD_SIZE),
            transcendentals=flops // 1280,
        ),
        name=f"attention_backward_{head}",
    )(order, cont, where, q, kv, grad_mixed, mixed, lse, cosine, sine)


def input_kernel(order_ref, cont_ref, where_ref, x_ref, gain_ref, wq_ref, wk_ref, wv_ref,
                 cos_start_ref, sin_start_ref, cos_in_ref, sin_in_ref,
                 first_ref, q_ref, kv_ref, cos_ref, sin_ref):
    count = cont_ref.shape[0]
    prompt_blocks = count // CONTS * PER_PROMPT
    lane = lax.broadcasted_iota(jnp.int32, (BLOCK, HEAD_SIZE), 1)

    def one_slot(slot, carry):
        quarter = slot_quarter(slot, where_ref[1])
        rows = pl.ds(pl.multiple_of(slot * BLOCK, BLOCK), BLOCK)
        full = x_ref[pl.ds(pl.multiple_of(quarter * BLOCK, BLOCK), BLOCK), :].astype(jnp.float32)
        inv = lax.rsqrt(jnp.mean(full * full, axis=-1, keepdims=True) + eps_norm)
        first_ref[rows, :] = (full * inv * gain_ref[...]).astype(jnp.bfloat16)
        own = order_ref[where_ref[0] * SLOTS + quarter]
        spot = jnp.where(
            own < prompt_blocks,
            lax.rem(own, PER_PROMPT),
            PER_PROMPT + lax.rem(own - prompt_blocks, PER_CONT),
        )
        cos_start, sin_start = cos_start_ref[pl.ds(spot, 1), :], sin_start_ref[pl.ds(spot, 1), :]
        cos_in, sin_in = cos_in_ref[...], sin_in_ref[...]
        sine = sin_start * cos_in + cos_start * sin_in
        cos_ref[rows, :] = cos_start * cos_in - sin_start * sin_in
        sin_ref[rows, :] = jnp.where(lane < HEAD_SIZE // 2, -sine, sine)
        return carry

    lax.fori_loop(0, SLOTS, one_slot, 0)
    first = first_ref[...]
    cosine, sine = cos_ref[...], sin_ref[...]
    kv_heads = wk_ref.shape[1] // HEAD_SIZE
    for h in range(kv_heads):
        cols = slice(h * HEAD_SIZE, (h + 1) * HEAD_SIZE)
        key = rotate(plain_dot(first, wk_ref[:, cols]), cosine, sine)
        value = plain_dot(first, wv_ref[:, cols])
        kv_ref[:, 2 * h * HEAD_SIZE : (2 * h + 1) * HEAD_SIZE] = key.astype(jnp.bfloat16)
        kv_ref[:, (2 * h + 1) * HEAD_SIZE : (2 * h + 2) * HEAD_SIZE] = value.astype(jnp.bfloat16)
    for h in range(wq_ref.shape[1] // HEAD_SIZE):
        cols = slice(h * HEAD_SIZE, (h + 1) * HEAD_SIZE)
        query = rotate(plain_dot(first, wq_ref[:, cols]), cosine, sine)
        q_ref[:, cols] = query.astype(jnp.bfloat16)


def input_stage(x, gain, wq, wk, wv, order, cont, where):
    rows, model = x.shape
    tables = angle_tables()
    smem = pl.BlockSpec(memory_space=pltpu.SMEM)
    vmem = pl.BlockSpec(memory_space=pltpu.VMEM)
    flops = 2 * rows * model * (wq.shape[1] + 2 * wk.shape[1])
    return pl.pallas_call(
        input_kernel,
        out_shape=(
            jax.ShapeDtypeStruct((rows, model), jnp.bfloat16),
            jax.ShapeDtypeStruct((rows, wq.shape[1]), jnp.bfloat16),
            jax.ShapeDtypeStruct((rows, 2 * wk.shape[1]), jnp.bfloat16),
            jax.ShapeDtypeStruct((rows, HEAD_SIZE), jnp.float32),
            jax.ShapeDtypeStruct((rows, HEAD_SIZE), jnp.float32),
        ),
        in_specs=[smem] * 3 + [vmem] * 9,
        out_specs=[vmem] * 5,
        compiler_params=pltpu.CompilerParams(vmem_limit_bytes=40 << 20),
        cost_estimate=pl.CostEstimate(
            flops=flops, bytes_accessed=4 * x.size + 2 * wq.size + 4 * wk.size, transcendentals=0
        ),
        name="input_stage",
    )(order, cont, where, x, gain.reshape(1, -1), wq, wk, wv, *tables)


def kv_finish_kernel(keep_ref, got_ref, cos_ref, sin_ref, gk_ref, gv_ref):
    total = keep_ref[...].astype(jnp.float32) + got_ref[...].astype(jnp.float32)
    total = total.astype(jnp.bfloat16)
    key = total[:, :HEAD_SIZE].astype(jnp.float32)
    gk_ref[...] = unrotate(key, cos_ref[...], sin_ref[...]).astype(jnp.bfloat16)
    gv_ref[...] = total[:, HEAD_SIZE:]


def kv_finish(keep, got, cosine, sine):
    rows = keep.shape[0]
    vmem = pl.BlockSpec(memory_space=pltpu.VMEM)
    shape = jax.ShapeDtypeStruct((rows, HEAD_SIZE), jnp.bfloat16)
    return pl.pallas_call(
        kv_finish_kernel,
        out_shape=(shape, shape),
        in_specs=[vmem] * 4,
        out_specs=[vmem] * 2,
        cost_estimate=pl.CostEstimate(
            flops=8 * keep.size, bytes_accessed=6 * keep.size, transcendentals=0
        ),
        name="kv_finish",
    )(keep, got, cosine, sine)


def flip(value, axis, mask):
    return lax.ppermute(value, axis, [(i, i ^ mask) for i in range(lax.axis_size(axis))])


def add(left, right):
    return (left.astype(jnp.float32) + right.astype(jnp.float32)).astype(jnp.bfloat16)


def slots_of(value, tensor):
    rows = value.shape[0] // SLOTS
    return jnp.concatenate(
        [
            lax.dynamic_slice_in_dim(value, (tensor ^ SLOT_XOR[u]) * rows, rows)
            for u in range(SLOTS)
        ]
    )


def gather_slots(own):
    other = flip(own, "tp", 2)
    return jnp.concatenate([own, other, flip(own, "tp", 1), flip(other, "tp", 1)])


def gather_rows(own, tensor):
    rows = own.shape[0]
    other = flip(own, "tp", 2)
    pieces = (own, other, flip(own, "tp", 1), flip(other, "tp", 1))
    result = jnp.zeros((SLOTS * rows,) + own.shape[1:], own.dtype)
    for u in range(SLOTS):
        result = lax.dynamic_update_slice_in_dim(
            result, pieces[u], (tensor ^ SLOT_XOR[u]) * rows, 0
        )
    return result


def scatter_slots(partial):
    half = partial.shape[0] // 2
    pair = add(partial[:half], flip(partial[half:], "tp", 1))
    quarter = half // 2
    return pair[:quarter], flip(pair[quarter:], "tp", 2)


def high_masks(ctx_count):
    masks, mask = [], ctx_count // 2
    while mask >= 4:
        masks.append(mask)
        mask //= 2
    return masks


def step(parts, axis_bits, mask, index):
    mine = lax.dynamic_index_in_dim(parts, index, axis_bits, keepdims=False)
    away = lax.dynamic_index_in_dim(parts, 1 - index, axis_bits, keepdims=False)
    return mine, flip(away, "ctx", mask)


def bits_of(ctx, ctx_count):
    return [(ctx // mask) % 2 for mask in high_masks(ctx_count)]


def reduce_attention(partial, ctx, ctx_count):
    highs = high_masks(ctx_count)
    width = partial.shape[1]
    rows = partial.shape[0] // ctx_count
    shaped = partial.astype(jnp.bfloat16).reshape((2,) * len(highs) + (2, 2, rows, width))
    mine, got = step(shaped, len(highs) + 1, 1, ctx % 2)
    shaped = add(mine, got)
    mine, got = step(shaped, len(highs), 2, ctx // 2 % 2)
    for mask, bit in zip(highs, bits_of(ctx, ctx_count)):
        shaped = add(mine, got)
        mine, got = step(shaped, 0, mask, bit)
    return mine.astype(jnp.float32) + got.astype(jnp.float32)


def reduce_ffn(partial, ctx, ctx_count):
    highs = high_masks(ctx_count)
    width = partial.shape[1]
    rows = partial.shape[0] // ctx_count
    shaped = partial.astype(jnp.bfloat16).reshape((2,) * len(highs) + (2, 2, rows, width))
    mine, got = step(shaped, len(highs) + 1, 1, ctx % 2)
    for mask, bit in zip(highs, bits_of(ctx, ctx_count)):
        shaped = add(mine, got)
        mine, got = step(shaped, 0, mask, bit)
    shaped = add(mine, got)
    pair = ctx // 2 % 2
    mine, got = step(shaped, 0, 2, pair)
    low, high = jnp.where(pair == 0, mine, got), jnp.where(pair == 0, got, mine)
    return jnp.concatenate([low, high], axis=1).astype(jnp.float32)


def reduce_kv(keep, send, ctx_count):
    got = flip(send, "ctx", 1)
    for mask in [2] + high_masks(ctx_count):
        total = add(keep, got)
        half = total.shape[0] // 2
        keep, got = total[:half], flip(total[half:], "ctx", mask)
    return keep, got


def norm_back(grad_out, normed, inv_scale, gain):
    scaled = grad_out * gain
    inner = jnp.mean(scaled * normed, axis=-1, keepdims=True)
    return (inv_scale * (scaled - normed * inner), jnp.sum(grad_out * normed, axis=0))


def body(
    layer_input,
    attn_gain,
    w_query,
    key_matrix,
    value_matrix,
    w_out,
    ffn_gain,
    w_gate,
    w_up,
    w_down,
    cotangent,
    block_order,
    cont_prompt,
):
    ctx_count = lax.axis_size("ctx")
    tp_count = lax.axis_size("tp")
    ctx, tensor = lax.axis_index("ctx"), lax.axis_index("tp")
    pair = ctx // 2 % 2
    where = jnp.stack([ctx, tensor]).astype(jnp.int32)
    quarter = layer_input.shape[0] // SLOTS
    kv_heads = key_matrix.shape[1] // HEAD_SIZE
    half_units = w_gate.shape[1] // 2

    first_input, queries, kv_local, cosine, sine = input_stage(
        layer_input, attn_gain, w_query, key_matrix, value_matrix, block_order, cont_prompt, where
    )
    kv_all = lax.all_gather(kv_local, "ctx", axis=0, tiled=True)

    gate_half = lax.dynamic_slice_in_dim(w_gate, pair * half_units, half_units, 1)
    up_half = lax.dynamic_slice_in_dim(w_up, pair * half_units, half_units, 1)
    down_half = lax.dynamic_slice_in_dim(w_down, pair * half_units, half_units, 0)
    cot_own = lax.dynamic_slice_in_dim(cotangent, tensor * quarter, quarter)
    cot_rows = jnp.concatenate(
        [slots_of(cotangent, tensor), gather_slots(flip(cot_own, "ctx", 2))]
    )
    grad_hidden = right_dot(cot_rows, down_half)

    mixed, log_total = attention_forward(
        queries, kv_all, block_order, cont_prompt, where
    )
    mine, got = scatter_slots(plain_dot(mixed, w_out).astype(jnp.bfloat16))
    own_input = lax.dynamic_slice_in_dim(layer_input, tensor * quarter, quarter)
    own_input = own_input.astype(jnp.float32)
    middle = own_input + (mine.astype(jnp.float32) + got.astype(jnp.float32))
    inv_two = lax.rsqrt(jnp.mean(middle * middle, axis=-1, keepdims=True) + eps_norm)
    normed_two = middle * inv_two
    second_own = (normed_two * ffn_gain).astype(jnp.bfloat16)
    second_in = jnp.concatenate(
        [gather_slots(second_own), gather_slots(flip(second_own, "ctx", 2))]
    )

    gate = plain_dot(second_in, gate_half)
    upward = plain_dot(second_in, up_half)
    sigma = jax.nn.sigmoid(gate)
    swish = gate * sigma
    hidden = (swish * upward).astype(jnp.bfloat16)
    grad_gate = (grad_hidden * upward * sigma * (1.0 + gate * (1.0 - sigma))).astype(jnp.bfloat16)
    grad_upward = (grad_hidden * swish).astype(jnp.bfloat16)

    sum_down = reduce_ffn(left_dot(cot_rows, hidden), ctx, ctx_count).T
    local = layer_input.shape[0]

    def pair_sum(partial):
        mine, got = scatter_slots(partial[local:])
        away = flip(add(mine, got), "ctx", 2)
        mine, got = scatter_slots(partial[:local])
        return (mine.astype(jnp.float32) + got.astype(jnp.float32)) + away.astype(jnp.float32)

    grad_second = pair_sum(
        (right_dot(grad_gate, gate_half) + right_dot(grad_upward, up_half)).astype(jnp.bfloat16)
    )
    sum_gate = reduce_ffn(left_dot(second_in, grad_gate), ctx, ctx_count)
    sum_up = reduce_ffn(left_dot(second_in, grad_upward), ctx, ctx_count)

    grad_norm_two, ffn_gain_part = norm_back(grad_second, normed_two, inv_two, ffn_gain)
    own_cot = cot_own.astype(jnp.float32)
    grad_middle = own_cot + grad_norm_two
    grad_branch = gather_slots(grad_middle.astype(jnp.bfloat16))
    grad_mixed = right_dot(grad_branch, w_out).astype(jnp.bfloat16)
    sum_out = reduce_attention(left_dot(grad_branch, mixed), ctx, ctx_count).T

    ffn_out = pair_sum(plain_dot(hidden, down_half).astype(jnp.bfloat16))
    output = gather_rows((middle + ffn_out).astype(jnp.bfloat16), tensor)

    grad_queries, grad_keys, grad_values = [], [], []
    for head in range(kv_heads):
        grad_q, keep, send = attention_backward(
            head, queries, kv_all, grad_mixed, mixed, log_total, cosine, sine,
            block_order, cont_prompt, where,
        )
        grad_queries.append(grad_q)
        grad_k, grad_v = kv_finish(*reduce_kv(keep, send, ctx_count), cosine, sine)
        grad_keys.append(grad_k)
        grad_values.append(grad_v)
    grad_query = jnp.concatenate(grad_queries, axis=1)
    grad_key = jnp.concatenate(grad_keys, axis=1)
    grad_value = jnp.concatenate(grad_values, axis=1)
    sum_query = reduce_attention(left_dot(first_input, grad_query), ctx, ctx_count)
    sum_kv = reduce_attention(
        jnp.concatenate(
            [left_dot(first_input, grad_key), left_dot(first_input, grad_value)], axis=1
        ),
        ctx,
        ctx_count,
    )
    sum_key, sum_value = jnp.split(sum_kv, 2, axis=1)
    grad_first_partial = (
        right_dot(grad_query, w_query)
        + right_dot(grad_key, key_matrix)
        + right_dot(grad_value, value_matrix)
    )
    mine, got = scatter_slots(grad_first_partial.astype(jnp.bfloat16))
    grad_first = mine.astype(jnp.float32) + got.astype(jnp.float32)
    inv_one = lax.rsqrt(jnp.mean(own_input * own_input, axis=-1, keepdims=True) + eps_norm)
    grad_norm_one, attn_gain_part = norm_back(grad_first, own_input * inv_one, inv_one, attn_gain)
    grad_input = gather_rows((grad_middle + grad_norm_one).astype(jnp.bfloat16), tensor)

    devices = ctx_count * tp_count
    gains = jnp.stack([attn_gain_part, ffn_gain_part]).reshape(2, devices, -1)
    gains = lax.all_to_all(gains, ("ctx", "tp"), 1, 1, tiled=True)
    gains = jnp.sum(gains, axis=1)
    return (
        output,
        grad_input,
        gains[0],
        sum_query,
        sum_key,
        sum_value,
        sum_out,
        gains[1],
        sum_gate,
        sum_up,
        sum_down,
    )


def solution(mesh):
    placed = (
        P("ctx", None),
        P(),
        P(None, "tp"),
        P(None, "tp"),
        P(None, "tp"),
        P("tp", None),
        P(),
        P(None, "tp"),
        P(None, "tp"),
        P("tp", None),
        P("ctx", None),
        P(),
        P(),
    )
    return jax.shard_map(
        body,
        mesh=mesh,
        in_specs=placed,
        out_specs=(
            P("ctx", None),
            P("ctx", None),
            P(("ctx", "tp")),
            P("ctx", "tp"),
            P("ctx", "tp"),
            P("ctx", "tp"),
            P("tp", "ctx"),
            P(("ctx", "tp")),
            P("ctx", "tp"),
            P("ctx", "tp"),
            P("tp", "ctx"),
        ),
        check_vma=False,
    )
```

```python
import functools
import math

import jax
import jax.numpy as jnp
import numpy as np
from jax import lax
from jax.experimental import pallas as pl
from jax.experimental.pallas import tpu as pltpu
from jax.sharding import PartitionSpec as P

HEAD_SIZE = 128
PROMPT = 2048
CONT_LEN = 256
CONTS = 8
BLOCK = 128
PER_PROMPT = PROMPT // BLOCK
PER_CONT = CONT_LEN // BLOCK
LOG2E = 1.4426950408889634
NEG = -1e30
SLOTS = 4

eps_norm = 1e-05
rope_base = 1000000.0

SLOT_XOR = (0, 2, 1, 3)


def plain_dot(left, right):
    return jnp.dot(left, right, preferred_element_type=jnp.float32)


def left_dot(left, right):
    return lax.dot_general(
        left, right, (((0,), (0,)), ((), ())), preferred_element_type=jnp.float32
    )


def right_dot(left, right):
    return lax.dot_general(
        left, right, (((1,), (1,)), ((), ())), preferred_element_type=jnp.float32
    )


def slot_quarter(slot, tensor):
    return ((slot & 1) * 2 + lax.shift_right_logical(slot, 1)) ^ tensor


def stored_block(index, tensor):
    return (index & ~3) + slot_quarter(index & 3, tensor)


def block_plan(order_ref, cont_ref, where_ref, slot):
    count = cont_ref.shape[0]
    prompt_blocks = count // CONTS * PER_PROMPT
    own = order_ref[where_ref[0] * SLOTS + slot_quarter(slot, where_ref[1])]
    is_prompt = own < prompt_blocks
    offset = own - prompt_blocks
    which = jnp.clip(lax.div(offset, PER_CONT), 0, count - 1)
    group = jnp.where(is_prompt, lax.div(own, PER_PROMPT), cont_ref[which])
    inner = jnp.where(is_prompt, lax.rem(own, PER_PROMPT), lax.rem(offset, PER_CONT))
    has_prev = lax.rem(inner, 2)
    pairs = jnp.where(is_prompt, lax.div(inner, 2), PER_PROMPT // 2)
    prev = own - has_prev
    return group * PER_PROMPT, pairs, prev, own, has_prev


def fill_inverse(order_ref, where_ref, inverse_ref):
    def put(index, carry):
        inverse_ref[order_ref[stored_block(index, where_ref[1])]] = index
        return carry

    lax.fori_loop(0, order_ref.shape[0], put, 0)


def rotate(vec, cosine, sine):
    return vec * cosine + pltpu.roll(vec, HEAD_SIZE // 2, 1) * sine


def unrotate(vec, cosine, sine):
    return vec * cosine + pltpu.roll(vec * sine, HEAD_SIZE // 2, 1)


def angle_tables():
    half = HEAD_SIZE // 2
    freq = np.float64(rope_base) ** (-(2.0 * np.arange(half) / HEAD_SIZE))
    freq = np.concatenate([freq, freq])
    starts = np.arange(-(-(PER_PROMPT + PER_CONT) // 8) * 8) * BLOCK
    start = starts[:, None] * freq[None]
    inner = np.arange(BLOCK)[:, None] * freq[None]
    return tuple(
        f(a).astype(np.float32) for a in (start, inner) for f in (np.cos, np.sin)
    )


def key_rows(inverse_ref, logical):
    return pl.ds(pl.multiple_of(inverse_ref[logical] * BLOCK, BLOCK), BLOCK)


def tile_pair(ref, rows_a, rows_b, column):
    cols = pl.ds(column, HEAD_SIZE)
    return jnp.concatenate([ref[rows_a, cols], ref[rows_b, cols]], axis=0)


def own_mask(has_prev, rep):
    shape = (2 * BLOCK, rep * BLOCK)
    row = lax.broadcasted_iota(jnp.int32, shape, 0)
    col = lax.broadcasted_iota(jnp.int32, shape, 1)
    first_row = BLOCK * (1 - has_prev)
    return (row >= first_row) & (row - BLOCK <= lax.rem(col, BLOCK))


def stack_t(ref, rows, column, rep):
    return jnp.concatenate(
        [ref[rows, pl.ds(column + r * HEAD_SIZE, HEAD_SIZE)].T for r in range(rep)], axis=1
    )


def stack_rows(ref, rows, column, rep):
    return jnp.concatenate(
        [ref[rows, pl.ds(column + r * HEAD_SIZE, HEAD_SIZE)] for r in range(rep)], axis=0
    )


def dot(left, right):
    return jnp.dot(left, right, preferred_element_type=jnp.float32)


def forward_kernel(rep, hps, order_ref, cont_ref, where_ref, q_ref, kv_ref, out_ref, lse_ref,
                   inverse_ref, qt_ref, acc_ref):
    fill_inverse(order_ref, where_ref, inverse_ref)
    q_blocks = q_ref.shape[0] // BLOCK
    factor = LOG2E / math.sqrt(HEAD_SIZE)
    width = rep * HEAD_SIZE

    def one_query_block(qb, carry):
        base, pairs, prev, own, has_prev = block_plan(order_ref, cont_ref, where_ref, qb)
        rows = pl.ds(pl.multiple_of(qb * BLOCK, BLOCK), BLOCK)
        mask = own_mask(has_prev, rep)
        rows_a, rows_b = key_rows(inverse_ref, prev), key_rows(inverse_ref, own)
        state = []
        for h in range(hps):
            qt = stack_t(q_ref, rows, h * width, rep)
            qt_ref[h] = qt
            scores = dot(tile_pair(kv_ref, rows_a, rows_b, 2 * h * HEAD_SIZE), qt) * factor
            scores = jnp.where(mask, scores, NEG)
            best = jnp.max(scores, axis=0, keepdims=True)
            weights = jnp.exp2(scores - best)
            total = jnp.sum(weights, axis=0, keepdims=True)
            values = tile_pair(kv_ref, rows_a, rows_b, (2 * h + 1) * HEAD_SIZE)
            acc_ref[h] = dot(values.T, weights.astype(jnp.bfloat16))
            state += [best, total]

        def one_pair(t, state):
            rows_a = key_rows(inverse_ref, base + 2 * t)
            rows_b = key_rows(inverse_ref, base + 2 * t + 1)
            after = []
            for h in range(hps):
                best, total = state[2 * h], state[2 * h + 1]
                keys = tile_pair(kv_ref, rows_a, rows_b, 2 * h * HEAD_SIZE)
                scores = dot(keys, qt_ref[h]) * factor
                newest = jnp.maximum(best, jnp.max(scores, axis=0, keepdims=True))
                weights = jnp.exp2(scores - newest)
                shrink = jnp.exp2(best - newest)
                total = total * shrink + jnp.sum(weights, axis=0, keepdims=True)
                values = tile_pair(kv_ref, rows_a, rows_b, (2 * h + 1) * HEAD_SIZE)
                acc_ref[h] = acc_ref[h] * shrink + dot(values.T, weights.astype(jnp.bfloat16))
                after += [newest, total]
            return tuple(after)

        state = lax.fori_loop(0, pairs, one_pair, tuple(state))
        for h in range(hps):
            best, total = state[2 * h], state[2 * h + 1]
            mixed = acc_ref[h] * (1.0 / total)
            for r in range(rep):
                part = mixed[:, r * BLOCK : (r + 1) * BLOCK]
                out_ref[rows, pl.ds(h * width + r * HEAD_SIZE, HEAD_SIZE)] = part.T.astype(
                    jnp.bfloat16
                )
            lse_ref[0, h, pl.ds(qb, 1), :] = best + jnp.log2(total)
        return carry

    lax.fori_loop(0, q_blocks, one_query_block, 0)


def backward_kernel(rep, hps, order_ref, cont_ref, where_ref, q_ref, kv_ref, gm_ref, mix_ref,
                    lse_ref, cos_ref, sin_ref, gq_ref, keep_ref, send_ref, inverse_ref, qt_ref, gmt_ref, gqt_ref, acc_ref):
    fill_inverse(order_ref, where_ref, inverse_ref)
    q_blocks = q_ref.shape[0] // BLOCK
    scale = 1.0 / math.sqrt(HEAD_SIZE)
    factor = LOG2E * scale
    width = rep * HEAD_SIZE

    def clear(i, carry):
        acc_ref[pl.ds(pl.multiple_of(i * BLOCK, BLOCK), BLOCK), :] = jnp.zeros(
            (BLOCK, acc_ref.shape[1]), jnp.float32
        )
        return carry

    lax.fori_loop(0, order_ref.shape[0], clear, 0)

    def tile_terms(h, rows_a, rows_b, lse, delta, q_rows, gm_rows, mask):
        kcol, vcol = 2 * h * HEAD_SIZE, (2 * h + 1) * HEAD_SIZE
        keys = tile_pair(kv_ref, rows_a, rows_b, kcol)
        values = tile_pair(kv_ref, rows_a, rows_b, vcol)
        weights = jnp.exp2(dot(keys, qt_ref[h]) * factor - lse)
        if mask is not None:
            weights = jnp.where(mask, weights, 0.0)
        grad_weights = dot(values, gmt_ref[h])
        grad_scores = (weights * (grad_weights - delta)).astype(jnp.bfloat16)
        gv = dot(weights.astype(jnp.bfloat16), gm_rows)
        gk = dot(grad_scores, q_rows)
        acc_ref[rows_a, pl.ds(kcol, HEAD_SIZE)] += gk[:BLOCK]
        acc_ref[rows_b, pl.ds(kcol, HEAD_SIZE)] += gk[BLOCK:]
        acc_ref[rows_a, pl.ds(vcol, HEAD_SIZE)] += gv[:BLOCK]
        acc_ref[rows_b, pl.ds(vcol, HEAD_SIZE)] += gv[BLOCK:]
        return dot(keys.T, grad_scores)

    def one_query_block(qb, carry):
        base, pairs, prev, own, has_prev = block_plan(order_ref, cont_ref, where_ref, qb)
        rows = pl.ds(pl.multiple_of(qb * BLOCK, BLOCK), BLOCK)
        mask = own_mask(has_prev, rep)
        rows_a, rows_b = key_rows(inverse_ref, prev), key_rows(inverse_ref, own)
        deltas, lses, q_stack, gm_stack = [], [], [], []
        for h in range(hps):
            qt_ref[h] = stack_t(q_ref, rows, h * width, rep)
            gmt = stack_t(gm_ref, rows, h * width, rep)
            gmt_ref[h] = gmt
            mixt = stack_t(mix_ref, rows, h * width, rep)
            deltas.append(
                jnp.sum(
                    gmt.astype(jnp.float32) * mixt.astype(jnp.float32), axis=0, keepdims=True
                )
            )
            lses.append(lse_ref[0, h, pl.ds(qb, 1), :])
        for h in range(hps):
            q_rows = stack_rows(q_ref, rows, h * width, rep)
            gm_rows = stack_rows(gm_ref, rows, h * width, rep)
            gqt_ref[h] = tile_terms(
                h, rows_a, rows_b, lses[h], deltas[h], q_rows, gm_rows, mask
            )

        def one_pair(t, carry):
            rows_a = key_rows(inverse_ref, base + 2 * t)
            rows_b = key_rows(inverse_ref, base + 2 * t + 1)
            for h in range(hps):
                q_rows = stack_rows(q_ref, rows, h * width, rep)
                gm_rows = stack_rows(gm_ref, rows, h * width, rep)
                gqt_ref[h] += tile_terms(
                    h, rows_a, rows_b, lses[h], deltas[h], q_rows, gm_rows, None
                )
            return carry

        lax.fori_loop(0, pairs, one_pair, 0)
        for h in range(hps):
            total = gqt_ref[h] * scale
            for r in range(rep):
                part = total[:, r * BLOCK : (r + 1) * BLOCK]
                rounded = part.T.astype(jnp.bfloat16).astype(jnp.float32)
                gq_ref[rows, pl.ds(h * width + r * HEAD_SIZE, HEAD_SIZE)] = unrotate(
                    rounded, cos_ref[rows, :], sin_ref[rows, :]
                ).astype(jnp.bfloat16)
        return carry

    lax.fori_loop(0, q_blocks, one_query_block, 0)

    blocks = order_ref.shape[0]
    ctx_count = blocks // SLOTS

    def place(index):
        chunk = lax.div(index, SLOTS) ^ where_ref[0]
        spot = (chunk & 1) * (ctx_count // 2) + (chunk & 2) // 2 * (ctx_count // 4) + (
            lax.shift_right_logical(chunk, 2)
        )
        return spot * SLOTS + (index & 3)

    def flush(i, carry):
        rows = pl.ds(pl.multiple_of(i * BLOCK, BLOCK), BLOCK)
        spot = place(i)
        parts = []
        for h in range(hps):
            parts.append(acc_ref[rows, pl.ds(2 * h * HEAD_SIZE, HEAD_SIZE)] * scale)
            parts.append(acc_ref[rows, pl.ds((2 * h + 1) * HEAD_SIZE, HEAD_SIZE)])
        value = jnp.concatenate(parts, axis=1).astype(jnp.bfloat16)

        @pl.when(spot < blocks // 2)
        def _():
            keep_ref[pl.ds(pl.multiple_of(spot * BLOCK, BLOCK), BLOCK), :] = value

        @pl.when(spot >= blocks // 2)
        def _():
            far = (spot - blocks // 2) * BLOCK
            send_ref[pl.ds(pl.multiple_of(far, BLOCK), BLOCK), :] = value

        return carry

    lax.fori_loop(0, blocks, flush, 0)


def attention_sizes(q, kv):
    kv_heads = kv.shape[1] // (2 * HEAD_SIZE)
    rep = q.shape[1] // HEAD_SIZE // kv_heads
    hps = kv_heads if kv.shape[0] <= 8192 else 1
    return kv_heads, rep, hps


def attention_forward(q, kv, order, cont, where):
    kv_heads, rep, hps = attention_sizes(q, kv)
    rows, tokens = q.shape[0], kv.shape[0]
    q_blocks = rows // BLOCK
    wide = hps * rep * HEAD_SIZE
    q_spec = pl.BlockSpec((rows, wide), lambda g, *_: (0, g))
    flops = 4 * rows * (tokens // 2) * q.shape[1]
    return pl.pallas_call(
        functools.partial(forward_kernel, rep, hps),
        out_shape=(
            jax.ShapeDtypeStruct(q.shape, jnp.bfloat16),
            jax.ShapeDtypeStruct((kv_heads // hps, hps, q_blocks, rep * BLOCK), jnp.float32),
        ),
        grid_spec=pltpu.PrefetchScalarGridSpec(
            num_scalar_prefetch=3,
            grid=(kv_heads // hps,),
            in_specs=[
                q_spec,
                pl.BlockSpec((tokens, 2 * hps * HEAD_SIZE), lambda g, *_: (0, g)),
            ],
            out_specs=[
                q_spec,
                pl.BlockSpec((1, hps, q_blocks, rep * BLOCK), lambda g, *_: (g, 0, 0, 0)),
            ],
            scratch_shapes=[
                pltpu.SMEM((order.shape[0],), jnp.int32),
                pltpu.VMEM((hps, HEAD_SIZE, rep * BLOCK), jnp.bfloat16),
                pltpu.VMEM((hps, HEAD_SIZE, rep * BLOCK), jnp.float32),
            ],
        ),
        compiler_params=pltpu.CompilerParams(vmem_limit_bytes=56 << 20),
        cost_estimate=pl.CostEstimate(
            flops=flops, bytes_accessed=2 * (q.size * 2 + kv.size), transcendentals=flops // 512
        ),
        name="attention_forward",
    )(order, cont, where, q, kv)


def attention_backward(head, q, kv, grad_mixed, mixed, lse, cosine, sine, order, cont, where):
    kv_heads, rep, _ = attention_sizes(q, kv)
    hps_forward = lse.shape[1]
    rows, tokens = q.shape[0], kv.shape[0]
    q_blocks = rows // BLOCK
    wide = rep * HEAD_SIZE
    q_spec = pl.BlockSpec((rows, wide), lambda g, *_: (0, head))
    kv_spec = pl.BlockSpec((tokens, 2 * HEAD_SIZE), lambda g, *_: (0, head))
    lse_spec = pl.BlockSpec(
        (1, 1, q_blocks, rep * BLOCK),
        lambda g, *_: (head // hps_forward, head % hps_forward, 0, 0),
    )
    whole = lambda g, *_: (0, 0)
    table_spec = pl.BlockSpec((rows, HEAD_SIZE), whole)
    half = (tokens // 2, 2 * HEAD_SIZE)
    flops = 10 * rows * (tokens // 2) * wide
    return pl.pallas_call(
        functools.partial(backward_kernel, rep, 1),
        out_shape=(
            jax.ShapeDtypeStruct((rows, wide), jnp.bfloat16),
            jax.ShapeDtypeStruct(half, jnp.bfloat16),
            jax.ShapeDtypeStruct(half, jnp.bfloat16),
        ),
        grid_spec=pltpu.PrefetchScalarGridSpec(
            num_scalar_prefetch=3,
            grid=(1,),
            in_specs=[q_spec, kv_spec, q_spec, q_spec, lse_spec, table_spec, table_spec],
            out_specs=[
                pl.BlockSpec((rows, wide), whole),
                pl.BlockSpec(half, whole),
                pl.BlockSpec(half, whole),
            ],
            scratch_shapes=[
                pltpu.SMEM((order.shape[0],), jnp.int32),
                pltpu.VMEM((1, HEAD_SIZE, rep * BLOCK), jnp.bfloat16),
                pltpu.VMEM((1, HEAD_SIZE, rep * BLOCK), jnp.bfloat16),
                pltpu.VMEM((1, HEAD_SIZE, rep * BLOCK), jnp.float32),
                pltpu.VMEM((tokens, 2 * HEAD_SIZE), jnp.float32),
            ],
        ),
        compiler_params=pltpu.CompilerParams(vmem_limit_bytes=56 << 20),
        cost_estimate=pl.CostEstimate(
            flops=flops,
            bytes_accessed=4 * (rows * wide * 2 + tokens * 2 * HEAD_SIZE),
            transcendentals=flops // 1280,
        ),
        name=f"attention_backward_{head}",
    )(order, cont, where, q, kv, grad_mixed, mixed, lse, cosine, sine)


def input_kernel(order_ref, cont_ref, where_ref, x_ref, gain_ref, wq_ref, wk_ref, wv_ref,
                 cos_start_ref, sin_start_ref, cos_in_ref, sin_in_ref,
                 first_ref, q_ref, kv_ref, cos_ref, sin_ref):
    count = cont_ref.shape[0]
    prompt_blocks = count // CONTS * PER_PROMPT
    lane = lax.broadcasted_iota(jnp.int32, (BLOCK, HEAD_SIZE), 1)

    def one_slot(slot, carry):
        quarter = slot_quarter(slot, where_ref[1])
        rows = pl.ds(pl.multiple_of(slot * BLOCK, BLOCK), BLOCK)
        full = x_ref[pl.ds(pl.multiple_of(quarter * BLOCK, BLOCK), BLOCK), :].astype(jnp.float32)
        inv = lax.rsqrt(jnp.mean(full * full, axis=-1, keepdims=True) + eps_norm)
        first_ref[rows, :] = (full * inv * gain_ref[...]).astype(jnp.bfloat16)
        own = order_ref[where_ref[0] * SLOTS + quarter]
        spot = jnp.where(
            own < prompt_blocks,
            lax.rem(own, PER_PROMPT),
            PER_PROMPT + lax.rem(own - prompt_blocks, PER_CONT),
        )
        cos_start, sin_start = cos_start_ref[pl.ds(spot, 1), :], sin_start_ref[pl.ds(spot, 1), :]
        cos_in, sin_in = cos_in_ref[...], sin_in_ref[...]
        sine = sin_start * cos_in + cos_start * sin_in
        cos_ref[rows, :] = cos_start * cos_in - sin_start * sin_in
        sin_ref[rows, :] = jnp.where(lane < HEAD_SIZE // 2, -sine, sine)
        return carry

    lax.fori_loop(0, SLOTS, one_slot, 0)
    first = first_ref[...]
    cosine, sine = cos_ref[...], sin_ref[...]
    kv_heads = wk_ref.shape[1] // HEAD_SIZE
    for h in range(kv_heads):
        cols = slice(h * HEAD_SIZE, (h + 1) * HEAD_SIZE)
        key = rotate(plain_dot(first, wk_ref[:, cols]), cosine, sine)
        value = plain_dot(first, wv_ref[:, cols])
        kv_ref[:, 2 * h * HEAD_SIZE : (2 * h + 1) * HEAD_SIZE] = key.astype(jnp.bfloat16)
        kv_ref[:, (2 * h + 1) * HEAD_SIZE : (2 * h + 2) * HEAD_SIZE] = value.astype(jnp.bfloat16)
    for h in range(wq_ref.shape[1] // HEAD_SIZE):
        cols = slice(h * HEAD_SIZE, (h + 1) * HEAD_SIZE)
        query = rotate(plain_dot(first, wq_ref[:, cols]), cosine, sine)
        q_ref[:, cols] = query.astype(jnp.bfloat16)


def input_stage(x, gain, wq, wk, wv, order, cont, where):
    rows, model = x.shape
    tables = angle_tables()
    smem = pl.BlockSpec(memory_space=pltpu.SMEM)
    vmem = pl.BlockSpec(memory_space=pltpu.VMEM)
    flops = 2 * rows * model * (wq.shape[1] + 2 * wk.shape[1])
    return pl.pallas_call(
        input_kernel,
        out_shape=(
            jax.ShapeDtypeStruct((rows, model), jnp.bfloat16),
            jax.ShapeDtypeStruct((rows, wq.shape[1]), jnp.bfloat16),
            jax.ShapeDtypeStruct((rows, 2 * wk.shape[1]), jnp.bfloat16),
            jax.ShapeDtypeStruct((rows, HEAD_SIZE), jnp.float32),
            jax.ShapeDtypeStruct((rows, HEAD_SIZE), jnp.float32),
        ),
        in_specs=[smem] * 3 + [vmem] * 9,
        out_specs=[vmem] * 5,
        compiler_params=pltpu.CompilerParams(vmem_limit_bytes=40 << 20),
        cost_estimate=pl.CostEstimate(
            flops=flops, bytes_accessed=4 * x.size + 2 * wq.size + 4 * wk.size, transcendentals=0
        ),
        name="input_stage",
    )(order, cont, where, x, gain.reshape(1, -1), wq, wk, wv, *tables)


def kv_finish_kernel(keep_ref, got_ref, cos_ref, sin_ref, gk_ref, gv_ref):
    total = keep_ref[...].astype(jnp.float32) + got_ref[...].astype(jnp.float32)
    total = total.astype(jnp.bfloat16)
    key = total[:, :HEAD_SIZE].astype(jnp.float32)
    gk_ref[...] = unrotate(key, cos_ref[...], sin_ref[...]).astype(jnp.bfloat16)
    gv_ref[...] = total[:, HEAD_SIZE:]


def kv_finish(keep, got, cosine, sine):
    rows = keep.shape[0]
    vmem = pl.BlockSpec(memory_space=pltpu.VMEM)
    shape = jax.ShapeDtypeStruct((rows, HEAD_SIZE), jnp.bfloat16)
    return pl.pallas_call(
        kv_finish_kernel,
        out_shape=(shape, shape),
        in_specs=[vmem] * 4,
        out_specs=[vmem] * 2,
        cost_estimate=pl.CostEstimate(
            flops=8 * keep.size, bytes_accessed=6 * keep.size, transcendentals=0
        ),
        name="kv_finish",
    )(keep, got, cosine, sine)


def flip(value, axis, mask):
    return lax.ppermute(value, axis, [(i, i ^ mask) for i in range(lax.axis_size(axis))])


def add(left, right):
    return (left.astype(jnp.float32) + right.astype(jnp.float32)).astype(jnp.bfloat16)


def slots_of(value, tensor):
    rows = value.shape[0] // SLOTS
    return jnp.concatenate(
        [
            lax.dynamic_slice_in_dim(value, (tensor ^ SLOT_XOR[u]) * rows, rows)
            for u in range(SLOTS)
        ]
    )


def after(dep, *values):
    held = lax.optimization_barrier((dep,) + values)[1:]
    return held[0] if len(held) == 1 else held


def gather_slots(own):
    near = jnp.concatenate([own, flip(own, "tp", 2)])
    return jnp.concatenate([near, flip(near, "tp", 1)])


def gather_pair(own):
    partner = flip(own, "ctx", 2)
    near = jnp.concatenate([own, partner, flip(own, "tp", 2), flip(partner, "tp", 2)])
    return jnp.concatenate([near, flip(near, "tp", 1)])


def gather_rows(own, tensor):
    rows = own.shape[0]
    slots = gather_slots(own)
    result = jnp.zeros_like(slots)
    for u in range(SLOTS):
        result = lax.dynamic_update_slice_in_dim(
            result, slots[u * rows : (u + 1) * rows], (tensor ^ SLOT_XOR[u]) * rows, 0
        )
    return result


def scatter_slots(partial):
    half = partial.shape[0] // 2
    pair = add(partial[:half], flip(partial[half:], "tp", 1))
    quarter = half // 2
    return pair[:quarter], flip(pair[quarter:], "tp", 2)


def high_masks(ctx_count):
    masks, mask = [], ctx_count // 2
    while mask >= 4:
        masks.append(mask)
        mask //= 2
    return masks


def step(parts, axis_bits, mask, index):
    mine = lax.dynamic_index_in_dim(parts, index, axis_bits, keepdims=False)
    away = lax.dynamic_index_in_dim(parts, 1 - index, axis_bits, keepdims=False)
    return mine, flip(away, "ctx", mask)


def bits_of(ctx, ctx_count):
    return [(ctx // mask) % 2 for mask in high_masks(ctx_count)]


def reduce_attention(partial, ctx, ctx_count):
    highs = high_masks(ctx_count)
    width = partial.shape[1]
    rows = partial.shape[0] // ctx_count
    shaped = partial.astype(jnp.bfloat16).reshape((2,) * len(highs) + (2, 2, rows, width))
    mine, got = step(shaped, len(highs) + 1, 1, ctx % 2)
    shaped = add(mine, got)
    mine, got = step(shaped, len(highs), 2, ctx // 2 % 2)
    for mask, bit in zip(highs, bits_of(ctx, ctx_count)):
        shaped = add(mine, got)
        mine, got = step(shaped, 0, mask, bit)
    return mine.astype(jnp.float32) + got.astype(jnp.float32)


class FfnReduce:
    def __init__(self, partial, ctx, ctx_count, dep=None):
        self.highs = high_masks(ctx_count)
        self.ctx, self.ctx_count = ctx, ctx_count
        if dep is not None:
            partial = after(dep, partial)
        rows, width = partial.shape[0] // ctx_count, partial.shape[1]
        shaped = partial.reshape((2,) * len(self.highs) + (2, 2, rows, width))
        self.mine, self.got = step(shaped, len(self.highs) + 1, 1, ctx % 2)

    def high(self, dep):
        mine, got = after(dep, self.mine, self.got)
        for mask, bit in zip(self.highs, bits_of(self.ctx, self.ctx_count)):
            self.shaped = add(mine, got)
            mine, got = step(self.shaped, 0, mask, bit)
        self.mine, self.got = mine, got

    def finish(self, dep):
        shaped = add(*after(dep, self.mine, self.got))
        pair = self.ctx // 2 % 2
        mine, got = step(shaped, 0, 2, pair)
        low, high = jnp.where(pair == 0, mine, got), jnp.where(pair == 0, got, mine)
        return jnp.concatenate([low, high], axis=1).astype(jnp.float32)


class KvReduce:
    def __init__(self, keep, send, ctx_count):
        self.ctx_count = ctx_count
        self.keep, self.got = keep, flip(send, "ctx", 1)

    def high(self, dep):
        keep, got = after(dep, self.keep, self.got)
        for mask in [2] + high_masks(self.ctx_count):
            total = add(keep, got)
            half = total.shape[0] // 2
            keep, got = total[:half], flip(total[half:], "ctx", mask)
        self.keep, self.got = keep, got


def norm_back(grad_out, normed, inv_scale, gain):
    scaled = grad_out * gain
    inner = jnp.mean(scaled * normed, axis=-1, keepdims=True)
    return (inv_scale * (scaled - normed * inner), jnp.sum(grad_out * normed, axis=0))


def body(
    layer_input,
    attn_gain,
    w_query,
    key_matrix,
    value_matrix,
    w_out,
    ffn_gain,
    w_gate,
    w_up,
    w_down,
    cotangent,
    block_order,
    cont_prompt,
):
    ctx_count = lax.axis_size("ctx")
    tp_count = lax.axis_size("tp")
    ctx, tensor = lax.axis_index("ctx"), lax.axis_index("tp")
    pair = ctx // 2 % 2
    where = jnp.stack([ctx, tensor]).astype(jnp.int32)
    quarter = layer_input.shape[0] // SLOTS
    kv_heads = key_matrix.shape[1] // HEAD_SIZE
    half_units = w_gate.shape[1] // 2

    first_input, queries, kv_local, cosine, sine = input_stage(
        layer_input, attn_gain, w_query, key_matrix, value_matrix, block_order, cont_prompt, where
    )
    kv_all = lax.all_gather(kv_local, "ctx", axis=0, tiled=True)

    gate_half = lax.dynamic_slice_in_dim(w_gate, pair * half_units, half_units, 1)
    up_half = lax.dynamic_slice_in_dim(w_up, pair * half_units, half_units, 1)
    down_half = lax.dynamic_slice_in_dim(w_down, pair * half_units, half_units, 0)
    cot_own = lax.dynamic_slice_in_dim(cotangent, tensor * quarter, quarter)
    cot_slots = slots_of(cotangent, tensor).reshape(SLOTS, 1, quarter, -1)
    cot_other = gather_slots(flip(cot_own, "ctx", 2)).reshape(SLOTS, 1, quarter, -1)
    cot_rows = jnp.concatenate([cot_slots, cot_other], axis=1).reshape(2 * SLOTS * quarter, -1)

    mixed, log_total = attention_forward(queries, kv_all, block_order, cont_prompt, where)
    mine, got = scatter_slots(plain_dot(mixed, w_out).astype(jnp.bfloat16))
    grad_hidden = right_dot(after(mine, cot_rows), down_half)
    own_input = lax.dynamic_slice_in_dim(layer_input, tensor * quarter, quarter)
    own_input = own_input.astype(jnp.float32)
    mine, got = after(grad_hidden, mine, got)
    middle = own_input + (mine.astype(jnp.float32) + got.astype(jnp.float32))
    inv_two = lax.rsqrt(jnp.mean(middle * middle, axis=-1, keepdims=True) + eps_norm)
    normed_two = middle * inv_two
    second_in = gather_pair((normed_two * ffn_gain).astype(jnp.bfloat16))

    gate = plain_dot(second_in, gate_half)
    upward = plain_dot(second_in, up_half)
    sigma = jax.nn.sigmoid(gate)
    swish = gate * sigma
    hidden = (swish * upward).astype(jnp.bfloat16)
    grad_gate = (grad_hidden * upward * sigma * (1.0 + gate * (1.0 - sigma))).astype(jnp.bfloat16)
    grad_upward = (grad_hidden * swish).astype(jnp.bfloat16)

    def pair_scatter(partial):
        half = partial.shape[0] // 2
        near = add(partial[:half], flip(partial[half:], "tp", 1))
        far = flip(near[3 * quarter :], "tp", 2)
        away = flip(add(near[quarter : 2 * quarter], far), "ctx", 2)
        got = flip(near[2 * quarter : 3 * quarter], "tp", 2)
        return near[:quarter], got, away

    def total(terms):
        return sum(term.astype(jnp.float32) for term in terms)

    part_down = left_dot(cot_rows, hidden).astype(jnp.bfloat16)
    down = FfnReduce(part_down, ctx, ctx_count)
    grad_gate, grad_upward = after(part_down, grad_gate, grad_upward)
    partial = (right_dot(grad_gate, gate_half) + right_dot(grad_upward, up_half)).astype(
        jnp.bfloat16
    )
    second_terms = pair_scatter(partial)
    grad_gate, second_in = after(partial, grad_gate, second_in)
    part_gate = left_dot(second_in, grad_gate).astype(jnp.bfloat16)
    grad_upward, second_in = after(part_gate, grad_upward, second_in)
    part_up = left_dot(second_in, grad_upward).astype(jnp.bfloat16)
    hidden = after(part_up, hidden)
    ffn_partial = plain_dot(hidden, down_half).astype(jnp.bfloat16)

    second_terms = after(ffn_partial, *second_terms)
    grad_norm_two, ffn_gain_part = norm_back(total(second_terms), normed_two, inv_two, ffn_gain)
    grad_middle = cot_own.astype(jnp.float32) + grad_norm_two
    grad_branch = gather_slots(grad_middle.astype(jnp.bfloat16))
    down.high(grad_middle)
    gate_w = FfnReduce(part_gate, ctx, ctx_count, down.shaped)
    grad_mixed = right_dot(grad_branch, w_out).astype(jnp.bfloat16)
    backward = []
    for head in range(kv_heads):
        backward.append(
            attention_backward(
                head, queries, kv_all, grad_mixed, mixed, log_total, cosine, sine,
                block_order, cont_prompt, where,
            )
        )
        grad_mixed = after(backward[-1][0], grad_mixed)
    grad_query = jnp.concatenate([item[0] for item in backward], axis=1)
    part_out = left_dot(grad_branch, after(grad_query, mixed)).astype(jnp.bfloat16)
    part_query = left_dot(first_input, grad_query).astype(jnp.bfloat16)
    query_first = right_dot(grad_query, w_query)
    gate_w.high(part_query)
    kv = [
        KvReduce(after(gate_w.shaped, item[1]), after(gate_w.shaped, item[2]), ctx_count)
        for item in backward
    ]
    ffn_terms = pair_scatter(after(gate_w.shaped, ffn_partial))
    sum_down = down.finish(gate_w.shaped).T
    for item in kv:
        item.high(sum_down)
    up_w = FfnReduce(part_up, ctx, ctx_count, kv[-1].keep)
    grad_keys, grad_values = [], []
    for item in kv:
        grad_k, grad_v = kv_finish(item.keep, item.got, cosine, sine)
        grad_keys.append(grad_k)
        grad_values.append(grad_v)
    grad_key = jnp.concatenate(grad_keys, axis=1)
    grad_value = jnp.concatenate(grad_values, axis=1)
    grad_first_partial = (
        query_first + right_dot(grad_key, key_matrix) + right_dot(grad_value, value_matrix)
    ).astype(jnp.bfloat16)
    first_terms = scatter_slots(grad_first_partial)
    grad_key, grad_value = after(grad_first_partial, grad_key, grad_value)
    part_kv = jnp.concatenate(
        [left_dot(first_input, grad_key), left_dot(first_input, grad_value)], axis=1
    ).astype(jnp.bfloat16)
    output = gather_rows((middle + total(ffn_terms)).astype(jnp.bfloat16), tensor)
    up_w.high(part_kv)
    rest = jnp.concatenate([part_out, part_query, part_kv], axis=1)
    rest_sum = reduce_attention(after(up_w.shaped, rest), ctx, ctx_count)
    sum_gate = gate_w.finish(up_w.shaped)
    inv_one = lax.rsqrt(jnp.mean(own_input * own_input, axis=-1, keepdims=True) + eps_norm)
    grad_norm_one, attn_gain_part = norm_back(
        total(first_terms), own_input * inv_one, inv_one, attn_gain
    )
    grad_input = gather_rows((grad_middle + grad_norm_one).astype(jnp.bfloat16), tensor)
    sum_up = up_w.finish(grad_input)
    width_q, width_k = w_query.shape[1], key_matrix.shape[1]
    sum_out = rest_sum[:, :width_q].T
    sum_query = rest_sum[:, width_q : 2 * width_q]
    sum_key = rest_sum[:, 2 * width_q : 2 * width_q + width_k]
    sum_value = rest_sum[:, 2 * width_q + width_k :]

    devices = ctx_count * tp_count
    gains = jnp.stack([attn_gain_part, ffn_gain_part]).reshape(2, devices, -1)
    gains = lax.all_to_all(gains, ("ctx", "tp"), 1, 1, tiled=True)
    gains = jnp.sum(gains, axis=1)
    return (
        output,
        grad_input,
        gains[0],
        sum_query,
        sum_key,
        sum_value,
        sum_out,
        gains[1],
        sum_gate,
        sum_up,
        sum_down,
    )


def solution(mesh):
    placed = (
        P("ctx", None),
        P(),
        P(None, "tp"),
        P(None, "tp"),
        P(None, "tp"),
        P("tp", None),
        P(),
        P(None, "tp"),
        P(None, "tp"),
        P("tp", None),
        P("ctx", None),
        P(),
        P(),
    )
    return jax.shard_map(
        body,
        mesh=mesh,
        in_specs=placed,
        out_specs=(
            P("ctx", None),
            P("ctx", None),
            P(("ctx", "tp")),
            P("ctx", "tp"),
            P("ctx", "tp"),
            P("ctx", "tp"),
            P("tp", "ctx"),
            P(("ctx", "tp")),
            P("ctx", "tp"),
            P("ctx", "tp"),
            P("tp", "ctx"),
        ),
        check_vma=False,
    )
```

```python
import functools
import math

import jax
import jax.numpy as jnp
import numpy as np
from jax import lax
from jax.experimental import pallas as pl
from jax.experimental.pallas import tpu as pltpu
from jax.sharding import PartitionSpec as P

HEAD_SIZE = 128
PROMPT = 2048
CONT_LEN = 256
CONTS = 8
BLOCK = 128
PER_PROMPT = PROMPT // BLOCK
PER_CONT = CONT_LEN // BLOCK
LOG2E = 1.4426950408889634
NEG = -1e30
SLOTS = 4

eps_norm = 1e-05
rope_base = 1000000.0

SLOT_XOR = (0, 2, 1, 3)


def plain_dot(left, right):
    return jnp.dot(left, right, preferred_element_type=jnp.float32)


def left_dot(left, right):
    return lax.dot_general(
        left, right, (((0,), (0,)), ((), ())), preferred_element_type=jnp.float32
    )


def right_dot(left, right):
    return lax.dot_general(
        left, right, (((1,), (1,)), ((), ())), preferred_element_type=jnp.float32
    )


def slot_quarter(slot, tensor):
    return ((slot & 1) * 2 + lax.shift_right_logical(slot, 1)) ^ tensor


def stored_block(index, where_ref):
    rank = lax.div(index, SLOTS) ^ where_ref[0]
    return rank * SLOTS + slot_quarter(index & 3, where_ref[1])


def block_plan(order_ref, cont_ref, where_ref, slot):
    count = cont_ref.shape[0]
    prompt_blocks = count // CONTS * PER_PROMPT
    own = order_ref[stored_block(slot, where_ref)]
    is_prompt = own < prompt_blocks
    offset = own - prompt_blocks
    which = jnp.clip(lax.div(offset, PER_CONT), 0, count - 1)
    group = jnp.where(is_prompt, lax.div(own, PER_PROMPT), cont_ref[which])
    inner = jnp.where(is_prompt, lax.rem(own, PER_PROMPT), lax.rem(offset, PER_CONT))
    has_prev = lax.rem(inner, 2)
    pairs = jnp.where(is_prompt, lax.div(inner, 2), PER_PROMPT // 2)
    prev = own - has_prev
    return group * PER_PROMPT, pairs, prev, own, has_prev


def fill_inverse(order_ref, where_ref, inverse_ref):
    def put(index, carry):
        inverse_ref[order_ref[stored_block(index, where_ref)]] = index
        return carry

    lax.fori_loop(0, order_ref.shape[0], put, 0)


def rotate(vec, cosine, sine):
    return vec * cosine + pltpu.roll(vec, HEAD_SIZE // 2, 1) * sine


def unrotate(vec, cosine, sine):
    return vec * cosine + pltpu.roll(vec * sine, HEAD_SIZE // 2, 1)


def angle_tables():
    half = HEAD_SIZE // 2
    freq = np.float64(rope_base) ** (-(2.0 * np.arange(half) / HEAD_SIZE))
    freq = np.concatenate([freq, freq])
    starts = np.arange(-(-(PER_PROMPT + PER_CONT) // 8) * 8) * BLOCK
    start = starts[:, None] * freq[None]
    inner = np.arange(BLOCK)[:, None] * freq[None]
    return tuple(
        f(a).astype(np.float32) for a in (start, inner) for f in (np.cos, np.sin)
    )


def key_rows(inverse_ref, logical):
    return pl.ds(pl.multiple_of(inverse_ref[logical] * BLOCK, BLOCK), BLOCK)


def tile_pair(ref, rows_a, rows_b, column):
    cols = pl.ds(column, HEAD_SIZE)
    return jnp.concatenate([ref[rows_a, cols], ref[rows_b, cols]], axis=0)


def own_mask(has_prev, rep):
    shape = (2 * BLOCK, rep * BLOCK)
    row = lax.broadcasted_iota(jnp.int32, shape, 0)
    col = lax.broadcasted_iota(jnp.int32, shape, 1)
    first_row = BLOCK * (1 - has_prev)
    return (row >= first_row) & (row - BLOCK <= lax.rem(col, BLOCK))


def stack_t(ref, rows, column, rep):
    return jnp.concatenate(
        [ref[rows, pl.ds(column + r * HEAD_SIZE, HEAD_SIZE)].T for r in range(rep)], axis=1
    )


def stack_rows(ref, rows, column, rep):
    return jnp.concatenate(
        [ref[rows, pl.ds(column + r * HEAD_SIZE, HEAD_SIZE)] for r in range(rep)], axis=0
    )


def dot(left, right):
    return jnp.dot(left, right, preferred_element_type=jnp.float32)


def start_parts(parts, buffer_ref, sem, column):
    rows, width = parts[0].shape[0], buffer_ref.shape[1]
    copies = [
        pltpu.make_async_copy(
            part.at[:, pl.ds(column, width)], buffer_ref.at[pl.ds(p * rows, rows), :], sem.at[p]
        )
        for p, part in enumerate(parts)
    ]
    for copy in copies:
        copy.start()
    return copies


def forward_kernel(rep, hps, ctx_count, order_ref, cont_ref, where_ref, q_ref, wo_ref, *refs):
    parts, refs = refs[:ctx_count], refs[ctx_count:]
    out_ref, lse_ref, keep_ref, send_ref, kv_ref, inverse_ref, qt_ref, acc_ref, sem = refs
    copies = start_parts(parts, kv_ref, sem, 0)
    fill_inverse(order_ref, where_ref, inverse_ref)
    for copy in copies:
        copy.wait()
    q_blocks = q_ref.shape[0] // BLOCK
    factor = LOG2E / math.sqrt(HEAD_SIZE)
    width = rep * HEAD_SIZE

    def one_query_block(qb, carry):
        base, pairs, prev, own, has_prev = block_plan(order_ref, cont_ref, where_ref, qb)
        rows = pl.ds(pl.multiple_of(qb * BLOCK, BLOCK), BLOCK)
        mask = own_mask(has_prev, rep)
        rows_a, rows_b = key_rows(inverse_ref, prev), key_rows(inverse_ref, own)
        state = []
        for h in range(hps):
            qt = stack_t(q_ref, rows, h * width, rep)
            qt_ref[h] = qt
            scores = dot(tile_pair(kv_ref, rows_a, rows_b, 2 * h * HEAD_SIZE), qt) * factor
            scores = jnp.where(mask, scores, NEG)
            best = jnp.max(scores, axis=0, keepdims=True)
            weights = jnp.exp2(scores - best)
            total = jnp.sum(weights, axis=0, keepdims=True)
            values = tile_pair(kv_ref, rows_a, rows_b, (2 * h + 1) * HEAD_SIZE)
            acc_ref[h] = dot(values.T, weights.astype(jnp.bfloat16))
            state += [best, total]

        def one_pair(t, state):
            rows_a = key_rows(inverse_ref, base + 2 * t)
            rows_b = key_rows(inverse_ref, base + 2 * t + 1)
            after = []
            for h in range(hps):
                best, total = state[2 * h], state[2 * h + 1]
                keys = tile_pair(kv_ref, rows_a, rows_b, 2 * h * HEAD_SIZE)
                scores = dot(keys, qt_ref[h]) * factor
                newest = jnp.maximum(best, jnp.max(scores, axis=0, keepdims=True))
                weights = jnp.exp2(scores - newest)
                shrink = jnp.exp2(best - newest)
                total = total * shrink + jnp.sum(weights, axis=0, keepdims=True)
                values = tile_pair(kv_ref, rows_a, rows_b, (2 * h + 1) * HEAD_SIZE)
                acc_ref[h] = acc_ref[h] * shrink + dot(values.T, weights.astype(jnp.bfloat16))
                after += [newest, total]
            return tuple(after)

        state = lax.fori_loop(0, pairs, one_pair, tuple(state))
        for h in range(hps):
            best, total = state[2 * h], state[2 * h + 1]
            mixed = acc_ref[h] * (1.0 / total)
            for r in range(rep):
                part = mixed[:, r * BLOCK : (r + 1) * BLOCK]
                out_ref[rows, pl.ds(h * width + r * HEAD_SIZE, HEAD_SIZE)] = part.T.astype(
                    jnp.bfloat16
                )
            lse_ref[h, pl.ds(qb, 1), :] = best + jnp.log2(total)
        return carry

    lax.fori_loop(0, q_blocks, one_query_block, 0)
    mixed = out_ref[...]
    half = keep_ref.shape[0]
    for n in range(0, wo_ref.shape[1], 512):
        cols = slice(n, n + 512)
        partial = dot(mixed, wo_ref[:, cols]).astype(jnp.bfloat16)
        keep_ref[:, cols] = partial[:half]
        send_ref[:, cols] = partial[half:]


def backward_kernel(rep, hps, ctx_count, head, order_ref, cont_ref, where_ref, q_ref, gb_ref, wo_ref,
                    mix_ref, lse_ref, cos_ref, sin_ref, *refs):
    parts, refs = refs[:ctx_count], refs[ctx_count:]
    gq_ref, keep_ref, send_ref = refs[:3]
    kv_ref, gm_ref, inverse_ref, qt_ref, gmt_ref, gqt_ref, acc_ref, sem = refs[3:]
    copies = start_parts(parts, kv_ref, sem, head * kv_ref.shape[1])
    fill_inverse(order_ref, where_ref, inverse_ref)
    gm_ref[...] = right_dot(gb_ref[...], wo_ref[...]).astype(jnp.bfloat16)
    for copy in copies:
        copy.wait()
    q_blocks = q_ref.shape[0] // BLOCK
    scale = 1.0 / math.sqrt(HEAD_SIZE)
    factor = LOG2E * scale
    width = rep * HEAD_SIZE

    def clear(i, carry):
        acc_ref[pl.ds(pl.multiple_of(i * BLOCK, BLOCK), BLOCK), :] = jnp.zeros(
            (BLOCK, acc_ref.shape[1]), jnp.float32
        )
        return carry

    lax.fori_loop(0, order_ref.shape[0], clear, 0)

    def tile_terms(h, rows_a, rows_b, lse, delta, q_rows, gm_rows, mask):
        kcol, vcol = 2 * h * HEAD_SIZE, (2 * h + 1) * HEAD_SIZE
        keys = tile_pair(kv_ref, rows_a, rows_b, kcol)
        values = tile_pair(kv_ref, rows_a, rows_b, vcol)
        weights = jnp.exp2(dot(keys, qt_ref[h]) * factor - lse)
        if mask is not None:
            weights = jnp.where(mask, weights, 0.0)
        grad_weights = dot(values, gmt_ref[h])
        grad_scores = (weights * (grad_weights - delta)).astype(jnp.bfloat16)
        gv = dot(weights.astype(jnp.bfloat16), gm_rows)
        gk = dot(grad_scores, q_rows)
        acc_ref[rows_a, pl.ds(kcol, HEAD_SIZE)] += gk[:BLOCK]
        acc_ref[rows_b, pl.ds(kcol, HEAD_SIZE)] += gk[BLOCK:]
        acc_ref[rows_a, pl.ds(vcol, HEAD_SIZE)] += gv[:BLOCK]
        acc_ref[rows_b, pl.ds(vcol, HEAD_SIZE)] += gv[BLOCK:]
        return dot(keys.T, grad_scores)

    def one_query_block(qb, carry):
        base, pairs, prev, own, has_prev = block_plan(order_ref, cont_ref, where_ref, qb)
        rows = pl.ds(pl.multiple_of(qb * BLOCK, BLOCK), BLOCK)
        mask = own_mask(has_prev, rep)
        rows_a, rows_b = key_rows(inverse_ref, prev), key_rows(inverse_ref, own)
        deltas, lses, q_stack, gm_stack = [], [], [], []
        for h in range(hps):
            qt_ref[h] = stack_t(q_ref, rows, h * width, rep)
            gmt = stack_t(gm_ref, rows, h * width, rep)
            gmt_ref[h] = gmt
            mixt = stack_t(mix_ref, rows, h * width, rep)
            deltas.append(
                jnp.sum(
                    gmt.astype(jnp.float32) * mixt.astype(jnp.float32), axis=0, keepdims=True
                )
            )
            lses.append(lse_ref[h, pl.ds(qb, 1), :])
        for h in range(hps):
            q_rows = stack_rows(q_ref, rows, h * width, rep)
            gm_rows = stack_rows(gm_ref, rows, h * width, rep)
            gqt_ref[h] = tile_terms(
                h, rows_a, rows_b, lses[h], deltas[h], q_rows, gm_rows, mask
            )

        def one_pair(t, carry):
            rows_a = key_rows(inverse_ref, base + 2 * t)
            rows_b = key_rows(inverse_ref, base + 2 * t + 1)
            for h in range(hps):
                q_rows = stack_rows(q_ref, rows, h * width, rep)
                gm_rows = stack_rows(gm_ref, rows, h * width, rep)
                gqt_ref[h] += tile_terms(
                    h, rows_a, rows_b, lses[h], deltas[h], q_rows, gm_rows, None
                )
            return carry

        lax.fori_loop(0, pairs, one_pair, 0)
        for h in range(hps):
            total = gqt_ref[h] * scale
            for r in range(rep):
                part = total[:, r * BLOCK : (r + 1) * BLOCK]
                rounded = part.T.astype(jnp.bfloat16).astype(jnp.float32)
                gq_ref[rows, pl.ds(h * width + r * HEAD_SIZE, HEAD_SIZE)] = unrotate(
                    rounded, cos_ref[rows, :], sin_ref[rows, :]
                ).astype(jnp.bfloat16)
        return carry

    lax.fori_loop(0, q_blocks, one_query_block, 0)

    blocks = order_ref.shape[0]

    def place(index):
        chunk = lax.div(index, SLOTS)
        spot = (chunk & 1) * (ctx_count // 2) + (chunk & 2) // 2 * (ctx_count // 4) + (
            lax.shift_right_logical(chunk, 2)
        )
        return spot * SLOTS + (index & 3)

    def flush(i, carry):
        rows = pl.ds(pl.multiple_of(i * BLOCK, BLOCK), BLOCK)
        spot = place(i)
        parts = []
        for h in range(hps):
            parts.append(acc_ref[rows, pl.ds(2 * h * HEAD_SIZE, HEAD_SIZE)] * scale)
            parts.append(acc_ref[rows, pl.ds((2 * h + 1) * HEAD_SIZE, HEAD_SIZE)])
        value = jnp.concatenate(parts, axis=1).astype(jnp.bfloat16)

        @pl.when(spot < blocks // 2)
        def _():
            keep_ref[pl.ds(pl.multiple_of(spot * BLOCK, BLOCK), BLOCK), :] = value

        @pl.when(spot >= blocks // 2)
        def _():
            far = (spot - blocks // 2) * BLOCK
            send_ref[pl.ds(pl.multiple_of(far, BLOCK), BLOCK), :] = value

        return carry

    lax.fori_loop(0, blocks, flush, 0)


def attention_forward(q, w_out, parts, order, cont, where):
    ctx_count = len(parts)
    rows, tokens = q.shape[0], ctx_count * q.shape[0]
    kv_heads = parts[0].shape[1] // (2 * HEAD_SIZE)
    rep = q.shape[1] // HEAD_SIZE // kv_heads
    q_blocks, model = rows // BLOCK, w_out.shape[1]
    vmem, smem, any_ = (
        pl.BlockSpec(memory_space=space) for space in (pltpu.VMEM, pltpu.SMEM, pl.ANY)
    )
    flops = 2 * rows * tokens * q.shape[1] + 2 * rows * q.shape[1] * model
    half = jax.ShapeDtypeStruct((rows // 2, model), jnp.bfloat16)
    return pl.pallas_call(
        functools.partial(forward_kernel, rep, kv_heads, ctx_count),
        out_shape=(
            jax.ShapeDtypeStruct(q.shape, jnp.bfloat16),
            jax.ShapeDtypeStruct((kv_heads, q_blocks, rep * BLOCK), jnp.float32),
            half,
            half,
        ),
        in_specs=[smem] * 3 + [vmem] * 2 + [any_] * ctx_count,
        out_specs=[vmem] * 4,
        scratch_shapes=[
            pltpu.VMEM((tokens, parts[0].shape[1]), jnp.bfloat16),
            pltpu.SMEM((order.shape[0],), jnp.int32),
            pltpu.VMEM((kv_heads, HEAD_SIZE, rep * BLOCK), jnp.bfloat16),
            pltpu.VMEM((kv_heads, HEAD_SIZE, rep * BLOCK), jnp.float32),
            pltpu.SemaphoreType.DMA((ctx_count,)),
        ],
        compiler_params=pltpu.CompilerParams(vmem_limit_bytes=40 << 20),
        cost_estimate=cost(flops, 2 * tokens * parts[0].shape[1] + 4 * rows * model),
        name="attention_forward",
    )(order, cont, where, q, w_out, *parts)


def attention_backward(head, q, grad_branch, w_out, mixed, lse, parts, cosine, sine, order, cont,
                       where):
    ctx_count = len(parts)
    rows, tokens = q.shape[0], ctx_count * q.shape[0]
    kv_heads = parts[0].shape[1] // (2 * HEAD_SIZE)
    rep = q.shape[1] // HEAD_SIZE // kv_heads
    q_blocks, model = rows // BLOCK, w_out.shape[1]
    wide = rep * HEAD_SIZE
    q_spec = pl.BlockSpec((rows, wide), lambda g, *_: (0, head))
    whole = lambda g, *_: (0, 0)
    table_spec = pl.BlockSpec((rows, HEAD_SIZE), whole)
    half = (tokens // 2, 2 * HEAD_SIZE)
    flops = 5 * rows * tokens * wide + 2 * rows * wide * model
    return pl.pallas_call(
        functools.partial(backward_kernel, rep, 1, ctx_count, head),
        out_shape=(
            jax.ShapeDtypeStruct((rows, wide), jnp.bfloat16),
            jax.ShapeDtypeStruct(half, jnp.bfloat16),
            jax.ShapeDtypeStruct(half, jnp.bfloat16),
        ),
        grid_spec=pltpu.PrefetchScalarGridSpec(
            num_scalar_prefetch=3,
            grid=(1,),
            in_specs=[
                q_spec,
                pl.BlockSpec((rows, model), whole),
                pl.BlockSpec((wide, model), lambda g, *_: (head, 0)),
                q_spec,
                pl.BlockSpec((1, q_blocks, rep * BLOCK), lambda g, *_: (head, 0, 0)),
                table_spec,
                table_spec,
            ]
            + [pl.BlockSpec(memory_space=pl.ANY)] * ctx_count,
            out_specs=[
                pl.BlockSpec((rows, wide), whole),
                pl.BlockSpec(half, whole),
                pl.BlockSpec(half, whole),
            ],
            scratch_shapes=[
                pltpu.VMEM((tokens, 2 * HEAD_SIZE), jnp.bfloat16),
                pltpu.VMEM((rows, wide), jnp.bfloat16),
                pltpu.SMEM((order.shape[0],), jnp.int32),
                pltpu.VMEM((1, HEAD_SIZE, rep * BLOCK), jnp.bfloat16),
                pltpu.VMEM((1, HEAD_SIZE, rep * BLOCK), jnp.bfloat16),
                pltpu.VMEM((1, HEAD_SIZE, rep * BLOCK), jnp.float32),
                pltpu.VMEM((tokens, 2 * HEAD_SIZE), jnp.float32),
                pltpu.SemaphoreType.DMA((ctx_count,)),
            ],
        ),
        compiler_params=pltpu.CompilerParams(vmem_limit_bytes=56 << 20),
        cost_estimate=cost(flops, 4 * tokens * wide + 2 * rows * model),
        name=f"attention_backward_{head}",
    )(order, cont, where, q, grad_branch, w_out, mixed, lse, cosine, sine, *parts)


def input_kernel(order_ref, cont_ref, where_ref, x_ref, gain_ref, wq_ref, wk_ref, wv_ref,
                 cos_start_ref, sin_start_ref, cos_in_ref, sin_in_ref,
                 first_ref, q_ref, kv_ref, cos_ref, sin_ref):
    count = cont_ref.shape[0]
    prompt_blocks = count // CONTS * PER_PROMPT
    lane = lax.broadcasted_iota(jnp.int32, (BLOCK, HEAD_SIZE), 1)

    def one_slot(slot, carry):
        quarter = slot_quarter(slot, where_ref[1])
        rows = pl.ds(pl.multiple_of(slot * BLOCK, BLOCK), BLOCK)
        full = x_ref[pl.ds(pl.multiple_of(quarter * BLOCK, BLOCK), BLOCK), :].astype(jnp.float32)
        inv = lax.rsqrt(jnp.mean(full * full, axis=-1, keepdims=True) + eps_norm)
        first_ref[rows, :] = (full * inv * gain_ref[...]).astype(jnp.bfloat16)
        own = order_ref[stored_block(slot, where_ref)]
        spot = jnp.where(
            own < prompt_blocks,
            lax.rem(own, PER_PROMPT),
            PER_PROMPT + lax.rem(own - prompt_blocks, PER_CONT),
        )
        cos_start, sin_start = cos_start_ref[pl.ds(spot, 1), :], sin_start_ref[pl.ds(spot, 1), :]
        cos_in, sin_in = cos_in_ref[...], sin_in_ref[...]
        sine = sin_start * cos_in + cos_start * sin_in
        cos_ref[rows, :] = cos_start * cos_in - sin_start * sin_in
        sin_ref[rows, :] = jnp.where(lane < HEAD_SIZE // 2, -sine, sine)
        return carry

    lax.fori_loop(0, SLOTS, one_slot, 0)
    first = first_ref[...]
    cosine, sine = cos_ref[...], sin_ref[...]
    kv_heads = wk_ref.shape[1] // HEAD_SIZE
    for h in range(kv_heads):
        cols = slice(h * HEAD_SIZE, (h + 1) * HEAD_SIZE)
        key = rotate(plain_dot(first, wk_ref[:, cols]), cosine, sine)
        value = plain_dot(first, wv_ref[:, cols])
        kv_ref[:, 2 * h * HEAD_SIZE : (2 * h + 1) * HEAD_SIZE] = key.astype(jnp.bfloat16)
        kv_ref[:, (2 * h + 1) * HEAD_SIZE : (2 * h + 2) * HEAD_SIZE] = value.astype(jnp.bfloat16)
    for h in range(wq_ref.shape[1] // HEAD_SIZE):
        cols = slice(h * HEAD_SIZE, (h + 1) * HEAD_SIZE)
        query = rotate(plain_dot(first, wq_ref[:, cols]), cosine, sine)
        q_ref[:, cols] = query.astype(jnp.bfloat16)


def input_stage(x, gain, wq, wk, wv, order, cont, where):
    rows, model = x.shape
    tables = angle_tables()
    smem = pl.BlockSpec(memory_space=pltpu.SMEM)
    vmem = pl.BlockSpec(memory_space=pltpu.VMEM)
    flops = 2 * rows * model * (wq.shape[1] + 2 * wk.shape[1])
    return pl.pallas_call(
        input_kernel,
        out_shape=(
            jax.ShapeDtypeStruct((rows, model), jnp.bfloat16),
            jax.ShapeDtypeStruct((rows, wq.shape[1]), jnp.bfloat16),
            jax.ShapeDtypeStruct((rows, 2 * wk.shape[1]), jnp.bfloat16),
            jax.ShapeDtypeStruct((rows, HEAD_SIZE), jnp.float32),
            jax.ShapeDtypeStruct((rows, HEAD_SIZE), jnp.float32),
        ),
        in_specs=[smem] * 3 + [vmem] * 9,
        out_specs=[vmem] * 5,
        compiler_params=pltpu.CompilerParams(vmem_limit_bytes=40 << 20),
        cost_estimate=cost(flops, 4 * x.size + 2 * wq.size + 4 * wk.size),
        name="input_stage",
    )(order, cont, where, x, gain.reshape(1, -1), wq, wk, wv, *tables)


def cost(flops, bytes_accessed):
    return pl.CostEstimate(
        flops=int(flops), bytes_accessed=int(bytes_accessed), transcendentals=0
    )


def put_share(value, index, x_bit, keep_ref, send_ref, swap_bits):
    spot = lax.shift_right_logical(index, 1)
    if swap_bits:
        spot = (spot & 1) * (keep_ref.shape[0] // 2) + lax.shift_right_logical(spot, 1)
    stays = (index & 1) == x_bit
    value = value.astype(keep_ref.dtype)

    @pl.when(stays)
    def _():
        keep_ref[pl.ds(spot, 1)] = value[None]

    @pl.when(jnp.logical_not(stays))
    def _():
        send_ref[pl.ds(spot, 1)] = value[None]


def ffn_kernel(where_ref, near_ref, far_ref, cot_near_ref, cot_far_ref, wg_ref, wu_ref, wd_ref,
               hid_ref, gg_ref, gu_ref, keep_ref, send_ref):
    rows = near_ref.shape[0]
    for k, (in_ref, cot_ref) in enumerate(((near_ref, cot_near_ref), (far_ref, cot_far_ref))):
        span = slice(k * rows, (k + 1) * rows)
        gate = dot(in_ref[...], wg_ref[...])
        upward = dot(in_ref[...], wu_ref[...])
        grad_hidden = right_dot(cot_ref[...], wd_ref[...])
        sigma = jax.nn.sigmoid(gate)
        swish = gate * sigma
        hid_ref[span, :] = (swish * upward).astype(jnp.bfloat16)
        gg_ref[span, :] = (
            grad_hidden * upward * sigma * (1.0 + gate * (1.0 - sigma))
        ).astype(jnp.bfloat16)
        gu_ref[span, :] = (grad_hidden * swish).astype(jnp.bfloat16)
    turned_near, turned_far = hid_ref[:rows, :].T, hid_ref[rows:, :].T
    share = keep_ref.shape[2]
    for f in range(cot_near_ref.shape[1] // share):
        cols = slice(f * share, (f + 1) * share)
        value = dot(turned_near, cot_near_ref[:, cols]) + dot(turned_far, cot_far_ref[:, cols])
        put_share(value, jnp.int32(f), where_ref[0] & 1, keep_ref, send_ref, False)


def ffn_stage(second, cot, w_gate, w_up, w_down, ctx_count, where):
    rows, model = second[0].shape
    units = w_gate.shape[1] // 2
    block = 256
    steps = units // block
    share = model // ctx_count
    pair = lambda where_ref: lax.shift_right_logical(where_ref[0], 1) & 1
    row_spec = pl.BlockSpec(
        (rows, model), lambda i, w: (0, 0), pipeline_mode=pl.Buffered(1)
    )
    col_spec = pl.BlockSpec((model, block), lambda i, w: (0, pair(w) * steps + i))
    unit_spec = pl.BlockSpec((2 * rows, block), lambda i, w: (0, i))
    share_spec = pl.BlockSpec((ctx_count // 2, block, share), lambda i, w: (0, i, 0))
    unit = jax.ShapeDtypeStruct((2 * rows, units), jnp.bfloat16)
    shares = jax.ShapeDtypeStruct((ctx_count // 2, units, share), jnp.bfloat16)
    return pl.pallas_call(
        ffn_kernel,
        out_shape=(unit, unit, unit, shares, shares),
        grid_spec=pltpu.PrefetchScalarGridSpec(
            num_scalar_prefetch=1,
            grid=(steps,),
            in_specs=[row_spec] * 4
            + [
                col_spec,
                col_spec,
                pl.BlockSpec((block, model), lambda i, w: (pair(w) * steps + i, 0)),
            ],
            out_specs=[unit_spec] * 3 + [share_spec] * 2,
        ),
        compiler_params=pltpu.CompilerParams(vmem_limit_bytes=44 << 20),
        cost_estimate=cost(16 * rows * model * units, 16 * rows * model),
        name="ffn_stage",
    )(where, *second, *cot, w_gate, w_up, w_down)


def grad_second_kernel(where_ref, gg_ref, gu_ref, wg_ref, wu_ref, keep_ref, send_ref):
    total = right_dot(gg_ref[...], wg_ref[...]) + right_dot(gu_ref[...], wu_ref[...])
    half = keep_ref.shape[0]
    keep_ref[...] = total[:half].astype(jnp.bfloat16)
    send_ref[...] = total[half:].astype(jnp.bfloat16)


def ffn_out_kernel(where_ref, hid_ref, wd_ref, keep_ref, send_ref):
    total = dot(hid_ref[...], wd_ref[...])
    half = keep_ref.shape[0]
    keep_ref[...] = total[:half].astype(jnp.bfloat16)
    send_ref[...] = total[half:].astype(jnp.bfloat16)


def unit_sum(kernel, name, lefts, rights, transposed, where):
    rows, units = lefts[0].shape
    model = rights[0].shape[0 if transposed else 1]
    block = 512
    pair = lambda where_ref: lax.shift_right_logical(where_ref[0], 1) & 1
    if transposed:
        right_spec = pl.BlockSpec((block, units), lambda n, w: (n, pair(w)))
    else:
        right_spec = pl.BlockSpec((units, block), lambda n, w: (pair(w), n))
    left_spec = pl.BlockSpec((rows, units), lambda n, w: (0, 0), pipeline_mode=pl.Buffered(1))
    half = jax.ShapeDtypeStruct((rows // 2, model), jnp.bfloat16)
    half_spec = pl.BlockSpec((rows // 2, block), lambda n, w: (0, n))
    return pl.pallas_call(
        kernel,
        out_shape=(half, half),
        grid_spec=pltpu.PrefetchScalarGridSpec(
            num_scalar_prefetch=1,
            grid=(model // block,),
            in_specs=[left_spec] * len(lefts) + [right_spec] * len(rights),
            out_specs=[half_spec, half_spec],
        ),
        compiler_params=pltpu.CompilerParams(vmem_limit_bytes=32 << 20),
        cost_estimate=cost(2 * len(lefts) * rows * units * model, 4 * rows * model),
        name=name,
    )(where, *lefts, *rights)


def shares_kernel(left_count, swap_bits, pairs, where_ref, *refs):
    lefts, refs = refs[:left_count], refs[left_count:]
    rights, (keep_ref, send_ref) = refs[:-2], refs[-2:]
    share = keep_ref.shape[1]
    turned = [left[...].T for left in lefts]
    step = pl.program_id(0)
    start = 0
    pieces = []
    for terms in pairs:
        pieces.append(
            sum(dot(turned[l], rights[r][rows, :]) for l, r, rows in terms)
        )
    value = pieces[0] if len(pieces) == 1 else jnp.concatenate(pieces, axis=1)
    per_step = value.shape[0] // share
    for k in range(per_step):
        put_share(
            value[k * share : (k + 1) * share],
            step * per_step + k,
            where_ref[0] & 1,
            keep_ref,
            send_ref,
            swap_bits,
        )


def weight_shares(name, lefts, rights, pairs, width, ctx_count, swap_bits, where):
    rows, model = lefts[0].shape
    block = 256
    share = model // ctx_count
    shares = jax.ShapeDtypeStruct((ctx_count // 2, share, width), jnp.bfloat16)
    share_spec = pl.BlockSpec(shares.shape, lambda i, w: (0, 0, 0))
    flops = 2 * model * sum(
        rights[r].shape[1] * lefts[l].shape[0] for terms in pairs for l, r, _ in terms
    )
    return pl.pallas_call(
        functools.partial(shares_kernel, len(lefts), swap_bits, pairs),
        out_shape=(shares, shares),
        grid_spec=pltpu.PrefetchScalarGridSpec(
            num_scalar_prefetch=1,
            grid=(model // block,),
            in_specs=[pl.BlockSpec((rows, block), lambda i, w: (0, i))] * len(lefts)
            + [
                pl.BlockSpec(r.shape, lambda i, w: (0, 0), pipeline_mode=pl.Buffered(1))
                for r in rights
            ],
            out_specs=[share_spec, share_spec],
        ),
        compiler_params=pltpu.CompilerParams(vmem_limit_bytes=36 << 20),
        cost_estimate=cost(flops, 4 * rows * model),
        name=name,
    )(where, *lefts, *rights)


def tail_kernel(kv_heads, where_ref, *refs):
    sums, refs = refs[: 2 * kv_heads], refs[2 * kv_heads :]
    cos_ref, sin_ref, refs = refs[0], refs[1], refs[2:]
    gq_refs, refs = refs[:kv_heads], refs[kv_heads:]
    wq_ref, wk_ref, wv_ref, keep_ref, send_ref, gkv_ref = refs
    cosine, sine = cos_ref[...], sin_ref[...]
    for h in range(kv_heads):
        total = sums[2 * h][...].astype(jnp.float32) + sums[2 * h + 1][...].astype(jnp.float32)
        total = total.astype(jnp.bfloat16)
        key = unrotate(total[:, :HEAD_SIZE].astype(jnp.float32), cosine, sine)
        cols = slice(h * HEAD_SIZE, (h + 1) * HEAD_SIZE)
        gkv_ref[:, cols] = key.astype(jnp.bfloat16)
        cols = slice((kv_heads + h) * HEAD_SIZE, (kv_heads + h + 1) * HEAD_SIZE)
        gkv_ref[:, cols] = total[:, HEAD_SIZE:]
    half = keep_ref.shape[0]
    key_width = kv_heads * HEAD_SIZE
    wide = gq_refs[0].shape[1]
    for n in range(0, wq_ref.shape[0], 512):
        span = slice(n, n + 512)
        total = right_dot(gkv_ref[:, :key_width], wk_ref[span, :])
        total += right_dot(gkv_ref[:, key_width:], wv_ref[span, :])
        for h in range(kv_heads):
            total += right_dot(gq_refs[h][...], wq_ref[span, h * wide : (h + 1) * wide])
        total = total.astype(jnp.bfloat16)
        keep_ref[:, span] = total[:half]
        send_ref[:, span] = total[half:]


def tail_stage(kv_sums, cosine, sine, grad_queries, wq, wk, wv, where):
    rows, model = cosine.shape[0], wq.shape[0]
    kv_heads = len(grad_queries)
    vmem = pl.BlockSpec(memory_space=pltpu.VMEM)
    half = jax.ShapeDtypeStruct((rows // 2, model), jnp.bfloat16)
    flat = [term for sums in kv_sums for term in sums]
    return pl.pallas_call(
        functools.partial(tail_kernel, kv_heads),
        out_shape=(
            half,
            half,
            jax.ShapeDtypeStruct((rows, 2 * kv_heads * HEAD_SIZE), jnp.bfloat16),
        ),
        in_specs=[pl.BlockSpec(memory_space=pltpu.SMEM)]
        + [vmem] * (len(flat) + 2 + kv_heads + 3),
        out_specs=[vmem] * 3,
        compiler_params=pltpu.CompilerParams(vmem_limit_bytes=32 << 20),
        cost_estimate=cost(
            2 * rows * model * (wq.shape[1] + 2 * wk.shape[1]), 4 * rows * model + 4 * wq.size
        ),
        name="tail_stage",
    )(where, *flat, cosine, sine, *grad_queries, wq, wk, wv)


def flip(value, axis, mask):
    return lax.ppermute(value, axis, [(i, i ^ mask) for i in range(lax.axis_size(axis))])


def add(left, right):
    return (left.astype(jnp.float32) + right.astype(jnp.float32)).astype(jnp.bfloat16)


def slots_of(value, tensor):
    rows = value.shape[0] // SLOTS
    return [
        lax.dynamic_slice_in_dim(value, (tensor ^ SLOT_XOR[u]) * rows, rows)
        for u in range(SLOTS)
    ]


def after(dep, *values):
    held = lax.optimization_barrier((dep,) + values)[1:]
    return held[0] if len(held) == 1 else held


def gather_slots(own):
    near = jnp.concatenate([own, flip(own, "tp", 2)])
    return jnp.concatenate([near, flip(near, "tp", 1)])


def gather_pair(own):
    partner = flip(own, "ctx", 2)
    near = jnp.concatenate([own, partner, flip(own, "tp", 2), flip(partner, "tp", 2)])
    return near, flip(near, "tp", 1)


def gather_rows(own, tensor):
    rows = own.shape[0]
    near = jnp.concatenate([own, flip(own, "tp", 2)])
    far = flip(near, "tp", 1)
    pieces = (near[:rows], near[rows:], far[:rows], far[rows:])
    result = jnp.zeros((SLOTS * rows,) + own.shape[1:], own.dtype)
    for u in range(SLOTS):
        result = lax.dynamic_update_slice_in_dim(
            result, pieces[u], (tensor ^ SLOT_XOR[u]) * rows, 0
        )
    return result


def scatter_slots(keep, send):
    got = flip(send, "tp", 1)
    quarter = keep.shape[0] // 2
    far = flip(add(keep[quarter:], got[quarter:]), "tp", 2)
    return add(keep[:quarter], got[:quarter]), far


def pair_scatter(keep, send):
    got = flip(send, "tp", 1)
    n = keep.shape[0] // 4
    near = [add(keep[k * n : (k + 1) * n], got[k * n : (k + 1) * n]) for k in (3, 1, 2, 0)]
    away = flip(add(near[1], flip(near[0], "tp", 2)), "ctx", 2)
    return near[3], flip(near[2], "tp", 2), away


def total(terms):
    return sum(term.astype(jnp.float32) for term in terms)


def gather_keys(kv_local, ctx_count):
    parts = {0: kv_local}
    for mask in range(2, ctx_count, 2):
        parts[mask] = flip(kv_local, "ctx", mask)
    for mask in range(0, ctx_count, 2):
        parts[mask + 1] = flip(parts[mask], "ctx", 1)
    return [parts[mask] for mask in range(ctx_count)]


class Reduce:
    def __init__(self, keep, send):
        self.keep, self.got = keep, flip(send, "ctx", 1)

    def halve(self, mask, ctx, dep=None):
        keep, got = self.keep, self.got
        if dep is not None:
            keep, got = after(dep, keep, got)
        n = keep.shape[0] // 2
        bit = lax.div(ctx, mask) % 2
        pick = lambda value, index: lax.dynamic_slice_in_dim(value, index * n, n, 0)
        away = flip(add(pick(keep, 1 - bit), pick(got, 1 - bit)), "ctx", mask)
        self.keep, self.got = add(pick(keep, bit), pick(got, bit)), away

    def sum(self):
        return (self.keep.astype(jnp.float32) + self.got.astype(jnp.float32))[0]


def high_masks(ctx_count):
    masks, mask = [], ctx_count // 2
    while mask >= 4:
        masks.append(mask)
        mask //= 2
    return masks


def both_halves(reduce, ctx, axis, dep=None):
    keep, got = reduce.keep, reduce.got
    if dep is not None:
        keep, got = after(dep, keep, got)
    pair = lax.div(ctx, 2) % 2
    pick = lambda value, index: lax.dynamic_slice_in_dim(value, index, 1, 0)[0]
    other = flip(add(pick(keep, 1 - pair), pick(got, 1 - pair)), "ctx", 2)
    own = add(pick(keep, pair), pick(got, pair))
    low, high = jnp.where(pair == 0, own, other), jnp.where(pair == 0, other, own)
    return jnp.concatenate([low, high], axis=axis).astype(jnp.float32)


class KvReduce:
    def __init__(self, keep, send, ctx_count):
        self.ctx_count = ctx_count
        self.keep, self.got = keep, flip(send, "ctx", 1)

    def high(self, dep):
        keep, got = after(dep, self.keep, self.got)
        for mask in [2] + high_masks(self.ctx_count):
            n = keep.shape[0] // 2
            away = flip(add(keep[n:], got[n:]), "ctx", mask)
            keep, got = add(keep[:n], got[:n]), away
        self.keep, self.got = keep, got


def norm_back(grad_out, normed, inv_scale, gain):
    scaled = grad_out * gain
    inner = jnp.mean(scaled * normed, axis=-1, keepdims=True)
    return (inv_scale * (scaled - normed * inner), jnp.sum(grad_out * normed, axis=0))


def body(
    layer_input,
    attn_gain,
    w_query,
    key_matrix,
    value_matrix,
    w_out,
    ffn_gain,
    w_gate,
    w_up,
    w_down,
    cotangent,
    block_order,
    cont_prompt,
):
    ctx_count = lax.axis_size("ctx")
    tp_count = lax.axis_size("tp")
    ctx, tensor = lax.axis_index("ctx"), lax.axis_index("tp")
    where = jnp.stack([ctx, tensor]).astype(jnp.int32)
    quarter = layer_input.shape[0] // SLOTS
    kv_heads = key_matrix.shape[1] // HEAD_SIZE
    highs = high_masks(ctx_count)

    first_input, queries, kv_local, cosine, sine = input_stage(
        layer_input, attn_gain, w_query, key_matrix, value_matrix, block_order, cont_prompt, where
    )
    parts = gather_keys(kv_local, ctx_count)

    cot_own = after(first_input, lax.dynamic_slice_in_dim(cotangent, tensor * quarter, quarter))
    cot_slots = slots_of(cotangent, tensor)
    cot_part = flip(cot_own, "ctx", 2)
    cot_part = jnp.concatenate([cot_part, flip(cot_part, "tp", 2)])
    cot_far = flip(cot_part, "tp", 1)
    cot = (
        jnp.concatenate([cot_slots[0], cot_part[:quarter], cot_slots[1], cot_part[quarter:]]),
        jnp.concatenate([cot_slots[2], cot_far[:quarter], cot_slots[3], cot_far[quarter:]]),
    )

    mixed, log_total, keep, send = attention_forward(
        queries, w_out, parts, block_order, cont_prompt, where
    )
    own_input = lax.dynamic_slice_in_dim(layer_input, tensor * quarter, quarter)
    own_input = own_input.astype(jnp.float32)
    middle = own_input + total(scatter_slots(keep, send))
    inv_two = lax.rsqrt(jnp.mean(middle * middle, axis=-1, keepdims=True) + eps_norm)
    normed_two = middle * inv_two
    second = gather_pair((normed_two * ffn_gain).astype(jnp.bfloat16))
    hidden, grad_gate, grad_up, keep, send = ffn_stage(
        second, cot, w_gate, w_up, w_down, ctx_count, where
    )

    down = Reduce(keep, send)
    second_terms = pair_scatter(
        *unit_sum(
            grad_second_kernel, "grad_second", (grad_gate, grad_up), (w_gate, w_up), True, where
        )
    )
    rows = second[0].shape[0]
    halves = (slice(0, rows), slice(rows, 2 * rows))

    def unit_shares(name, grad, dep):
        return weight_shares(
            name, second, (after(dep, grad),), (tuple((k, 0, halves[k]) for k in range(2)),),
            grad.shape[1], ctx_count, False, where,
        )

    gate_shares = unit_shares("gate_shares", grad_gate, second_terms[0])
    up_shares = unit_shares("up_shares", grad_up, gate_shares[0])
    ffn_halves = unit_sum(
        ffn_out_kernel, "ffn_out", (after(up_shares[0], hidden),), (w_down,), False, where
    )

    grad_norm_two, ffn_gain_part = norm_back(
        total(after(ffn_halves[0], *second_terms)), normed_two, inv_two, ffn_gain
    )
    grad_middle = cot_own.astype(jnp.float32) + grad_norm_two
    grad_branch = gather_slots(grad_middle.astype(jnp.bfloat16))
    for mask in highs:
        down.halve(mask, ctx, grad_middle)
    gate = Reduce(*after(down.keep, *gate_shares))
    backward = []
    held = grad_branch
    for head in range(kv_heads):
        backward.append(
            attention_backward(
                head, queries, held, w_out, mixed, log_total, parts, cosine, sine,
                block_order, cont_prompt, where,
            )
        )
        held = after(backward[-1][0], grad_branch)
    grad_queries = [item[0] for item in backward]
    spans = slice(0, first_input.shape[0])
    wide = grad_queries[0].shape[1]
    last_query = grad_queries[-1]
    branch_shares = weight_shares(
        "branch_shares",
        (first_input, grad_branch),
        grad_queries + [after(last_query, mixed)],
        tuple(((0, h, spans),) for h in range(kv_heads)) + (((1, kv_heads, spans),),),
        2 * w_query.shape[1],
        ctx_count,
        True,
        where,
    )
    for mask in highs:
        gate.halve(mask, ctx, branch_shares[0])
    kv = [KvReduce(*after(gate.keep, item[1], item[2]), ctx_count) for item in backward]
    ffn_terms = pair_scatter(*after(gate.keep, *ffn_halves))
    sum_down = both_halves(down, ctx, 0, gate.keep)
    for item in kv:
        item.high(sum_down)
    up = Reduce(*after(kv[-1].keep, *up_shares))
    keep, send, grad_kv = tail_stage(
        [(item.keep, item.got) for item in kv], cosine, sine, grad_queries,
        w_query, key_matrix, value_matrix, where,
    )
    first_terms = scatter_slots(keep, send)
    kv_shares = weight_shares(
        "kv_shares", (first_input,), (grad_kv,), (((0, 0, spans),),), grad_kv.shape[1],
        ctx_count, True, where,
    )
    output = gather_rows((middle + total(ffn_terms)).astype(jnp.bfloat16), tensor)
    for mask in highs:
        up.halve(mask, ctx, kv_shares[0])
    branch = Reduce(*after(up.keep, *branch_shares))
    last = Reduce(*after(up.keep, *kv_shares))
    sum_gate = both_halves(gate, ctx, 1, up.keep)
    inv_one = lax.rsqrt(jnp.mean(own_input * own_input, axis=-1, keepdims=True) + eps_norm)
    grad_norm_one, attn_gain_part = norm_back(
        total(first_terms), own_input * inv_one, inv_one, attn_gain
    )
    grad_input = gather_rows((grad_middle + grad_norm_one).astype(jnp.bfloat16), tensor)
    sum_up = both_halves(up, ctx, 1, grad_input)
    for item in (branch, last):
        for mask in [2] + highs:
            item.halve(mask, ctx, sum_up if mask == 2 else None)
    width_q, width_k = w_query.shape[1], key_matrix.shape[1]
    branch_sum, last_sum = branch.sum(), last.sum()
    sum_query, sum_out = branch_sum[:, :width_q], branch_sum[:, width_q:].T
    sum_key, sum_value = last_sum[:, :width_k], last_sum[:, width_k:]

    devices = ctx_count * tp_count
    gains = jnp.stack([attn_gain_part, ffn_gain_part]).reshape(2, devices, -1)
    gains = lax.all_to_all(gains, ("ctx", "tp"), 1, 1, tiled=True)
    gains = jnp.sum(gains, axis=1)
    return (
        output,
        grad_input,
        gains[0],
        sum_query,
        sum_key,
        sum_value,
        sum_out,
        gains[1],
        sum_gate,
        sum_up,
        sum_down,
    )


def solution(mesh):
    placed = (
        P("ctx", None),
        P(),
        P(None, "tp"),
        P(None, "tp"),
        P(None, "tp"),
        P("tp", None),
        P(),
        P(None, "tp"),
        P(None, "tp"),
        P("tp", None),
        P("ctx", None),
        P(),
        P(),
    )
    return jax.shard_map(
        body,
        mesh=mesh,
        in_specs=placed,
        out_specs=(
            P("ctx", None),
            P("ctx", None),
            P(("ctx", "tp")),
            P("ctx", "tp"),
            P("ctx", "tp"),
            P("ctx", "tp"),
            P("tp", "ctx"),
            P(("ctx", "tp")),
            P("ctx", "tp"),
            P("ctx", "tp"),
            P("tp", "ctx"),
        ),
        check_vma=False,
    )
```

```python
import functools
import math

import jax
import jax.numpy as jnp
import numpy as np
from jax import lax
from jax.experimental import pallas as pl
from jax.experimental.pallas import tpu as pltpu
from jax.sharding import PartitionSpec as P

HEAD_SIZE = 128
PROMPT = 2048
CONT_LEN = 256
CONTS = 8
BLOCK = 128
PER_PROMPT = PROMPT // BLOCK
PER_CONT = CONT_LEN // BLOCK
LOG2E = 1.4426950408889634
NEG = -1e30
SLOTS = 4

eps_norm = 1e-05
rope_base = 1000000.0

SLOT_XOR = (0, 2, 1, 3)


def plain_dot(left, right):
    return jnp.dot(left, right, preferred_element_type=jnp.float32)


def left_dot(left, right):
    return lax.dot_general(
        left, right, (((0,), (0,)), ((), ())), preferred_element_type=jnp.float32
    )


def right_dot(left, right):
    return lax.dot_general(
        left, right, (((1,), (1,)), ((), ())), preferred_element_type=jnp.float32
    )


def slot_quarter(slot, tensor):
    return ((slot & 1) * 2 + lax.shift_right_logical(slot, 1)) ^ tensor


def stored_block(index, where_ref):
    rank = lax.div(index, SLOTS) ^ where_ref[0]
    return rank * SLOTS + slot_quarter(index & 3, where_ref[1])


def block_plan(order_ref, cont_ref, where_ref, slot):
    count = cont_ref.shape[0]
    prompt_blocks = count // CONTS * PER_PROMPT
    own = order_ref[stored_block(slot, where_ref)]
    is_prompt = own < prompt_blocks
    offset = own - prompt_blocks
    which = jnp.clip(lax.div(offset, PER_CONT), 0, count - 1)
    group = jnp.where(is_prompt, lax.div(own, PER_PROMPT), cont_ref[which])
    inner = jnp.where(is_prompt, lax.rem(own, PER_PROMPT), lax.rem(offset, PER_CONT))
    has_prev = lax.rem(inner, 2)
    pairs = jnp.where(is_prompt, lax.div(inner, 2), PER_PROMPT // 2)
    prev = own - has_prev
    return group * PER_PROMPT, pairs, prev, own, has_prev


def fill_inverse(order_ref, where_ref, inverse_ref):
    def put(index, carry):
        inverse_ref[order_ref[stored_block(index, where_ref)]] = index
        return carry

    lax.fori_loop(0, order_ref.shape[0], put, 0)


def rotate(vec, cosine, sine):
    return vec * cosine + pltpu.roll(vec, HEAD_SIZE // 2, 1) * sine


def unrotate(vec, cosine, sine):
    return vec * cosine + pltpu.roll(vec * sine, HEAD_SIZE // 2, 1)


def angle_tables():
    half = HEAD_SIZE // 2
    freq = np.float64(rope_base) ** (-(2.0 * np.arange(half) / HEAD_SIZE))
    freq = np.concatenate([freq, freq])
    starts = np.arange(-(-(PER_PROMPT + PER_CONT) // 8) * 8) * BLOCK
    start = starts[:, None] * freq[None]
    inner = np.arange(BLOCK)[:, None] * freq[None]
    return tuple(
        f(a).astype(np.float32) for a in (start, inner) for f in (np.cos, np.sin)
    )


def key_rows(inverse_ref, logical):
    return pl.ds(pl.multiple_of(inverse_ref[logical] * BLOCK, BLOCK), BLOCK)


def tile_pair(ref, rows_a, rows_b, column):
    cols = pl.ds(column, HEAD_SIZE)
    return jnp.concatenate([ref[rows_a, cols], ref[rows_b, cols]], axis=0)


def own_mask(has_prev, rep):
    shape = (2 * BLOCK, rep * BLOCK)
    row = lax.broadcasted_iota(jnp.int32, shape, 0)
    col = lax.broadcasted_iota(jnp.int32, shape, 1)
    first_row = BLOCK * (1 - has_prev)
    return (row >= first_row) & (row - BLOCK <= lax.rem(col, BLOCK))


def stack_t(ref, rows, column, rep):
    return jnp.concatenate(
        [ref[rows, pl.ds(column + r * HEAD_SIZE, HEAD_SIZE)].T for r in range(rep)], axis=1
    )


def stack_rows(ref, rows, column, rep):
    return jnp.concatenate(
        [ref[rows, pl.ds(column + r * HEAD_SIZE, HEAD_SIZE)] for r in range(rep)], axis=0
    )


def dot(left, right):
    return jnp.dot(left, right, preferred_element_type=jnp.float32)


def start_parts(parts, buffer_ref, sem, column):
    rows, width = parts[0].shape[0], buffer_ref.shape[1]
    copies = [
        pltpu.make_async_copy(
            part.at[:, pl.ds(column, width)], buffer_ref.at[pl.ds(p * rows, rows), :], sem.at[p]
        )
        for p, part in enumerate(parts)
    ]
    for copy in copies:
        copy.start()
    return copies


def forward_kernel(rep, hps, ctx_count, order_ref, cont_ref, where_ref, q_ref, wo_ref, *refs):
    parts, refs = refs[:ctx_count], refs[ctx_count:]
    out_ref, lse_ref, keep_ref, send_ref, kv_ref, inverse_ref, qt_ref, acc_ref, sem = refs
    copies = start_parts(parts, kv_ref, sem, 0)
    fill_inverse(order_ref, where_ref, inverse_ref)
    for copy in copies:
        copy.wait()
    q_blocks = q_ref.shape[0] // BLOCK
    factor = LOG2E / math.sqrt(HEAD_SIZE)
    width = rep * HEAD_SIZE

    def one_query_block(qb, carry):
        base, pairs, prev, own, has_prev = block_plan(order_ref, cont_ref, where_ref, qb)
        rows = pl.ds(pl.multiple_of(qb * BLOCK, BLOCK), BLOCK)
        mask = own_mask(has_prev, rep)
        rows_a, rows_b = key_rows(inverse_ref, prev), key_rows(inverse_ref, own)
        state = []
        for h in range(hps):
            qt = stack_t(q_ref, rows, h * width, rep)
            qt_ref[h] = qt
            scores = dot(tile_pair(kv_ref, rows_a, rows_b, 2 * h * HEAD_SIZE), qt) * factor
            scores = jnp.where(mask, scores, NEG)
            best = jnp.max(scores, axis=0, keepdims=True)
            weights = jnp.exp2(scores - best)
            total = jnp.sum(weights, axis=0, keepdims=True)
            values = tile_pair(kv_ref, rows_a, rows_b, (2 * h + 1) * HEAD_SIZE)
            acc_ref[h] = dot(values.T, weights.astype(jnp.bfloat16))
            state += [best, total]

        def one_pair(t, state):
            rows_a = key_rows(inverse_ref, base + 2 * t)
            rows_b = key_rows(inverse_ref, base + 2 * t + 1)
            after = []
            for h in range(hps):
                best, total = state[2 * h], state[2 * h + 1]
                keys = tile_pair(kv_ref, rows_a, rows_b, 2 * h * HEAD_SIZE)
                scores = dot(keys, qt_ref[h]) * factor
                newest = jnp.maximum(best, jnp.max(scores, axis=0, keepdims=True))
                weights = jnp.exp2(scores - newest)
                shrink = jnp.exp2(best - newest)
                total = total * shrink + jnp.sum(weights, axis=0, keepdims=True)
                values = tile_pair(kv_ref, rows_a, rows_b, (2 * h + 1) * HEAD_SIZE)
                acc_ref[h] = acc_ref[h] * shrink + dot(values.T, weights.astype(jnp.bfloat16))
                after += [newest, total]
            return tuple(after)

        state = lax.fori_loop(0, pairs, one_pair, tuple(state))
        for h in range(hps):
            best, total = state[2 * h], state[2 * h + 1]
            mixed = acc_ref[h] * (1.0 / total)
            for r in range(rep):
                part = mixed[:, r * BLOCK : (r + 1) * BLOCK]
                out_ref[rows, pl.ds(h * width + r * HEAD_SIZE, HEAD_SIZE)] = part.T.astype(
                    jnp.bfloat16
                )
            lse_ref[h, pl.ds(qb, 1), :] = best + jnp.log2(total)
        return carry

    lax.fori_loop(0, q_blocks, one_query_block, 0)
    mixed = out_ref[...]
    half = keep_ref.shape[0]
    for n in range(0, wo_ref.shape[1], 512):
        cols = slice(n, n + 512)
        partial = dot(mixed, wo_ref[:, cols]).astype(jnp.bfloat16)
        keep_ref[:, cols] = partial[:half]
        send_ref[:, cols] = partial[half:]


def backward_kernel(rep, hps, ctx_count, head, order_ref, cont_ref, where_ref, q_ref, gb_ref, wo_ref,
                    mix_ref, lse_ref, cos_ref, sin_ref, *refs):
    parts, refs = refs[:ctx_count], refs[ctx_count:]
    gq_ref, keep_ref, send_ref = refs[:3]
    kv_ref, gm_ref, inverse_ref, qt_ref, gmt_ref, gqt_ref, acc_ref, sem = refs[3:]
    copies = start_parts(parts, kv_ref, sem, head * kv_ref.shape[1])
    fill_inverse(order_ref, where_ref, inverse_ref)
    gm_ref[...] = right_dot(gb_ref[...], wo_ref[...]).astype(jnp.bfloat16)
    for copy in copies:
        copy.wait()
    q_blocks = q_ref.shape[0] // BLOCK
    scale = 1.0 / math.sqrt(HEAD_SIZE)
    factor = LOG2E * scale
    width = rep * HEAD_SIZE

    def clear(i, carry):
        acc_ref[pl.ds(pl.multiple_of(i * BLOCK, BLOCK), BLOCK), :] = jnp.zeros(
            (BLOCK, acc_ref.shape[1]), jnp.float32
        )
        return carry

    lax.fori_loop(0, order_ref.shape[0], clear, 0)

    def tile_terms(h, rows_a, rows_b, lse, delta, q_rows, gm_rows, mask):
        kcol, vcol = 2 * h * HEAD_SIZE, (2 * h + 1) * HEAD_SIZE
        keys = tile_pair(kv_ref, rows_a, rows_b, kcol)
        values = tile_pair(kv_ref, rows_a, rows_b, vcol)
        weights = jnp.exp2(dot(keys, qt_ref[h]) * factor - lse)
        if mask is not None:
            weights = jnp.where(mask, weights, 0.0)
        grad_weights = dot(values, gmt_ref[h])
        grad_scores = (weights * (grad_weights - delta)).astype(jnp.bfloat16)
        gv = dot(weights.astype(jnp.bfloat16), gm_rows)
        gk = dot(grad_scores, q_rows)
        acc_ref[rows_a, pl.ds(kcol, HEAD_SIZE)] += gk[:BLOCK]
        acc_ref[rows_b, pl.ds(kcol, HEAD_SIZE)] += gk[BLOCK:]
        acc_ref[rows_a, pl.ds(vcol, HEAD_SIZE)] += gv[:BLOCK]
        acc_ref[rows_b, pl.ds(vcol, HEAD_SIZE)] += gv[BLOCK:]
        return dot(keys.T, grad_scores)

    def one_query_block(qb, carry):
        base, pairs, prev, own, has_prev = block_plan(order_ref, cont_ref, where_ref, qb)
        rows = pl.ds(pl.multiple_of(qb * BLOCK, BLOCK), BLOCK)
        mask = own_mask(has_prev, rep)
        rows_a, rows_b = key_rows(inverse_ref, prev), key_rows(inverse_ref, own)
        deltas, lses, q_stack, gm_stack = [], [], [], []
        for h in range(hps):
            qt_ref[h] = stack_t(q_ref, rows, h * width, rep)
            gmt = stack_t(gm_ref, rows, h * width, rep)
            gmt_ref[h] = gmt
            mixt = stack_t(mix_ref, rows, h * width, rep)
            deltas.append(
                jnp.sum(
                    gmt.astype(jnp.float32) * mixt.astype(jnp.float32), axis=0, keepdims=True
                )
            )
            lses.append(lse_ref[h, pl.ds(qb, 1), :])
        for h in range(hps):
            q_rows = stack_rows(q_ref, rows, h * width, rep)
            gm_rows = stack_rows(gm_ref, rows, h * width, rep)
            gqt_ref[h] = tile_terms(
                h, rows_a, rows_b, lses[h], deltas[h], q_rows, gm_rows, mask
            )

        def one_pair(t, carry):
            rows_a = key_rows(inverse_ref, base + 2 * t)
            rows_b = key_rows(inverse_ref, base + 2 * t + 1)
            for h in range(hps):
                q_rows = stack_rows(q_ref, rows, h * width, rep)
                gm_rows = stack_rows(gm_ref, rows, h * width, rep)
                gqt_ref[h] += tile_terms(
                    h, rows_a, rows_b, lses[h], deltas[h], q_rows, gm_rows, None
                )
            return carry

        lax.fori_loop(0, pairs, one_pair, 0)
        for h in range(hps):
            total = gqt_ref[h] * scale
            for r in range(rep):
                part = total[:, r * BLOCK : (r + 1) * BLOCK]
                rounded = part.T.astype(jnp.bfloat16).astype(jnp.float32)
                gq_ref[rows, pl.ds(h * width + r * HEAD_SIZE, HEAD_SIZE)] = unrotate(
                    rounded, cos_ref[rows, :], sin_ref[rows, :]
                ).astype(jnp.bfloat16)
        return carry

    lax.fori_loop(0, q_blocks, one_query_block, 0)

    blocks = order_ref.shape[0]

    def place(index):
        chunk = lax.div(index, SLOTS)
        spot = (chunk & 1) * (ctx_count // 2) + (chunk & 2) // 2 * (ctx_count // 4) + (
            lax.shift_right_logical(chunk, 2)
        )
        return spot * SLOTS + (index & 3)

    def flush(i, carry):
        rows = pl.ds(pl.multiple_of(i * BLOCK, BLOCK), BLOCK)
        spot = place(i)
        parts = []
        for h in range(hps):
            parts.append(acc_ref[rows, pl.ds(2 * h * HEAD_SIZE, HEAD_SIZE)] * scale)
            parts.append(acc_ref[rows, pl.ds((2 * h + 1) * HEAD_SIZE, HEAD_SIZE)])
        value = jnp.concatenate(parts, axis=1).astype(jnp.bfloat16)

        @pl.when(spot < blocks // 2)
        def _():
            keep_ref[pl.ds(pl.multiple_of(spot * BLOCK, BLOCK), BLOCK), :] = value

        @pl.when(spot >= blocks // 2)
        def _():
            far = (spot - blocks // 2) * BLOCK
            send_ref[pl.ds(pl.multiple_of(far, BLOCK), BLOCK), :] = value

        return carry

    lax.fori_loop(0, blocks, flush, 0)


def attention_forward(q, w_out, parts, order, cont, where):
    ctx_count = len(parts)
    rows, tokens = q.shape[0], ctx_count * q.shape[0]
    kv_heads = parts[0].shape[1] // (2 * HEAD_SIZE)
    rep = q.shape[1] // HEAD_SIZE // kv_heads
    q_blocks, model = rows // BLOCK, w_out.shape[1]
    vmem, smem, any_ = (
        pl.BlockSpec(memory_space=space) for space in (pltpu.VMEM, pltpu.SMEM, pl.ANY)
    )
    flops = 2 * rows * tokens * q.shape[1] + 2 * rows * q.shape[1] * model
    half = jax.ShapeDtypeStruct((rows // 2, model), jnp.bfloat16)
    return pl.pallas_call(
        functools.partial(forward_kernel, rep, kv_heads, ctx_count),
        out_shape=(
            jax.ShapeDtypeStruct(q.shape, jnp.bfloat16),
            jax.ShapeDtypeStruct((kv_heads, q_blocks, rep * BLOCK), jnp.float32),
            half,
            half,
        ),
        in_specs=[smem] * 3 + [vmem] * 2 + [any_] * ctx_count,
        out_specs=[vmem] * 4,
        scratch_shapes=[
            pltpu.VMEM((tokens, parts[0].shape[1]), jnp.bfloat16),
            pltpu.SMEM((order.shape[0],), jnp.int32),
            pltpu.VMEM((kv_heads, HEAD_SIZE, rep * BLOCK), jnp.bfloat16),
            pltpu.VMEM((kv_heads, HEAD_SIZE, rep * BLOCK), jnp.float32),
            pltpu.SemaphoreType.DMA((ctx_count,)),
        ],
        compiler_params=pltpu.CompilerParams(vmem_limit_bytes=40 << 20),
        cost_estimate=cost(flops, 2 * tokens * parts[0].shape[1] + 4 * rows * model),
        name="attention_forward",
    )(order, cont, where, q, w_out, *parts)


def attention_backward(head, q, grad_branch, w_out, mixed, lse, parts, cosine, sine, order, cont,
                       where):
    ctx_count = len(parts)
    rows, tokens = q.shape[0], ctx_count * q.shape[0]
    kv_heads = parts[0].shape[1] // (2 * HEAD_SIZE)
    rep = q.shape[1] // HEAD_SIZE // kv_heads
    q_blocks, model = rows // BLOCK, w_out.shape[1]
    wide = rep * HEAD_SIZE
    q_spec = pl.BlockSpec((rows, wide), lambda g, *_: (0, head))
    whole = lambda g, *_: (0, 0)
    table_spec = pl.BlockSpec((rows, HEAD_SIZE), whole)
    half = (tokens // 2, 2 * HEAD_SIZE)
    flops = 5 * rows * tokens * wide + 2 * rows * wide * model
    return pl.pallas_call(
        functools.partial(backward_kernel, rep, 1, ctx_count, head),
        out_shape=(
            jax.ShapeDtypeStruct((rows, wide), jnp.bfloat16),
            jax.ShapeDtypeStruct(half, jnp.bfloat16),
            jax.ShapeDtypeStruct(half, jnp.bfloat16),
        ),
        grid_spec=pltpu.PrefetchScalarGridSpec(
            num_scalar_prefetch=3,
            grid=(1,),
            in_specs=[
                q_spec,
                pl.BlockSpec((rows, model), whole),
                pl.BlockSpec((wide, model), lambda g, *_: (head, 0)),
                q_spec,
                pl.BlockSpec((1, q_blocks, rep * BLOCK), lambda g, *_: (head, 0, 0)),
                table_spec,
                table_spec,
            ]
            + [pl.BlockSpec(memory_space=pl.ANY)] * ctx_count,
            out_specs=[
                pl.BlockSpec((rows, wide), whole),
                pl.BlockSpec(half, whole),
                pl.BlockSpec(half, whole),
            ],
            scratch_shapes=[
                pltpu.VMEM((tokens, 2 * HEAD_SIZE), jnp.bfloat16),
                pltpu.VMEM((rows, wide), jnp.bfloat16),
                pltpu.SMEM((order.shape[0],), jnp.int32),
                pltpu.VMEM((1, HEAD_SIZE, rep * BLOCK), jnp.bfloat16),
                pltpu.VMEM((1, HEAD_SIZE, rep * BLOCK), jnp.bfloat16),
                pltpu.VMEM((1, HEAD_SIZE, rep * BLOCK), jnp.float32),
                pltpu.VMEM((tokens, 2 * HEAD_SIZE), jnp.float32),
                pltpu.SemaphoreType.DMA((ctx_count,)),
            ],
        ),
        compiler_params=pltpu.CompilerParams(vmem_limit_bytes=56 << 20),
        cost_estimate=cost(flops, 4 * tokens * wide + 2 * rows * model),
        name=f"attention_backward_{head}",
    )(order, cont, where, q, grad_branch, w_out, mixed, lse, cosine, sine, *parts)


def input_kernel(order_ref, cont_ref, where_ref, gain_ref, x_hbm, wq_hbm, wk_hbm, wv_hbm, table_hbm,
                 first_ref, q_ref, kv_ref, cos_ref, sin_ref,
                 x_ref, wq_ref, wk_ref, wv_ref, table_ref, sem):
    pairs = ((x_hbm, x_ref), (table_hbm, table_ref), (wk_hbm, wk_ref), (wv_hbm, wv_ref),
             (wq_hbm, wq_ref))
    copies = [
        pltpu.make_async_copy(source, target, sem.at[n])
        for n, (source, target) in enumerate(pairs)
    ]
    for copy in copies:
        copy.start()
    count = cont_ref.shape[0]
    prompt_blocks = count // CONTS * PER_PROMPT
    starts = (table_ref.shape[0] - 2 * BLOCK) // 2
    lane = lax.broadcasted_iota(jnp.int32, (BLOCK, HEAD_SIZE), 1)
    copies[0].wait()
    copies[1].wait()

    def one_slot(slot, carry):
        quarter = slot_quarter(slot, where_ref[1])
        rows = pl.ds(pl.multiple_of(slot * BLOCK, BLOCK), BLOCK)
        full = x_ref[pl.ds(pl.multiple_of(quarter * BLOCK, BLOCK), BLOCK), :].astype(jnp.float32)
        inv = lax.rsqrt(jnp.mean(full * full, axis=-1, keepdims=True) + eps_norm)
        first_ref[rows, :] = (full * inv * gain_ref[...]).astype(jnp.bfloat16)
        own = order_ref[stored_block(slot, where_ref)]
        spot = jnp.where(
            own < prompt_blocks,
            lax.rem(own, PER_PROMPT),
            PER_PROMPT + lax.rem(own - prompt_blocks, PER_CONT),
        )
        cos_start = table_ref[pl.ds(2 * BLOCK + spot, 1), :]
        sin_start = table_ref[pl.ds(2 * BLOCK + starts + spot, 1), :]
        cos_in, sin_in = table_ref[:BLOCK, :], table_ref[BLOCK : 2 * BLOCK, :]
        sine = sin_start * cos_in + cos_start * sin_in
        cos_ref[rows, :] = cos_start * cos_in - sin_start * sin_in
        sin_ref[rows, :] = jnp.where(lane < HEAD_SIZE // 2, -sine, sine)
        return carry

    lax.fori_loop(0, SLOTS, one_slot, 0)
    first = first_ref[...]
    cosine, sine = cos_ref[...], sin_ref[...]
    copies[2].wait()
    copies[3].wait()
    keys = dot(first, wk_ref[...])
    values = dot(first, wv_ref[...])
    for h in range(wk_ref.shape[1] // HEAD_SIZE):
        cols = slice(h * HEAD_SIZE, (h + 1) * HEAD_SIZE)
        low, high = 2 * h * HEAD_SIZE, (2 * h + 1) * HEAD_SIZE
        key = rotate(keys[:, cols], cosine, sine)
        kv_ref[:, low:high] = key.astype(jnp.bfloat16)
        kv_ref[:, high : high + HEAD_SIZE] = values[:, cols].astype(jnp.bfloat16)
    copies[4].wait()
    for n in range(0, wq_ref.shape[1], 256):
        queries = dot(first, wq_ref[:, n : n + 256])
        for m in range(0, 256, HEAD_SIZE):
            query = rotate(queries[:, m : m + HEAD_SIZE], cosine, sine)
            q_ref[:, n + m : n + m + HEAD_SIZE] = query.astype(jnp.bfloat16)


def input_stage(x, gain, wq, wk, wv, order, cont, where):
    rows, model = x.shape
    cos_start, sin_start, cos_in, sin_in = angle_tables()
    table = np.concatenate([cos_in, sin_in, cos_start, sin_start])
    vmem, smem, any_ = (
        pl.BlockSpec(memory_space=space) for space in (pltpu.VMEM, pltpu.SMEM, pl.ANY)
    )
    flops = 2 * rows * model * (wq.shape[1] + 2 * wk.shape[1])
    return pl.pallas_call(
        input_kernel,
        out_shape=(
            jax.ShapeDtypeStruct((rows, model), jnp.bfloat16),
            jax.ShapeDtypeStruct((rows, wq.shape[1]), jnp.bfloat16),
            jax.ShapeDtypeStruct((rows, 2 * wk.shape[1]), jnp.bfloat16),
            jax.ShapeDtypeStruct((rows, HEAD_SIZE), jnp.float32),
            jax.ShapeDtypeStruct((rows, HEAD_SIZE), jnp.float32),
        ),
        in_specs=[smem] * 3 + [vmem] + [any_] * 5,
        out_specs=[vmem] * 5,
        scratch_shapes=[
            pltpu.VMEM(a.shape, a.dtype) for a in (x, wq, wk, wv)
        ]
        + [pltpu.VMEM(table.shape, jnp.float32), pltpu.SemaphoreType.DMA((5,))],
        compiler_params=pltpu.CompilerParams(vmem_limit_bytes=40 << 20),
        cost_estimate=cost(flops, 4 * x.size + 2 * wq.size + 4 * wk.size),
        name="input_stage",
    )(order, cont, where, gain.reshape(1, -1), x, wq, wk, wv, table)


def cost(flops, bytes_accessed):
    return pl.CostEstimate(
        flops=int(flops), bytes_accessed=int(bytes_accessed), transcendentals=0
    )


def put_share(value, index, x_bit, keep_ref, send_ref, swap_bits):
    spot = lax.shift_right_logical(index, 1)
    if swap_bits:
        spot = (spot & 1) * (keep_ref.shape[0] // 2) + lax.shift_right_logical(spot, 1)
    stays = (index & 1) == x_bit
    value = value.astype(keep_ref.dtype)

    @pl.when(stays)
    def _():
        keep_ref[pl.ds(spot, 1)] = value[None]

    @pl.when(jnp.logical_not(stays))
    def _():
        send_ref[pl.ds(spot, 1)] = value[None]


def pair_bit(where_ref):
    return lax.shift_right_logical(where_ref[0], 1) & 1


def grad_hidden_kernel(where_ref, cot_ref, wd_ref, out_ref):
    out_ref[...] = right_dot(cot_ref[...], wd_ref[...])


def grad_hidden_stage(cot, w_down, where):
    rows, model = cot.shape
    units = w_down.shape[0] // 2
    block = 256
    steps = units // block
    return pl.pallas_call(
        grad_hidden_kernel,
        out_shape=jax.ShapeDtypeStruct((rows, units), jnp.float32),
        grid_spec=pltpu.PrefetchScalarGridSpec(
            num_scalar_prefetch=1,
            grid=(steps,),
            in_specs=[
                pl.BlockSpec((rows, model), lambda i, w: (0, 0), pipeline_mode=pl.Buffered(1)),
                pl.BlockSpec((block, model), lambda i, w: (pair_bit(w) * steps + i, 0)),
            ],
            out_specs=pl.BlockSpec((rows, block), lambda i, w: (0, i)),
        ),
        compiler_params=pltpu.CompilerParams(vmem_limit_bytes=32 << 20),
        cost_estimate=cost(2 * rows * model * units, 4 * rows * model),
        name="grad_hidden",
    )(where, cot, w_down)


def ffn_kernel(where_ref, in_ref, gh_ref, wg_ref, wu_ref, hid_ref, gg_ref, gu_ref):
    gate = dot(in_ref[...], wg_ref[...])
    upward = dot(in_ref[...], wu_ref[...])
    grad_hidden = gh_ref[...]
    sigma = jax.nn.sigmoid(gate)
    swish = gate * sigma
    hid_ref[...] = (swish * upward).astype(jnp.bfloat16)
    gg_ref[...] = (grad_hidden * upward * sigma * (1.0 + gate * (1.0 - sigma))).astype(
        jnp.bfloat16
    )
    gu_ref[...] = (grad_hidden * swish).astype(jnp.bfloat16)


def ffn_stage(second, grad_hidden, w_gate, w_up, where):
    rows, model = second.shape
    units = w_gate.shape[1] // 2
    block = 256
    steps = units // block
    col_spec = pl.BlockSpec((model, block), lambda i, w: (0, pair_bit(w) * steps + i))
    unit_spec = pl.BlockSpec((rows, block), lambda i, w: (0, i))
    unit = jax.ShapeDtypeStruct((rows, units), jnp.bfloat16)
    return pl.pallas_call(
        ffn_kernel,
        out_shape=(unit, unit, unit),
        grid_spec=pltpu.PrefetchScalarGridSpec(
            num_scalar_prefetch=1,
            grid=(steps,),
            in_specs=[
                pl.BlockSpec((rows, model), lambda i, w: (0, 0), pipeline_mode=pl.Buffered(1)),
                unit_spec,
                col_spec,
                col_spec,
            ],
            out_specs=[unit_spec] * 3,
        ),
        compiler_params=pltpu.CompilerParams(vmem_limit_bytes=44 << 20),
        cost_estimate=cost(4 * rows * model * units, 6 * rows * model),
        name="ffn_stage",
    )(where, second, grad_hidden, w_gate, w_up)


def grad_second_kernel(where_ref, gg_ref, gu_ref, wg_ref, wu_ref, keep_ref, send_ref):
    total = right_dot(gg_ref[...], wg_ref[...]) + right_dot(gu_ref[...], wu_ref[...])
    half = keep_ref.shape[0]
    keep_ref[...] = total[:half].astype(jnp.bfloat16)
    send_ref[...] = total[half:].astype(jnp.bfloat16)


def ffn_out_kernel(where_ref, hid_ref, wd_ref, keep_ref, send_ref):
    total = dot(hid_ref[...], wd_ref[...])
    half = keep_ref.shape[0]
    keep_ref[...] = total[:half].astype(jnp.bfloat16)
    send_ref[...] = total[half:].astype(jnp.bfloat16)


def unit_sum(kernel, name, lefts, rights, transposed, where):
    rows, units = lefts[0].shape
    model = rights[0].shape[0 if transposed else 1]
    block = 512
    if transposed:
        right_spec = pl.BlockSpec((block, units), lambda n, w: (n, pair_bit(w)))
    else:
        right_spec = pl.BlockSpec((units, block), lambda n, w: (pair_bit(w), n))
    left_spec = pl.BlockSpec((rows, units), lambda n, w: (0, 0), pipeline_mode=pl.Buffered(1))
    half = jax.ShapeDtypeStruct((rows // 2, model), jnp.bfloat16)
    half_spec = pl.BlockSpec((rows // 2, block), lambda n, w: (0, n))
    return pl.pallas_call(
        kernel,
        out_shape=(half, half),
        grid_spec=pltpu.PrefetchScalarGridSpec(
            num_scalar_prefetch=1,
            grid=(model // block,),
            in_specs=[left_spec] * len(lefts) + [right_spec] * len(rights),
            out_specs=[half_spec, half_spec],
        ),
        compiler_params=pltpu.CompilerParams(vmem_limit_bytes=32 << 20),
        cost_estimate=cost(2 * len(lefts) * rows * units * model, 4 * rows * model),
        name=name,
    )(where, *lefts, *rights)


def shares_kernel(left_count, swap_bits, pairs, where_ref, *refs):
    lefts, refs = refs[:left_count], refs[left_count:]
    rights, (keep_ref, send_ref) = refs[:-2], refs[-2:]
    share = keep_ref.shape[1]
    step = pl.program_id(0)
    pieces = [left_dot(lefts[l][...], rights[r][...]) for l, r in pairs]
    per_step = lefts[0].shape[1] // share
    for k in range(per_step):
        rows = slice(k * share, (k + 1) * share)
        value = jnp.concatenate([piece[rows] for piece in pieces], axis=1)
        index = step * per_step + k
        put_share(value, index, where_ref[0] & 1, keep_ref, send_ref, swap_bits)


def weight_shares(name, lefts, rights, pairs, ctx_count, swap_bits, where):
    rows, model = lefts[0].shape
    block = 256
    share = model // ctx_count
    width = sum(rights[r].shape[1] for _, r in pairs)
    shares = jax.ShapeDtypeStruct((ctx_count // 2, share, width), jnp.bfloat16)
    share_spec = pl.BlockSpec(shares.shape, lambda i, w: (0, 0, 0))
    return pl.pallas_call(
        functools.partial(shares_kernel, len(lefts), swap_bits, pairs),
        out_shape=(shares, shares),
        grid_spec=pltpu.PrefetchScalarGridSpec(
            num_scalar_prefetch=1,
            grid=(model // block,),
            in_specs=[pl.BlockSpec((rows, block), lambda i, w: (0, i))] * len(lefts)
            + [
                pl.BlockSpec(r.shape, lambda i, w: (0, 0), pipeline_mode=pl.Buffered(1))
                for r in rights
            ],
            out_specs=[share_spec, share_spec],
        ),
        compiler_params=pltpu.CompilerParams(vmem_limit_bytes=36 << 20),
        cost_estimate=cost(2 * rows * model * width, 4 * rows * model),
        name=name,
    )(where, *lefts, *rights)


def tail_kernel(kv_heads, where_ref, *refs):
    sums, refs = refs[: 2 * kv_heads], refs[2 * kv_heads :]
    cos_ref, sin_ref, refs = refs[0], refs[1], refs[2:]
    gq_refs, refs = refs[:kv_heads], refs[kv_heads:]
    wq_ref, wk_ref, wv_ref, keep_ref, send_ref, gkv_ref = refs
    cosine, sine = cos_ref[...], sin_ref[...]
    for h in range(kv_heads):
        total = sums[2 * h][...].astype(jnp.float32) + sums[2 * h + 1][...].astype(jnp.float32)
        total = total.astype(jnp.bfloat16)
        key = unrotate(total[:, :HEAD_SIZE].astype(jnp.float32), cosine, sine)
        cols = slice(h * HEAD_SIZE, (h + 1) * HEAD_SIZE)
        gkv_ref[:, cols] = key.astype(jnp.bfloat16)
        cols = slice((kv_heads + h) * HEAD_SIZE, (kv_heads + h + 1) * HEAD_SIZE)
        gkv_ref[:, cols] = total[:, HEAD_SIZE:]
    half = keep_ref.shape[0]
    key_width = kv_heads * HEAD_SIZE
    wide = gq_refs[0].shape[1]
    for n in range(0, wq_ref.shape[0], 512):
        span = slice(n, n + 512)
        total = right_dot(gkv_ref[:, :key_width], wk_ref[span, :])
        total += right_dot(gkv_ref[:, key_width:], wv_ref[span, :])
        for h in range(kv_heads):
            total += right_dot(gq_refs[h][...], wq_ref[span, h * wide : (h + 1) * wide])
        total = total.astype(jnp.bfloat16)
        keep_ref[:, span] = total[:half]
        send_ref[:, span] = total[half:]


def tail_stage(kv_sums, cosine, sine, grad_queries, wq, wk, wv, where):
    rows, model = cosine.shape[0], wq.shape[0]
    kv_heads = len(grad_queries)
    vmem = pl.BlockSpec(memory_space=pltpu.VMEM)
    half = jax.ShapeDtypeStruct((rows // 2, model), jnp.bfloat16)
    flat = [term for sums in kv_sums for term in sums]
    return pl.pallas_call(
        functools.partial(tail_kernel, kv_heads),
        out_shape=(
            half,
            half,
            jax.ShapeDtypeStruct((rows, 2 * kv_heads * HEAD_SIZE), jnp.bfloat16),
        ),
        in_specs=[pl.BlockSpec(memory_space=pltpu.SMEM)]
        + [vmem] * (len(flat) + 2 + kv_heads + 3),
        out_specs=[vmem] * 3,
        compiler_params=pltpu.CompilerParams(vmem_limit_bytes=32 << 20),
        cost_estimate=cost(
            2 * rows * model * (wq.shape[1] + 2 * wk.shape[1]), 4 * rows * model + 4 * wq.size
        ),
        name="tail_stage",
    )(where, *flat, cosine, sine, *grad_queries, wq, wk, wv)


def flip(value, axis, mask):
    return lax.ppermute(value, axis, [(i, i ^ mask) for i in range(lax.axis_size(axis))])


def add(left, right):
    return (left.astype(jnp.float32) + right.astype(jnp.float32)).astype(jnp.bfloat16)


def slots_of(value, tensor):
    rows = value.shape[0] // SLOTS
    return [
        lax.dynamic_slice_in_dim(value, (tensor ^ SLOT_XOR[u]) * rows, rows)
        for u in range(SLOTS)
    ]


def after(dep, *values):
    held = lax.optimization_barrier((dep,) + values)[1:]
    return held[0] if len(held) == 1 else held


def gather_slots(own):
    near = jnp.concatenate([own, flip(own, "tp", 2)])
    return jnp.concatenate([near, flip(near, "tp", 1)])


def gather_pair(own):
    partner = flip(own, "ctx", 2)
    near = jnp.concatenate([own, partner, flip(own, "tp", 2), flip(partner, "tp", 2)])
    return jnp.concatenate([near, flip(near, "tp", 1)])


def gather_rows(own, tensor):
    rows = own.shape[0]
    near = jnp.concatenate([own, flip(own, "tp", 2)])
    far = flip(near, "tp", 1)
    pieces = (near[:rows], near[rows:], far[:rows], far[rows:])
    result = jnp.zeros((SLOTS * rows,) + own.shape[1:], own.dtype)
    for u in range(SLOTS):
        result = lax.dynamic_update_slice_in_dim(
            result, pieces[u], (tensor ^ SLOT_XOR[u]) * rows, 0
        )
    return result


def scatter_slots(keep, send):
    got = flip(send, "tp", 1)
    quarter = keep.shape[0] // 2
    far = flip(add(keep[quarter:], got[quarter:]), "tp", 2)
    return add(keep[:quarter], got[:quarter]), far


def pair_scatter(keep, send):
    got = flip(send, "tp", 1)
    n = keep.shape[0] // 4
    near = [add(keep[k * n : (k + 1) * n], got[k * n : (k + 1) * n]) for k in (3, 1, 2, 0)]
    away = flip(add(near[1], flip(near[0], "tp", 2)), "ctx", 2)
    return near[3], flip(near[2], "tp", 2), away


def total(terms):
    return sum(term.astype(jnp.float32) for term in terms)


def gather_keys(kv_local, ctx_count):
    parts = {0: kv_local}
    for bit in reversed(high_masks(ctx_count)):
        for mask in list(parts):
            parts[mask + bit] = flip(parts[mask], "ctx", bit)
    for bit in (2, 1):
        for mask in list(parts):
            parts[mask + bit] = flip(parts[mask], "ctx", bit)
    return [parts[mask] for mask in range(ctx_count)]


def all_sum(value, ctx_count):
    for axis, mask in [("tp", 1), ("tp", 2), ("ctx", 1), ("ctx", 2)] + [
        ("ctx", mask) for mask in high_masks(ctx_count)
    ]:
        value = value + flip(value, axis, mask)
    return value


class Reduce:
    def __init__(self, keep, send):
        self.keep, self.got = keep, flip(send, "ctx", 1)

    def halve(self, mask, ctx, dep=None):
        keep, got = self.keep, self.got
        if dep is not None:
            keep, got = after(dep, keep, got)
        n = keep.shape[0] // 2
        bit = lax.div(ctx, mask) % 2
        pick = lambda value, index: lax.dynamic_slice_in_dim(value, index * n, n, 0)
        away = flip(add(pick(keep, 1 - bit), pick(got, 1 - bit)), "ctx", mask)
        self.keep, self.got = add(pick(keep, bit), pick(got, bit)), away

    def sum(self):
        return (self.keep.astype(jnp.float32) + self.got.astype(jnp.float32))[0]


def high_masks(ctx_count):
    masks, mask = [], ctx_count // 2
    while mask >= 4:
        masks.append(mask)
        mask //= 2
    return masks


def both_halves(reduce, ctx, axis, dep=None):
    keep, got = reduce.keep, reduce.got
    if dep is not None:
        keep, got = after(dep, keep, got)
    pair = lax.div(ctx, 2) % 2
    pick = lambda value, index: lax.dynamic_slice_in_dim(value, index, 1, 0)[0]
    other = flip(add(pick(keep, 1 - pair), pick(got, 1 - pair)), "ctx", 2)
    own = add(pick(keep, pair), pick(got, pair))
    low, high = jnp.where(pair == 0, own, other), jnp.where(pair == 0, other, own)
    return jnp.concatenate([low, high], axis=axis).astype(jnp.float32)


class KvReduce:
    def __init__(self, keep, send):
        self.keep, self.got = keep, flip(send, "ctx", 1)

    def halve(self, mask, dep):
        keep, got = after(dep, self.keep, self.got)
        n = keep.shape[0] // 2
        away = flip(add(keep[n:], got[n:]), "ctx", mask)
        self.keep, self.got = add(keep[:n], got[:n]), away


def norm_back(grad_out, normed, inv_scale, gain):
    scaled = grad_out * gain
    inner = jnp.mean(scaled * normed, axis=-1, keepdims=True)
    return (inv_scale * (scaled - normed * inner), jnp.sum(grad_out * normed, axis=0))


def body(
    layer_input,
    attn_gain,
    w_query,
    key_matrix,
    value_matrix,
    w_out,
    ffn_gain,
    w_gate,
    w_up,
    w_down,
    cotangent,
    block_order,
    cont_prompt,
):
    ctx_count = lax.axis_size("ctx")
    tp_count = lax.axis_size("tp")
    ctx, tensor = lax.axis_index("ctx"), lax.axis_index("tp")
    where = jnp.stack([ctx, tensor]).astype(jnp.int32)
    quarter = layer_input.shape[0] // SLOTS
    kv_heads = key_matrix.shape[1] // HEAD_SIZE
    highs = high_masks(ctx_count)

    first_input, queries, kv_local, cosine, sine = input_stage(
        layer_input, attn_gain, w_query, key_matrix, value_matrix, block_order, cont_prompt, where
    )
    cot_own = lax.dynamic_slice_in_dim(cotangent, tensor * quarter, quarter)
    cot_slots = slots_of(cotangent, tensor)
    cot_part = flip(cot_own, "ctx", 2)
    parts = gather_keys(after(cot_part, kv_local), ctx_count)
    cot_part = jnp.concatenate([cot_part, flip(cot_part, "tp", 2)])
    cot_far = flip(cot_part, "tp", 1)
    cot = jnp.concatenate(
        [cot_slots[0], cot_part[:quarter], cot_slots[1], cot_part[quarter:]]
        + [cot_slots[2], cot_far[:quarter], cot_slots[3], cot_far[quarter:]]
    )
    grad_hidden = grad_hidden_stage(cot, w_down, where)

    mixed, log_total, keep, send = attention_forward(
        after(grad_hidden, queries), w_out, parts, block_order, cont_prompt, where
    )
    own_input = lax.dynamic_slice_in_dim(layer_input, tensor * quarter, quarter)
    own_input = own_input.astype(jnp.float32)
    middle = own_input + total(scatter_slots(keep, send))
    inv_two = lax.rsqrt(jnp.mean(middle * middle, axis=-1, keepdims=True) + eps_norm)
    normed_two = middle * inv_two
    second = gather_pair((normed_two * ffn_gain).astype(jnp.bfloat16))
    hidden, grad_gate, grad_up = ffn_stage(second, grad_hidden, w_gate, w_up, where)

    down_shares = weight_shares(
        "down_shares", (cot,), (hidden,), ((0, 0),), ctx_count, False, where
    )
    down = Reduce(*down_shares)
    grad_gate, grad_up = after(down_shares[0], grad_gate, grad_up)
    partial = unit_sum(
        grad_second_kernel, "grad_second", (grad_gate, grad_up), (w_gate, w_up), True, where
    )
    second_terms = pair_scatter(*partial)

    def unit_shares(name, grad, dep):
        return weight_shares(
            name, (second,), (after(dep, grad),), ((0, 0),), ctx_count, False, where
        )

    gate_shares = unit_shares("gate_shares", grad_gate, partial[0])
    up_shares = unit_shares("up_shares", grad_up, gate_shares[0])
    ffn_halves = unit_sum(
        ffn_out_kernel, "ffn_out", (after(up_shares[0], hidden),), (w_down,), False, where
    )
    dep = ffn_halves[0]
    for mask in highs:
        down.halve(mask, ctx, dep)
        dep = down.keep
    gate = Reduce(*after(dep, *gate_shares))
    grad_norm_two, ffn_gain_part = norm_back(
        total(after(dep, *second_terms)), normed_two, inv_two, ffn_gain
    )
    grad_middle = cot_own.astype(jnp.float32) + grad_norm_two
    grad_branch = gather_slots(grad_middle.astype(jnp.bfloat16))
    backward, kv = [], []
    held = grad_branch
    for head in range(kv_heads):
        backward.append(
            attention_backward(
                head, queries, held, w_out, mixed, log_total, parts, cosine, sine,
                block_order, cont_prompt, where,
            )
        )
        held = after(backward[-1][0], grad_branch)
        kv.append(KvReduce(*backward[-1][1:]))
    grad_queries = [item[0] for item in backward]
    dep = grad_queries[-1]
    for mask in highs:
        gate.halve(mask, ctx, dep)
        dep = gate.keep
    branch_shares = weight_shares(
        "branch_shares",
        (first_input, grad_branch),
        grad_queries + [after(dep, mixed)],
        tuple((0, h) for h in range(kv_heads)) + ((1, kv_heads),),
        ctx_count,
        True,
        where,
    )
    kv[0].halve(2, branch_shares[0])
    ffn_terms = pair_scatter(*after(kv[0].keep, *ffn_halves))
    for item in kv[1:]:
        item.halve(2, kv[0].keep)
    up = Reduce(*after(kv[-1].keep, *up_shares))
    for mask in highs:
        for item in kv:
            item.halve(mask, kv[-1].keep)
    sum_down = both_halves(down, ctx, 1, kv[0].keep).T
    keep, send, grad_kv = tail_stage(
        [(item.keep, item.got) for item in kv], cosine, sine, grad_queries,
        w_query, key_matrix, value_matrix, where,
    )
    first_terms = scatter_slots(keep, send)
    kv_shares = weight_shares(
        "kv_shares", (first_input,), (grad_kv,), ((0, 0),), ctx_count, True, where
    )
    dep = kv_shares[0]
    for mask in highs:
        up.halve(mask, ctx, dep)
        dep = up.keep
    branch = Reduce(*after(dep, *branch_shares))
    inv_one = lax.rsqrt(jnp.mean(own_input * own_input, axis=-1, keepdims=True) + eps_norm)
    grad_norm_one, attn_gain_part = norm_back(
        total(after(dep, *first_terms)), own_input * inv_one, inv_one, attn_gain
    )
    grad_input = (grad_middle + grad_norm_one).astype(jnp.bfloat16)
    output = gather_rows((middle + total(ffn_terms)).astype(jnp.bfloat16), tensor)
    sum_gate = both_halves(gate, ctx, 1, grad_input)
    grad_input = gather_rows(grad_input, tensor)
    gains = all_sum(jnp.stack([attn_gain_part, ffn_gain_part]), ctx_count)
    branch.halve(2, ctx)
    last = Reduce(*after(branch.keep, *kv_shares))
    for mask in highs:
        branch.halve(mask, ctx)
    sum_up = both_halves(up, ctx, 1)
    for mask in [2] + highs:
        last.halve(mask, ctx)
    width_q, width_k = w_query.shape[1], key_matrix.shape[1]
    branch_sum, last_sum = branch.sum(), last.sum()
    sum_query, sum_out = branch_sum[:, :width_q], branch_sum[:, width_q:].T
    sum_key, sum_value = last_sum[:, :width_k], last_sum[:, width_k:]

    gains = gains.reshape(2, ctx_count * tp_count, -1)
    gains = lax.dynamic_index_in_dim(gains, ctx * tp_count + tensor, 1, keepdims=False)
    return (
        output,
        grad_input,
        gains[0],
        sum_query,
        sum_key,
        sum_value,
        sum_out,
        gains[1],
        sum_gate,
        sum_up,
        sum_down,
    )


def solution(mesh):
    placed = (
        P("ctx", None),
        P(),
        P(None, "tp"),
        P(None, "tp"),
        P(None, "tp"),
        P("tp", None),
        P(),
        P(None, "tp"),
        P(None, "tp"),
        P("tp", None),
        P("ctx", None),
        P(),
        P(),
    )
    return jax.shard_map(
        body,
        mesh=mesh,
        in_specs=placed,
        out_specs=(
            P("ctx", None),
            P("ctx", None),
            P(("ctx", "tp")),
            P("ctx", "tp"),
            P("ctx", "tp"),
            P("ctx", "tp"),
            P("tp", "ctx"),
            P(("ctx", "tp")),
            P("ctx", "tp"),
            P("ctx", "tp"),
            P("tp", "ctx"),
        ),
        check_vma=False,
    )
```

```python
import functools
import math

import jax
import jax.numpy as jnp
import numpy as np
from jax import lax
from jax.experimental import pallas as pl
from jax.experimental.pallas import tpu as pltpu
from jax.sharding import PartitionSpec as P

HEAD_SIZE = 128
PROMPT = 2048
CONT_LEN = 256
CONTS = 8
BLOCK = 128
PER_PROMPT = PROMPT // BLOCK
PER_CONT = CONT_LEN // BLOCK
LOG2E = 1.4426950408889634
NEG = -1e30
SLOTS = 4
VMEM_LIMIT = 60 << 20

eps_norm = 1e-05
rope_base = 1000000.0

SLOT_XOR = (0, 2, 1, 3)


def plain_dot(left, right):
    return jnp.dot(left, right, preferred_element_type=jnp.float32)


def left_dot(left, right):
    return lax.dot_general(
        left, right, (((0,), (0,)), ((), ())), preferred_element_type=jnp.float32
    )


def right_dot(left, right):
    return lax.dot_general(
        left, right, (((1,), (1,)), ((), ())), preferred_element_type=jnp.float32
    )


def slot_quarter(slot, tensor):
    return ((slot & 1) * 2 + lax.shift_right_logical(slot, 1)) ^ tensor


def stored_block(index, where_ref):
    rank = lax.div(index, SLOTS) ^ where_ref[0]
    return rank * SLOTS + slot_quarter(index & 3, where_ref[1])


def block_plan(order_ref, cont_ref, where_ref, slot):
    count = cont_ref.shape[0]
    prompt_blocks = count // CONTS * PER_PROMPT
    own = order_ref[stored_block(slot, where_ref)]
    is_prompt = own < prompt_blocks
    offset = own - prompt_blocks
    which = jnp.clip(lax.div(offset, PER_CONT), 0, count - 1)
    group = jnp.where(is_prompt, lax.div(own, PER_PROMPT), cont_ref[which])
    inner = jnp.where(is_prompt, lax.rem(own, PER_PROMPT), lax.rem(offset, PER_CONT))
    has_prev = lax.rem(inner, 2)
    pairs = jnp.where(is_prompt, lax.div(inner, 2), PER_PROMPT // 2)
    prev = own - has_prev
    return group * PER_PROMPT, pairs, prev, own, has_prev


def fill_inverse(order_ref, where_ref, inverse_ref):
    def put(index, carry):
        inverse_ref[order_ref[stored_block(index, where_ref)]] = index
        return carry

    lax.fori_loop(0, order_ref.shape[0], put, 0)


def rotate(vec, cosine, sine):
    return vec * cosine + pltpu.roll(vec, HEAD_SIZE // 2, 1) * sine


def unrotate(vec, cosine, sine):
    return vec * cosine + pltpu.roll(vec * sine, HEAD_SIZE // 2, 1)


def angle_tables():
    half = HEAD_SIZE // 2
    freq = np.float64(rope_base) ** (-(2.0 * np.arange(half) / HEAD_SIZE))
    freq = np.concatenate([freq, freq])
    starts = np.arange(-(-(PER_PROMPT + PER_CONT) // 8) * 8) * BLOCK
    start = starts[:, None] * freq[None]
    inner = np.arange(BLOCK)[:, None] * freq[None]
    return tuple(
        f(a).astype(np.float32) for a in (start, inner) for f in (np.cos, np.sin)
    )


def key_rows(inverse_ref, logical):
    return pl.ds(pl.multiple_of(inverse_ref[logical] * BLOCK, BLOCK), BLOCK)


def tile_pair(ref, rows_a, rows_b, column):
    cols = pl.ds(column, HEAD_SIZE)
    return jnp.concatenate([ref[rows_a, cols], ref[rows_b, cols]], axis=0)


def own_mask(has_prev, rep):
    shape = (2 * BLOCK, rep * BLOCK)
    row = lax.broadcasted_iota(jnp.int32, shape, 0)
    col = lax.broadcasted_iota(jnp.int32, shape, 1)
    first_row = BLOCK * (1 - has_prev)
    return (row >= first_row) & (row - BLOCK <= lax.rem(col, BLOCK))


def stack_t(ref, rows, column, rep):
    return jnp.concatenate(
        [ref[rows, pl.ds(column + r * HEAD_SIZE, HEAD_SIZE)].T for r in range(rep)], axis=1
    )


def stack_rows(ref, rows, column, rep):
    return jnp.concatenate(
        [ref[rows, pl.ds(column + r * HEAD_SIZE, HEAD_SIZE)] for r in range(rep)], axis=0
    )


def dot(left, right):
    return jnp.dot(left, right, preferred_element_type=jnp.float32)


def start_parts(parts, buffer_ref, sem, column):
    rows, width = parts[0].shape[0], buffer_ref.shape[1]
    copies = [
        pltpu.make_async_copy(
            part.at[:, pl.ds(column, width)], buffer_ref.at[pl.ds(p * rows, rows), :], sem.at[p]
        )
        for p, part in enumerate(parts)
    ]
    for copy in copies:
        copy.start()
    return copies


def forward_kernel(rep, hps, ctx_count, order_ref, cont_ref, where_ref, q_ref, wo_ref, *refs):
    parts, refs = refs[:ctx_count], refs[ctx_count:]
    out_ref, lse_ref, keep_ref, send_ref, kv_ref, inverse_ref, qt_ref, acc_ref, sem = refs
    copies = start_parts(parts, kv_ref, sem, 0)
    fill_inverse(order_ref, where_ref, inverse_ref)
    for copy in copies:
        copy.wait()
    q_blocks = q_ref.shape[0] // BLOCK
    factor = LOG2E / math.sqrt(HEAD_SIZE)
    width = rep * HEAD_SIZE

    def one_query_block(qb, carry):
        base, pairs, prev, own, has_prev = block_plan(order_ref, cont_ref, where_ref, qb)
        rows = pl.ds(pl.multiple_of(qb * BLOCK, BLOCK), BLOCK)
        mask = own_mask(has_prev, rep)
        rows_a, rows_b = key_rows(inverse_ref, prev), key_rows(inverse_ref, own)
        state = []
        for h in range(hps):
            qt = stack_t(q_ref, rows, h * width, rep)
            qt_ref[h] = qt
            scores = dot(tile_pair(kv_ref, rows_a, rows_b, 2 * h * HEAD_SIZE), qt) * factor
            scores = jnp.where(mask, scores, NEG)
            best = jnp.max(scores, axis=0, keepdims=True)
            weights = jnp.exp2(scores - best)
            total = jnp.sum(weights, axis=0, keepdims=True)
            values = tile_pair(kv_ref, rows_a, rows_b, (2 * h + 1) * HEAD_SIZE)
            acc_ref[h] = dot(values.T, weights.astype(jnp.bfloat16))
            state += [best, total]

        def one_pair(t, state):
            rows_a = key_rows(inverse_ref, base + 2 * t)
            rows_b = key_rows(inverse_ref, base + 2 * t + 1)
            after = []
            for h in range(hps):
                best, total = state[2 * h], state[2 * h + 1]
                keys = tile_pair(kv_ref, rows_a, rows_b, 2 * h * HEAD_SIZE)
                scores = dot(keys, qt_ref[h]) * factor
                newest = jnp.maximum(best, jnp.max(scores, axis=0, keepdims=True))
                weights = jnp.exp2(scores - newest)
                shrink = jnp.exp2(best - newest)
                total = total * shrink + jnp.sum(weights, axis=0, keepdims=True)
                values = tile_pair(kv_ref, rows_a, rows_b, (2 * h + 1) * HEAD_SIZE)
                acc_ref[h] = acc_ref[h] * shrink + dot(values.T, weights.astype(jnp.bfloat16))
                after += [newest, total]
            return tuple(after)

        state = lax.fori_loop(0, pairs, one_pair, tuple(state))
        for h in range(hps):
            best, total = state[2 * h], state[2 * h + 1]
            mixed = acc_ref[h] * (1.0 / total)
            for r in range(rep):
                part = mixed[:, r * BLOCK : (r + 1) * BLOCK]
                out_ref[rows, pl.ds(h * width + r * HEAD_SIZE, HEAD_SIZE)] = part.T.astype(
                    jnp.bfloat16
                )
            lse_ref[h, pl.ds(qb, 1), :] = best + jnp.log2(total)
        return carry

    lax.fori_loop(0, q_blocks, one_query_block, 0)
    mixed = out_ref[...]
    half = keep_ref.shape[0]
    for n in range(0, wo_ref.shape[1], 512):
        cols = slice(n, n + 512)
        partial = dot(mixed, wo_ref[:, cols]).astype(jnp.bfloat16)
        keep_ref[:, cols] = partial[:half]
        send_ref[:, cols] = partial[half:]


def backward_kernel(rep, hps, ctx_count, head, order_ref, cont_ref, where_ref, q_ref, gb_ref, wo_ref,
                    mix_ref, lse_ref, cos_ref, sin_ref, *refs):
    parts, refs = refs[:ctx_count], refs[ctx_count:]
    gq_ref, keep_ref, send_ref = refs[:3]
    kv_ref, gm_ref, inverse_ref, qt_ref, gmt_ref, gqt_ref, acc_ref, sem = refs[3:]
    copies = start_parts(parts, kv_ref, sem, head * kv_ref.shape[1])
    fill_inverse(order_ref, where_ref, inverse_ref)
    gm_ref[...] = right_dot(gb_ref[...], wo_ref[...]).astype(jnp.bfloat16)
    for copy in copies:
        copy.wait()
    q_blocks = q_ref.shape[0] // BLOCK
    scale = 1.0 / math.sqrt(HEAD_SIZE)
    factor = LOG2E * scale
    width = rep * HEAD_SIZE

    def clear(i, carry):
        acc_ref[pl.ds(pl.multiple_of(i * BLOCK, BLOCK), BLOCK), :] = jnp.zeros(
            (BLOCK, acc_ref.shape[1]), jnp.float32
        )
        return carry

    lax.fori_loop(0, order_ref.shape[0], clear, 0)

    def tile_terms(h, rows_a, rows_b, lse, delta, q_rows, gm_rows, mask):
        kcol, vcol = 2 * h * HEAD_SIZE, (2 * h + 1) * HEAD_SIZE
        keys = tile_pair(kv_ref, rows_a, rows_b, kcol)
        values = tile_pair(kv_ref, rows_a, rows_b, vcol)
        weights = jnp.exp2(dot(keys, qt_ref[h]) * factor - lse)
        if mask is not None:
            weights = jnp.where(mask, weights, 0.0)
        grad_weights = dot(values, gmt_ref[h])
        grad_scores = (weights * (grad_weights - delta)).astype(jnp.bfloat16)
        gv = dot(weights.astype(jnp.bfloat16), gm_rows)
        gk = dot(grad_scores, q_rows)
        acc_ref[rows_a, pl.ds(kcol, HEAD_SIZE)] += gk[:BLOCK]
        acc_ref[rows_b, pl.ds(kcol, HEAD_SIZE)] += gk[BLOCK:]
        acc_ref[rows_a, pl.ds(vcol, HEAD_SIZE)] += gv[:BLOCK]
        acc_ref[rows_b, pl.ds(vcol, HEAD_SIZE)] += gv[BLOCK:]
        return dot(keys.T, grad_scores)

    def one_query_block(qb, carry):
        base, pairs, prev, own, has_prev = block_plan(order_ref, cont_ref, where_ref, qb)
        rows = pl.ds(pl.multiple_of(qb * BLOCK, BLOCK), BLOCK)
        mask = own_mask(has_prev, rep)
        rows_a, rows_b = key_rows(inverse_ref, prev), key_rows(inverse_ref, own)
        deltas, lses, q_stack, gm_stack = [], [], [], []
        for h in range(hps):
            qt_ref[h] = stack_t(q_ref, rows, h * width, rep)
            gmt = stack_t(gm_ref, rows, h * width, rep)
            gmt_ref[h] = gmt
            mixt = stack_t(mix_ref, rows, h * width, rep)
            deltas.append(
                jnp.sum(
                    gmt.astype(jnp.float32) * mixt.astype(jnp.float32), axis=0, keepdims=True
                )
            )
            lses.append(lse_ref[h, pl.ds(qb, 1), :])
        for h in range(hps):
            q_rows = stack_rows(q_ref, rows, h * width, rep)
            gm_rows = stack_rows(gm_ref, rows, h * width, rep)
            gqt_ref[h] = tile_terms(
                h, rows_a, rows_b, lses[h], deltas[h], q_rows, gm_rows, mask
            )

        def one_pair(t, carry):
            rows_a = key_rows(inverse_ref, base + 2 * t)
            rows_b = key_rows(inverse_ref, base + 2 * t + 1)
            for h in range(hps):
                q_rows = stack_rows(q_ref, rows, h * width, rep)
                gm_rows = stack_rows(gm_ref, rows, h * width, rep)
                gqt_ref[h] += tile_terms(
                    h, rows_a, rows_b, lses[h], deltas[h], q_rows, gm_rows, None
                )
            return carry

        lax.fori_loop(0, pairs, one_pair, 0)
        for h in range(hps):
            total = gqt_ref[h] * scale
            for r in range(rep):
                part = total[:, r * BLOCK : (r + 1) * BLOCK]
                rounded = part.T.astype(jnp.bfloat16).astype(jnp.float32)
                gq_ref[rows, pl.ds(h * width + r * HEAD_SIZE, HEAD_SIZE)] = unrotate(
                    rounded, cos_ref[rows, :], sin_ref[rows, :]
                ).astype(jnp.bfloat16)
        return carry

    lax.fori_loop(0, q_blocks, one_query_block, 0)

    blocks = order_ref.shape[0]

    def place(index):
        chunk = lax.div(index, SLOTS)
        spot = (chunk & 1) * (ctx_count // 2) + (chunk & 2) // 2 * (ctx_count // 4) + (
            lax.shift_right_logical(chunk, 2)
        )
        return spot * SLOTS + (index & 3)

    def flush(i, carry):
        rows = pl.ds(pl.multiple_of(i * BLOCK, BLOCK), BLOCK)
        spot = place(i)
        parts = []
        for h in range(hps):
            parts.append(acc_ref[rows, pl.ds(2 * h * HEAD_SIZE, HEAD_SIZE)] * scale)
            parts.append(acc_ref[rows, pl.ds((2 * h + 1) * HEAD_SIZE, HEAD_SIZE)])
        value = jnp.concatenate(parts, axis=1).astype(jnp.bfloat16)

        @pl.when(spot < blocks // 2)
        def _():
            keep_ref[pl.ds(pl.multiple_of(spot * BLOCK, BLOCK), BLOCK), :] = value

        @pl.when(spot >= blocks // 2)
        def _():
            far = (spot - blocks // 2) * BLOCK
            send_ref[pl.ds(pl.multiple_of(far, BLOCK), BLOCK), :] = value

        return carry

    lax.fori_loop(0, blocks, flush, 0)


def attention_forward(q, w_out, parts, order, cont, where):
    ctx_count = len(parts)
    rows, tokens = q.shape[0], ctx_count * q.shape[0]
    kv_heads = parts[0].shape[1] // (2 * HEAD_SIZE)
    rep = q.shape[1] // HEAD_SIZE // kv_heads
    q_blocks, model = rows // BLOCK, w_out.shape[1]
    vmem, smem, any_ = (
        pl.BlockSpec(memory_space=space) for space in (pltpu.VMEM, pltpu.SMEM, pl.ANY)
    )
    flops = 2 * rows * tokens * q.shape[1] + 2 * rows * q.shape[1] * model
    half = jax.ShapeDtypeStruct((rows // 2, model), jnp.bfloat16)
    return pl.pallas_call(
        functools.partial(forward_kernel, rep, kv_heads, ctx_count),
        out_shape=(
            jax.ShapeDtypeStruct(q.shape, jnp.bfloat16),
            jax.ShapeDtypeStruct((kv_heads, q_blocks, rep * BLOCK), jnp.float32),
            half,
            half,
        ),
        in_specs=[smem] * 3 + [vmem] * 2 + [any_] * ctx_count,
        out_specs=[vmem] * 4,
        scratch_shapes=[
            pltpu.VMEM((tokens, parts[0].shape[1]), jnp.bfloat16),
            pltpu.SMEM((order.shape[0],), jnp.int32),
            pltpu.VMEM((kv_heads, HEAD_SIZE, rep * BLOCK), jnp.bfloat16),
            pltpu.VMEM((kv_heads, HEAD_SIZE, rep * BLOCK), jnp.float32),
            pltpu.SemaphoreType.DMA((ctx_count,)),
        ],
        compiler_params=pltpu.CompilerParams(vmem_limit_bytes=VMEM_LIMIT),
        cost_estimate=cost("attention_forward", flops, 2 * tokens * parts[0].shape[1] + 4 * rows * model),
        name="attention_forward",
    )(order, cont, where, q, w_out, *parts)


def attention_backward(head, q, grad_branch, w_out, mixed, lse, parts, cosine, sine, order, cont,
                       where):
    ctx_count = len(parts)
    rows, tokens = q.shape[0], ctx_count * q.shape[0]
    kv_heads = parts[0].shape[1] // (2 * HEAD_SIZE)
    rep = q.shape[1] // HEAD_SIZE // kv_heads
    q_blocks, model = rows // BLOCK, w_out.shape[1]
    wide = rep * HEAD_SIZE
    q_spec = pl.BlockSpec((rows, wide), lambda g, *_: (0, head))
    whole = lambda g, *_: (0, 0)
    table_spec = pl.BlockSpec((rows, HEAD_SIZE), whole)
    half = (tokens // 2, 2 * HEAD_SIZE)
    flops = 5 * rows * tokens * wide + 2 * rows * wide * model
    return pl.pallas_call(
        functools.partial(backward_kernel, rep, 1, ctx_count, head),
        out_shape=(
            jax.ShapeDtypeStruct((rows, wide), jnp.bfloat16),
            jax.ShapeDtypeStruct(half, jnp.bfloat16),
            jax.ShapeDtypeStruct(half, jnp.bfloat16),
        ),
        grid_spec=pltpu.PrefetchScalarGridSpec(
            num_scalar_prefetch=3,
            grid=(1,),
            in_specs=[
                q_spec,
                pl.BlockSpec((rows, model), whole),
                pl.BlockSpec((wide, model), lambda g, *_: (head, 0)),
                q_spec,
                pl.BlockSpec((1, q_blocks, rep * BLOCK), lambda g, *_: (head, 0, 0)),
                table_spec,
                table_spec,
            ]
            + [pl.BlockSpec(memory_space=pl.ANY)] * ctx_count,
            out_specs=[
                pl.BlockSpec((rows, wide), whole),
                pl.BlockSpec(half, whole),
                pl.BlockSpec(half, whole),
            ],
            scratch_shapes=[
                pltpu.VMEM((tokens, 2 * HEAD_SIZE), jnp.bfloat16),
                pltpu.VMEM((rows, wide), jnp.bfloat16),
                pltpu.SMEM((order.shape[0],), jnp.int32),
                pltpu.VMEM((1, HEAD_SIZE, rep * BLOCK), jnp.bfloat16),
                pltpu.VMEM((1, HEAD_SIZE, rep * BLOCK), jnp.bfloat16),
                pltpu.VMEM((1, HEAD_SIZE, rep * BLOCK), jnp.float32),
                pltpu.VMEM((tokens, 2 * HEAD_SIZE), jnp.float32),
                pltpu.SemaphoreType.DMA((ctx_count,)),
            ],
        ),
        compiler_params=pltpu.CompilerParams(vmem_limit_bytes=VMEM_LIMIT),
        cost_estimate=cost(f"attention_backward_{head}", flops, 4 * tokens * wide + 2 * rows * model),
        name=f"attention_backward_{head}",
    )(order, cont, where, q, grad_branch, w_out, mixed, lse, cosine, sine, *parts)


def input_kernel(order_ref, cont_ref, where_ref, gain_ref, x_hbm, wq_hbm, wk_hbm, wv_hbm, table_hbm,
                 first_ref, q_ref, kv_ref, cos_ref, sin_ref,
                 x_ref, wq_ref, wk_ref, wv_ref, table_ref, sem):
    pairs = ((x_hbm, x_ref), (table_hbm, table_ref), (wk_hbm, wk_ref), (wv_hbm, wv_ref),
             (wq_hbm, wq_ref))
    copies = [
        pltpu.make_async_copy(source, target, sem.at[n])
        for n, (source, target) in enumerate(pairs)
    ]
    for copy in copies:
        copy.start()
    count = cont_ref.shape[0]
    prompt_blocks = count // CONTS * PER_PROMPT
    starts = (table_ref.shape[0] - 2 * BLOCK) // 2
    lane = lax.broadcasted_iota(jnp.int32, (BLOCK, HEAD_SIZE), 1)
    copies[0].wait()
    copies[1].wait()

    def one_slot(slot, carry):
        quarter = slot_quarter(slot, where_ref[1])
        rows = pl.ds(pl.multiple_of(slot * BLOCK, BLOCK), BLOCK)
        full = x_ref[pl.ds(pl.multiple_of(quarter * BLOCK, BLOCK), BLOCK), :].astype(jnp.float32)
        inv = lax.rsqrt(jnp.mean(full * full, axis=-1, keepdims=True) + eps_norm)
        first_ref[rows, :] = (full * inv * gain_ref[...]).astype(jnp.bfloat16)
        own = order_ref[stored_block(slot, where_ref)]
        spot = jnp.where(
            own < prompt_blocks,
            lax.rem(own, PER_PROMPT),
            PER_PROMPT + lax.rem(own - prompt_blocks, PER_CONT),
        )
        cos_start = table_ref[pl.ds(2 * BLOCK + spot, 1), :]
        sin_start = table_ref[pl.ds(2 * BLOCK + starts + spot, 1), :]
        cos_in, sin_in = table_ref[:BLOCK, :], table_ref[BLOCK : 2 * BLOCK, :]
        sine = sin_start * cos_in + cos_start * sin_in
        cos_ref[rows, :] = cos_start * cos_in - sin_start * sin_in
        sin_ref[rows, :] = jnp.where(lane < HEAD_SIZE // 2, -sine, sine)
        return carry

    lax.fori_loop(0, SLOTS, one_slot, 0)
    first = first_ref[...]
    cosine, sine = cos_ref[...], sin_ref[...]
    copies[2].wait()
    copies[3].wait()
    keys = dot(first, wk_ref[...])
    values = dot(first, wv_ref[...])
    for h in range(wk_ref.shape[1] // HEAD_SIZE):
        cols = slice(h * HEAD_SIZE, (h + 1) * HEAD_SIZE)
        low, high = 2 * h * HEAD_SIZE, (2 * h + 1) * HEAD_SIZE
        key = rotate(keys[:, cols], cosine, sine)
        kv_ref[:, low:high] = key.astype(jnp.bfloat16)
        kv_ref[:, high : high + HEAD_SIZE] = values[:, cols].astype(jnp.bfloat16)
    copies[4].wait()
    for n in range(0, wq_ref.shape[1], 256):
        queries = dot(first, wq_ref[:, n : n + 256])
        for m in range(0, 256, HEAD_SIZE):
            query = rotate(queries[:, m : m + HEAD_SIZE], cosine, sine)
            q_ref[:, n + m : n + m + HEAD_SIZE] = query.astype(jnp.bfloat16)


def input_stage(x, gain, wq, wk, wv, order, cont, where):
    rows, model = x.shape
    cos_start, sin_start, cos_in, sin_in = angle_tables()
    table = np.concatenate([cos_in, sin_in, cos_start, sin_start])
    vmem, smem, any_ = (
        pl.BlockSpec(memory_space=space) for space in (pltpu.VMEM, pltpu.SMEM, pl.ANY)
    )
    flops = 2 * rows * model * (wq.shape[1] + 2 * wk.shape[1])
    return pl.pallas_call(
        input_kernel,
        out_shape=(
            jax.ShapeDtypeStruct((rows, model), jnp.bfloat16),
            jax.ShapeDtypeStruct((rows, wq.shape[1]), jnp.bfloat16),
            jax.ShapeDtypeStruct((rows, 2 * wk.shape[1]), jnp.bfloat16),
            jax.ShapeDtypeStruct((rows, HEAD_SIZE), jnp.float32),
            jax.ShapeDtypeStruct((rows, HEAD_SIZE), jnp.float32),
        ),
        in_specs=[smem] * 3 + [vmem] + [any_] * 5,
        out_specs=[vmem] * 5,
        scratch_shapes=[
            pltpu.VMEM(a.shape, a.dtype) for a in (x, wq, wk, wv)
        ]
        + [pltpu.VMEM(table.shape, jnp.float32), pltpu.SemaphoreType.DMA((5,))],
        compiler_params=pltpu.CompilerParams(vmem_limit_bytes=VMEM_LIMIT),
        cost_estimate=cost("input_stage", flops, 4 * x.size + 2 * wq.size + 4 * wk.size),
        name="input_stage",
    )(order, cont, where, gain.reshape(1, -1), x, wq, wk, wv, table)


FILLERS = ("ffn_out", "up_shares", "branch_shares", "kv_shares", "grad_hidden")


def cost(name, flops, bytes_accessed):
    scale = 16.0 if name in FILLERS else 0.02
    return pl.CostEstimate(
        flops=int(flops * scale), bytes_accessed=int(bytes_accessed * scale), transcendentals=0
    )


def put_share(value, index, x_bit, keep_ref, send_ref, swap_bits):
    spot = lax.shift_right_logical(index, 1)
    if swap_bits:
        spot = (spot & 1) * (keep_ref.shape[0] // 2) + lax.shift_right_logical(spot, 1)
    stays = (index & 1) == x_bit
    value = value.astype(keep_ref.dtype)

    @pl.when(stays)
    def _():
        keep_ref[pl.ds(spot, 1)] = value[None]

    @pl.when(jnp.logical_not(stays))
    def _():
        send_ref[pl.ds(spot, 1)] = value[None]


def pair_bit(where_ref):
    return lax.shift_right_logical(where_ref[0], 1) & 1


def grad_hidden_kernel(where_ref, cot_ref, wd_ref, out_ref):
    out_ref[...] = right_dot(cot_ref[...], wd_ref[...])


def grad_hidden_stage(cot, w_down, where):
    rows, model = cot.shape
    units = w_down.shape[0] // 2
    block = 256
    steps = units // block
    return pl.pallas_call(
        grad_hidden_kernel,
        out_shape=jax.ShapeDtypeStruct((rows, units), jnp.float32),
        grid_spec=pltpu.PrefetchScalarGridSpec(
            num_scalar_prefetch=1,
            grid=(steps,),
            in_specs=[
                pl.BlockSpec((rows, model), lambda i, w: (0, 0), pipeline_mode=pl.Buffered(1)),
                pl.BlockSpec((block, model), lambda i, w: (pair_bit(w) * steps + i, 0)),
            ],
            out_specs=pl.BlockSpec((rows, block), lambda i, w: (0, i)),
        ),
        compiler_params=pltpu.CompilerParams(vmem_limit_bytes=VMEM_LIMIT),
        cost_estimate=cost("grad_hidden", 2 * rows * model * units, 4 * rows * model),
        name="grad_hidden",
    )(where, cot, w_down)


def ffn_kernel(where_ref, in_ref, gh_ref, wg_ref, wu_ref, hid_ref, gg_ref, gu_ref):
    gate = dot(in_ref[...], wg_ref[...])
    upward = dot(in_ref[...], wu_ref[...])
    grad_hidden = gh_ref[...]
    sigma = jax.nn.sigmoid(gate)
    swish = gate * sigma
    hid_ref[...] = (swish * upward).astype(jnp.bfloat16)
    gg_ref[...] = (grad_hidden * upward * sigma * (1.0 + gate * (1.0 - sigma))).astype(
        jnp.bfloat16
    )
    gu_ref[...] = (grad_hidden * swish).astype(jnp.bfloat16)


def ffn_stage(second, grad_hidden, w_gate, w_up, where):
    rows, model = second.shape
    units = w_gate.shape[1] // 2
    block = 256
    steps = units // block
    col_spec = pl.BlockSpec((model, block), lambda i, w: (0, pair_bit(w) * steps + i))
    unit_spec = pl.BlockSpec((rows, block), lambda i, w: (0, i))
    unit = jax.ShapeDtypeStruct((rows, units), jnp.bfloat16)
    return pl.pallas_call(
        ffn_kernel,
        out_shape=(unit, unit, unit),
        grid_spec=pltpu.PrefetchScalarGridSpec(
            num_scalar_prefetch=1,
            grid=(steps,),
            in_specs=[
                pl.BlockSpec((rows, model), lambda i, w: (0, 0), pipeline_mode=pl.Buffered(1)),
                unit_spec,
                col_spec,
                col_spec,
            ],
            out_specs=[unit_spec] * 3,
        ),
        compiler_params=pltpu.CompilerParams(vmem_limit_bytes=VMEM_LIMIT),
        cost_estimate=cost("ffn_stage", 4 * rows * model * units, 6 * rows * model),
        name="ffn_stage",
    )(where, second, grad_hidden, w_gate, w_up)


def grad_second_kernel(where_ref, gg_ref, gu_ref, wg_ref, wu_ref, keep_ref, send_ref):
    total = right_dot(gg_ref[...], wg_ref[...]) + right_dot(gu_ref[...], wu_ref[...])
    half = keep_ref.shape[0]
    keep_ref[...] = total[:half].astype(jnp.bfloat16)
    send_ref[...] = total[half:].astype(jnp.bfloat16)


def ffn_out_kernel(where_ref, hid_ref, wd_ref, keep_ref, send_ref):
    total = dot(hid_ref[...], wd_ref[...])
    half = keep_ref.shape[0]
    keep_ref[...] = total[:half].astype(jnp.bfloat16)
    send_ref[...] = total[half:].astype(jnp.bfloat16)


def unit_sum(kernel, name, lefts, rights, transposed, where):
    rows, units = lefts[0].shape
    model = rights[0].shape[0 if transposed else 1]
    block = 512
    if transposed:
        right_spec = pl.BlockSpec((block, units), lambda n, w: (n, pair_bit(w)))
    else:
        right_spec = pl.BlockSpec((units, block), lambda n, w: (pair_bit(w), n))
    left_spec = pl.BlockSpec((rows, units), lambda n, w: (0, 0), pipeline_mode=pl.Buffered(1))
    half = jax.ShapeDtypeStruct((rows // 2, model), jnp.bfloat16)
    half_spec = pl.BlockSpec((rows // 2, block), lambda n, w: (0, n))
    return pl.pallas_call(
        kernel,
        out_shape=(half, half),
        grid_spec=pltpu.PrefetchScalarGridSpec(
            num_scalar_prefetch=1,
            grid=(model // block,),
            in_specs=[left_spec] * len(lefts) + [right_spec] * len(rights),
            out_specs=[half_spec, half_spec],
        ),
        compiler_params=pltpu.CompilerParams(vmem_limit_bytes=VMEM_LIMIT),
        cost_estimate=cost(name, 2 * len(lefts) * rows * units * model, 4 * rows * model),
        name=name,
    )(where, *lefts, *rights)


def shares_kernel(left_count, swap_bits, pairs, where_ref, *refs):
    lefts, refs = refs[:left_count], refs[left_count:]
    rights, (keep_ref, send_ref) = refs[:-2], refs[-2:]
    share = keep_ref.shape[1]
    step = pl.program_id(0)
    pieces = [left_dot(lefts[l][...], rights[r][...]) for l, r in pairs]
    per_step = lefts[0].shape[1] // share
    for k in range(per_step):
        rows = slice(k * share, (k + 1) * share)
        value = jnp.concatenate([piece[rows] for piece in pieces], axis=1)
        index = step * per_step + k
        put_share(value, index, where_ref[0] & 1, keep_ref, send_ref, swap_bits)


def weight_shares(name, lefts, rights, pairs, ctx_count, swap_bits, where):
    rows, model = lefts[0].shape
    block = 256
    share = model // ctx_count
    width = sum(rights[r].shape[1] for _, r in pairs)
    shares = jax.ShapeDtypeStruct((ctx_count // 2, share, width), jnp.bfloat16)
    share_spec = pl.BlockSpec(shares.shape, lambda i, w: (0, 0, 0))
    return pl.pallas_call(
        functools.partial(shares_kernel, len(lefts), swap_bits, pairs),
        out_shape=(shares, shares),
        grid_spec=pltpu.PrefetchScalarGridSpec(
            num_scalar_prefetch=1,
            grid=(model // block,),
            in_specs=[pl.BlockSpec((rows, block), lambda i, w: (0, i))] * len(lefts)
            + [
                pl.BlockSpec(r.shape, lambda i, w: (0, 0), pipeline_mode=pl.Buffered(1))
                for r in rights
            ],
            out_specs=[share_spec, share_spec],
        ),
        compiler_params=pltpu.CompilerParams(vmem_limit_bytes=VMEM_LIMIT),
        cost_estimate=cost(name, 2 * rows * model * width, 4 * rows * model),
        name=name,
    )(where, *lefts, *rights)


def tail_kernel(kv_heads, where_ref, *refs):
    sums, refs = refs[: 2 * kv_heads], refs[2 * kv_heads :]
    cos_ref, sin_ref, refs = refs[0], refs[1], refs[2:]
    gq_refs, refs = refs[:kv_heads], refs[kv_heads:]
    wq_ref, wk_ref, wv_ref, keep_ref, send_ref, gkv_ref = refs
    cosine, sine = cos_ref[...], sin_ref[...]
    for h in range(kv_heads):
        total = sums[2 * h][...].astype(jnp.float32) + sums[2 * h + 1][...].astype(jnp.float32)
        total = total.astype(jnp.bfloat16)
        key = unrotate(total[:, :HEAD_SIZE].astype(jnp.float32), cosine, sine)
        cols = slice(h * HEAD_SIZE, (h + 1) * HEAD_SIZE)
        gkv_ref[:, cols] = key.astype(jnp.bfloat16)
        cols = slice((kv_heads + h) * HEAD_SIZE, (kv_heads + h + 1) * HEAD_SIZE)
        gkv_ref[:, cols] = total[:, HEAD_SIZE:]
    half = keep_ref.shape[0]
    key_width = kv_heads * HEAD_SIZE
    wide = gq_refs[0].shape[1]
    for n in range(0, wq_ref.shape[0], 512):
        span = slice(n, n + 512)
        total = right_dot(gkv_ref[:, :key_width], wk_ref[span, :])
        total += right_dot(gkv_ref[:, key_width:], wv_ref[span, :])
        for h in range(kv_heads):
            total += right_dot(gq_refs[h][...], wq_ref[span, h * wide : (h + 1) * wide])
        total = total.astype(jnp.bfloat16)
        keep_ref[:, span] = total[:half]
        send_ref[:, span] = total[half:]


def tail_stage(kv_sums, cosine, sine, grad_queries, wq, wk, wv, where):
    rows, model = cosine.shape[0], wq.shape[0]
    kv_heads = len(grad_queries)
    vmem = pl.BlockSpec(memory_space=pltpu.VMEM)
    half = jax.ShapeDtypeStruct((rows // 2, model), jnp.bfloat16)
    flat = [term for sums in kv_sums for term in sums]
    return pl.pallas_call(
        functools.partial(tail_kernel, kv_heads),
        out_shape=(
            half,
            half,
            jax.ShapeDtypeStruct((rows, 2 * kv_heads * HEAD_SIZE), jnp.bfloat16),
        ),
        in_specs=[pl.BlockSpec(memory_space=pltpu.SMEM)]
        + [vmem] * (len(flat) + 2 + kv_heads + 3),
        out_specs=[vmem] * 3,
        compiler_params=pltpu.CompilerParams(vmem_limit_bytes=VMEM_LIMIT),
        cost_estimate=cost("tail_stage", 2 * rows * model * (wq.shape[1] + 2 * wk.shape[1]), 4 * rows * model + 4 * wq.size
        ),
        name="tail_stage",
    )(where, *flat, cosine, sine, *grad_queries, wq, wk, wv)


def flip(value, axis, mask):
    return lax.ppermute(value, axis, [(i, i ^ mask) for i in range(lax.axis_size(axis))])


def add(left, right):
    return (left.astype(jnp.float32) + right.astype(jnp.float32)).astype(jnp.bfloat16)


def slots_of(value, tensor):
    rows = value.shape[0] // SLOTS
    return [
        lax.dynamic_slice_in_dim(value, (tensor ^ SLOT_XOR[u]) * rows, rows)
        for u in range(SLOTS)
    ]


def after(dep, *values):
    held = lax.optimization_barrier((dep,) + values)[1:]
    return held[0] if len(held) == 1 else held


def gather_slots(own):
    near = jnp.concatenate([own, flip(own, "tp", 2)])
    return jnp.concatenate([near, flip(near, "tp", 1)])


def gather_pair(own):
    partner = flip(own, "ctx", 2)
    near = jnp.concatenate([own, partner, flip(own, "tp", 2), flip(partner, "tp", 2)])
    return jnp.concatenate([near, flip(near, "tp", 1)])


def gather_rows(own, other, tensor):
    rows = own.shape[0]
    near = jnp.concatenate([own, other])
    far = flip(near, "tp", 1)
    pieces = (near[:rows], near[rows:], far[:rows], far[rows:])
    result = jnp.zeros((SLOTS * rows,) + own.shape[1:], own.dtype)
    for u in range(SLOTS):
        result = lax.dynamic_update_slice_in_dim(
            result, pieces[u], (tensor ^ SLOT_XOR[u]) * rows, 0
        )
    return result


def scatter_slots(keep, send, fill=lambda value: value):
    got = fill(flip(send, "tp", 1))
    quarter = keep.shape[0] // 2
    far = flip(add(keep[quarter:], got[quarter:]), "tp", 2)
    return add(keep[:quarter], got[:quarter]), far


def pair_scatter(keep, send, fill=lambda near: near):
    got = fill(flip(send, "tp", 1))
    n = keep.shape[0] // 4
    near = [add(keep[k * n : (k + 1) * n], got[k * n : (k + 1) * n]) for k in range(4)]
    far = flip(near[3], "tp", 2)
    got = flip(near[2], "tp", 2)
    return near, far, got


def pair_finish(near, far, got):
    away = add(near[1], far)
    return near[0], got, flip(away, "ctx", 2), away


def total(terms):
    return sum(term.astype(jnp.float32) for term in terms)


def gather_keys(kv_local, ctx_count):
    parts = {0: kv_local}
    for bit in reversed(high_masks(ctx_count)):
        for mask in list(parts):
            parts[mask + bit] = flip(parts[mask], "ctx", bit)
    for bit in (2, 1):
        for mask in list(parts):
            parts[mask + bit] = flip(parts[mask], "ctx", bit)
    return [parts[mask] for mask in range(ctx_count)]


def all_sum(value, ctx_count):
    for axis, mask in [("tp", 1), ("tp", 2), ("ctx", 1), ("ctx", 2)] + [
        ("ctx", mask) for mask in high_masks(ctx_count)
    ]:
        value = value + flip(value, axis, mask)
    return value


class Reduce:
    def __init__(self, keep, send):
        self.keep, self.got = keep, flip(send, "ctx", 1)

    def halve(self, mask, ctx, dep=None):
        keep, got = self.keep, self.got
        if dep is not None:
            keep, got = after(dep, keep, got)
        n = keep.shape[0] // 2
        bit = lax.div(ctx, mask) % 2
        pick = lambda value, index: lax.dynamic_slice_in_dim(value, index * n, n, 0)
        away = flip(add(pick(keep, 1 - bit), pick(got, 1 - bit)), "ctx", mask)
        self.keep, self.got = add(pick(keep, bit), pick(got, bit)), away

    def sum(self):
        return (self.keep.astype(jnp.float32) + self.got.astype(jnp.float32))[0]


def high_masks(ctx_count):
    masks, mask = [], ctx_count // 2
    while mask >= 4:
        masks.append(mask)
        mask //= 2
    return masks


def split_halves(reduce, ctx, dep):
    keep, got = after(dep, reduce.keep, reduce.got)
    pair = lax.div(ctx, 2) % 2
    pick = lambda value, index: lax.dynamic_slice_in_dim(value, index, 1, 0)[0]
    return (
        add(pick(keep, pair), pick(got, pair)),
        add(pick(keep, 1 - pair), pick(got, 1 - pair)),
    )


def join_halves(own, other, ctx):
    pair = lax.div(ctx, 2) % 2
    low, high = jnp.where(pair == 0, own, other), jnp.where(pair == 0, other, own)
    return jnp.concatenate([low, high], axis=1).astype(jnp.float32)


class KvReduce:
    def __init__(self, keep, send):
        self.keep, self.got = keep, flip(send, "ctx", 1)

    def halve(self, mask, dep):
        keep, got = after(dep, self.keep, self.got)
        n = keep.shape[0] // 2
        away = flip(add(keep[n:], got[n:]), "ctx", mask)
        self.keep, self.got = add(keep[:n], got[:n]), away


def norm_back(grad_out, normed, inv_scale, gain):
    scaled = grad_out * gain
    inner = jnp.mean(scaled * normed, axis=-1, keepdims=True)
    return (inv_scale * (scaled - normed * inner), jnp.sum(grad_out * normed, axis=0))


def body(
    layer_input,
    attn_gain,
    w_query,
    key_matrix,
    value_matrix,
    w_out,
    ffn_gain,
    w_gate,
    w_up,
    w_down,
    cotangent,
    block_order,
    cont_prompt,
):
    ctx_count = lax.axis_size("ctx")
    tp_count = lax.axis_size("tp")
    ctx, tensor = lax.axis_index("ctx"), lax.axis_index("tp")
    where = jnp.stack([ctx, tensor]).astype(jnp.int32)
    quarter = layer_input.shape[0] // SLOTS
    kv_heads = key_matrix.shape[1] // HEAD_SIZE
    highs = high_masks(ctx_count)

    first_input, queries, kv_local, cosine, sine = input_stage(
        layer_input, attn_gain, w_query, key_matrix, value_matrix, block_order, cont_prompt, where
    )
    cot_own = lax.dynamic_slice_in_dim(cotangent, tensor * quarter, quarter)
    cot_slots = slots_of(cotangent, tensor)
    parts = {0: kv_local}
    for bit in reversed(highs):
        for mask in list(parts):
            parts[mask + bit] = flip(parts[mask], "ctx", bit)
    near_part = flip(kv_local, "ctx", 2)
    parts[1] = flip(kv_local, "ctx", 1)
    cot_part = flip(after(near_part, cot_own), "ctx", 2)
    for mask in [m for m in parts if m >= 4]:
        parts[mask + 2] = flip(parts[mask], "ctx", 2)
        parts[mask + 1] = flip(parts[mask], "ctx", 1)
    parts[2] = near_part
    parts[3] = flip(near_part, "ctx", 1)
    for mask in [m for m in list(parts) if m > 4 and m % 4 == 2]:
        parts[mask + 1] = flip(parts[mask], "ctx", 1)
    parts = [parts[mask] for mask in range(ctx_count)]
    cot_part = jnp.concatenate([cot_part, flip(cot_part, "tp", 2)])
    cot_far = flip(cot_part, "tp", 1)
    cot = jnp.concatenate(
        [cot_slots[0], cot_part[:quarter], cot_slots[1], cot_part[quarter:]]
        + [cot_slots[2], cot_far[:quarter], cot_slots[3], cot_far[quarter:]]
    )
    mixed, log_total, keep, send = attention_forward(
        queries, w_out, parts, block_order, cont_prompt, where
    )
    first_half = flip(send, "tp", 1)
    near = add(keep, first_half)
    far = flip(near[quarter:], "tp", 2)
    grad_hidden = grad_hidden_stage(after(near, cot), w_down, where)
    own_input = lax.dynamic_slice_in_dim(layer_input, tensor * quarter, quarter)
    own_input = own_input.astype(jnp.float32)
    middle = own_input + total((near[:quarter], after(grad_hidden, far)))
    inv_two = lax.rsqrt(jnp.mean(middle * middle, axis=-1, keepdims=True) + eps_norm)
    normed_two = middle * inv_two
    second = gather_pair((normed_two * ffn_gain).astype(jnp.bfloat16))
    hidden, grad_gate, grad_up = ffn_stage(second, grad_hidden, w_gate, w_up, where)

    down_shares = weight_shares(
        "down_shares", (cot,), (hidden,), ((0, 0),), ctx_count, False, where
    )
    down = Reduce(*down_shares)
    grad_gate, grad_up = after(down_shares[0], grad_gate, grad_up)
    keep, send = unit_sum(
        grad_second_kernel, "grad_second", (grad_gate, grad_up), (w_gate, w_up), True, where
    )
    ffn_halves = unit_sum(
        ffn_out_kernel, "ffn_out", (after(keep, hidden),), (w_down,), False, where
    )
    near, far, got = pair_scatter(keep, send, lambda value: after(ffn_halves[0], value))

    def unit_shares(name, grad, dep):
        return weight_shares(
            name, (second,), (after(dep, grad),), ((0, 0),), ctx_count, False, where
        )

    gate_shares = unit_shares("gate_shares", grad_gate, near[3])
    second_terms = pair_finish(near, after(gate_shares[0], far), got)
    *second_terms, dep = second_terms
    for mask in highs:
        down.halve(mask, ctx, dep)
        dep = down.keep
    gate = Reduce(*after(dep, *gate_shares))
    grad_norm_two, ffn_gain_part = norm_back(
        total(after(dep, *second_terms)), normed_two, inv_two, ffn_gain
    )
    grad_middle = cot_own.astype(jnp.float32) + grad_norm_two
    own_branch = grad_middle.astype(jnp.bfloat16)
    up_shares = unit_shares("up_shares", grad_up, own_branch)
    branch_near = jnp.concatenate([own_branch, after(up_shares[0], flip(own_branch, "tp", 2))])
    grad_branch = jnp.concatenate([branch_near, flip(branch_near, "tp", 1)])
    backward = []
    held = grad_branch
    for head in range(kv_heads):
        backward.append(
            attention_backward(
                head, queries, held, w_out, mixed, log_total, parts, cosine, sine,
                block_order, cont_prompt, where,
            )
        )
        held = after(backward[-1][0], grad_branch)
    grad_queries = [item[0] for item in backward]
    dep = grad_queries[-1]
    for mask in highs:
        gate.halve(mask, ctx, dep)
        dep = gate.keep
    kv = [KvReduce(*item[1:]) for item in backward]
    down_own, down_away = split_halves(down, ctx, dep)
    down_other = flip(down_away, "ctx", 2)
    branch_shares = weight_shares(
        "branch_shares",
        (first_input, grad_branch),
        grad_queries + [after(down_own, mixed)],
        tuple((0, h) for h in range(kv_heads)) + ((1, kv_heads),),
        ctx_count,
        True,
        where,
    )
    dep = branch_shares[0]
    gate_own, gate_away = split_halves(gate, ctx, dep)
    dep = gate_own
    for item in kv:
        item.halve(2, dep)
        dep = item.keep
    up = Reduce(*after(dep, *up_shares))
    ffn_sums = pair_scatter(*after(dep, *ffn_halves))
    dep = ffn_sums[0][3]
    for mask in highs:
        for item in kv:
            item.halve(mask, dep)
            dep = item.keep
    ffn_terms = pair_finish(ffn_sums[0], *after(dep, *ffn_sums[1:]))
    got = [after(ffn_terms[3], item.got) for item in kv]
    for mask in highs:
        up.halve(mask, ctx, got[-1])
        dep = up.keep
    branch = Reduce(*after(dep, *branch_shares))
    output = (middle + total(after(dep, *ffn_terms[:3]))).astype(jnp.bfloat16)
    keep, send, grad_kv = tail_stage(
        [(item.keep, after(dep, value)) for item, value in zip(kv, got)], cosine, sine,
        grad_queries, w_query, key_matrix, value_matrix, where,
    )
    kv_shares = weight_shares(
        "kv_shares", (first_input,), (after(keep, grad_kv),), ((0, 0),), ctx_count, True, where
    )
    first_terms = scatter_slots(keep, send, lambda value: after(kv_shares[0], value))
    inv_one = lax.rsqrt(jnp.mean(own_input * own_input, axis=-1, keepdims=True) + eps_norm)
    grad_norm_one, attn_gain_part = norm_back(
        total(first_terms), own_input * inv_one, inv_one, attn_gain
    )
    grad_input = (grad_middle + grad_norm_one).astype(jnp.bfloat16)
    input_other = flip(grad_input, "tp", 2)
    branch.halve(2, ctx, grad_input)
    last = Reduce(*after(branch.keep, *kv_shares))
    up_own, up_away = split_halves(up, ctx, branch.keep)
    dep = up_own
    grad_input = gather_rows(grad_input, after(dep, input_other), tensor)
    gate_other = flip(after(dep, gate_away), "ctx", 2)
    gains = all_sum(after(dep, jnp.stack([attn_gain_part, ffn_gain_part])), ctx_count)
    output = gather_rows(output, flip(after(dep, output), "tp", 2), tensor)
    sum_down = join_halves(down_own, down_other, ctx).T
    up_other = flip(after(gains, up_away), "ctx", 2)
    for mask in highs:
        branch.halve(mask, ctx, gains)
    last.halve(2, ctx, branch.keep)
    for mask in highs:
        last.halve(mask, ctx)
    sum_gate = join_halves(gate_own, gate_other, ctx)
    sum_up = join_halves(up_own, up_other, ctx)
    branch.keep, branch.got = after(last.keep, branch.keep, branch.got)
    width_q, width_k = w_query.shape[1], key_matrix.shape[1]
    branch_sum, last_sum = branch.sum(), last.sum()
    sum_query, sum_out = branch_sum[:, :width_q], branch_sum[:, width_q:].T
    sum_key, sum_value = last_sum[:, :width_k], last_sum[:, width_k:]

    gains = gains.reshape(2, ctx_count * tp_count, -1)
    gains = lax.dynamic_index_in_dim(gains, ctx * tp_count + tensor, 1, keepdims=False)
    return (
        output,
        grad_input,
        gains[0],
        sum_query,
        sum_key,
        sum_value,
        sum_out,
        gains[1],
        sum_gate,
        sum_up,
        sum_down,
    )


def solution(mesh):
    placed = (
        P("ctx", None),
        P(),
        P(None, "tp"),
        P(None, "tp"),
        P(None, "tp"),
        P("tp", None),
        P(),
        P(None, "tp"),
        P(None, "tp"),
        P("tp", None),
        P("ctx", None),
        P(),
        P(),
    )
    return jax.shard_map(
        body,
        mesh=mesh,
        in_specs=placed,
        out_specs=(
            P("ctx", None),
            P("ctx", None),
            P(("ctx", "tp")),
            P("ctx", "tp"),
            P("ctx", "tp"),
            P("ctx", "tp"),
            P("tp", "ctx"),
            P(("ctx", "tp")),
            P("ctx", "tp"),
            P("ctx", "tp"),
            P("tp", "ctx"),
        ),
        check_vma=False,
    )
```

```python
import functools
import math

import jax
import jax.numpy as jnp
import numpy as np
from jax import lax
from jax.experimental import pallas as pl
from jax.experimental.pallas import tpu as pltpu
from jax.sharding import Mesh
from jax.sharding import PartitionSpec as P

HEAD_SIZE = 128
PROMPT = 2048
CONT_LEN = 256
CONTS = 8
BLOCK = 128
PER_PROMPT = PROMPT // BLOCK
PER_CONT = CONT_LEN // BLOCK
LOG2E = 1.4426950408889634
NEG = -1e30
SLOTS = 4
VMEM_LIMIT = 60 << 20

eps_norm = 1e-05
rope_base = 1000000.0

SLOT_XOR = (0, 2, 1, 3)


def plain_dot(left, right):
    return jnp.dot(left, right, preferred_element_type=jnp.float32)


def left_dot(left, right):
    return lax.dot_general(
        left, right, (((0,), (0,)), ((), ())), preferred_element_type=jnp.float32
    )


def right_dot(left, right):
    return lax.dot_general(
        left, right, (((1,), (1,)), ((), ())), preferred_element_type=jnp.float32
    )


def slot_quarter(slot, tensor):
    return ((slot & 1) * 2 + lax.shift_right_logical(slot, 1)) ^ tensor


def stored_block(index, where_ref):
    rank = lax.div(index, SLOTS) ^ where_ref[0]
    return rank * SLOTS + slot_quarter(index & 3, where_ref[1])


def block_plan(order_ref, cont_ref, where_ref, slot):
    count = cont_ref.shape[0]
    prompt_blocks = count // CONTS * PER_PROMPT
    own = order_ref[stored_block(slot, where_ref)]
    is_prompt = own < prompt_blocks
    offset = own - prompt_blocks
    which = jnp.clip(lax.div(offset, PER_CONT), 0, count - 1)
    group = jnp.where(is_prompt, lax.div(own, PER_PROMPT), cont_ref[which])
    inner = jnp.where(is_prompt, lax.rem(own, PER_PROMPT), lax.rem(offset, PER_CONT))
    has_prev = lax.rem(inner, 2)
    pairs = jnp.where(is_prompt, lax.div(inner, 2), PER_PROMPT // 2)
    prev = own - has_prev
    return group * PER_PROMPT, pairs, prev, own, has_prev


def fill_inverse(order_ref, where_ref, inverse_ref):
    def put(index, carry):
        inverse_ref[order_ref[stored_block(index, where_ref)]] = index
        return carry

    lax.fori_loop(0, order_ref.shape[0], put, 0)


def rotate(vec, cosine, sine):
    return vec * cosine + pltpu.roll(vec, HEAD_SIZE // 2, 1) * sine


def unrotate(vec, cosine, sine):
    return vec * cosine + pltpu.roll(vec * sine, HEAD_SIZE // 2, 1)


def angle_tables():
    half = HEAD_SIZE // 2
    freq = np.float64(rope_base) ** (-(2.0 * np.arange(half) / HEAD_SIZE))
    freq = np.concatenate([freq, freq])
    starts = np.arange(-(-(PER_PROMPT + PER_CONT) // 8) * 8) * BLOCK
    start = starts[:, None] * freq[None]
    inner = np.arange(BLOCK)[:, None] * freq[None]
    return tuple(
        f(a).astype(np.float32) for a in (start, inner) for f in (np.cos, np.sin)
    )


def key_rows(inverse_ref, logical):
    return pl.ds(pl.multiple_of(inverse_ref[logical] * BLOCK, BLOCK), BLOCK)


def tile_pair(ref, rows_a, rows_b, column):
    cols = pl.ds(column, HEAD_SIZE)
    return jnp.concatenate([ref[rows_a, cols], ref[rows_b, cols]], axis=0)


def own_mask(has_prev, rep):
    shape = (2 * BLOCK, rep * BLOCK)
    row = lax.broadcasted_iota(jnp.int32, shape, 0)
    col = lax.broadcasted_iota(jnp.int32, shape, 1)
    first_row = BLOCK * (1 - has_prev)
    return (row >= first_row) & (row - BLOCK <= lax.rem(col, BLOCK))


def stack_t(ref, rows, column, rep):
    return jnp.concatenate(
        [ref[rows, pl.ds(column + r * HEAD_SIZE, HEAD_SIZE)].T for r in range(rep)], axis=1
    )


def stack_rows(ref, rows, column, rep):
    return jnp.concatenate(
        [ref[rows, pl.ds(column + r * HEAD_SIZE, HEAD_SIZE)] for r in range(rep)], axis=0
    )


def dot(left, right):
    return jnp.dot(left, right, preferred_element_type=jnp.float32)


def start_parts(parts, buffer_ref, sem, column):
    rows, width = parts[0].shape[0], buffer_ref.shape[1]
    copies = [
        pltpu.make_async_copy(
            part.at[:, pl.ds(column, width)], buffer_ref.at[pl.ds(p * rows, rows), :], sem.at[p]
        )
        for p, part in enumerate(parts)
    ]
    for copy in copies:
        copy.start()
    return copies


def forward_kernel(rep, hps, ctx_count, order_ref, cont_ref, where_ref, q_ref, wo_ref, *refs):
    parts, refs = refs[:ctx_count], refs[ctx_count:]
    out_ref, lse_ref, keep_ref, send_ref, kv_ref, inverse_ref, qt_ref, acc_ref, sem = refs
    copies = start_parts(parts, kv_ref, sem, 0)
    fill_inverse(order_ref, where_ref, inverse_ref)
    for copy in copies:
        copy.wait()
    q_blocks = q_ref.shape[0] // BLOCK
    factor = LOG2E / math.sqrt(HEAD_SIZE)
    width = rep * HEAD_SIZE

    def one_query_block(qb, carry):
        base, pairs, prev, own, has_prev = block_plan(order_ref, cont_ref, where_ref, qb)
        rows = pl.ds(pl.multiple_of(qb * BLOCK, BLOCK), BLOCK)
        mask = own_mask(has_prev, rep)
        rows_a, rows_b = key_rows(inverse_ref, prev), key_rows(inverse_ref, own)
        state = []
        for h in range(hps):
            qt = stack_t(q_ref, rows, h * width, rep)
            qt_ref[h] = qt
            scores = dot(tile_pair(kv_ref, rows_a, rows_b, 2 * h * HEAD_SIZE), qt) * factor
            scores = jnp.where(mask, scores, NEG)
            best = jnp.max(scores, axis=0, keepdims=True)
            weights = jnp.exp2(scores - best)
            total = jnp.sum(weights, axis=0, keepdims=True)
            values = tile_pair(kv_ref, rows_a, rows_b, (2 * h + 1) * HEAD_SIZE)
            acc_ref[h] = dot(values.T, weights.astype(jnp.bfloat16))
            state += [best, total]

        def one_pair(t, state):
            rows_a = key_rows(inverse_ref, base + 2 * t)
            rows_b = key_rows(inverse_ref, base + 2 * t + 1)
            after = []
            for h in range(hps):
                best, total = state[2 * h], state[2 * h + 1]
                keys = tile_pair(kv_ref, rows_a, rows_b, 2 * h * HEAD_SIZE)
                scores = dot(keys, qt_ref[h]) * factor
                newest = jnp.maximum(best, jnp.max(scores, axis=0, keepdims=True))
                weights = jnp.exp2(scores - newest)
                shrink = jnp.exp2(best - newest)
                total = total * shrink + jnp.sum(weights, axis=0, keepdims=True)
                values = tile_pair(kv_ref, rows_a, rows_b, (2 * h + 1) * HEAD_SIZE)
                acc_ref[h] = acc_ref[h] * shrink + dot(values.T, weights.astype(jnp.bfloat16))
                after += [newest, total]
            return tuple(after)

        state = lax.fori_loop(0, pairs, one_pair, tuple(state))
        for h in range(hps):
            best, total = state[2 * h], state[2 * h + 1]
            mixed = acc_ref[h] * (1.0 / total)
            for r in range(rep):
                part = mixed[:, r * BLOCK : (r + 1) * BLOCK]
                out_ref[rows, pl.ds(h * width + r * HEAD_SIZE, HEAD_SIZE)] = part.T.astype(
                    jnp.bfloat16
                )
            lse_ref[h, pl.ds(qb, 1), :] = best + jnp.log2(total)
        return carry

    lax.fori_loop(0, q_blocks, one_query_block, 0)
    mixed = out_ref[...]
    half = keep_ref.shape[0]
    for n in range(0, wo_ref.shape[1], 512):
        cols = slice(n, n + 512)
        partial = dot(mixed, wo_ref[:, cols]).astype(jnp.bfloat16)
        keep_ref[:, cols] = partial[:half]
        send_ref[:, cols] = partial[half:]


def backward_kernel(rep, hps, ctx_count, head, order_ref, cont_ref, where_ref, q_ref, gb_ref, wo_ref,
                    mix_ref, lse_ref, cos_ref, sin_ref, *refs):
    parts, refs = refs[:ctx_count], refs[ctx_count:]
    gq_ref, keep_ref, send_ref = refs[:3]
    kv_ref, gm_ref, inverse_ref, qt_ref, gmt_ref, gqt_ref, acc_ref, sem = refs[3:]
    copies = start_parts(parts, kv_ref, sem, head * kv_ref.shape[1])
    fill_inverse(order_ref, where_ref, inverse_ref)
    gm_ref[...] = right_dot(gb_ref[...], wo_ref[...]).astype(jnp.bfloat16)
    for copy in copies:
        copy.wait()
    q_blocks = q_ref.shape[0] // BLOCK
    scale = 1.0 / math.sqrt(HEAD_SIZE)
    factor = LOG2E * scale
    width = rep * HEAD_SIZE

    def clear(i, carry):
        acc_ref[pl.ds(pl.multiple_of(i * BLOCK, BLOCK), BLOCK), :] = jnp.zeros(
            (BLOCK, acc_ref.shape[1]), jnp.float32
        )
        return carry

    lax.fori_loop(0, order_ref.shape[0], clear, 0)

    def tile_terms(h, rows_a, rows_b, lse, delta, q_rows, gm_rows, mask):
        kcol, vcol = 2 * h * HEAD_SIZE, (2 * h + 1) * HEAD_SIZE
        keys = tile_pair(kv_ref, rows_a, rows_b, kcol)
        values = tile_pair(kv_ref, rows_a, rows_b, vcol)
        weights = jnp.exp2(dot(keys, qt_ref[h]) * factor - lse)
        if mask is not None:
            weights = jnp.where(mask, weights, 0.0)
        grad_weights = dot(values, gmt_ref[h])
        grad_scores = (weights * (grad_weights - delta)).astype(jnp.bfloat16)
        gv = dot(weights.astype(jnp.bfloat16), gm_rows)
        gk = dot(grad_scores, q_rows)
        acc_ref[rows_a, pl.ds(kcol, HEAD_SIZE)] += gk[:BLOCK]
        acc_ref[rows_b, pl.ds(kcol, HEAD_SIZE)] += gk[BLOCK:]
        acc_ref[rows_a, pl.ds(vcol, HEAD_SIZE)] += gv[:BLOCK]
        acc_ref[rows_b, pl.ds(vcol, HEAD_SIZE)] += gv[BLOCK:]
        return dot(keys.T, grad_scores)

    def one_query_block(qb, carry):
        base, pairs, prev, own, has_prev = block_plan(order_ref, cont_ref, where_ref, qb)
        rows = pl.ds(pl.multiple_of(qb * BLOCK, BLOCK), BLOCK)
        mask = own_mask(has_prev, rep)
        rows_a, rows_b = key_rows(inverse_ref, prev), key_rows(inverse_ref, own)
        deltas, lses, q_stack, gm_stack = [], [], [], []
        for h in range(hps):
            qt_ref[h] = stack_t(q_ref, rows, h * width, rep)
            gmt = stack_t(gm_ref, rows, h * width, rep)
            gmt_ref[h] = gmt
            mixt = stack_t(mix_ref, rows, h * width, rep)
            deltas.append(
                jnp.sum(
                    gmt.astype(jnp.float32) * mixt.astype(jnp.float32), axis=0, keepdims=True
                )
            )
            lses.append(lse_ref[h, pl.ds(qb, 1), :])
        for h in range(hps):
            q_rows = stack_rows(q_ref, rows, h * width, rep)
            gm_rows = stack_rows(gm_ref, rows, h * width, rep)
            gqt_ref[h] = tile_terms(
                h, rows_a, rows_b, lses[h], deltas[h], q_rows, gm_rows, mask
            )

        def one_pair(t, carry):
            rows_a = key_rows(inverse_ref, base + 2 * t)
            rows_b = key_rows(inverse_ref, base + 2 * t + 1)
            for h in range(hps):
                q_rows = stack_rows(q_ref, rows, h * width, rep)
                gm_rows = stack_rows(gm_ref, rows, h * width, rep)
                gqt_ref[h] += tile_terms(
                    h, rows_a, rows_b, lses[h], deltas[h], q_rows, gm_rows, None
                )
            return carry

        lax.fori_loop(0, pairs, one_pair, 0)
        for h in range(hps):
            total = gqt_ref[h] * scale
            for r in range(rep):
                part = total[:, r * BLOCK : (r + 1) * BLOCK]
                rounded = part.T.astype(jnp.bfloat16).astype(jnp.float32)
                gq_ref[rows, pl.ds(h * width + r * HEAD_SIZE, HEAD_SIZE)] = unrotate(
                    rounded, cos_ref[rows, :], sin_ref[rows, :]
                ).astype(jnp.bfloat16)
        return carry

    lax.fori_loop(0, q_blocks, one_query_block, 0)

    blocks = order_ref.shape[0]

    def place(index):
        chunk = lax.div(index, SLOTS)
        spot = (chunk & 1) * (ctx_count // 2) + (chunk & 2) // 2 * (ctx_count // 4) + (
            lax.shift_right_logical(chunk, 2)
        )
        return spot * SLOTS + (index & 3)

    def flush(i, carry):
        rows = pl.ds(pl.multiple_of(i * BLOCK, BLOCK), BLOCK)
        spot = place(i)
        parts = []
        for h in range(hps):
            parts.append(acc_ref[rows, pl.ds(2 * h * HEAD_SIZE, HEAD_SIZE)] * scale)
            parts.append(acc_ref[rows, pl.ds((2 * h + 1) * HEAD_SIZE, HEAD_SIZE)])
        value = jnp.concatenate(parts, axis=1).astype(jnp.bfloat16)

        @pl.when(spot < blocks // 2)
        def _():
            keep_ref[pl.ds(pl.multiple_of(spot * BLOCK, BLOCK), BLOCK), :] = value

        @pl.when(spot >= blocks // 2)
        def _():
            far = (spot - blocks // 2) * BLOCK
            send_ref[pl.ds(pl.multiple_of(far, BLOCK), BLOCK), :] = value

        return carry

    lax.fori_loop(0, blocks, flush, 0)


def attention_forward(q, w_out, parts, order, cont, where):
    ctx_count = len(parts)
    rows, tokens = q.shape[0], ctx_count * q.shape[0]
    kv_heads = parts[0].shape[1] // (2 * HEAD_SIZE)
    rep = q.shape[1] // HEAD_SIZE // kv_heads
    q_blocks, model = rows // BLOCK, w_out.shape[1]
    vmem, smem, any_ = (
        pl.BlockSpec(memory_space=space) for space in (pltpu.VMEM, pltpu.SMEM, pl.ANY)
    )
    flops = 2 * rows * tokens * q.shape[1] + 2 * rows * q.shape[1] * model
    half = jax.ShapeDtypeStruct((rows // 2, model), jnp.bfloat16)
    return pl.pallas_call(
        functools.partial(forward_kernel, rep, kv_heads, ctx_count),
        out_shape=(
            jax.ShapeDtypeStruct(q.shape, jnp.bfloat16),
            jax.ShapeDtypeStruct((kv_heads, q_blocks, rep * BLOCK), jnp.float32),
            half,
            half,
        ),
        in_specs=[smem] * 3 + [vmem] * 2 + [any_] * ctx_count,
        out_specs=[vmem] * 4,
        scratch_shapes=[
            pltpu.VMEM((tokens, parts[0].shape[1]), jnp.bfloat16),
            pltpu.SMEM((order.shape[0],), jnp.int32),
            pltpu.VMEM((kv_heads, HEAD_SIZE, rep * BLOCK), jnp.bfloat16),
            pltpu.VMEM((kv_heads, HEAD_SIZE, rep * BLOCK), jnp.float32),
            pltpu.SemaphoreType.DMA((ctx_count,)),
        ],
        compiler_params=pltpu.CompilerParams(vmem_limit_bytes=VMEM_LIMIT),
        cost_estimate=cost("attention_forward", flops, 2 * tokens * parts[0].shape[1] + 4 * rows * model),
        name="attention_forward",
    )(order, cont, where, q, w_out, *parts)


def attention_backward(head, q, grad_branch, w_out, mixed, lse, parts, cosine, sine, order, cont,
                       where):
    ctx_count = len(parts)
    rows, tokens = q.shape[0], ctx_count * q.shape[0]
    kv_heads = parts[0].shape[1] // (2 * HEAD_SIZE)
    rep = q.shape[1] // HEAD_SIZE // kv_heads
    q_blocks, model = rows // BLOCK, w_out.shape[1]
    wide = rep * HEAD_SIZE
    q_spec = pl.BlockSpec((rows, wide), lambda g, *_: (0, head))
    whole = lambda g, *_: (0, 0)
    table_spec = pl.BlockSpec((rows, HEAD_SIZE), whole)
    half = (tokens // 2, 2 * HEAD_SIZE)
    flops = 5 * rows * tokens * wide + 2 * rows * wide * model
    return pl.pallas_call(
        functools.partial(backward_kernel, rep, 1, ctx_count, head),
        out_shape=(
            jax.ShapeDtypeStruct((rows, wide), jnp.bfloat16),
            jax.ShapeDtypeStruct(half, jnp.bfloat16),
            jax.ShapeDtypeStruct(half, jnp.bfloat16),
        ),
        grid_spec=pltpu.PrefetchScalarGridSpec(
            num_scalar_prefetch=3,
            grid=(1,),
            in_specs=[
                q_spec,
                pl.BlockSpec((rows, model), whole),
                pl.BlockSpec((wide, model), lambda g, *_: (head, 0)),
                q_spec,
                pl.BlockSpec((1, q_blocks, rep * BLOCK), lambda g, *_: (head, 0, 0)),
                table_spec,
                table_spec,
            ]
            + [pl.BlockSpec(memory_space=pl.ANY)] * ctx_count,
            out_specs=[
                pl.BlockSpec((rows, wide), whole),
                pl.BlockSpec(half, whole),
                pl.BlockSpec(half, whole),
            ],
            scratch_shapes=[
                pltpu.VMEM((tokens, 2 * HEAD_SIZE), jnp.bfloat16),
                pltpu.VMEM((rows, wide), jnp.bfloat16),
                pltpu.SMEM((order.shape[0],), jnp.int32),
                pltpu.VMEM((1, HEAD_SIZE, rep * BLOCK), jnp.bfloat16),
                pltpu.VMEM((1, HEAD_SIZE, rep * BLOCK), jnp.bfloat16),
                pltpu.VMEM((1, HEAD_SIZE, rep * BLOCK), jnp.float32),
                pltpu.VMEM((tokens, 2 * HEAD_SIZE), jnp.float32),
                pltpu.SemaphoreType.DMA((ctx_count,)),
            ],
        ),
        compiler_params=pltpu.CompilerParams(vmem_limit_bytes=VMEM_LIMIT),
        cost_estimate=cost(f"attention_backward_{head}", flops, 4 * tokens * wide + 2 * rows * model),
        name=f"attention_backward_{head}",
    )(order, cont, where, q, grad_branch, w_out, mixed, lse, cosine, sine, *parts)


def input_kernel(order_ref, cont_ref, where_ref, gain_ref, x_hbm, wq_hbm, wk_hbm, wv_hbm, table_hbm,
                 first_ref, q_ref, kv_ref, cos_ref, sin_ref,
                 x_ref, wq_ref, wk_ref, wv_ref, table_ref, sem):
    pairs = ((x_hbm, x_ref), (table_hbm, table_ref), (wk_hbm, wk_ref), (wv_hbm, wv_ref),
             (wq_hbm, wq_ref))
    copies = [
        pltpu.make_async_copy(source, target, sem.at[n])
        for n, (source, target) in enumerate(pairs)
    ]
    for copy in copies:
        copy.start()
    count = cont_ref.shape[0]
    prompt_blocks = count // CONTS * PER_PROMPT
    starts = (table_ref.shape[0] - 2 * BLOCK) // 2
    lane = lax.broadcasted_iota(jnp.int32, (BLOCK, HEAD_SIZE), 1)
    copies[0].wait()
    copies[1].wait()

    def one_slot(slot, carry):
        quarter = slot_quarter(slot, where_ref[1])
        rows = pl.ds(pl.multiple_of(slot * BLOCK, BLOCK), BLOCK)
        full = x_ref[pl.ds(pl.multiple_of(quarter * BLOCK, BLOCK), BLOCK), :].astype(jnp.float32)
        inv = lax.rsqrt(jnp.mean(full * full, axis=-1, keepdims=True) + eps_norm)
        first_ref[rows, :] = (full * inv * gain_ref[...]).astype(jnp.bfloat16)
        own = order_ref[stored_block(slot, where_ref)]
        spot = jnp.where(
            own < prompt_blocks,
            lax.rem(own, PER_PROMPT),
            PER_PROMPT + lax.rem(own - prompt_blocks, PER_CONT),
        )
        cos_start = table_ref[pl.ds(2 * BLOCK + spot, 1), :]
        sin_start = table_ref[pl.ds(2 * BLOCK + starts + spot, 1), :]
        cos_in, sin_in = table_ref[:BLOCK, :], table_ref[BLOCK : 2 * BLOCK, :]
        sine = sin_start * cos_in + cos_start * sin_in
        cos_ref[rows, :] = cos_start * cos_in - sin_start * sin_in
        sin_ref[rows, :] = jnp.where(lane < HEAD_SIZE // 2, -sine, sine)
        return carry

    lax.fori_loop(0, SLOTS, one_slot, 0)
    first = first_ref[...]
    cosine, sine = cos_ref[...], sin_ref[...]
    copies[2].wait()
    copies[3].wait()
    keys = dot(first, wk_ref[...])
    values = dot(first, wv_ref[...])
    for h in range(wk_ref.shape[1] // HEAD_SIZE):
        cols = slice(h * HEAD_SIZE, (h + 1) * HEAD_SIZE)
        low, high = 2 * h * HEAD_SIZE, (2 * h + 1) * HEAD_SIZE
        key = rotate(keys[:, cols], cosine, sine)
        kv_ref[:, low:high] = key.astype(jnp.bfloat16)
        kv_ref[:, high : high + HEAD_SIZE] = values[:, cols].astype(jnp.bfloat16)
    copies[4].wait()
    for n in range(0, wq_ref.shape[1], 256):
        queries = dot(first, wq_ref[:, n : n + 256])
        for m in range(0, 256, HEAD_SIZE):
            query = rotate(queries[:, m : m + HEAD_SIZE], cosine, sine)
            q_ref[:, n + m : n + m + HEAD_SIZE] = query.astype(jnp.bfloat16)


def input_stage(x, gain, wq, wk, wv, order, cont, where):
    rows, model = x.shape
    cos_start, sin_start, cos_in, sin_in = angle_tables()
    table = np.concatenate([cos_in, sin_in, cos_start, sin_start])
    vmem, smem, any_ = (
        pl.BlockSpec(memory_space=space) for space in (pltpu.VMEM, pltpu.SMEM, pl.ANY)
    )
    flops = 2 * rows * model * (wq.shape[1] + 2 * wk.shape[1])
    return pl.pallas_call(
        input_kernel,
        out_shape=(
            jax.ShapeDtypeStruct((rows, model), jnp.bfloat16),
            jax.ShapeDtypeStruct((rows, wq.shape[1]), jnp.bfloat16),
            jax.ShapeDtypeStruct((rows, 2 * wk.shape[1]), jnp.bfloat16),
            jax.ShapeDtypeStruct((rows, HEAD_SIZE), jnp.float32),
            jax.ShapeDtypeStruct((rows, HEAD_SIZE), jnp.float32),
        ),
        in_specs=[smem] * 3 + [vmem] + [any_] * 5,
        out_specs=[vmem] * 5,
        scratch_shapes=[
            pltpu.VMEM(a.shape, a.dtype) for a in (x, wq, wk, wv)
        ]
        + [pltpu.VMEM(table.shape, jnp.float32), pltpu.SemaphoreType.DMA((5,))],
        compiler_params=pltpu.CompilerParams(vmem_limit_bytes=VMEM_LIMIT),
        cost_estimate=cost("input_stage", flops, 4 * x.size + 2 * wq.size + 4 * wk.size),
        name="input_stage",
    )(order, cont, where, gain.reshape(1, -1), x, wq, wk, wv, table)


FILLERS = ("ffn_out", "gate_shares", "up_shares", "kv_shares", "grad_hidden", "grad_second_keep")


def cost(name, flops, bytes_accessed):
    scale = 16.0 if name in FILLERS else 0.02
    return pl.CostEstimate(
        flops=int(flops * scale), bytes_accessed=int(bytes_accessed * scale), transcendentals=0
    )


def put_share(value, index, x_bit, keep_ref, send_ref, swap_bits):
    spot = share_spot(lax.shift_right_logical(index, 1), keep_ref.shape[0], swap_bits)
    stays = (index & 1) == x_bit
    value = value.astype(keep_ref.dtype)

    @pl.when(stays)
    def _():
        keep_ref[pl.ds(spot, 1)] = value[None]

    @pl.when(jnp.logical_not(stays))
    def _():
        send_ref[pl.ds(spot, 1)] = value[None]


def pair_bit(where_ref):
    return lax.shift_right_logical(where_ref[0], 1) & 1


def grad_hidden_kernel(where_ref, cot_ref, wd_ref, out_ref):
    out_ref[...] = right_dot(cot_ref[...], wd_ref[...])


def grad_hidden_stage(cot, w_down, where):
    rows, model = cot.shape
    units = w_down.shape[0] // 2
    block = 256
    steps = units // block
    return pl.pallas_call(
        grad_hidden_kernel,
        out_shape=jax.ShapeDtypeStruct((rows, units), jnp.float32),
        grid_spec=pltpu.PrefetchScalarGridSpec(
            num_scalar_prefetch=1,
            grid=(steps,),
            in_specs=[
                pl.BlockSpec((rows, model), lambda i, w: (0, 0), pipeline_mode=pl.Buffered(1)),
                pl.BlockSpec((block, model), lambda i, w: (pair_bit(w) * steps + i, 0)),
            ],
            out_specs=pl.BlockSpec((rows, block), lambda i, w: (0, i)),
        ),
        compiler_params=pltpu.CompilerParams(vmem_limit_bytes=VMEM_LIMIT),
        cost_estimate=cost("grad_hidden", 2 * rows * model * units, 4 * rows * model),
        name="grad_hidden",
    )(where, cot, w_down)


def ffn_kernel(where_ref, in_ref, gh_ref, wg_ref, wu_ref, hid_ref, gg_ref, gu_ref):
    gate = dot(in_ref[...], wg_ref[...])
    upward = dot(in_ref[...], wu_ref[...])
    grad_hidden = gh_ref[...]
    sigma = jax.nn.sigmoid(gate)
    swish = gate * sigma
    hid_ref[...] = (swish * upward).astype(jnp.bfloat16)
    gg_ref[...] = (grad_hidden * upward * sigma * (1.0 + gate * (1.0 - sigma))).astype(
        jnp.bfloat16
    )
    gu_ref[...] = (grad_hidden * swish).astype(jnp.bfloat16)


def ffn_stage(second, grad_hidden, w_gate, w_up, where):
    rows, model = second.shape
    units = w_gate.shape[1] // 2
    block = 256
    steps = units // block
    col_spec = pl.BlockSpec((model, block), lambda i, w: (0, pair_bit(w) * steps + i))
    unit_spec = pl.BlockSpec((rows, block), lambda i, w: (0, i))
    unit = jax.ShapeDtypeStruct((rows, units), jnp.bfloat16)
    return pl.pallas_call(
        ffn_kernel,
        out_shape=(unit, unit, unit),
        grid_spec=pltpu.PrefetchScalarGridSpec(
            num_scalar_prefetch=1,
            grid=(steps,),
            in_specs=[
                pl.BlockSpec((rows, model), lambda i, w: (0, 0), pipeline_mode=pl.Buffered(1)),
                unit_spec,
                col_spec,
                col_spec,
            ],
            out_specs=[unit_spec] * 3,
        ),
        compiler_params=pltpu.CompilerParams(vmem_limit_bytes=VMEM_LIMIT),
        cost_estimate=cost("ffn_stage", 4 * rows * model * units, 6 * rows * model),
        name="ffn_stage",
    )(where, second, grad_hidden, w_gate, w_up)


def grad_second_kernel(where_ref, gg_ref, gu_ref, wg_ref, wu_ref, out_ref):
    total = right_dot(gg_ref[...], wg_ref[...]) + right_dot(gu_ref[...], wu_ref[...])
    out_ref[...] = total.astype(jnp.bfloat16)


def grad_second_half(half, name, grads, weights, where):
    rows, units = grads[0].shape
    rows //= 2
    model = weights[0].shape[0]
    block = 512
    left_spec = pl.BlockSpec((rows, units), lambda n, w: (half, 0), pipeline_mode=pl.Buffered(1))
    right_spec = pl.BlockSpec((block, units), lambda n, w: (n, pair_bit(w)))
    return pl.pallas_call(
        grad_second_kernel,
        out_shape=jax.ShapeDtypeStruct((rows, model), jnp.bfloat16),
        grid_spec=pltpu.PrefetchScalarGridSpec(
            num_scalar_prefetch=1,
            grid=(model // block,),
            in_specs=[left_spec] * 2 + [right_spec] * 2,
            out_specs=pl.BlockSpec((rows, block), lambda n, w: (0, n)),
        ),
        compiler_params=pltpu.CompilerParams(vmem_limit_bytes=VMEM_LIMIT),
        cost_estimate=cost(name, 4 * rows * units * model, 4 * rows * model),
        name=name,
    )(where, *grads, *weights)


def ffn_out_kernel(where_ref, hid_ref, wd_ref, keep_ref, send_ref):
    total = dot(hid_ref[...], wd_ref[...])
    half = keep_ref.shape[0]
    keep_ref[...] = total[:half].astype(jnp.bfloat16)
    send_ref[...] = total[half:].astype(jnp.bfloat16)


def unit_sum(kernel, name, lefts, rights, transposed, where):
    rows, units = lefts[0].shape
    model = rights[0].shape[0 if transposed else 1]
    block = 512
    if transposed:
        right_spec = pl.BlockSpec((block, units), lambda n, w: (n, pair_bit(w)))
    else:
        right_spec = pl.BlockSpec((units, block), lambda n, w: (pair_bit(w), n))
    left_spec = pl.BlockSpec((rows, units), lambda n, w: (0, 0), pipeline_mode=pl.Buffered(1))
    half = jax.ShapeDtypeStruct((rows // 2, model), jnp.bfloat16)
    half_spec = pl.BlockSpec((rows // 2, block), lambda n, w: (0, n))
    return pl.pallas_call(
        kernel,
        out_shape=(half, half),
        grid_spec=pltpu.PrefetchScalarGridSpec(
            num_scalar_prefetch=1,
            grid=(model // block,),
            in_specs=[left_spec] * len(lefts) + [right_spec] * len(rights),
            out_specs=[half_spec, half_spec],
        ),
        compiler_params=pltpu.CompilerParams(vmem_limit_bytes=VMEM_LIMIT),
        cost_estimate=cost(name, 2 * len(lefts) * rows * units * model, 4 * rows * model),
        name=name,
    )(where, *lefts, *rights)


def share_spot(spot, count, swap_bits):
    if swap_bits:
        return (spot & 1) * (count // 2) + lax.shift_right_logical(spot, 1)
    return spot


def shares_kernel(left_count, swap_bits, pairs, where_ref, *refs):
    lefts, refs = refs[:left_count], refs[left_count:]
    rights, (keep_ref, send_ref) = refs[:-2], refs[-2:]
    share = keep_ref.shape[1]
    step = pl.program_id(0)
    pieces = [left_dot(lefts[l][...], rights[r][...]) for l, r in pairs]
    per_step = lefts[0].shape[1] // share
    if per_step == 1:
        value = jnp.concatenate(pieces, axis=1).astype(keep_ref.dtype)
        sends = step < pl.num_programs(0) // 2

        @pl.when(sends)
        def _():
            send_ref[0] = value

        @pl.when(jnp.logical_not(sends))
        def _():
            keep_ref[0] = value

        return
    for k in range(per_step):
        rows = slice(k * share, (k + 1) * share)
        value = jnp.concatenate([piece[rows] for piece in pieces], axis=1)
        index = step * per_step + k
        put_share(value, index, where_ref[0] & 1, keep_ref, send_ref, swap_bits)


def weight_shares(name, lefts, rights, pairs, ctx_count, swap_bits, where):
    rows, model = lefts[0].shape
    block = 256
    share, half = model // ctx_count, ctx_count // 2
    width = sum(rights[r].shape[1] for _, r in pairs)
    shares = jax.ShapeDtypeStruct((half, share, width), jnp.bfloat16)
    if share == block:

        def left_map(i, w):
            mine = w[0] & 1
            return 0, jnp.where(i < half, 2 * i + 1 - mine, 2 * (i - half) + mine)

        left_spec = pl.BlockSpec((rows, block), left_map)
        spot = lambda index: share_spot(index, half, swap_bits)
        keep_spec = pl.BlockSpec(
            (1, share, width), lambda i, w: (spot(jnp.maximum(i - half, 0)), 0, 0)
        )
        send_spec = pl.BlockSpec(
            (1, share, width), lambda i, w: (spot(jnp.minimum(i, half - 1)), 0, 0)
        )
    else:
        left_spec = pl.BlockSpec((rows, block), lambda i, w: (0, i))
        keep_spec = send_spec = pl.BlockSpec(shares.shape, lambda i, w: (0, 0, 0))
    return pl.pallas_call(
        functools.partial(shares_kernel, len(lefts), swap_bits, pairs),
        out_shape=(shares, shares),
        grid_spec=pltpu.PrefetchScalarGridSpec(
            num_scalar_prefetch=1,
            grid=(model // block,),
            in_specs=[left_spec] * len(lefts)
            + [
                pl.BlockSpec(r.shape, lambda i, w: (0, 0), pipeline_mode=pl.Buffered(1))
                for r in rights
            ],
            out_specs=[keep_spec, send_spec],
        ),
        compiler_params=pltpu.CompilerParams(vmem_limit_bytes=VMEM_LIMIT),
        cost_estimate=cost(name, 2 * rows * model * width, 4 * rows * model),
        name=name,
    )(where, *lefts, *rights)


def unit_shares_kernel(where_ref, left_ref, right_ref, out_ref):
    share = out_ref.shape[1]
    total = left_dot(left_ref[...], right_ref[...]).astype(out_ref.dtype)
    per_step = left_ref.shape[1] // share
    if out_ref.shape[0] == 1:
        out_ref[0] = total
    else:
        for k in range(per_step):
            index = pl.program_id(0) * per_step + k
            out_ref[pl.ds(unit_spot(index), 1)] = total[k * share : (k + 1) * share][None]


def unit_spot(index):
    return (index & ~3) + (index & 1) * 2 + (lax.shift_right_logical(index, 1) & 1)


def unit_shares(name, left, right, ctx_count, where):
    rows, model = left.shape
    block, width = 256, right.shape[1]
    share = model // ctx_count
    shares = jax.ShapeDtypeStruct((ctx_count, share, width), jnp.bfloat16)
    if share == block:
        out_spec = pl.BlockSpec((1, share, width), lambda i, w: (unit_spot(i), 0, 0))
    else:
        out_spec = pl.BlockSpec(shares.shape, lambda i, w: (0, 0, 0))
    return pl.pallas_call(
        unit_shares_kernel,
        out_shape=shares,
        grid_spec=pltpu.PrefetchScalarGridSpec(
            num_scalar_prefetch=1,
            grid=(model // block,),
            in_specs=[
                pl.BlockSpec((rows, block), lambda i, w: (0, i)),
                pl.BlockSpec(right.shape, lambda i, w: (0, 0), pipeline_mode=pl.Buffered(1)),
            ],
            out_specs=out_spec,
        ),
        compiler_params=pltpu.CompilerParams(vmem_limit_bytes=VMEM_LIMIT),
        cost_estimate=cost(name, 2 * rows * model * width, 4 * rows * model),
        name=name,
    )(where, left, right)


def tail_kernel(kv_heads, where_ref, *refs):
    sums, refs = refs[: 2 * kv_heads], refs[2 * kv_heads :]
    cos_ref, sin_ref, refs = refs[0], refs[1], refs[2:]
    gq_refs, refs = refs[:kv_heads], refs[kv_heads:]
    wq_ref, wk_ref, wv_ref, keep_ref, send_ref, gkv_ref = refs
    cosine, sine = cos_ref[...], sin_ref[...]
    for h in range(kv_heads):
        total = sums[2 * h][...].astype(jnp.float32) + sums[2 * h + 1][...].astype(jnp.float32)
        total = total.astype(jnp.bfloat16)
        key = unrotate(total[:, :HEAD_SIZE].astype(jnp.float32), cosine, sine)
        cols = slice(h * HEAD_SIZE, (h + 1) * HEAD_SIZE)
        gkv_ref[:, cols] = key.astype(jnp.bfloat16)
        cols = slice((kv_heads + h) * HEAD_SIZE, (kv_heads + h + 1) * HEAD_SIZE)
        gkv_ref[:, cols] = total[:, HEAD_SIZE:]
    half = keep_ref.shape[0]
    key_width = kv_heads * HEAD_SIZE
    wide = gq_refs[0].shape[1]
    for n in range(0, wq_ref.shape[0], 512):
        span = slice(n, n + 512)
        total = right_dot(gkv_ref[:, :key_width], wk_ref[span, :])
        total += right_dot(gkv_ref[:, key_width:], wv_ref[span, :])
        for h in range(kv_heads):
            total += right_dot(gq_refs[h][...], wq_ref[span, h * wide : (h + 1) * wide])
        total = total.astype(jnp.bfloat16)
        keep_ref[:, span] = total[:half]
        send_ref[:, span] = total[half:]


def tail_stage(kv_sums, cosine, sine, grad_queries, wq, wk, wv, where):
    rows, model = cosine.shape[0], wq.shape[0]
    kv_heads = len(grad_queries)
    vmem = pl.BlockSpec(memory_space=pltpu.VMEM)
    half = jax.ShapeDtypeStruct((rows // 2, model), jnp.bfloat16)
    flat = [term for sums in kv_sums for term in sums]
    return pl.pallas_call(
        functools.partial(tail_kernel, kv_heads),
        out_shape=(
            half,
            half,
            jax.ShapeDtypeStruct((rows, 2 * kv_heads * HEAD_SIZE), jnp.bfloat16),
        ),
        in_specs=[pl.BlockSpec(memory_space=pltpu.SMEM)]
        + [vmem] * (len(flat) + 2 + kv_heads + 3),
        out_specs=[vmem] * 3,
        compiler_params=pltpu.CompilerParams(vmem_limit_bytes=VMEM_LIMIT),
        cost_estimate=cost("tail_stage", 2 * rows * model * (wq.shape[1] + 2 * wk.shape[1]), 4 * rows * model + 4 * wq.size
        ),
        name="tail_stage",
    )(where, *flat, cosine, sine, *grad_queries, wq, wk, wv)


def flip(value, axis, mask=1):
    return lax.ppermute(value, axis, [(i, i ^ mask) for i in range(lax.axis_size(axis))])


def ctx_flip(value, mask):
    if mask == 1:
        return flip(value, "x")
    if mask == 2:
        return flip(value, "l")
    return flip(value, "hi", mask // 4)


def add(left, right):
    return (left.astype(jnp.float32) + right.astype(jnp.float32)).astype(jnp.bfloat16)


def slots_of(value, tensor):
    rows = value.shape[0] // SLOTS
    return [
        lax.dynamic_slice_in_dim(value, (tensor ^ SLOT_XOR[u]) * rows, rows)
        for u in range(SLOTS)
    ]


def after(dep, *values):
    deps = dep if isinstance(dep, tuple) else (dep,)
    held = lax.optimization_barrier(deps + values)[len(deps) :]
    return held[0] if len(held) == 1 else held


class Stages:
    def __init__(self, block_order):
        self.live = block_order[0] >= 0

    def __call__(self, function, *args):
        shapes = jax.eval_shape(function, *args)
        empty = lambda *_: jax.tree.map(lambda a: jnp.zeros(a.shape, a.dtype), shapes)
        return lax.cond(self.live, function, empty, *args)


def gather_pair(own):
    partner = ctx_flip(own, 2)
    near = jnp.concatenate([own, partner, flip(own, "y"), flip(partner, "y")])
    return jnp.concatenate([near, flip(near, "core")])


def gather_slots(own):
    near = jnp.concatenate([own, flip(own, "y")])
    return near, flip(near, "core")


def place_rows(own, near, core, far, tensor):
    rows = own.shape[0]
    result = jnp.zeros((SLOTS * rows,) + own.shape[1:], own.dtype)
    for u, piece in enumerate((own, near, core, far)):
        result = lax.dynamic_update_slice_in_dim(
            result, piece, (tensor ^ SLOT_XOR[u]) * rows, 0
        )
    return result


def scatter_slots(keep, send, fill=lambda value: value):
    got = fill(flip(send, "core"))
    quarter = keep.shape[0] // 2
    far = flip(add(keep[quarter:], got[quarter:]), "y")
    return add(keep[:quarter], got[:quarter]), far


def pair_scatter(keep, send, fill=lambda near: near):
    got = fill(flip(send, "core"))
    n = keep.shape[0] // 4
    near = [add(keep[k * n : (k + 1) * n], got[k * n : (k + 1) * n]) for k in range(4)]
    far = flip(near[3], "y")
    got = flip(near[2], "y")
    return near, far, got


def pair_finish(near, far, got):
    away = add(near[1], far)
    return near[0], got, ctx_flip(away, 2), away


def total(terms):
    return sum(term.astype(jnp.float32) for term in terms)


class Reduce:
    def __init__(self, keep, send):
        self.keep, self.got = keep, ctx_flip(send, 1)

    def halve(self, mask, ctx, dep=None):
        keep, got = self.keep, self.got
        if dep is not None:
            keep, got = after(dep, keep, got)
        n = keep.shape[0] // 2
        bit = lax.div(ctx, mask) % 2
        pick = lambda value, index: lax.dynamic_slice_in_dim(value, index * n, n, 0)
        away = ctx_flip(add(pick(keep, 1 - bit), pick(got, 1 - bit)), mask)
        self.keep, self.got = add(pick(keep, bit), pick(got, bit)), away

    def sum(self):
        return (self.keep.astype(jnp.float32) + self.got.astype(jnp.float32))[0]


def high_masks(ctx_count):
    masks, mask = [], ctx_count // 2
    while mask >= 4:
        masks.append(mask)
        mask //= 2
    return masks


def unit_sum_over(shares):
    return lax.psum_scatter(shares, ("hi", "x"), scatter_dimension=0, tiled=True)


def split_halves(summed, ctx, dep):
    summed = after(dep, summed)
    pair = lax.div(ctx, 2) % 2
    pick = lambda index: lax.dynamic_index_in_dim(summed, index, 0, keepdims=False)
    return pick(pair), pick(1 - pair)


def join_halves(own, other, ctx):
    pair = lax.div(ctx, 2) % 2
    low, high = jnp.where(pair == 0, own, other), jnp.where(pair == 0, other, own)
    return jnp.concatenate([low, high], axis=1).astype(jnp.float32)


class KvReduce:
    def __init__(self, keep, got):
        self.keep, self.got = keep, got

    def merge(self, dep):
        keep, got = after(dep, self.keep, self.got)
        n = keep.shape[0] // 2
        return add(keep[:n], got[:n]), add(keep[n:], got[n:])


def norm_back(grad_out, normed, inv_scale, gain):
    scaled = grad_out * gain
    inner = jnp.mean(scaled * normed, axis=-1, keepdims=True)
    return (inv_scale * (scaled - normed * inner), jnp.sum(grad_out * normed, axis=0))


def body(
    layer_input,
    attn_gain,
    w_query,
    key_matrix,
    value_matrix,
    w_out,
    ffn_gain,
    w_gate,
    w_up,
    w_down,
    cotangent,
    block_order,
    cont_prompt,
):
    ctx_count = lax.axis_size("hi") * 4
    ctx = (lax.axis_index("hi") * 2 + lax.axis_index("l")) * 2 + lax.axis_index("x")
    tensor = lax.axis_index("y") * 2 + lax.axis_index("core")
    where = jnp.stack([ctx, tensor]).astype(jnp.int32)
    quarter = layer_input.shape[0] // SLOTS
    kv_heads = key_matrix.shape[1] // HEAD_SIZE
    highs = high_masks(ctx_count)

    stage = Stages(block_order)
    cot_own = lax.dynamic_slice_in_dim(cotangent, tensor * quarter, quarter)
    cot_slots = slots_of(cotangent, tensor)
    first_input, queries, kv_local, cosine, sine = input_stage(
        layer_input, attn_gain, w_query, key_matrix, value_matrix, block_order, cont_prompt, where
    )
    parts = {0: kv_local}
    parts[2], parts[1] = stage(lambda kv: (ctx_flip(kv, 2), ctx_flip(kv, 1)), kv_local)
    high_parts = {0: after(parts[1], kv_local)}
    for bit in reversed(highs):
        for mask in list(high_parts):
            high_parts[mask + bit] = ctx_flip(high_parts[mask], bit)
    del high_parts[0]
    parts.update(high_parts)
    parts[3], cot_part = stage(
        lambda kv, cot: (ctx_flip(kv, 1), ctx_flip(cot, 2)), parts[2], cot_own
    )
    dep = parts[3]
    for mask in high_parts:
        parts[mask + 2], parts[mask + 1], more = stage(
            lambda kv, cot: (ctx_flip(kv, 2), ctx_flip(kv, 1), flip(cot, "y")),
            after(dep, parts[mask]),
            cot_part,
        )
        dep = parts[mask + 1]
    cot_part = jnp.concatenate([cot_part, more])
    for mask in high_parts:
        parts[mask + 3], cot_far = stage(
            lambda kv, cot: (ctx_flip(kv, 1), flip(cot, "core")), parts[mask + 2], cot_part
        )
    parts = [parts[mask] for mask in range(ctx_count)]
    cot = jnp.concatenate(
        [cot_slots[0], cot_part[:quarter], cot_slots[1], cot_part[quarter:]]
        + [cot_slots[2], cot_far[:quarter], cot_slots[3], cot_far[quarter:]]
    )
    mixed, log_total, keep, send = attention_forward(
        after(cot, queries), w_out, parts, block_order, cont_prompt, where
    )
    first_half = flip(send, "core")
    near = add(keep, first_half)
    far = flip(near[quarter:], "y")
    grad_hidden = grad_hidden_stage(after(near, cot), w_down, where)
    own_input = lax.dynamic_slice_in_dim(layer_input, tensor * quarter, quarter)
    own_input = own_input.astype(jnp.float32)
    middle = own_input + total((near[:quarter], after(grad_hidden, far)))
    inv_two = lax.rsqrt(jnp.mean(middle * middle, axis=-1, keepdims=True) + eps_norm)
    normed_two = middle * inv_two
    second = gather_pair((normed_two * ffn_gain).astype(jnp.bfloat16))
    hidden, grad_gate, grad_up = ffn_stage(second, grad_hidden, w_gate, w_up, where)

    down_shares = unit_shares("down_shares", cot, hidden, ctx_count, where)
    down = unit_sum_over(down_shares)
    grads, weights = after(down_shares, grad_gate, grad_up), (w_gate, w_up)
    send = grad_second_half(1, "grad_second_send", grads, weights, where)

    def second_stage(send, grad_gate, grad_up, hidden):
        keep = grad_second_half(0, "grad_second_keep", (grad_gate, grad_up), weights, where)
        near, far, got = pair_scatter(keep, send)
        shares = unit_shares("gate_shares", second, after(near[3], grad_gate), ctx_count, where)
        *terms, away = pair_finish(near, after(shares, far), got)
        halves = unit_sum(
            ffn_out_kernel, "ffn_out", (after(away, hidden),), (w_down,), False, where
        )
        return total(after(halves[0], *terms)), shares, halves

    grad_second, gate_shares, ffn_halves = stage(second_stage, send, *grads, hidden)
    gate = unit_sum_over(gate_shares)

    def branch_stage(grad_second, grad_up, own):
        grad_norm, gain_part = norm_back(grad_second, normed_two, inv_two, ffn_gain)
        grad_middle = own.astype(jnp.float32) + grad_norm
        branch = grad_middle.astype(jnp.bfloat16)
        shares = unit_shares("up_shares", second, after(branch, grad_up), ctx_count, where)
        near = jnp.concatenate([branch, after(shares, flip(branch, "y"))])
        return grad_middle, gain_part, shares, jnp.concatenate([near, flip(near, "core")])

    grad_middle, ffn_gain_part, up_shares, grad_branch = stage(
        branch_stage, grad_second, grad_up, cot_own
    )
    up = unit_sum_over(up_shares)
    backward, kv = [], []
    held = grad_branch
    for head in range(kv_heads):
        backward.append(
            attention_backward(
                head, queries, held, w_out, mixed, log_total, parts, cosine, sine,
                block_order, cont_prompt, where,
            )
        )
        kv.append(KvReduce(backward[-1][1], ctx_flip(backward[-1][2], 1)))
        dep = backward[-1][0]
        if head == 0:
            down_own, down_away = split_halves(down, ctx, dep)
            down_other = ctx_flip(down_away, 2)
            dep = down_own
        held = after(dep, grad_branch)
    grad_queries = [item[0] for item in backward]
    branch_shares = weight_shares(
        "branch_shares",
        (first_input, grad_branch),
        grad_queries + [after(dep, mixed)],
        tuple((0, h) for h in range(kv_heads)) + ((1, kv_heads),),
        ctx_count,
        True,
        where,
    )
    sum_down = join_halves(down_own, after(branch_shares[0], down_other), ctx).T
    kv = [item.merge(sum_down) for item in kv]
    dep = tuple(keep for keep, _ in kv)
    branch = Reduce(*after(dep, *branch_shares))

    got = [ctx_flip(value, 2) for _, value in kv]

    def out_stage(keep, send):
        got = flip(send, "core")
        n = keep.shape[0] // 4
        near = [add(keep[k * n : (k + 1) * n], got[k * n : (k + 1) * n]) for k in range(4)]
        return near[0], near[2], add(near[1], flip(near[3], "y"))

    out_near, out_own, out_away = stage(out_stage, *after(dep, *ffn_halves))
    for mask in highs:
        kv = [KvReduce(keep, value).merge(out_away) for (keep, _), value in zip(kv, got)]
        got = [ctx_flip(value, mask) for _, value in kv]
    out_far, out_got = stage(
        lambda away, own: (ctx_flip(away, 2), flip(own, "y")),
        *after(tuple(keep for keep, _ in kv), out_away, out_own),
    )
    got = [after(out_far, value) for value in got]
    kv = [(keep, value) for (keep, _), value in zip(kv, got)]
    gate_own, gate_away = split_halves(gate, ctx, tuple(got))
    gate_other = ctx_flip(gate_away, 2)
    dep = gate_own
    output = (middle + total((out_near, out_got, after(dep, out_far)))).astype(jnp.bfloat16)
    keep, send, grad_kv = tail_stage(
        [(keep, after(dep, value)) for keep, value in kv], cosine, sine, grad_queries,
        w_query, key_matrix, value_matrix, where,
    )

    def first_stage(keep, send, grad_kv, own_input, grad_middle):
        shares = weight_shares(
            "kv_shares", (first_input,), (grad_kv,), ((0, 0),), ctx_count, True, where
        )
        terms = scatter_slots(keep, send, lambda value: after(shares[0], value))
        inv = lax.rsqrt(jnp.mean(own_input * own_input, axis=-1, keepdims=True) + eps_norm)
        grad_norm, gain_part = norm_back(total(terms), own_input * inv, inv, attn_gain)
        return shares, gain_part, (grad_middle + grad_norm).astype(jnp.bfloat16)

    kv_shares, attn_gain_part, grad_input = stage(
        first_stage, keep, send, grad_kv, own_input, grad_middle
    )
    near = jnp.concatenate([grad_input, after(grad_input, output)])
    near_other = flip(near, "y")
    branch.halve(2, ctx, grad_input)
    last = Reduce(*after(branch.keep, *kv_shares))
    sum_gate = join_halves(gate_own, after(branch.keep, gate_other), ctx)
    dep = sum_gate
    for mask in highs:
        branch.halve(mask, ctx, dep)
        dep = branch.keep
    last.halve(2, ctx, dep)
    near = jnp.concatenate([near, after(last.keep, near_other)])
    far = flip(near, "core")
    quarters = [near[n * quarter : (n + 1) * quarter] for n in range(4)]
    quarters += [far[n * quarter : (n + 1) * quarter] for n in range(4)]
    grad_input, output = [
        place_rows(quarters[k], quarters[k + 2], quarters[k + 4], quarters[k + 6], tensor)
        for k in range(2)
    ]
    dep = (grad_input, output)
    for mask in highs:
        last.halve(mask, ctx, dep)
        dep = last.keep

    def gain_stage(gains):
        gains = gains + flip(gains, "core")
        gains = gains + flip(gains, "y")
        for mask in [1, 2] + highs:
            gains = gains + ctx_flip(gains, mask)
        return gains

    gains = stage(gain_stage, after(dep, jnp.stack([attn_gain_part, ffn_gain_part])))
    up_own, up_away = split_halves(up, ctx, dep)
    up_other = ctx_flip(up_away, 2)
    sum_up = join_halves(up_own, after(gains, up_other), ctx)
    branch.keep, branch.got = after(gains, branch.keep, branch.got)
    width_q, width_k = w_query.shape[1], key_matrix.shape[1]
    branch_sum, last_sum = branch.sum(), last.sum()
    sum_query, sum_out = branch_sum[:, :width_q], branch_sum[:, width_q:].T
    sum_key, sum_value = last_sum[:, :width_k], last_sum[:, width_k:]

    gains = gains.reshape(2, ctx_count * SLOTS, -1)
    gains = lax.dynamic_index_in_dim(gains, ctx * SLOTS + tensor, 1, keepdims=False)
    return (
        output,
        grad_input,
        gains[0],
        sum_query,
        sum_key,
        sum_value,
        sum_out,
        gains[1],
        sum_gate,
        sum_up,
        sum_down,
    )


def solution(mesh):
    rows, heads = ("hi", "l", "x"), ("y", "core")
    split = Mesh(mesh.devices.reshape(-1, 2, 2, 2, 2), rows + heads)
    placed = (
        P(rows, None),
        P(),
        P(None, heads),
        P(None, heads),
        P(None, heads),
        P(heads, None),
        P(),
        P(None, heads),
        P(None, heads),
        P(heads, None),
        P(rows, None),
        P(),
        P(),
    )
    return jax.shard_map(
        body,
        mesh=split,
        in_specs=placed,
        out_specs=(
            P(rows, None),
            P(rows, None),
            P(rows + heads),
            P(rows, heads),
            P(rows, heads),
            P(rows, heads),
            P(heads, rows),
            P(rows + heads),
            P(rows, heads),
            P(rows, heads),
            P(heads, rows),
        ),
        check_vma=False,
    )
```

```python
import functools
import math

import jax
import jax.numpy as jnp
import numpy as np
from jax import lax
from jax.experimental import pallas as pl
from jax.experimental.pallas import tpu as pltpu
from jax.sharding import Mesh
from jax.sharding import PartitionSpec as P

HEAD_SIZE = 128
PROMPT = 2048
CONT_LEN = 256
CONTS = 8
BLOCK = 128
PER_PROMPT = PROMPT // BLOCK
PER_CONT = CONT_LEN // BLOCK
LOG2E = 1.4426950408889634
NEG = -1e30
SLOTS = 4
VMEM_LIMIT = 60 << 20

eps_norm = 1e-05
rope_base = 1000000.0

SLOT_XOR = (0, 2, 1, 3)


def plain_dot(left, right):
    return jnp.dot(left, right, preferred_element_type=jnp.float32)


def left_dot(left, right):
    return lax.dot_general(
        left, right, (((0,), (0,)), ((), ())), preferred_element_type=jnp.float32
    )


def right_dot(left, right):
    return lax.dot_general(
        left, right, (((1,), (1,)), ((), ())), preferred_element_type=jnp.float32
    )


def slot_quarter(slot, tensor):
    return ((slot & 1) * 2 + lax.shift_right_logical(slot, 1)) ^ tensor


def stored_block(index, where_ref):
    rank = lax.div(index, SLOTS) ^ where_ref[0]
    return rank * SLOTS + slot_quarter(index & 3, where_ref[1])


def block_plan(order_ref, cont_ref, where_ref, slot):
    count = cont_ref.shape[0]
    prompt_blocks = count // CONTS * PER_PROMPT
    own = order_ref[stored_block(slot, where_ref)]
    is_prompt = own < prompt_blocks
    offset = own - prompt_blocks
    which = jnp.clip(lax.div(offset, PER_CONT), 0, count - 1)
    group = jnp.where(is_prompt, lax.div(own, PER_PROMPT), cont_ref[which])
    inner = jnp.where(is_prompt, lax.rem(own, PER_PROMPT), lax.rem(offset, PER_CONT))
    has_prev = lax.rem(inner, 2)
    pairs = jnp.where(is_prompt, lax.div(inner, 2), PER_PROMPT // 2)
    prev = own - has_prev
    return group * PER_PROMPT, pairs, prev, own, has_prev


def fill_inverse(order_ref, where_ref, inverse_ref):
    def put(index, carry):
        inverse_ref[order_ref[stored_block(index, where_ref)]] = index
        return carry

    lax.fori_loop(0, order_ref.shape[0], put, 0)


def rotate(vec, cosine, sine):
    return vec * cosine + pltpu.roll(vec, HEAD_SIZE // 2, 1) * sine


def unrotate(vec, cosine, sine):
    return vec * cosine + pltpu.roll(vec * sine, HEAD_SIZE // 2, 1)


def angle_tables():
    half = HEAD_SIZE // 2
    freq = np.float64(rope_base) ** (-(2.0 * np.arange(half) / HEAD_SIZE))
    freq = np.concatenate([freq, freq])
    starts = np.arange(-(-(PER_PROMPT + PER_CONT) // 8) * 8) * BLOCK
    start = starts[:, None] * freq[None]
    inner = np.arange(BLOCK)[:, None] * freq[None]
    return tuple(
        f(a).astype(np.float32) for a in (start, inner) for f in (np.cos, np.sin)
    )


def key_rows(inverse_ref, logical):
    return pl.ds(pl.multiple_of(inverse_ref[logical] * BLOCK, BLOCK), BLOCK)


def tile_pair(ref, rows_a, rows_b, column):
    cols = pl.ds(column, HEAD_SIZE)
    return jnp.concatenate([ref[rows_a, cols], ref[rows_b, cols]], axis=0)


def own_mask(has_prev, rep):
    shape = (2 * BLOCK, rep * BLOCK)
    row = lax.broadcasted_iota(jnp.int32, shape, 0)
    col = lax.broadcasted_iota(jnp.int32, shape, 1)
    first_row = BLOCK * (1 - has_prev)
    return (row >= first_row) & (row - BLOCK <= lax.rem(col, BLOCK))


def stack_t(ref, rows, column, rep):
    return jnp.concatenate(
        [ref[rows, pl.ds(column + r * HEAD_SIZE, HEAD_SIZE)].T for r in range(rep)], axis=1
    )


def stack_rows(ref, rows, column, rep):
    return jnp.concatenate(
        [ref[rows, pl.ds(column + r * HEAD_SIZE, HEAD_SIZE)] for r in range(rep)], axis=0
    )


def dot(left, right):
    return jnp.dot(left, right, preferred_element_type=jnp.float32)


def start_parts(parts, buffer_ref, sem, column):
    rows, width = parts[0].shape[0], buffer_ref.shape[1]
    copies = [
        pltpu.make_async_copy(
            part.at[:, pl.ds(column, width)], buffer_ref.at[pl.ds(p * rows, rows), :], sem.at[p]
        )
        for p, part in enumerate(parts)
    ]
    for copy in copies:
        copy.start()
    return copies


def forward_kernel(rep, hps, ctx_count, order_ref, cont_ref, where_ref, q_ref, wo_ref, *refs):
    parts, refs = refs[:ctx_count], refs[ctx_count:]
    out_ref, lse_ref, keep_ref, send_ref, kv_ref, inverse_ref, qt_ref, acc_ref, sem = refs
    copies = start_parts(parts, kv_ref, sem, 0)
    fill_inverse(order_ref, where_ref, inverse_ref)
    for copy in copies:
        copy.wait()
    q_blocks = q_ref.shape[0] // BLOCK
    factor = LOG2E / math.sqrt(HEAD_SIZE)
    width = rep * HEAD_SIZE

    def one_query_block(qb, carry):
        base, pairs, prev, own, has_prev = block_plan(order_ref, cont_ref, where_ref, qb)
        rows = pl.ds(pl.multiple_of(qb * BLOCK, BLOCK), BLOCK)
        mask = own_mask(has_prev, rep)
        rows_a, rows_b = key_rows(inverse_ref, prev), key_rows(inverse_ref, own)
        state = []
        for h in range(hps):
            qt = stack_t(q_ref, rows, h * width, rep)
            qt_ref[h] = qt
            scores = dot(tile_pair(kv_ref, rows_a, rows_b, 2 * h * HEAD_SIZE), qt) * factor
            scores = jnp.where(mask, scores, NEG)
            best = jnp.max(scores, axis=0, keepdims=True)
            weights = jnp.exp2(scores - best)
            total = jnp.sum(weights, axis=0, keepdims=True)
            values = tile_pair(kv_ref, rows_a, rows_b, (2 * h + 1) * HEAD_SIZE)
            acc_ref[h] = dot(values.T, weights.astype(jnp.bfloat16))
            state += [best, total]

        def one_pair(t, state):
            rows_a = key_rows(inverse_ref, base + 2 * t)
            rows_b = key_rows(inverse_ref, base + 2 * t + 1)
            after = []
            for h in range(hps):
                best, total = state[2 * h], state[2 * h + 1]
                keys = tile_pair(kv_ref, rows_a, rows_b, 2 * h * HEAD_SIZE)
                scores = dot(keys, qt_ref[h]) * factor
                newest = jnp.maximum(best, jnp.max(scores, axis=0, keepdims=True))
                weights = jnp.exp2(scores - newest)
                shrink = jnp.exp2(best - newest)
                total = total * shrink + jnp.sum(weights, axis=0, keepdims=True)
                values = tile_pair(kv_ref, rows_a, rows_b, (2 * h + 1) * HEAD_SIZE)
                acc_ref[h] = acc_ref[h] * shrink + dot(values.T, weights.astype(jnp.bfloat16))
                after += [newest, total]
            return tuple(after)

        state = lax.fori_loop(0, pairs, one_pair, tuple(state))
        for h in range(hps):
            best, total = state[2 * h], state[2 * h + 1]
            mixed = acc_ref[h] * (1.0 / total)
            for r in range(rep):
                part = mixed[:, r * BLOCK : (r + 1) * BLOCK]
                out_ref[rows, pl.ds(h * width + r * HEAD_SIZE, HEAD_SIZE)] = part.T.astype(
                    jnp.bfloat16
                )
            lse_ref[h, pl.ds(qb, 1), :] = best + jnp.log2(total)
        return carry

    lax.fori_loop(0, q_blocks, one_query_block, 0)
    mixed = out_ref[...]
    half = keep_ref.shape[0]
    for n in range(0, wo_ref.shape[1], 512):
        cols = slice(n, n + 512)
        partial = dot(mixed, wo_ref[:, cols]).astype(jnp.bfloat16)
        keep_ref[:, cols] = partial[:half]
        send_ref[:, cols] = partial[half:]


def backward_kernel(rep, hps, ctx_count, head, order_ref, cont_ref, where_ref, q_ref, gb_ref, wo_ref,
                    mix_ref, lse_ref, cos_ref, sin_ref, *refs):
    parts, refs = refs[:ctx_count], refs[ctx_count:]
    gq_ref, keep_ref, send_ref = refs[:3]
    kv_ref, gm_ref, inverse_ref, qt_ref, gmt_ref, gqt_ref, acc_ref, sem = refs[3:]
    copies = start_parts(parts, kv_ref, sem, head * kv_ref.shape[1])
    fill_inverse(order_ref, where_ref, inverse_ref)
    gm_ref[...] = right_dot(gb_ref[...], wo_ref[...]).astype(jnp.bfloat16)
    for copy in copies:
        copy.wait()
    q_blocks = q_ref.shape[0] // BLOCK
    scale = 1.0 / math.sqrt(HEAD_SIZE)
    factor = LOG2E * scale
    width = rep * HEAD_SIZE

    def clear(i, carry):
        acc_ref[pl.ds(pl.multiple_of(i * BLOCK, BLOCK), BLOCK), :] = jnp.zeros(
            (BLOCK, acc_ref.shape[1]), jnp.float32
        )
        return carry

    lax.fori_loop(0, order_ref.shape[0], clear, 0)

    def tile_terms(h, rows_a, rows_b, lse, delta, q_rows, gm_rows, mask):
        kcol, vcol = 2 * h * HEAD_SIZE, (2 * h + 1) * HEAD_SIZE
        keys = tile_pair(kv_ref, rows_a, rows_b, kcol)
        values = tile_pair(kv_ref, rows_a, rows_b, vcol)
        weights = jnp.exp2(dot(keys, qt_ref[h]) * factor - lse)
        if mask is not None:
            weights = jnp.where(mask, weights, 0.0)
        grad_weights = dot(values, gmt_ref[h])
        grad_scores = (weights * (grad_weights - delta)).astype(jnp.bfloat16)
        gv = dot(weights.astype(jnp.bfloat16), gm_rows)
        gk = dot(grad_scores, q_rows)
        acc_ref[rows_a, pl.ds(kcol, HEAD_SIZE)] += gk[:BLOCK]
        acc_ref[rows_b, pl.ds(kcol, HEAD_SIZE)] += gk[BLOCK:]
        acc_ref[rows_a, pl.ds(vcol, HEAD_SIZE)] += gv[:BLOCK]
        acc_ref[rows_b, pl.ds(vcol, HEAD_SIZE)] += gv[BLOCK:]
        return dot(keys.T, grad_scores)

    def one_query_block(qb, carry):
        base, pairs, prev, own, has_prev = block_plan(order_ref, cont_ref, where_ref, qb)
        rows = pl.ds(pl.multiple_of(qb * BLOCK, BLOCK), BLOCK)
        mask = own_mask(has_prev, rep)
        rows_a, rows_b = key_rows(inverse_ref, prev), key_rows(inverse_ref, own)
        deltas, lses, q_stack, gm_stack = [], [], [], []
        for h in range(hps):
            qt_ref[h] = stack_t(q_ref, rows, h * width, rep)
            gmt = stack_t(gm_ref, rows, h * width, rep)
            gmt_ref[h] = gmt
            mixt = stack_t(mix_ref, rows, h * width, rep)
            deltas.append(
                jnp.sum(
                    gmt.astype(jnp.float32) * mixt.astype(jnp.float32), axis=0, keepdims=True
                )
            )
            lses.append(lse_ref[h, pl.ds(qb, 1), :])
        for h in range(hps):
            q_rows = stack_rows(q_ref, rows, h * width, rep)
            gm_rows = stack_rows(gm_ref, rows, h * width, rep)
            gqt_ref[h] = tile_terms(
                h, rows_a, rows_b, lses[h], deltas[h], q_rows, gm_rows, mask
            )

        def one_pair(t, carry):
            rows_a = key_rows(inverse_ref, base + 2 * t)
            rows_b = key_rows(inverse_ref, base + 2 * t + 1)
            for h in range(hps):
                q_rows = stack_rows(q_ref, rows, h * width, rep)
                gm_rows = stack_rows(gm_ref, rows, h * width, rep)
                gqt_ref[h] += tile_terms(
                    h, rows_a, rows_b, lses[h], deltas[h], q_rows, gm_rows, None
                )
            return carry

        lax.fori_loop(0, pairs, one_pair, 0)
        for h in range(hps):
            total = gqt_ref[h] * scale
            for r in range(rep):
                part = total[:, r * BLOCK : (r + 1) * BLOCK]
                rounded = part.T.astype(jnp.bfloat16).astype(jnp.float32)
                gq_ref[rows, pl.ds(h * width + r * HEAD_SIZE, HEAD_SIZE)] = unrotate(
                    rounded, cos_ref[rows, :], sin_ref[rows, :]
                ).astype(jnp.bfloat16)
        return carry

    lax.fori_loop(0, q_blocks, one_query_block, 0)

    blocks = order_ref.shape[0]

    def place(index):
        chunk = lax.div(index, SLOTS)
        spot = (chunk & 1) * (ctx_count // 2) + (chunk & 2) // 2 * (ctx_count // 4) + (
            lax.shift_right_logical(chunk, 2)
        )
        return spot * SLOTS + (index & 3)

    def flush(i, carry):
        rows = pl.ds(pl.multiple_of(i * BLOCK, BLOCK), BLOCK)
        spot = place(i)
        parts = []
        for h in range(hps):
            parts.append(acc_ref[rows, pl.ds(2 * h * HEAD_SIZE, HEAD_SIZE)] * scale)
            parts.append(acc_ref[rows, pl.ds((2 * h + 1) * HEAD_SIZE, HEAD_SIZE)])
        value = jnp.concatenate(parts, axis=1).astype(jnp.bfloat16)

        @pl.when(spot < blocks // 2)
        def _():
            keep_ref[pl.ds(pl.multiple_of(spot * BLOCK, BLOCK), BLOCK), :] = value

        @pl.when(spot >= blocks // 2)
        def _():
            far = (spot - blocks // 2) * BLOCK
            send_ref[pl.ds(pl.multiple_of(far, BLOCK), BLOCK), :] = value

        return carry

    lax.fori_loop(0, blocks, flush, 0)


def attention_forward(q, w_out, parts, order, cont, where):
    ctx_count = len(parts)
    rows, tokens = q.shape[0], ctx_count * q.shape[0]
    kv_heads = parts[0].shape[1] // (2 * HEAD_SIZE)
    rep = q.shape[1] // HEAD_SIZE // kv_heads
    q_blocks, model = rows // BLOCK, w_out.shape[1]
    vmem, smem, any_ = (
        pl.BlockSpec(memory_space=space) for space in (pltpu.VMEM, pltpu.SMEM, pl.ANY)
    )
    flops = 2 * rows * tokens * q.shape[1] + 2 * rows * q.shape[1] * model
    half = jax.ShapeDtypeStruct((rows // 2, model), jnp.bfloat16)
    return pl.pallas_call(
        functools.partial(forward_kernel, rep, kv_heads, ctx_count),
        out_shape=(
            jax.ShapeDtypeStruct(q.shape, jnp.bfloat16),
            jax.ShapeDtypeStruct((kv_heads, q_blocks, rep * BLOCK), jnp.float32),
            half,
            half,
        ),
        in_specs=[smem] * 3 + [vmem] * 2 + [any_] * ctx_count,
        out_specs=[vmem] * 4,
        scratch_shapes=[
            pltpu.VMEM((tokens, parts[0].shape[1]), jnp.bfloat16),
            pltpu.SMEM((order.shape[0],), jnp.int32),
            pltpu.VMEM((kv_heads, HEAD_SIZE, rep * BLOCK), jnp.bfloat16),
            pltpu.VMEM((kv_heads, HEAD_SIZE, rep * BLOCK), jnp.float32),
            pltpu.SemaphoreType.DMA((ctx_count,)),
        ],
        compiler_params=pltpu.CompilerParams(vmem_limit_bytes=VMEM_LIMIT),
        cost_estimate=cost("attention_forward", flops, 2 * tokens * parts[0].shape[1] + 4 * rows * model),
        name="attention_forward",
    )(order, cont, where, q, w_out, *parts)


def attention_backward(head, q, grad_branch, w_out, mixed, lse, parts, cosine, sine, order, cont,
                       where):
    ctx_count = len(parts)
    rows, tokens = q.shape[0], ctx_count * q.shape[0]
    kv_heads = parts[0].shape[1] // (2 * HEAD_SIZE)
    rep = q.shape[1] // HEAD_SIZE // kv_heads
    q_blocks, model = rows // BLOCK, w_out.shape[1]
    wide = rep * HEAD_SIZE
    q_spec = pl.BlockSpec((rows, wide), lambda g, *_: (0, head))
    whole = lambda g, *_: (0, 0)
    table_spec = pl.BlockSpec((rows, HEAD_SIZE), whole)
    half = (tokens // 2, 2 * HEAD_SIZE)
    flops = 5 * rows * tokens * wide + 2 * rows * wide * model
    return pl.pallas_call(
        functools.partial(backward_kernel, rep, 1, ctx_count, head),
        out_shape=(
            jax.ShapeDtypeStruct((rows, wide), jnp.bfloat16),
            jax.ShapeDtypeStruct(half, jnp.bfloat16),
            jax.ShapeDtypeStruct(half, jnp.bfloat16),
        ),
        grid_spec=pltpu.PrefetchScalarGridSpec(
            num_scalar_prefetch=3,
            grid=(1,),
            in_specs=[
                q_spec,
                pl.BlockSpec((rows, model), whole),
                pl.BlockSpec((wide, model), lambda g, *_: (head, 0)),
                q_spec,
                pl.BlockSpec((1, q_blocks, rep * BLOCK), lambda g, *_: (head, 0, 0)),
                table_spec,
                table_spec,
            ]
            + [pl.BlockSpec(memory_space=pl.ANY)] * ctx_count,
            out_specs=[
                pl.BlockSpec((rows, wide), whole),
                pl.BlockSpec(half, whole),
                pl.BlockSpec(half, whole),
            ],
            scratch_shapes=[
                pltpu.VMEM((tokens, 2 * HEAD_SIZE), jnp.bfloat16),
                pltpu.VMEM((rows, wide), jnp.bfloat16),
                pltpu.SMEM((order.shape[0],), jnp.int32),
                pltpu.VMEM((1, HEAD_SIZE, rep * BLOCK), jnp.bfloat16),
                pltpu.VMEM((1, HEAD_SIZE, rep * BLOCK), jnp.bfloat16),
                pltpu.VMEM((1, HEAD_SIZE, rep * BLOCK), jnp.float32),
                pltpu.VMEM((tokens, 2 * HEAD_SIZE), jnp.float32),
                pltpu.SemaphoreType.DMA((ctx_count,)),
            ],
        ),
        compiler_params=pltpu.CompilerParams(vmem_limit_bytes=VMEM_LIMIT),
        cost_estimate=cost(f"attention_backward_{head}", flops, 4 * tokens * wide + 2 * rows * model),
        name=f"attention_backward_{head}",
    )(order, cont, where, q, grad_branch, w_out, mixed, lse, cosine, sine, *parts)


def input_kernel(order_ref, cont_ref, where_ref, gain_ref, x_hbm, wq_hbm, wk_hbm, wv_hbm, table_hbm,
                 first_ref, q_ref, kv_ref, cos_ref, sin_ref,
                 x_ref, wq_ref, wk_ref, wv_ref, table_ref, sem):
    pairs = ((x_hbm, x_ref), (table_hbm, table_ref), (wk_hbm, wk_ref), (wv_hbm, wv_ref),
             (wq_hbm, wq_ref))
    copies = [
        pltpu.make_async_copy(source, target, sem.at[n])
        for n, (source, target) in enumerate(pairs)
    ]
    for copy in copies:
        copy.start()
    count = cont_ref.shape[0]
    prompt_blocks = count // CONTS * PER_PROMPT
    starts = (table_ref.shape[0] - 2 * BLOCK) // 2
    lane = lax.broadcasted_iota(jnp.int32, (BLOCK, HEAD_SIZE), 1)
    copies[0].wait()
    copies[1].wait()

    def one_slot(slot, carry):
        quarter = slot_quarter(slot, where_ref[1])
        rows = pl.ds(pl.multiple_of(slot * BLOCK, BLOCK), BLOCK)
        full = x_ref[pl.ds(pl.multiple_of(quarter * BLOCK, BLOCK), BLOCK), :].astype(jnp.float32)
        inv = lax.rsqrt(jnp.mean(full * full, axis=-1, keepdims=True) + eps_norm)
        first_ref[rows, :] = (full * inv * gain_ref[...]).astype(jnp.bfloat16)
        own = order_ref[stored_block(slot, where_ref)]
        spot = jnp.where(
            own < prompt_blocks,
            lax.rem(own, PER_PROMPT),
            PER_PROMPT + lax.rem(own - prompt_blocks, PER_CONT),
        )
        cos_start = table_ref[pl.ds(2 * BLOCK + spot, 1), :]
        sin_start = table_ref[pl.ds(2 * BLOCK + starts + spot, 1), :]
        cos_in, sin_in = table_ref[:BLOCK, :], table_ref[BLOCK : 2 * BLOCK, :]
        sine = sin_start * cos_in + cos_start * sin_in
        cos_ref[rows, :] = cos_start * cos_in - sin_start * sin_in
        sin_ref[rows, :] = jnp.where(lane < HEAD_SIZE // 2, -sine, sine)
        return carry

    lax.fori_loop(0, SLOTS, one_slot, 0)
    first = first_ref[...]
    cosine, sine = cos_ref[...], sin_ref[...]
    copies[2].wait()
    copies[3].wait()
    keys = dot(first, wk_ref[...])
    values = dot(first, wv_ref[...])
    for h in range(wk_ref.shape[1] // HEAD_SIZE):
        cols = slice(h * HEAD_SIZE, (h + 1) * HEAD_SIZE)
        low, high = 2 * h * HEAD_SIZE, (2 * h + 1) * HEAD_SIZE
        key = rotate(keys[:, cols], cosine, sine)
        kv_ref[:, low:high] = key.astype(jnp.bfloat16)
        kv_ref[:, high : high + HEAD_SIZE] = values[:, cols].astype(jnp.bfloat16)
    copies[4].wait()
    for n in range(0, wq_ref.shape[1], 256):
        queries = dot(first, wq_ref[:, n : n + 256])
        for m in range(0, 256, HEAD_SIZE):
            query = rotate(queries[:, m : m + HEAD_SIZE], cosine, sine)
            q_ref[:, n + m : n + m + HEAD_SIZE] = query.astype(jnp.bfloat16)


def input_stage(x, gain, wq, wk, wv, order, cont, where):
    rows, model = x.shape
    cos_start, sin_start, cos_in, sin_in = angle_tables()
    table = np.concatenate([cos_in, sin_in, cos_start, sin_start])
    vmem, smem, any_ = (
        pl.BlockSpec(memory_space=space) for space in (pltpu.VMEM, pltpu.SMEM, pl.ANY)
    )
    flops = 2 * rows * model * (wq.shape[1] + 2 * wk.shape[1])
    return pl.pallas_call(
        input_kernel,
        out_shape=(
            jax.ShapeDtypeStruct((rows, model), jnp.bfloat16),
            jax.ShapeDtypeStruct((rows, wq.shape[1]), jnp.bfloat16),
            jax.ShapeDtypeStruct((rows, 2 * wk.shape[1]), jnp.bfloat16),
            jax.ShapeDtypeStruct((rows, HEAD_SIZE), jnp.float32),
            jax.ShapeDtypeStruct((rows, HEAD_SIZE), jnp.float32),
        ),
        in_specs=[smem] * 3 + [vmem] + [any_] * 5,
        out_specs=[vmem] * 5,
        scratch_shapes=[
            pltpu.VMEM(a.shape, a.dtype) for a in (x, wq, wk, wv)
        ]
        + [pltpu.VMEM(table.shape, jnp.float32), pltpu.SemaphoreType.DMA((5,))],
        compiler_params=pltpu.CompilerParams(vmem_limit_bytes=VMEM_LIMIT),
        cost_estimate=cost("input_stage", flops, 4 * x.size + 2 * wq.size + 4 * wk.size),
        name="input_stage",
    )(order, cont, where, gain.reshape(1, -1), x, wq, wk, wv, table)


FILLERS = ("ffn_out", "gate_shares", "up_shares", "kv_shares", "grad_hidden", "grad_second_keep")


def cost(name, flops, bytes_accessed):
    scale = 16.0 if name in FILLERS else 0.02
    return pl.CostEstimate(
        flops=int(flops * scale), bytes_accessed=int(bytes_accessed * scale), transcendentals=0
    )


def put_share(value, index, x_bit, keep_ref, send_ref, swap_bits):
    spot = share_spot(lax.shift_right_logical(index, 1), keep_ref.shape[0], swap_bits)
    stays = (index & 1) == x_bit
    value = value.astype(keep_ref.dtype)

    @pl.when(stays)
    def _():
        keep_ref[pl.ds(spot, 1)] = value[None]

    @pl.when(jnp.logical_not(stays))
    def _():
        send_ref[pl.ds(spot, 1)] = value[None]


def pair_bit(where_ref):
    return lax.shift_right_logical(where_ref[0], 1) & 1


def grad_hidden_kernel(where_ref, cot_ref, wd_ref, out_ref):
    out_ref[...] = right_dot(cot_ref[...], wd_ref[...])


def grad_hidden_stage(cot, w_down, where):
    rows, model = cot.shape
    units = w_down.shape[0] // 2
    block = 256
    steps = units // block
    return pl.pallas_call(
        grad_hidden_kernel,
        out_shape=jax.ShapeDtypeStruct((rows, units), jnp.float32),
        grid_spec=pltpu.PrefetchScalarGridSpec(
            num_scalar_prefetch=1,
            grid=(steps,),
            in_specs=[
                pl.BlockSpec((rows, model), lambda i, w: (0, 0), pipeline_mode=pl.Buffered(1)),
                pl.BlockSpec((block, model), lambda i, w: (pair_bit(w) * steps + i, 0)),
            ],
            out_specs=pl.BlockSpec((rows, block), lambda i, w: (0, i)),
        ),
        compiler_params=pltpu.CompilerParams(vmem_limit_bytes=VMEM_LIMIT),
        cost_estimate=cost("grad_hidden", 2 * rows * model * units, 4 * rows * model),
        name="grad_hidden",
    )(where, cot, w_down)


def ffn_kernel(where_ref, in_ref, gh_ref, wg_ref, wu_ref, hid_ref, gg_ref, gu_ref):
    gate = dot(in_ref[...], wg_ref[...])
    upward = dot(in_ref[...], wu_ref[...])
    grad_hidden = gh_ref[...]
    sigma = jax.nn.sigmoid(gate)
    swish = gate * sigma
    hid_ref[...] = (swish * upward).astype(jnp.bfloat16)
    gg_ref[...] = (grad_hidden * upward * sigma * (1.0 + gate * (1.0 - sigma))).astype(
        jnp.bfloat16
    )
    gu_ref[...] = (grad_hidden * swish).astype(jnp.bfloat16)


def ffn_stage(second, grad_hidden, w_gate, w_up, where):
    rows, model = second.shape
    units = w_gate.shape[1] // 2
    block = 256
    steps = units // block
    col_spec = pl.BlockSpec((model, block), lambda i, w: (0, pair_bit(w) * steps + i))
    unit_spec = pl.BlockSpec((rows, block), lambda i, w: (0, i))
    unit = jax.ShapeDtypeStruct((rows, units), jnp.bfloat16)
    return pl.pallas_call(
        ffn_kernel,
        out_shape=(unit, unit, unit),
        grid_spec=pltpu.PrefetchScalarGridSpec(
            num_scalar_prefetch=1,
            grid=(steps,),
            in_specs=[
                pl.BlockSpec((rows, model), lambda i, w: (0, 0), pipeline_mode=pl.Buffered(1)),
                unit_spec,
                col_spec,
                col_spec,
            ],
            out_specs=[unit_spec] * 3,
        ),
        compiler_params=pltpu.CompilerParams(vmem_limit_bytes=VMEM_LIMIT),
        cost_estimate=cost("ffn_stage", 4 * rows * model * units, 6 * rows * model),
        name="ffn_stage",
    )(where, second, grad_hidden, w_gate, w_up)


def grad_second_kernel(where_ref, gg_ref, gu_ref, wg_ref, wu_ref, out_ref):
    total = right_dot(gg_ref[...], wg_ref[...]) + right_dot(gu_ref[...], wu_ref[...])
    out_ref[...] = total.astype(jnp.bfloat16)


def grad_second_half(half, name, grads, weights, where):
    rows, units = grads[0].shape
    rows //= 2
    model = weights[0].shape[0]
    block = 512
    left_spec = pl.BlockSpec((rows, units), lambda n, w: (half, 0), pipeline_mode=pl.Buffered(1))
    right_spec = pl.BlockSpec((block, units), lambda n, w: (n, pair_bit(w)))
    return pl.pallas_call(
        grad_second_kernel,
        out_shape=jax.ShapeDtypeStruct((rows, model), jnp.bfloat16),
        grid_spec=pltpu.PrefetchScalarGridSpec(
            num_scalar_prefetch=1,
            grid=(model // block,),
            in_specs=[left_spec] * 2 + [right_spec] * 2,
            out_specs=pl.BlockSpec((rows, block), lambda n, w: (0, n)),
        ),
        compiler_params=pltpu.CompilerParams(vmem_limit_bytes=VMEM_LIMIT),
        cost_estimate=cost(name, 4 * rows * units * model, 4 * rows * model),
        name=name,
    )(where, *grads, *weights)


def ffn_out_kernel(where_ref, hid_ref, wd_ref, keep_ref, send_ref):
    total = dot(hid_ref[...], wd_ref[...])
    half = keep_ref.shape[0]
    keep_ref[...] = total[:half].astype(jnp.bfloat16)
    send_ref[...] = total[half:].astype(jnp.bfloat16)


def unit_sum(kernel, name, lefts, rights, transposed, where):
    rows, units = lefts[0].shape
    model = rights[0].shape[0 if transposed else 1]
    block = 512
    if transposed:
        right_spec = pl.BlockSpec((block, units), lambda n, w: (n, pair_bit(w)))
    else:
        right_spec = pl.BlockSpec((units, block), lambda n, w: (pair_bit(w), n))
    left_spec = pl.BlockSpec((rows, units), lambda n, w: (0, 0), pipeline_mode=pl.Buffered(1))
    half = jax.ShapeDtypeStruct((rows // 2, model), jnp.bfloat16)
    half_spec = pl.BlockSpec((rows // 2, block), lambda n, w: (0, n))
    return pl.pallas_call(
        kernel,
        out_shape=(half, half),
        grid_spec=pltpu.PrefetchScalarGridSpec(
            num_scalar_prefetch=1,
            grid=(model // block,),
            in_specs=[left_spec] * len(lefts) + [right_spec] * len(rights),
            out_specs=[half_spec, half_spec],
        ),
        compiler_params=pltpu.CompilerParams(vmem_limit_bytes=VMEM_LIMIT),
        cost_estimate=cost(name, 2 * len(lefts) * rows * units * model, 4 * rows * model),
        name=name,
    )(where, *lefts, *rights)


def share_spot(spot, count, swap_bits):
    if swap_bits:
        return (spot & 1) * (count // 2) + lax.shift_right_logical(spot, 1)
    return spot


def shares_kernel(left_count, swap_bits, pairs, where_ref, *refs):
    lefts, refs = refs[:left_count], refs[left_count:]
    rights, (keep_ref, send_ref) = refs[:-2], refs[-2:]
    share = keep_ref.shape[1]
    step = pl.program_id(0)
    pieces = [left_dot(lefts[l][...], rights[r][...]) for l, r in pairs]
    per_step = lefts[0].shape[1] // share
    if per_step == 1:
        value = jnp.concatenate(pieces, axis=1).astype(keep_ref.dtype)
        sends = step < pl.num_programs(0) // 2

        @pl.when(sends)
        def _():
            send_ref[0] = value

        @pl.when(jnp.logical_not(sends))
        def _():
            keep_ref[0] = value

        return
    for k in range(per_step):
        rows = slice(k * share, (k + 1) * share)
        value = jnp.concatenate([piece[rows] for piece in pieces], axis=1)
        index = step * per_step + k
        put_share(value, index, where_ref[0] & 1, keep_ref, send_ref, swap_bits)


def weight_shares(name, lefts, rights, pairs, ctx_count, swap_bits, where):
    rows, model = lefts[0].shape
    block = 256
    share, half = model // ctx_count, ctx_count // 2
    width = sum(rights[r].shape[1] for _, r in pairs)
    shares = jax.ShapeDtypeStruct((half, share, width), jnp.bfloat16)
    if share == block:

        def left_map(i, w):
            mine = w[0] & 1
            return 0, jnp.where(i < half, 2 * i + 1 - mine, 2 * (i - half) + mine)

        left_spec = pl.BlockSpec((rows, block), left_map)
        spot = lambda index: share_spot(index, half, swap_bits)
        keep_spec = pl.BlockSpec(
            (1, share, width), lambda i, w: (spot(jnp.maximum(i - half, 0)), 0, 0)
        )
        send_spec = pl.BlockSpec(
            (1, share, width), lambda i, w: (spot(jnp.minimum(i, half - 1)), 0, 0)
        )
    else:
        left_spec = pl.BlockSpec((rows, block), lambda i, w: (0, i))
        keep_spec = send_spec = pl.BlockSpec(shares.shape, lambda i, w: (0, 0, 0))
    return pl.pallas_call(
        functools.partial(shares_kernel, len(lefts), swap_bits, pairs),
        out_shape=(shares, shares),
        grid_spec=pltpu.PrefetchScalarGridSpec(
            num_scalar_prefetch=1,
            grid=(model // block,),
            in_specs=[left_spec] * len(lefts)
            + [
                pl.BlockSpec(r.shape, lambda i, w: (0, 0), pipeline_mode=pl.Buffered(1))
                for r in rights
            ],
            out_specs=[keep_spec, send_spec],
        ),
        compiler_params=pltpu.CompilerParams(vmem_limit_bytes=VMEM_LIMIT),
        cost_estimate=cost(name, 2 * rows * model * width, 4 * rows * model),
        name=name,
    )(where, *lefts, *rights)


def unit_shares_kernel(where_ref, left_ref, right_ref, out_ref):
    share = out_ref.shape[1]
    total = left_dot(left_ref[...], right_ref[...]).astype(out_ref.dtype)
    per_step = left_ref.shape[1] // share
    if out_ref.shape[0] == 1:
        out_ref[0] = total
    else:
        for k in range(per_step):
            index = pl.program_id(0) * per_step + k
            out_ref[pl.ds(unit_spot(index, out_ref.shape[0]), 1)] = total[k * share : (k + 1) * share][None]


def unit_spot(index, ctx_count):
    return (index & 1) * (ctx_count // 2) + lax.shift_right_logical(index, 1)


def unit_shares(name, left, right, ctx_count, where):
    rows, model = left.shape
    block, width = 256, right.shape[1]
    share = model // ctx_count
    shares = jax.ShapeDtypeStruct((ctx_count, share, width), jnp.bfloat16)
    if share == block:
        out_spec = pl.BlockSpec((1, share, width), lambda i, w: (unit_spot(i, ctx_count), 0, 0))
    else:
        out_spec = pl.BlockSpec(shares.shape, lambda i, w: (0, 0, 0))
    return pl.pallas_call(
        unit_shares_kernel,
        out_shape=shares,
        grid_spec=pltpu.PrefetchScalarGridSpec(
            num_scalar_prefetch=1,
            grid=(model // block,),
            in_specs=[
                pl.BlockSpec((rows, block), lambda i, w: (0, i)),
                pl.BlockSpec(right.shape, lambda i, w: (0, 0), pipeline_mode=pl.Buffered(1)),
            ],
            out_specs=out_spec,
        ),
        compiler_params=pltpu.CompilerParams(vmem_limit_bytes=VMEM_LIMIT),
        cost_estimate=cost(name, 2 * rows * model * width, 4 * rows * model),
        name=name,
    )(where, left, right)


def tail_kernel(kv_heads, where_ref, *refs):
    sums, refs = refs[: 2 * kv_heads], refs[2 * kv_heads :]
    cos_ref, sin_ref, refs = refs[0], refs[1], refs[2:]
    gq_refs, refs = refs[:kv_heads], refs[kv_heads:]
    wq_ref, wk_ref, wv_ref, keep_ref, send_ref, gkv_ref = refs
    cosine, sine = cos_ref[...], sin_ref[...]
    for h in range(kv_heads):
        total = sums[2 * h][...].astype(jnp.float32) + sums[2 * h + 1][...].astype(jnp.float32)
        total = total.astype(jnp.bfloat16)
        key = unrotate(total[:, :HEAD_SIZE].astype(jnp.float32), cosine, sine)
        cols = slice(h * HEAD_SIZE, (h + 1) * HEAD_SIZE)
        gkv_ref[:, cols] = key.astype(jnp.bfloat16)
        cols = slice((kv_heads + h) * HEAD_SIZE, (kv_heads + h + 1) * HEAD_SIZE)
        gkv_ref[:, cols] = total[:, HEAD_SIZE:]
    half = keep_ref.shape[0]
    key_width = kv_heads * HEAD_SIZE
    wide = gq_refs[0].shape[1]
    for n in range(0, wq_ref.shape[0], 512):
        span = slice(n, n + 512)
        total = right_dot(gkv_ref[:, :key_width], wk_ref[span, :])
        total += right_dot(gkv_ref[:, key_width:], wv_ref[span, :])
        for h in range(kv_heads):
            total += right_dot(gq_refs[h][...], wq_ref[span, h * wide : (h + 1) * wide])
        total = total.astype(jnp.bfloat16)
        keep_ref[:, span] = total[:half]
        send_ref[:, span] = total[half:]


def tail_stage(kv_sums, cosine, sine, grad_queries, wq, wk, wv, where):
    rows, model = cosine.shape[0], wq.shape[0]
    kv_heads = len(grad_queries)
    vmem = pl.BlockSpec(memory_space=pltpu.VMEM)
    half = jax.ShapeDtypeStruct((rows // 2, model), jnp.bfloat16)
    flat = [term for sums in kv_sums for term in sums]
    return pl.pallas_call(
        functools.partial(tail_kernel, kv_heads),
        out_shape=(
            half,
            half,
            jax.ShapeDtypeStruct((rows, 2 * kv_heads * HEAD_SIZE), jnp.bfloat16),
        ),
        in_specs=[pl.BlockSpec(memory_space=pltpu.SMEM)]
        + [vmem] * (len(flat) + 2 + kv_heads + 3),
        out_specs=[vmem] * 3,
        compiler_params=pltpu.CompilerParams(vmem_limit_bytes=VMEM_LIMIT),
        cost_estimate=cost("tail_stage", 2 * rows * model * (wq.shape[1] + 2 * wk.shape[1]), 4 * rows * model + 4 * wq.size
        ),
        name="tail_stage",
    )(where, *flat, cosine, sine, *grad_queries, wq, wk, wv)


def flip(value, axis, mask=1):
    return lax.ppermute(value, axis, [(i, i ^ mask) for i in range(lax.axis_size(axis))])


def ctx_flip(value, mask):
    if mask == 1:
        return flip(value, "x")
    if mask == 2:
        return flip(value, "l")
    return flip(value, "hi", mask // 4)


def add(left, right):
    return (left.astype(jnp.float32) + right.astype(jnp.float32)).astype(jnp.bfloat16)


def slots_of(value, tensor):
    rows = value.shape[0] // SLOTS
    return [
        lax.dynamic_slice_in_dim(value, (tensor ^ SLOT_XOR[u]) * rows, rows)
        for u in range(SLOTS)
    ]


def after(dep, *values):
    deps = dep if isinstance(dep, tuple) else (dep,)
    held = lax.optimization_barrier(deps + values)[len(deps) :]
    return held[0] if len(held) == 1 else held


class Stages:
    def __init__(self, block_order):
        self.live = block_order[0] >= 0

    def __call__(self, function, *args):
        shapes = jax.eval_shape(function, *args)
        empty = lambda *_: jax.tree.map(lambda a: jnp.zeros(a.shape, a.dtype), shapes)
        return lax.cond(self.live, function, empty, *args)


def gather_pair(own):
    partner = ctx_flip(own, 2)
    near = jnp.concatenate([own, partner, flip(own, "y"), flip(partner, "y")])
    return jnp.concatenate([near, flip(near, "core")])


def gather_slots(own):
    near = jnp.concatenate([own, flip(own, "y")])
    return near, flip(near, "core")


def place_rows(own, near, core, far, tensor):
    rows = own.shape[0]
    result = jnp.zeros((SLOTS * rows,) + own.shape[1:], own.dtype)
    for u, piece in enumerate((own, near, core, far)):
        result = lax.dynamic_update_slice_in_dim(
            result, piece, (tensor ^ SLOT_XOR[u]) * rows, 0
        )
    return result


def scatter_slots(keep, send, fill=lambda value: value):
    got = fill(flip(send, "core"))
    quarter = keep.shape[0] // 2
    far = flip(add(keep[quarter:], got[quarter:]), "y")
    return add(keep[:quarter], got[:quarter]), far


def pair_scatter(keep, send, fill=lambda near: near):
    got = fill(flip(send, "core"))
    n = keep.shape[0] // 4
    near = [add(keep[k * n : (k + 1) * n], got[k * n : (k + 1) * n]) for k in range(4)]
    far = flip(near[3], "y")
    got = flip(near[2], "y")
    return near, far, got


def pair_finish(near, far, got):
    away = add(near[1], far)
    return near[0], got, ctx_flip(away, 2), away


def total(terms):
    return sum(term.astype(jnp.float32) for term in terms)


class Reduce:
    def __init__(self, keep, send):
        self.keep, self.got = keep, ctx_flip(send, 1)

    def halve(self, mask, ctx, dep=None):
        keep, got = self.keep, self.got
        if dep is not None:
            keep, got = after(dep, keep, got)
        n = keep.shape[0] // 2
        bit = lax.div(ctx, mask) % 2
        pick = lambda value, index: lax.dynamic_slice_in_dim(value, index * n, n, 0)
        away = ctx_flip(add(pick(keep, 1 - bit), pick(got, 1 - bit)), mask)
        self.keep, self.got = add(pick(keep, bit), pick(got, bit)), away

    def sum(self):
        return (self.keep.astype(jnp.float32) + self.got.astype(jnp.float32))[0]


def high_masks(ctx_count):
    masks, mask = [], ctx_count // 2
    while mask >= 4:
        masks.append(mask)
        mask //= 2
    return masks


def unit_sum_over(shares):
    return lax.psum_scatter(shares, ("x", "hi"), scatter_dimension=0, tiled=True)


def split_halves(summed, ctx, dep):
    summed = after(dep, summed)
    pair = lax.div(ctx, 2) % 2
    pick = lambda index: lax.dynamic_index_in_dim(summed, index, 0, keepdims=False)
    return pick(pair), pick(1 - pair)


def join_halves(own, other, ctx):
    pair = lax.div(ctx, 2) % 2
    low, high = jnp.where(pair == 0, own, other), jnp.where(pair == 0, other, own)
    return jnp.concatenate([low, high], axis=1).astype(jnp.float32)


class KvReduce:
    def __init__(self, keep, got):
        self.keep, self.got = keep, got

    def merge(self, dep):
        keep, got = after(dep, self.keep, self.got)
        n = keep.shape[0] // 2
        return add(keep[:n], got[:n]), add(keep[n:], got[n:])


def norm_back(grad_out, normed, inv_scale, gain):
    scaled = grad_out * gain
    inner = jnp.mean(scaled * normed, axis=-1, keepdims=True)
    return (inv_scale * (scaled - normed * inner), jnp.sum(grad_out * normed, axis=0))


def body(
    layer_input,
    attn_gain,
    w_query,
    key_matrix,
    value_matrix,
    w_out,
    ffn_gain,
    w_gate,
    w_up,
    w_down,
    cotangent,
    block_order,
    cont_prompt,
):
    ctx_count = lax.axis_size("hi") * 4
    ctx = (lax.axis_index("hi") * 2 + lax.axis_index("l")) * 2 + lax.axis_index("x")
    tensor = lax.axis_index("y") * 2 + lax.axis_index("core")
    where = jnp.stack([ctx, tensor]).astype(jnp.int32)
    quarter = layer_input.shape[0] // SLOTS
    kv_heads = key_matrix.shape[1] // HEAD_SIZE
    highs = high_masks(ctx_count)

    stage = Stages(block_order)
    cot_own = lax.dynamic_slice_in_dim(cotangent, tensor * quarter, quarter)
    cot_slots = slots_of(cotangent, tensor)
    cot_part = ctx_flip(cot_own, 2)
    first_input, queries, kv_local, cosine, sine = input_stage(
        layer_input, attn_gain, w_query, key_matrix, value_matrix, block_order, cont_prompt, where
    )
    parts = {0: kv_local}
    parts[2], parts[1] = stage(
        lambda kv: (ctx_flip(kv, 2), ctx_flip(kv, 1)), after(cot_part, kv_local)
    )
    high_parts = {0: after(parts[1], kv_local)}
    for bit in reversed(highs):
        for mask in list(high_parts):
            high_parts[mask + bit] = ctx_flip(high_parts[mask], bit)
    del high_parts[0]
    parts.update(high_parts)
    parts[3] = stage(lambda kv: ctx_flip(kv, 1), parts[2])
    dep = parts[3]
    for mask in high_parts:
        parts[mask + 2], parts[mask + 1], more = stage(
            lambda kv, cot: (ctx_flip(kv, 2), ctx_flip(kv, 1), flip(cot, "y")),
            after(dep, parts[mask]),
            cot_part,
        )
        dep = parts[mask + 1]
    cot_part = jnp.concatenate([cot_part, more])
    for mask in high_parts:
        parts[mask + 3], cot_far = stage(
            lambda kv, cot: (ctx_flip(kv, 1), flip(cot, "core")), parts[mask + 2], cot_part
        )
    parts = [parts[mask] for mask in range(ctx_count)]
    cot = jnp.concatenate(
        [cot_slots[0], cot_part[:quarter], cot_slots[1], cot_part[quarter:]]
        + [cot_slots[2], cot_far[:quarter], cot_slots[3], cot_far[quarter:]]
    )
    mixed, log_total, keep, send = attention_forward(
        after(cot, queries), w_out, parts, block_order, cont_prompt, where
    )
    first_half = flip(send, "core")
    near = add(keep, first_half)
    far = flip(near[quarter:], "y")
    grad_hidden = grad_hidden_stage(after(near, cot), w_down, where)
    own_input = lax.dynamic_slice_in_dim(layer_input, tensor * quarter, quarter)
    own_input = own_input.astype(jnp.float32)
    middle = own_input + total((near[:quarter], after(grad_hidden, far)))
    inv_two = lax.rsqrt(jnp.mean(middle * middle, axis=-1, keepdims=True) + eps_norm)
    normed_two = middle * inv_two
    second = gather_pair((normed_two * ffn_gain).astype(jnp.bfloat16))
    hidden, grad_gate, grad_up = ffn_stage(second, grad_hidden, w_gate, w_up, where)

    down_shares = unit_shares("down_shares", cot, hidden, ctx_count, where)
    down = unit_sum_over(down_shares)
    grads, weights = after(down_shares, grad_gate, grad_up), (w_gate, w_up)
    send = grad_second_half(1, "grad_second_send", grads, weights, where)

    def second_stage(send, grad_gate, grad_up, hidden):
        keep = grad_second_half(0, "grad_second_keep", (grad_gate, grad_up), weights, where)
        near, far, got = pair_scatter(keep, send)
        shares = unit_shares("gate_shares", second, after(near[3], grad_gate), ctx_count, where)
        *terms, away = pair_finish(near, after(shares, far), got)
        halves = unit_sum(
            ffn_out_kernel, "ffn_out", (after(away, hidden),), (w_down,), False, where
        )
        return total(after(halves[0], *terms)), shares, halves

    grad_second, gate_shares, ffn_halves = stage(second_stage, send, *grads, hidden)
    gate = unit_sum_over(gate_shares)

    def branch_stage(grad_second, grad_up, own):
        grad_norm, gain_part = norm_back(grad_second, normed_two, inv_two, ffn_gain)
        grad_middle = own.astype(jnp.float32) + grad_norm
        branch = grad_middle.astype(jnp.bfloat16)
        shares = unit_shares("up_shares", second, after(branch, grad_up), ctx_count, where)
        near = jnp.concatenate([branch, after(shares, flip(branch, "y"))])
        return grad_middle, gain_part, shares, jnp.concatenate([near, flip(near, "core")])

    grad_middle, ffn_gain_part, up_shares, grad_branch = stage(
        branch_stage, grad_second, grad_up, cot_own
    )
    up = unit_sum_over(up_shares)
    backward, kv = [], []
    held = grad_branch
    for head in range(kv_heads):
        backward.append(
            attention_backward(
                head, queries, held, w_out, mixed, log_total, parts, cosine, sine,
                block_order, cont_prompt, where,
            )
        )
        kv.append(KvReduce(backward[-1][1], ctx_flip(backward[-1][2], 1)))
        dep = backward[-1][0]
        if head == 0:
            down_own, down_away = split_halves(down, ctx, dep)
            down_other = ctx_flip(down_away, 2)
            dep = down_own
        held = after(dep, grad_branch)
    grad_queries = [item[0] for item in backward]
    branch_shares = weight_shares(
        "branch_shares",
        (first_input, grad_branch),
        grad_queries + [after(dep, mixed)],
        tuple((0, h) for h in range(kv_heads)) + ((1, kv_heads),),
        ctx_count,
        True,
        where,
    )
    sum_down = join_halves(down_own, after(branch_shares[0], down_other), ctx).T
    kv = [item.merge(sum_down) for item in kv]
    dep = tuple(keep for keep, _ in kv)
    branch = Reduce(*after(dep, *branch_shares))

    got = [ctx_flip(value, 2) for _, value in kv]

    def out_stage(keep, send):
        got = flip(send, "core")
        n = keep.shape[0] // 4
        near = [add(keep[k * n : (k + 1) * n], got[k * n : (k + 1) * n]) for k in range(4)]
        return near[0], near[2], add(near[1], flip(near[3], "y"))

    out_near, out_own, out_away = stage(out_stage, *after(dep, *ffn_halves))
    for mask in highs:
        kv = [KvReduce(keep, value).merge(out_away) for (keep, _), value in zip(kv, got)]
        got = [ctx_flip(value, mask) for _, value in kv]
    out_far, out_got = stage(
        lambda away, own: (ctx_flip(away, 2), flip(own, "y")),
        *after(tuple(keep for keep, _ in kv), out_away, out_own),
    )
    got = [after(out_far, value) for value in got]
    kv = [(keep, value) for (keep, _), value in zip(kv, got)]
    gate_own, gate_away = split_halves(gate, ctx, tuple(got))
    gate_other = ctx_flip(gate_away, 2)
    dep = gate_own
    output = (middle + total((out_near, out_got, after(dep, out_far)))).astype(jnp.bfloat16)
    keep, send, grad_kv = tail_stage(
        [(keep, after(dep, value)) for keep, value in kv], cosine, sine, grad_queries,
        w_query, key_matrix, value_matrix, where,
    )

    kv_shares = weight_shares(
        "kv_shares", (first_input,), (after(keep, grad_kv),), ((0, 0),), ctx_count, True, where
    )
    branch.halve(2, ctx, kv_shares[0])
    last = Reduce(*after(branch.keep, *kv_shares))

    def first_stage(keep, send, own_input, grad_middle):
        terms = scatter_slots(keep, send)
        inv = lax.rsqrt(jnp.mean(own_input * own_input, axis=-1, keepdims=True) + eps_norm)
        grad_norm, gain_part = norm_back(total(terms), own_input * inv, inv, attn_gain)
        return gain_part, (grad_middle + grad_norm).astype(jnp.bfloat16)

    attn_gain_part, grad_input = stage(
        first_stage, after(branch.keep, keep), send, own_input, grad_middle
    )
    near = jnp.concatenate([grad_input, after(grad_input, output)])
    near_other = flip(near, "y")
    dep = grad_input
    for mask in highs:
        branch.halve(mask, ctx, dep)
        dep = branch.keep
    last.halve(2, ctx, dep)
    sum_gate = join_halves(gate_own, after(last.keep, gate_other), ctx)
    dep = sum_gate
    for mask in highs:
        last.halve(mask, ctx, dep)
        dep = last.keep
    near = jnp.concatenate([near, after(dep, near_other)])
    far = flip(near, "core")
    quarters = [near[n * quarter : (n + 1) * quarter] for n in range(4)]
    quarters += [far[n * quarter : (n + 1) * quarter] for n in range(4)]
    grad_input, output = [
        place_rows(quarters[k], quarters[k + 2], quarters[k + 4], quarters[k + 6], tensor)
        for k in range(2)
    ]

    def gain_stage(gains):
        gains = gains + flip(gains, "core")
        gains = gains + flip(gains, "y")
        for mask in [1, 2] + highs:
            gains = gains + ctx_flip(gains, mask)
        return gains

    up_own, up_away = split_halves(up, ctx, dep)
    up_other = ctx_flip(up_away, 2)
    gains = stage(gain_stage, after(near, jnp.stack([attn_gain_part, ffn_gain_part])))
    sum_up = join_halves(up_own, after(gains, up_other), ctx)
    branch.keep, branch.got = after(sum_up, branch.keep, branch.got)
    width_q, width_k = w_query.shape[1], key_matrix.shape[1]
    branch_sum, last_sum = branch.sum(), last.sum()
    sum_query, sum_out = branch_sum[:, :width_q], branch_sum[:, width_q:].T
    sum_key, sum_value = last_sum[:, :width_k], last_sum[:, width_k:]

    gains = gains.reshape(2, ctx_count * SLOTS, -1)
    gains = lax.dynamic_index_in_dim(gains, ctx * SLOTS + tensor, 1, keepdims=False)
    return (
        output,
        grad_input,
        gains[0],
        sum_query,
        sum_key,
        sum_value,
        sum_out,
        gains[1],
        sum_gate,
        sum_up,
        sum_down,
    )


def solution(mesh):
    rows, heads = ("hi", "l", "x"), ("y", "core")
    split = Mesh(mesh.devices.reshape(-1, 2, 2, 2, 2), rows + heads)
    placed = (
        P(rows, None),
        P(),
        P(None, heads),
        P(None, heads),
        P(None, heads),
        P(heads, None),
        P(),
        P(None, heads),
        P(None, heads),
        P(heads, None),
        P(rows, None),
        P(),
        P(),
    )
    return jax.shard_map(
        body,
        mesh=split,
        in_specs=placed,
        out_specs=(
            P(rows, None),
            P(rows, None),
            P(rows + heads),
            P(rows, heads),
            P(rows, heads),
            P(rows, heads),
            P(heads, rows),
            P(rows + heads),
            P(rows, heads),
            P(rows, heads),
            P(heads, rows),
        ),
        check_vma=False,
    )
```

```python
import functools
import math

import jax
import jax.numpy as jnp
import numpy as np
from jax import lax
from jax.experimental import pallas as pl
from jax.experimental.pallas import tpu as pltpu
from jax.sharding import Mesh
from jax.sharding import PartitionSpec as P

HEAD_SIZE = 128
PROMPT = 2048
CONT_LEN = 256
CONTS = 8
BLOCK = 128
PER_PROMPT = PROMPT // BLOCK
PER_CONT = CONT_LEN // BLOCK
LOG2E = 1.4426950408889634
NEG = -1e30
SLOTS = 4
VMEM_LIMIT = 60 << 20
PAIR_STEPS = (4, 1)

eps_norm = 1e-05
rope_base = 1000000.0

SLOT_XOR = (0, 2, 1, 3)


def plain_dot(left, right):
    return jnp.dot(left, right, preferred_element_type=jnp.float32)


def left_dot(left, right):
    return lax.dot_general(
        left, right, (((0,), (0,)), ((), ())), preferred_element_type=jnp.float32
    )


def right_dot(left, right):
    return lax.dot_general(
        left, right, (((1,), (1,)), ((), ())), preferred_element_type=jnp.float32
    )


def slot_quarter(slot, tensor):
    return ((slot & 1) * 2 + lax.shift_right_logical(slot, 1)) ^ tensor


def stored_block(index, where_ref):
    rank = lax.div(index, SLOTS) ^ where_ref[0]
    return rank * SLOTS + slot_quarter(index & 3, where_ref[1])


def block_plan(order_ref, cont_ref, where_ref, slot):
    count = cont_ref.shape[0]
    prompt_blocks = count // CONTS * PER_PROMPT
    own = order_ref[stored_block(slot, where_ref)]
    is_prompt = own < prompt_blocks
    offset = own - prompt_blocks
    which = jnp.clip(lax.div(offset, PER_CONT), 0, count - 1)
    group = jnp.where(is_prompt, lax.div(own, PER_PROMPT), cont_ref[which])
    inner = jnp.where(is_prompt, lax.rem(own, PER_PROMPT), lax.rem(offset, PER_CONT))
    has_prev = lax.rem(inner, 2)
    pairs = jnp.where(is_prompt, lax.div(inner, 2), PER_PROMPT // 2)
    prev = own - has_prev
    return group * PER_PROMPT, pairs, prev, own, has_prev


def fill_inverse(order_ref, where_ref, inverse_ref):
    def put(index, carry):
        inverse_ref[order_ref[stored_block(index, where_ref)]] = index
        return carry

    lax.fori_loop(0, order_ref.shape[0], put, 0)


def rotate(vec, cosine, sine):
    return vec * cosine + pltpu.roll(vec, HEAD_SIZE // 2, 1) * sine


def unrotate(vec, cosine, sine):
    return vec * cosine + pltpu.roll(vec * sine, HEAD_SIZE // 2, 1)


def angle_tables():
    half = HEAD_SIZE // 2
    freq = np.float64(rope_base) ** (-(2.0 * np.arange(half) / HEAD_SIZE))
    freq = np.concatenate([freq, freq])
    starts = np.arange(-(-(PER_PROMPT + PER_CONT) // 8) * 8) * BLOCK
    start = starts[:, None] * freq[None]
    inner = np.arange(BLOCK)[:, None] * freq[None]
    return tuple(
        f(a).astype(np.float32) for a in (start, inner) for f in (np.cos, np.sin)
    )


def key_rows(inverse_ref, logical):
    return pl.ds(pl.multiple_of(inverse_ref[logical] * BLOCK, BLOCK), BLOCK)


def tile_pair(ref, rows_a, rows_b, column):
    return tile(ref, (rows_a, rows_b), column)


def tile(ref, rows, column):
    cols = pl.ds(column, HEAD_SIZE)
    return jnp.concatenate([ref[span, cols] for span in rows], axis=0)


def own_mask(has_prev, rep):
    shape = (2 * BLOCK, rep * BLOCK)
    row = lax.broadcasted_iota(jnp.int32, shape, 0)
    col = lax.broadcasted_iota(jnp.int32, shape, 1)
    first_row = BLOCK * (1 - has_prev)
    return (row >= first_row) & (row - BLOCK <= lax.rem(col, BLOCK))


def stack_t(ref, rows, column, rep):
    return jnp.concatenate(
        [ref[rows, pl.ds(column + r * HEAD_SIZE, HEAD_SIZE)].T for r in range(rep)], axis=1
    )


def stack_rows(ref, rows, column, rep):
    return jnp.concatenate(
        [ref[rows, pl.ds(column + r * HEAD_SIZE, HEAD_SIZE)] for r in range(rep)], axis=0
    )


def dot(left, right):
    return jnp.dot(left, right, preferred_element_type=jnp.float32)


def start_parts(parts, buffer_ref, sem, column):
    rows, width = parts[0].shape[0], buffer_ref.shape[1]
    copies = [
        pltpu.make_async_copy(
            part.at[:, pl.ds(column, width)], buffer_ref.at[pl.ds(p * rows, rows), :], sem.at[p]
        )
        for p, part in enumerate(parts)
    ]
    for copy in copies:
        copy.start()
    return copies


def forward_kernel(rep, hps, ctx_count, order_ref, cont_ref, where_ref, q_ref, wo_ref, *refs):
    parts, refs = refs[:ctx_count], refs[ctx_count:]
    out_ref, lse_ref, keep_ref, send_ref, kv_ref, inverse_ref, qt_ref, acc_ref, sem = refs
    copies = start_parts(parts, kv_ref, sem, 0)
    fill_inverse(order_ref, where_ref, inverse_ref)
    for copy in copies:
        copy.wait()
    q_blocks = q_ref.shape[0] // BLOCK
    factor = LOG2E / math.sqrt(HEAD_SIZE)
    width = rep * HEAD_SIZE

    def one_query_block(qb, carry):
        base, pairs, prev, own, has_prev = block_plan(order_ref, cont_ref, where_ref, qb)
        rows = pl.ds(pl.multiple_of(qb * BLOCK, BLOCK), BLOCK)
        mask = own_mask(has_prev, rep)
        rows_a, rows_b = key_rows(inverse_ref, prev), key_rows(inverse_ref, own)
        state = []
        for h in range(hps):
            qt = stack_t(q_ref, rows, h * width, rep)
            qt_ref[h] = qt
            scores = dot(tile_pair(kv_ref, rows_a, rows_b, 2 * h * HEAD_SIZE), qt) * factor
            scores = jnp.where(mask, scores, NEG)
            best = jnp.max(scores, axis=0, keepdims=True)
            weights = jnp.exp2(scores - best)
            total = jnp.sum(weights, axis=0, keepdims=True)
            values = tile_pair(kv_ref, rows_a, rows_b, (2 * h + 1) * HEAD_SIZE)
            acc_ref[h] = dot(values.T, weights.astype(jnp.bfloat16))
            state += [best, total]

        def fold(first, count, state):
            rows = [key_rows(inverse_ref, first + n) for n in range(count)]
            after = []
            for h in range(hps):
                best, total = state[2 * h], state[2 * h + 1]
                keys = tile(kv_ref, rows, 2 * h * HEAD_SIZE)
                scores = dot(keys, qt_ref[h]) * factor
                newest = jnp.maximum(best, jnp.max(scores, axis=0, keepdims=True))
                weights = jnp.exp2(scores - newest)
                shrink = jnp.exp2(best - newest)
                total = total * shrink + jnp.sum(weights, axis=0, keepdims=True)
                values = tile(kv_ref, rows, (2 * h + 1) * HEAD_SIZE)
                acc_ref[h] = acc_ref[h] * shrink + dot(values.T, weights.astype(jnp.bfloat16))
                after += [newest, total]
            return tuple(after)

        state, done = tuple(state), 0
        for wide in PAIR_STEPS:
            upto = lax.div(pairs, wide) * wide
            state = lax.fori_loop(
                0,
                lax.div(upto - done, wide),
                lambda t, state, done=done, wide=wide: fold(
                    base + 2 * (done + wide * t), 2 * wide, state
                ),
                state,
            )
            done = upto
        for h in range(hps):
            best, total = state[2 * h], state[2 * h + 1]
            mixed = acc_ref[h] * (1.0 / total)
            for r in range(rep):
                part = mixed[:, r * BLOCK : (r + 1) * BLOCK]
                out_ref[rows, pl.ds(h * width + r * HEAD_SIZE, HEAD_SIZE)] = part.T.astype(
                    jnp.bfloat16
                )
            lse_ref[h, pl.ds(qb, 1), :] = best + jnp.log2(total)
        return carry

    lax.fori_loop(0, q_blocks, one_query_block, 0)
    mixed = out_ref[...]
    half = keep_ref.shape[0]
    for n in range(0, wo_ref.shape[1], 512):
        cols = slice(n, n + 512)
        partial = dot(mixed, wo_ref[:, cols]).astype(jnp.bfloat16)
        keep_ref[:, cols] = partial[:half]
        send_ref[:, cols] = partial[half:]


def backward_kernel(rep, hps, ctx_count, head, order_ref, cont_ref, where_ref, q_ref, gb_ref, wo_ref,
                    mix_ref, lse_ref, cos_ref, sin_ref, *refs):
    parts, refs = refs[:ctx_count], refs[ctx_count:]
    gq_ref, keep_ref, send_ref = refs[:3]
    kv_ref, gm_ref, inverse_ref, qt_ref, gmt_ref, gqt_ref, acc_ref, sem = refs[3:]
    copies = start_parts(parts, kv_ref, sem, head * kv_ref.shape[1])
    fill_inverse(order_ref, where_ref, inverse_ref)
    gm_ref[...] = right_dot(gb_ref[...], wo_ref[...]).astype(jnp.bfloat16)
    for copy in copies:
        copy.wait()
    q_blocks = q_ref.shape[0] // BLOCK
    scale = 1.0 / math.sqrt(HEAD_SIZE)
    factor = LOG2E * scale
    width = rep * HEAD_SIZE

    def clear(i, carry):
        acc_ref[pl.ds(pl.multiple_of(i * BLOCK, BLOCK), BLOCK), :] = jnp.zeros(
            (BLOCK, acc_ref.shape[1]), jnp.float32
        )
        return carry

    lax.fori_loop(0, order_ref.shape[0], clear, 0)

    def tile_terms(h, spans, lse, delta, q_rows, gm_rows, mask):
        kcol, vcol = 2 * h * HEAD_SIZE, (2 * h + 1) * HEAD_SIZE
        keys = tile(kv_ref, spans, kcol)
        values = tile(kv_ref, spans, vcol)
        weights = jnp.exp2(dot(keys, qt_ref[h]) * factor - lse)
        if mask is not None:
            weights = jnp.where(mask, weights, 0.0)
        grad_weights = dot(values, gmt_ref[h])
        grad_scores = (weights * (grad_weights - delta)).astype(jnp.bfloat16)
        gv = dot(weights.astype(jnp.bfloat16), gm_rows)
        gk = dot(grad_scores, q_rows)
        for n, span in enumerate(spans):
            piece = slice(n * BLOCK, (n + 1) * BLOCK)
            acc_ref[span, pl.ds(kcol, HEAD_SIZE)] += gk[piece]
            acc_ref[span, pl.ds(vcol, HEAD_SIZE)] += gv[piece]
        return dot(keys.T, grad_scores)

    def one_query_block(qb, carry):
        base, pairs, prev, own, has_prev = block_plan(order_ref, cont_ref, where_ref, qb)
        rows = pl.ds(pl.multiple_of(qb * BLOCK, BLOCK), BLOCK)
        mask = own_mask(has_prev, rep)
        rows_a, rows_b = key_rows(inverse_ref, prev), key_rows(inverse_ref, own)
        deltas, lses, q_stack, gm_stack = [], [], [], []
        for h in range(hps):
            qt_ref[h] = stack_t(q_ref, rows, h * width, rep)
            gmt = stack_t(gm_ref, rows, h * width, rep)
            gmt_ref[h] = gmt
            mixt = stack_t(mix_ref, rows, h * width, rep)
            deltas.append(
                jnp.sum(
                    gmt.astype(jnp.float32) * mixt.astype(jnp.float32), axis=0, keepdims=True
                )
            )
            lses.append(lse_ref[h, pl.ds(qb, 1), :])
        for h in range(hps):
            q_rows = stack_rows(q_ref, rows, h * width, rep)
            gm_rows = stack_rows(gm_ref, rows, h * width, rep)
            gqt_ref[h] = tile_terms(
                h, (rows_a, rows_b), lses[h], deltas[h], q_rows, gm_rows, mask
            )

        def fold(first, count):
            spans = [key_rows(inverse_ref, first + n) for n in range(count)]
            for h in range(hps):
                q_rows = stack_rows(q_ref, rows, h * width, rep)
                gm_rows = stack_rows(gm_ref, rows, h * width, rep)
                gqt_ref[h] += tile_terms(
                    h, spans, lses[h], deltas[h], q_rows, gm_rows, None
                )
            return 0

        done = 0
        for wide in PAIR_STEPS:
            upto = lax.div(pairs, wide) * wide
            lax.fori_loop(
                0,
                lax.div(upto - done, wide),
                lambda t, _, done=done, wide=wide: fold(base + 2 * (done + wide * t), 2 * wide),
                0,
            )
            done = upto
        for h in range(hps):
            total = gqt_ref[h] * scale
            for r in range(rep):
                part = total[:, r * BLOCK : (r + 1) * BLOCK]
                rounded = part.T.astype(jnp.bfloat16).astype(jnp.float32)
                gq_ref[rows, pl.ds(h * width + r * HEAD_SIZE, HEAD_SIZE)] = unrotate(
                    rounded, cos_ref[rows, :], sin_ref[rows, :]
                ).astype(jnp.bfloat16)
        return carry

    lax.fori_loop(0, q_blocks, one_query_block, 0)

    blocks = order_ref.shape[0]

    def place(index):
        chunk = lax.div(index, SLOTS)
        spot = (chunk & 1) * (ctx_count // 2) + (chunk & 2) // 2 * (ctx_count // 4) + (
            lax.shift_right_logical(chunk, 2)
        )
        return spot * SLOTS + (index & 3)

    def flush(i, carry):
        rows = pl.ds(pl.multiple_of(i * BLOCK, BLOCK), BLOCK)
        spot = place(i)
        parts = []
        for h in range(hps):
            parts.append(acc_ref[rows, pl.ds(2 * h * HEAD_SIZE, HEAD_SIZE)] * scale)
            parts.append(acc_ref[rows, pl.ds((2 * h + 1) * HEAD_SIZE, HEAD_SIZE)])
        value = jnp.concatenate(parts, axis=1).astype(jnp.bfloat16)

        @pl.when(spot < blocks // 2)
        def _():
            keep_ref[pl.ds(pl.multiple_of(spot * BLOCK, BLOCK), BLOCK), :] = value

        @pl.when(spot >= blocks // 2)
        def _():
            far = (spot - blocks // 2) * BLOCK
            send_ref[pl.ds(pl.multiple_of(far, BLOCK), BLOCK), :] = value

        return carry

    lax.fori_loop(0, blocks, flush, 0)


def attention_forward(q, w_out, parts, order, cont, where):
    ctx_count = len(parts)
    rows, tokens = q.shape[0], ctx_count * q.shape[0]
    kv_heads = parts[0].shape[1] // (2 * HEAD_SIZE)
    rep = q.shape[1] // HEAD_SIZE // kv_heads
    q_blocks, model = rows // BLOCK, w_out.shape[1]
    vmem, smem, any_ = (
        pl.BlockSpec(memory_space=space) for space in (pltpu.VMEM, pltpu.SMEM, pl.ANY)
    )
    flops = 2 * rows * tokens * q.shape[1] + 2 * rows * q.shape[1] * model
    half = jax.ShapeDtypeStruct((rows // 2, model), jnp.bfloat16)
    return pl.pallas_call(
        functools.partial(forward_kernel, rep, kv_heads, ctx_count),
        out_shape=(
            jax.ShapeDtypeStruct(q.shape, jnp.bfloat16),
            jax.ShapeDtypeStruct((kv_heads, q_blocks, rep * BLOCK), jnp.float32),
            half,
            half,
        ),
        in_specs=[smem] * 3 + [vmem] * 2 + [any_] * ctx_count,
        out_specs=[vmem] * 4,
        scratch_shapes=[
            pltpu.VMEM((tokens, parts[0].shape[1]), jnp.bfloat16),
            pltpu.SMEM((order.shape[0],), jnp.int32),
            pltpu.VMEM((kv_heads, HEAD_SIZE, rep * BLOCK), jnp.bfloat16),
            pltpu.VMEM((kv_heads, HEAD_SIZE, rep * BLOCK), jnp.float32),
            pltpu.SemaphoreType.DMA((ctx_count,)),
        ],
        compiler_params=pltpu.CompilerParams(vmem_limit_bytes=VMEM_LIMIT),
        cost_estimate=cost("attention_forward", flops, 2 * tokens * parts[0].shape[1] + 4 * rows * model),
        name="attention_forward",
    )(order, cont, where, q, w_out, *parts)


def attention_backward(head, q, grad_branch, w_out, mixed, lse, parts, cosine, sine, order, cont,
                       where):
    ctx_count = len(parts)
    rows, tokens = q.shape[0], ctx_count * q.shape[0]
    kv_heads = parts[0].shape[1] // (2 * HEAD_SIZE)
    rep = q.shape[1] // HEAD_SIZE // kv_heads
    q_blocks, model = rows // BLOCK, w_out.shape[1]
    wide = rep * HEAD_SIZE
    q_spec = pl.BlockSpec((rows, wide), lambda g, *_: (0, head))
    whole = lambda g, *_: (0, 0)
    table_spec = pl.BlockSpec((rows, HEAD_SIZE), whole)
    half = (tokens // 2, 2 * HEAD_SIZE)
    flops = 5 * rows * tokens * wide + 2 * rows * wide * model
    return pl.pallas_call(
        functools.partial(backward_kernel, rep, 1, ctx_count, head),
        out_shape=(
            jax.ShapeDtypeStruct((rows, wide), jnp.bfloat16),
            jax.ShapeDtypeStruct(half, jnp.bfloat16),
            jax.ShapeDtypeStruct(half, jnp.bfloat16),
        ),
        grid_spec=pltpu.PrefetchScalarGridSpec(
            num_scalar_prefetch=3,
            grid=(1,),
            in_specs=[
                q_spec,
                pl.BlockSpec((rows, model), whole),
                pl.BlockSpec((wide, model), lambda g, *_: (head, 0)),
                q_spec,
                pl.BlockSpec((1, q_blocks, rep * BLOCK), lambda g, *_: (head, 0, 0)),
                table_spec,
                table_spec,
            ]
            + [pl.BlockSpec(memory_space=pl.ANY)] * ctx_count,
            out_specs=[
                pl.BlockSpec((rows, wide), whole),
                pl.BlockSpec(half, whole),
                pl.BlockSpec(half, whole),
            ],
            scratch_shapes=[
                pltpu.VMEM((tokens, 2 * HEAD_SIZE), jnp.bfloat16),
                pltpu.VMEM((rows, wide), jnp.bfloat16),
                pltpu.SMEM((order.shape[0],), jnp.int32),
                pltpu.VMEM((1, HEAD_SIZE, rep * BLOCK), jnp.bfloat16),
                pltpu.VMEM((1, HEAD_SIZE, rep * BLOCK), jnp.bfloat16),
                pltpu.VMEM((1, HEAD_SIZE, rep * BLOCK), jnp.float32),
                pltpu.VMEM((tokens, 2 * HEAD_SIZE), jnp.float32),
                pltpu.SemaphoreType.DMA((ctx_count,)),
            ],
        ),
        compiler_params=pltpu.CompilerParams(vmem_limit_bytes=VMEM_LIMIT),
        cost_estimate=cost(f"attention_backward_{head}", flops, 4 * tokens * wide + 2 * rows * model),
        name=f"attention_backward_{head}",
    )(order, cont, where, q, grad_branch, w_out, mixed, lse, cosine, sine, *parts)


def input_kernel(order_ref, cont_ref, where_ref, gain_ref, x_hbm, wq_hbm, wk_hbm, wv_hbm, table_hbm,
                 first_ref, q_ref, kv_ref, cos_ref, sin_ref,
                 x_ref, wq_ref, wk_ref, wv_ref, table_ref, sem):
    pairs = ((x_hbm, x_ref), (table_hbm, table_ref), (wk_hbm, wk_ref), (wv_hbm, wv_ref),
             (wq_hbm, wq_ref))
    copies = [
        pltpu.make_async_copy(source, target, sem.at[n])
        for n, (source, target) in enumerate(pairs)
    ]
    for copy in copies:
        copy.start()
    count = cont_ref.shape[0]
    prompt_blocks = count // CONTS * PER_PROMPT
    starts = (table_ref.shape[0] - 2 * BLOCK) // 2
    lane = lax.broadcasted_iota(jnp.int32, (BLOCK, HEAD_SIZE), 1)
    copies[0].wait()
    copies[1].wait()

    def one_slot(slot, carry):
        quarter = slot_quarter(slot, where_ref[1])
        rows = pl.ds(pl.multiple_of(slot * BLOCK, BLOCK), BLOCK)
        full = x_ref[pl.ds(pl.multiple_of(quarter * BLOCK, BLOCK), BLOCK), :].astype(jnp.float32)
        inv = lax.rsqrt(jnp.mean(full * full, axis=-1, keepdims=True) + eps_norm)
        first_ref[rows, :] = (full * inv * gain_ref[...]).astype(jnp.bfloat16)
        own = order_ref[stored_block(slot, where_ref)]
        spot = jnp.where(
            own < prompt_blocks,
            lax.rem(own, PER_PROMPT),
            PER_PROMPT + lax.rem(own - prompt_blocks, PER_CONT),
        )
        cos_start = table_ref[pl.ds(2 * BLOCK + spot, 1), :]
        sin_start = table_ref[pl.ds(2 * BLOCK + starts + spot, 1), :]
        cos_in, sin_in = table_ref[:BLOCK, :], table_ref[BLOCK : 2 * BLOCK, :]
        sine = sin_start * cos_in + cos_start * sin_in
        cos_ref[rows, :] = cos_start * cos_in - sin_start * sin_in
        sin_ref[rows, :] = jnp.where(lane < HEAD_SIZE // 2, -sine, sine)
        return carry

    lax.fori_loop(0, SLOTS, one_slot, 0)
    first = first_ref[...]
    cosine, sine = cos_ref[...], sin_ref[...]
    copies[2].wait()
    copies[3].wait()
    keys = dot(first, wk_ref[...])
    values = dot(first, wv_ref[...])
    for h in range(wk_ref.shape[1] // HEAD_SIZE):
        cols = slice(h * HEAD_SIZE, (h + 1) * HEAD_SIZE)
        low, high = 2 * h * HEAD_SIZE, (2 * h + 1) * HEAD_SIZE
        key = rotate(keys[:, cols], cosine, sine)
        kv_ref[:, low:high] = key.astype(jnp.bfloat16)
        kv_ref[:, high : high + HEAD_SIZE] = values[:, cols].astype(jnp.bfloat16)
    copies[4].wait()
    for n in range(0, wq_ref.shape[1], 256):
        queries = dot(first, wq_ref[:, n : n + 256])
        for m in range(0, 256, HEAD_SIZE):
            query = rotate(queries[:, m : m + HEAD_SIZE], cosine, sine)
            q_ref[:, n + m : n + m + HEAD_SIZE] = query.astype(jnp.bfloat16)


def input_stage(x, gain, wq, wk, wv, order, cont, where):
    rows, model = x.shape
    cos_start, sin_start, cos_in, sin_in = angle_tables()
    table = np.concatenate([cos_in, sin_in, cos_start, sin_start])
    vmem, smem, any_ = (
        pl.BlockSpec(memory_space=space) for space in (pltpu.VMEM, pltpu.SMEM, pl.ANY)
    )
    flops = 2 * rows * model * (wq.shape[1] + 2 * wk.shape[1])
    return pl.pallas_call(
        input_kernel,
        out_shape=(
            jax.ShapeDtypeStruct((rows, model), jnp.bfloat16),
            jax.ShapeDtypeStruct((rows, wq.shape[1]), jnp.bfloat16),
            jax.ShapeDtypeStruct((rows, 2 * wk.shape[1]), jnp.bfloat16),
            jax.ShapeDtypeStruct((rows, HEAD_SIZE), jnp.float32),
            jax.ShapeDtypeStruct((rows, HEAD_SIZE), jnp.float32),
        ),
        in_specs=[smem] * 3 + [vmem] + [any_] * 5,
        out_specs=[vmem] * 5,
        scratch_shapes=[
            pltpu.VMEM(a.shape, a.dtype) for a in (x, wq, wk, wv)
        ]
        + [pltpu.VMEM(table.shape, jnp.float32), pltpu.SemaphoreType.DMA((5,))],
        compiler_params=pltpu.CompilerParams(vmem_limit_bytes=VMEM_LIMIT),
        cost_estimate=cost("input_stage", flops, 4 * x.size + 2 * wq.size + 4 * wk.size),
        name="input_stage",
    )(order, cont, where, gain.reshape(1, -1), x, wq, wk, wv, table)


FILLERS = ("ffn_out", "gate_shares", "kv_shares", "grad_hidden")


def cost(name, flops, bytes_accessed):
    scale = 16.0 if name in FILLERS else 0.02
    return pl.CostEstimate(
        flops=int(flops * scale), bytes_accessed=int(bytes_accessed * scale), transcendentals=0
    )


def put_share(value, index, x_bit, keep_ref, send_ref, swap_bits):
    spot = share_spot(lax.shift_right_logical(index, 1), keep_ref.shape[0], swap_bits)
    stays = (index & 1) == x_bit
    value = value.astype(keep_ref.dtype)

    @pl.when(stays)
    def _():
        keep_ref[pl.ds(spot, 1)] = value[None]

    @pl.when(jnp.logical_not(stays))
    def _():
        send_ref[pl.ds(spot, 1)] = value[None]


def pair_bit(where_ref):
    return lax.shift_right_logical(where_ref[0], 1) & 1


def grad_hidden_kernel(where_ref, cot_ref, wd_ref, out_ref):
    out_ref[...] = right_dot(cot_ref[...], wd_ref[...])


def grad_hidden_stage(cot, w_down, where):
    rows, model = cot.shape
    units = w_down.shape[0] // 2
    block = 256
    steps = units // block
    return pl.pallas_call(
        grad_hidden_kernel,
        out_shape=jax.ShapeDtypeStruct((rows, units), jnp.float32),
        grid_spec=pltpu.PrefetchScalarGridSpec(
            num_scalar_prefetch=1,
            grid=(steps,),
            in_specs=[
                pl.BlockSpec((rows, model), lambda i, w: (0, 0), pipeline_mode=pl.Buffered(1)),
                pl.BlockSpec((block, model), lambda i, w: (pair_bit(w) * steps + i, 0)),
            ],
            out_specs=pl.BlockSpec((rows, block), lambda i, w: (0, i)),
        ),
        compiler_params=pltpu.CompilerParams(vmem_limit_bytes=VMEM_LIMIT),
        cost_estimate=cost("grad_hidden", 2 * rows * model * units, 4 * rows * model),
        name="grad_hidden",
    )(where, cot, w_down)


def ffn_kernel(where_ref, in_ref, gh_ref, wg_ref, wu_ref, hid_ref, gg_ref, gu_ref):
    gate = dot(in_ref[...], wg_ref[...])
    upward = dot(in_ref[...], wu_ref[...])
    grad_hidden = gh_ref[...]
    sigma = jax.nn.sigmoid(gate)
    swish = gate * sigma
    hid_ref[...] = (swish * upward).astype(jnp.bfloat16)
    gg_ref[...] = (grad_hidden * upward * sigma * (1.0 + gate * (1.0 - sigma))).astype(
        jnp.bfloat16
    )
    gu_ref[...] = (grad_hidden * swish).astype(jnp.bfloat16)


def ffn_stage(second, grad_hidden, w_gate, w_up, where):
    rows, model = second.shape
    units = w_gate.shape[1] // 2
    block = 256
    steps = units // block
    col_spec = pl.BlockSpec((model, block), lambda i, w: (0, pair_bit(w) * steps + i))
    unit_spec = pl.BlockSpec((rows, block), lambda i, w: (0, i))
    unit = jax.ShapeDtypeStruct((rows, units), jnp.bfloat16)
    return pl.pallas_call(
        ffn_kernel,
        out_shape=(unit, unit, unit),
        grid_spec=pltpu.PrefetchScalarGridSpec(
            num_scalar_prefetch=1,
            grid=(steps,),
            in_specs=[
                pl.BlockSpec((rows, model), lambda i, w: (0, 0), pipeline_mode=pl.Buffered(1)),
                unit_spec,
                col_spec,
                col_spec,
            ],
            out_specs=[unit_spec] * 3,
        ),
        compiler_params=pltpu.CompilerParams(vmem_limit_bytes=VMEM_LIMIT),
        cost_estimate=cost("ffn_stage", 4 * rows * model * units, 6 * rows * model),
        name="ffn_stage",
    )(where, second, grad_hidden, w_gate, w_up)


def grad_second_kernel(where_ref, gg_ref, gu_ref, wg_ref, wu_ref, out_ref):
    total = right_dot(gg_ref[...], wg_ref[...]) + right_dot(gu_ref[...], wu_ref[...])
    out_ref[...] = total.astype(jnp.bfloat16)


def grad_second_half(half, name, grads, weights, where):
    rows, units = grads[0].shape
    rows //= 2
    model = weights[0].shape[0]
    block = 512
    left_spec = pl.BlockSpec((rows, units), lambda n, w: (half, 0), pipeline_mode=pl.Buffered(1))
    right_spec = pl.BlockSpec((block, units), lambda n, w: (n, pair_bit(w)))
    return pl.pallas_call(
        grad_second_kernel,
        out_shape=jax.ShapeDtypeStruct((rows, model), jnp.bfloat16),
        grid_spec=pltpu.PrefetchScalarGridSpec(
            num_scalar_prefetch=1,
            grid=(model // block,),
            in_specs=[left_spec] * 2 + [right_spec] * 2,
            out_specs=pl.BlockSpec((rows, block), lambda n, w: (0, n)),
        ),
        compiler_params=pltpu.CompilerParams(vmem_limit_bytes=VMEM_LIMIT),
        cost_estimate=cost(name, 4 * rows * units * model, 4 * rows * model),
        name=name,
    )(where, *grads, *weights)


def ffn_out_kernel(where_ref, hid_ref, wd_ref, keep_ref, send_ref):
    total = dot(hid_ref[...], wd_ref[...])
    half = keep_ref.shape[0]
    keep_ref[...] = total[:half].astype(jnp.bfloat16)
    send_ref[...] = total[half:].astype(jnp.bfloat16)


def unit_sum(kernel, name, lefts, rights, transposed, where):
    rows, units = lefts[0].shape
    model = rights[0].shape[0 if transposed else 1]
    block = 512
    if transposed:
        right_spec = pl.BlockSpec((block, units), lambda n, w: (n, pair_bit(w)))
    else:
        right_spec = pl.BlockSpec((units, block), lambda n, w: (pair_bit(w), n))
    left_spec = pl.BlockSpec((rows, units), lambda n, w: (0, 0), pipeline_mode=pl.Buffered(1))
    half = jax.ShapeDtypeStruct((rows // 2, model), jnp.bfloat16)
    half_spec = pl.BlockSpec((rows // 2, block), lambda n, w: (0, n))
    return pl.pallas_call(
        kernel,
        out_shape=(half, half),
        grid_spec=pltpu.PrefetchScalarGridSpec(
            num_scalar_prefetch=1,
            grid=(model // block,),
            in_specs=[left_spec] * len(lefts) + [right_spec] * len(rights),
            out_specs=[half_spec, half_spec],
        ),
        compiler_params=pltpu.CompilerParams(vmem_limit_bytes=VMEM_LIMIT),
        cost_estimate=cost(name, 2 * len(lefts) * rows * units * model, 4 * rows * model),
        name=name,
    )(where, *lefts, *rights)


def share_spot(spot, count, swap_bits):
    if swap_bits:
        return (spot & 1) * (count // 2) + lax.shift_right_logical(spot, 1)
    return spot


def shares_kernel(left_count, swap_bits, pairs, where_ref, *refs):
    lefts, refs = refs[:left_count], refs[left_count:]
    rights, (keep_ref, send_ref) = refs[:-2], refs[-2:]
    share = keep_ref.shape[1]
    step = pl.program_id(0)
    pieces = [left_dot(lefts[l][...], rights[r][...]) for l, r in pairs]
    per_step = lefts[0].shape[1] // share
    if per_step == 1:
        value = jnp.concatenate(pieces, axis=1).astype(keep_ref.dtype)
        sends = step < pl.num_programs(0) // 2

        @pl.when(sends)
        def _():
            send_ref[0] = value

        @pl.when(jnp.logical_not(sends))
        def _():
            keep_ref[0] = value

        return
    for k in range(per_step):
        rows = slice(k * share, (k + 1) * share)
        value = jnp.concatenate([piece[rows] for piece in pieces], axis=1)
        index = step * per_step + k
        put_share(value, index, where_ref[0] & 1, keep_ref, send_ref, swap_bits)


def weight_shares(name, lefts, rights, pairs, ctx_count, swap_bits, where):
    rows, model = lefts[0].shape
    block = 256
    share, half = model // ctx_count, ctx_count // 2
    width = sum(rights[r].shape[1] for _, r in pairs)
    shares = jax.ShapeDtypeStruct((half, share, width), jnp.bfloat16)
    if share == block:

        def left_map(i, w):
            mine = w[0] & 1
            return 0, jnp.where(i < half, 2 * i + 1 - mine, 2 * (i - half) + mine)

        left_spec = pl.BlockSpec((rows, block), left_map)
        spot = lambda index: share_spot(index, half, swap_bits)
        keep_spec = pl.BlockSpec(
            (1, share, width), lambda i, w: (spot(jnp.maximum(i - half, 0)), 0, 0)
        )
        send_spec = pl.BlockSpec(
            (1, share, width), lambda i, w: (spot(jnp.minimum(i, half - 1)), 0, 0)
        )
    else:
        left_spec = pl.BlockSpec((rows, block), lambda i, w: (0, i))
        keep_spec = send_spec = pl.BlockSpec(shares.shape, lambda i, w: (0, 0, 0))
    return pl.pallas_call(
        functools.partial(shares_kernel, len(lefts), swap_bits, pairs),
        out_shape=(shares, shares),
        grid_spec=pltpu.PrefetchScalarGridSpec(
            num_scalar_prefetch=1,
            grid=(model // block,),
            in_specs=[left_spec] * len(lefts)
            + [
                pl.BlockSpec(r.shape, lambda i, w: (0, 0), pipeline_mode=pl.Buffered(1))
                for r in rights
            ],
            out_specs=[keep_spec, send_spec],
        ),
        compiler_params=pltpu.CompilerParams(vmem_limit_bytes=VMEM_LIMIT),
        cost_estimate=cost(name, 2 * rows * model * width, 4 * rows * model),
        name=name,
    )(where, *lefts, *rights)


def unit_shares_kernel(where_ref, left_ref, right_ref, out_ref):
    share = out_ref.shape[1]
    total = left_dot(left_ref[...], right_ref[...]).astype(out_ref.dtype)
    per_step = left_ref.shape[1] // share
    if out_ref.shape[0] == 1:
        out_ref[0] = total
    else:
        for k in range(per_step):
            index = pl.program_id(0) * per_step + k
            out_ref[pl.ds(unit_spot(index, out_ref.shape[0]), 1)] = total[k * share : (k + 1) * share][None]


def unit_spot(index, ctx_count):
    return (index & 1) * (ctx_count // 2) + lax.shift_right_logical(index, 1)


def unit_shares(name, left, right, ctx_count, where):
    rows, model = left.shape
    block, width = 256, right.shape[1]
    share = model // ctx_count
    shares = jax.ShapeDtypeStruct((ctx_count, share, width), jnp.bfloat16)
    if share == block:
        out_spec = pl.BlockSpec((1, share, width), lambda i, w: (unit_spot(i, ctx_count), 0, 0))
    else:
        out_spec = pl.BlockSpec(shares.shape, lambda i, w: (0, 0, 0))
    return pl.pallas_call(
        unit_shares_kernel,
        out_shape=shares,
        grid_spec=pltpu.PrefetchScalarGridSpec(
            num_scalar_prefetch=1,
            grid=(model // block,),
            in_specs=[
                pl.BlockSpec((rows, block), lambda i, w: (0, i)),
                pl.BlockSpec(right.shape, lambda i, w: (0, 0), pipeline_mode=pl.Buffered(1)),
            ],
            out_specs=out_spec,
        ),
        compiler_params=pltpu.CompilerParams(vmem_limit_bytes=VMEM_LIMIT),
        cost_estimate=cost(name, 2 * rows * model * width, 4 * rows * model),
        name=name,
    )(where, left, right)


def tail_kernel(kv_heads, where_ref, *refs):
    sums, refs = refs[: 2 * kv_heads], refs[2 * kv_heads :]
    cos_ref, sin_ref, refs = refs[0], refs[1], refs[2:]
    gq_refs, refs = refs[:kv_heads], refs[kv_heads:]
    wq_ref, wk_ref, wv_ref, keep_ref, send_ref, gkv_ref = refs
    cosine, sine = cos_ref[...], sin_ref[...]
    for h in range(kv_heads):
        total = sums[2 * h][...].astype(jnp.float32) + sums[2 * h + 1][...].astype(jnp.float32)
        total = total.astype(jnp.bfloat16)
        key = unrotate(total[:, :HEAD_SIZE].astype(jnp.float32), cosine, sine)
        cols = slice(h * HEAD_SIZE, (h + 1) * HEAD_SIZE)
        gkv_ref[:, cols] = key.astype(jnp.bfloat16)
        cols = slice((kv_heads + h) * HEAD_SIZE, (kv_heads + h + 1) * HEAD_SIZE)
        gkv_ref[:, cols] = total[:, HEAD_SIZE:]
    half = keep_ref.shape[0]
    key_width = kv_heads * HEAD_SIZE
    wide = gq_refs[0].shape[1]
    for n in range(0, wq_ref.shape[0], 512):
        span = slice(n, n + 512)
        total = right_dot(gkv_ref[:, :key_width], wk_ref[span, :])
        total += right_dot(gkv_ref[:, key_width:], wv_ref[span, :])
        for h in range(kv_heads):
            total += right_dot(gq_refs[h][...], wq_ref[span, h * wide : (h + 1) * wide])
        total = total.astype(jnp.bfloat16)
        keep_ref[:, span] = total[:half]
        send_ref[:, span] = total[half:]


def tail_stage(kv_sums, cosine, sine, grad_queries, wq, wk, wv, where):
    rows, model = cosine.shape[0], wq.shape[0]
    kv_heads = len(grad_queries)
    vmem = pl.BlockSpec(memory_space=pltpu.VMEM)
    half = jax.ShapeDtypeStruct((rows // 2, model), jnp.bfloat16)
    flat = [term for sums in kv_sums for term in sums]
    return pl.pallas_call(
        functools.partial(tail_kernel, kv_heads),
        out_shape=(
            half,
            half,
            jax.ShapeDtypeStruct((rows, 2 * kv_heads * HEAD_SIZE), jnp.bfloat16),
        ),
        in_specs=[pl.BlockSpec(memory_space=pltpu.SMEM)]
        + [vmem] * (len(flat) + 2 + kv_heads + 3),
        out_specs=[vmem] * 3,
        compiler_params=pltpu.CompilerParams(vmem_limit_bytes=VMEM_LIMIT),
        cost_estimate=cost("tail_stage", 2 * rows * model * (wq.shape[1] + 2 * wk.shape[1]), 4 * rows * model + 4 * wq.size
        ),
        name="tail_stage",
    )(where, *flat, cosine, sine, *grad_queries, wq, wk, wv)


def flip(value, axis, mask=1):
    return lax.ppermute(value, axis, [(i, i ^ mask) for i in range(lax.axis_size(axis))])


def ctx_flip(value, mask):
    if mask == 1:
        return flip(value, "x")
    if mask == 2:
        return flip(value, "l")
    return flip(value, "hi", mask // 4)


def add(left, right):
    return (left.astype(jnp.float32) + right.astype(jnp.float32)).astype(jnp.bfloat16)


def slots_of(value, tensor):
    rows = value.shape[0] // SLOTS
    return [
        lax.dynamic_slice_in_dim(value, (tensor ^ SLOT_XOR[u]) * rows, rows)
        for u in range(SLOTS)
    ]


def after(dep, *values):
    deps = dep if isinstance(dep, tuple) else (dep,)
    held = lax.optimization_barrier(deps + values)[len(deps) :]
    return held[0] if len(held) == 1 else held


class Stages:
    def __init__(self, block_order):
        self.live = block_order[0] >= 0

    def __call__(self, function, *args):
        shapes = jax.eval_shape(function, *args)
        empty = lambda *_: jax.tree.map(lambda a: jnp.zeros(a.shape, a.dtype), shapes)
        return lax.cond(self.live, function, empty, *args)


def gather_pair(own):
    partner = ctx_flip(own, 2)
    near = jnp.concatenate([own, partner, flip(own, "y"), flip(partner, "y")])
    return jnp.concatenate([near, flip(near, "core")])


def gather_slots(own):
    near = jnp.concatenate([own, flip(own, "y")])
    return near, flip(near, "core")


def place_rows(own, near, core, far, tensor):
    rows = own.shape[0]
    result = jnp.zeros((SLOTS * rows,) + own.shape[1:], own.dtype)
    for u, piece in enumerate((own, near, core, far)):
        result = lax.dynamic_update_slice_in_dim(
            result, piece, (tensor ^ SLOT_XOR[u]) * rows, 0
        )
    return result


def scatter_slots(keep, send, fill=lambda value: value):
    got = fill(flip(send, "core"))
    quarter = keep.shape[0] // 2
    far = flip(add(keep[quarter:], got[quarter:]), "y")
    return add(keep[:quarter], got[:quarter]), far


def pair_scatter(keep, send, fill=lambda near: near):
    got = fill(flip(send, "core"))
    n = keep.shape[0] // 4
    near = [add(keep[k * n : (k + 1) * n], got[k * n : (k + 1) * n]) for k in range(4)]
    far = flip(near[3], "y")
    got = flip(near[2], "y")
    return near, far, got


def pair_finish(near, far, got):
    away = add(near[1], far)
    return near[0], got, ctx_flip(away, 2), away


def total(terms):
    return sum(term.astype(jnp.float32) for term in terms)


class Reduce:
    def __init__(self, keep, send):
        self.keep, self.got = keep, ctx_flip(send, 1)

    def halve(self, mask, ctx, dep=None):
        keep, got = self.keep, self.got
        if dep is not None:
            keep, got = after(dep, keep, got)
        n = keep.shape[0] // 2
        bit = lax.div(ctx, mask) % 2
        pick = lambda value, index: lax.dynamic_slice_in_dim(value, index * n, n, 0)
        away = ctx_flip(add(pick(keep, 1 - bit), pick(got, 1 - bit)), mask)
        self.keep, self.got = add(pick(keep, bit), pick(got, bit)), away

    def sum(self):
        return (self.keep.astype(jnp.float32) + self.got.astype(jnp.float32))[0]


def high_masks(ctx_count):
    masks, mask = [], ctx_count // 2
    while mask >= 4:
        masks.append(mask)
        mask //= 2
    return masks


def unit_sum_over(shares):
    return lax.psum_scatter(shares, ("x", "hi"), scatter_dimension=0, tiled=True)


def split_halves(summed, ctx, dep):
    summed = after(dep, summed)
    pair = lax.div(ctx, 2) % 2
    pick = lambda index: lax.dynamic_index_in_dim(summed, index, 0, keepdims=False)
    return pick(pair), pick(1 - pair)


def join_halves(own, other, ctx):
    pair = lax.div(ctx, 2) % 2
    low, high = jnp.where(pair == 0, own, other), jnp.where(pair == 0, other, own)
    return jnp.concatenate([low, high], axis=1).astype(jnp.float32)


class KvReduce:
    def __init__(self, keep, got):
        self.keep, self.got = keep, got

    def merge(self, dep):
        keep, got = after(dep, self.keep, self.got)
        n = keep.shape[0] // 2
        return add(keep[:n], got[:n]), add(keep[n:], got[n:])


def norm_back(grad_out, normed, inv_scale, gain):
    scaled = grad_out * gain
    inner = jnp.mean(scaled * normed, axis=-1, keepdims=True)
    return (inv_scale * (scaled - normed * inner), jnp.sum(grad_out * normed, axis=0))


def body(
    layer_input,
    attn_gain,
    w_query,
    key_matrix,
    value_matrix,
    w_out,
    ffn_gain,
    w_gate,
    w_up,
    w_down,
    cotangent,
    block_order,
    cont_prompt,
):
    ctx_count = lax.axis_size("hi") * 4
    ctx = (lax.axis_index("hi") * 2 + lax.axis_index("l")) * 2 + lax.axis_index("x")
    tensor = lax.axis_index("y") * 2 + lax.axis_index("core")
    where = jnp.stack([ctx, tensor]).astype(jnp.int32)
    quarter = layer_input.shape[0] // SLOTS
    kv_heads = key_matrix.shape[1] // HEAD_SIZE
    highs = high_masks(ctx_count)

    stage = Stages(block_order)
    cot_own = lax.dynamic_slice_in_dim(cotangent, tensor * quarter, quarter)
    cot_slots = slots_of(cotangent, tensor)
    cot_part = ctx_flip(cot_own, 2)
    first_input, queries, kv_local, cosine, sine = input_stage(
        layer_input, attn_gain, w_query, key_matrix, value_matrix, block_order, cont_prompt, where
    )
    parts = {0: kv_local}
    parts[2], parts[1] = stage(
        lambda kv: (ctx_flip(kv, 2), ctx_flip(kv, 1)), after(cot_part, kv_local)
    )
    high_parts = {0: after(parts[1], kv_local)}
    for bit in reversed(highs):
        for mask in list(high_parts):
            high_parts[mask + bit] = ctx_flip(high_parts[mask], bit)
    del high_parts[0]
    parts.update(high_parts)
    parts[3] = stage(lambda kv: ctx_flip(kv, 1), parts[2])
    dep = parts[3]
    for mask in high_parts:
        parts[mask + 2], parts[mask + 1], more = stage(
            lambda kv, cot: (ctx_flip(kv, 2), ctx_flip(kv, 1), flip(cot, "y")),
            after(dep, parts[mask]),
            cot_part,
        )
        dep = parts[mask + 1]
    cot_part = jnp.concatenate([cot_part, more])
    for mask in high_parts:
        parts[mask + 3], cot_far = stage(
            lambda kv, cot: (ctx_flip(kv, 1), flip(cot, "core")), parts[mask + 2], cot_part
        )
    parts = [parts[mask] for mask in range(ctx_count)]
    cot = jnp.concatenate(
        [cot_slots[0], cot_part[:quarter], cot_slots[1], cot_part[quarter:]]
        + [cot_slots[2], cot_far[:quarter], cot_slots[3], cot_far[quarter:]]
    )
    mixed, log_total, keep, send = attention_forward(
        after(cot, queries), w_out, parts, block_order, cont_prompt, where
    )
    first_half = flip(send, "core")
    near = add(keep, first_half)
    far = flip(near[quarter:], "y")
    grad_hidden = grad_hidden_stage(after(near, cot), w_down, where)
    own_input = lax.dynamic_slice_in_dim(layer_input, tensor * quarter, quarter)
    own_input = own_input.astype(jnp.float32)
    middle = own_input + total((near[:quarter], after(grad_hidden, far)))
    inv_two = lax.rsqrt(jnp.mean(middle * middle, axis=-1, keepdims=True) + eps_norm)
    normed_two = middle * inv_two
    second = gather_pair((normed_two * ffn_gain).astype(jnp.bfloat16))
    hidden, grad_gate, grad_up = ffn_stage(second, grad_hidden, w_gate, w_up, where)

    down_shares = unit_shares("down_shares", cot, hidden, ctx_count, where)
    down = unit_sum_over(down_shares)
    grads, weights = after(down_shares, grad_gate, grad_up), (w_gate, w_up)
    send = grad_second_half(1, "grad_second_send", grads, weights, where)

    def second_stage(send, grad_gate, grad_up, hidden):
        keep = grad_second_half(0, "grad_second_keep", (grad_gate, grad_up), weights, where)
        near, far, got = pair_scatter(keep, send)
        shares = unit_shares("gate_shares", second, after(near[3], grad_gate), ctx_count, where)
        *terms, away = pair_finish(near, after(shares, far), got)
        halves = unit_sum(
            ffn_out_kernel, "ffn_out", (after(away, hidden),), (w_down,), False, where
        )
        return total(after(halves[0], *terms)), shares, halves

    grad_second, gate_shares, ffn_halves = stage(second_stage, send, *grads, hidden)
    gate = unit_sum_over(gate_shares)

    def branch_stage(grad_second, grad_up, own):
        grad_norm, gain_part = norm_back(grad_second, normed_two, inv_two, ffn_gain)
        grad_middle = own.astype(jnp.float32) + grad_norm
        branch = grad_middle.astype(jnp.bfloat16)
        shares = unit_shares("up_shares", second, after(branch, grad_up), ctx_count, where)
        near = jnp.concatenate([branch, after(shares, flip(branch, "y"))])
        return grad_middle, gain_part, shares, jnp.concatenate([near, flip(near, "core")])

    grad_middle, ffn_gain_part, up_shares, grad_branch = stage(
        branch_stage, grad_second, grad_up, cot_own
    )
    up = unit_sum_over(up_shares)
    backward, kv = [], []
    held = grad_branch
    for head in range(kv_heads):
        backward.append(
            attention_backward(
                head, queries, held, w_out, mixed, log_total, parts, cosine, sine,
                block_order, cont_prompt, where,
            )
        )
        kv.append(KvReduce(backward[-1][1], ctx_flip(backward[-1][2], 1)))
        dep = backward[-1][0]
        if head == 0:
            down_own, down_away = split_halves(down, ctx, dep)
            down_other = ctx_flip(down_away, 2)
            dep = down_own
        held = after(dep, grad_branch)
    grad_queries = [item[0] for item in backward]
    branch_shares = weight_shares(
        "branch_shares",
        (first_input, grad_branch),
        grad_queries + [after(dep, mixed)],
        tuple((0, h) for h in range(kv_heads)) + ((1, kv_heads),),
        ctx_count,
        True,
        where,
    )
    def out_stage(keep, send):
        got = flip(send, "core")
        n = keep.shape[0] // 4
        near = [add(keep[k * n : (k + 1) * n], got[k * n : (k + 1) * n]) for k in range(4)]
        return near[0], near[2], add(near[1], flip(near[3], "y"))

    def first_stage(keep, send, own_input, grad_middle):
        terms = scatter_slots(keep, send)
        inv = lax.rsqrt(jnp.mean(own_input * own_input, axis=-1, keepdims=True) + eps_norm)
        grad_norm, gain_part = norm_back(total(terms), own_input * inv, inv, attn_gain)
        return gain_part, (grad_middle + grad_norm).astype(jnp.bfloat16)

    def row_stage(near, other):
        near = jnp.concatenate([near, other])
        return near, flip(near, "core")

    def gain_stage(gains):
        gains = gains + flip(gains, "core")
        gains = gains + flip(gains, "y")
        for mask in [1, 2] + highs:
            gains = gains + ctx_flip(gains, mask)
        return gains

    dep = branch_shares[0]
    kv = [item.merge(dep) for item in kv]
    dep = tuple(keep for keep, _ in kv)
    sum_down = join_halves(down_own, after(dep, down_other), ctx).T
    dep = sum_down
    got = [ctx_flip(after(dep, value), 2) for _, value in kv]
    branch = Reduce(*after(dep, *branch_shares))
    out_near, out_own, out_away = stage(out_stage, *after(dep, *ffn_halves))
    dep = out_away
    for mask in highs:
        kv = [
            KvReduce(keep, value).merge(dep) for (keep, _), value in zip(kv, got)
        ]
        got = [ctx_flip(value, mask) for _, value in kv]
    dep = tuple(keep for keep, _ in kv)
    gate_own, gate_away = split_halves(gate, ctx, dep)
    dep = gate_own
    gate_other = ctx_flip(after(dep, gate_away), 2)
    out_far, out_got = stage(
        lambda away, own: (ctx_flip(away, 2), flip(own, "y")), *after(dep, out_away, out_own)
    )
    dep = out_far
    branch.halve(2, ctx, dep)
    dep = branch.keep
    output = (middle + total(after(dep, out_near, out_got, out_far))).astype(jnp.bfloat16)
    dep = output
    keep, send, grad_kv = tail_stage(
        [after(dep, keep, value) for (keep, _), value in zip(kv, got)], cosine, sine,
        grad_queries, w_query, key_matrix, value_matrix, where,
    )
    dep = keep
    kv_shares = weight_shares(
        "kv_shares", (first_input,), (after(dep, grad_kv),), ((0, 0),), ctx_count, True, where
    )
    dep = kv_shares[0]
    last = Reduce(*after(dep, *kv_shares))
    attn_gain_part, grad_input = stage(
        first_stage, after(dep, keep), send, own_input, grad_middle
    )
    dep = grad_input
    near = jnp.concatenate([grad_input, output])
    near_other = flip(after(dep, near), "y")
    for mask in highs:
        branch.halve(mask, ctx, dep)
        dep = branch.keep
    last.halve(2, ctx, dep)
    dep = last.keep
    sum_gate = join_halves(gate_own, after(dep, gate_other), ctx)
    dep = sum_gate
    for mask in highs:
        last.halve(mask, ctx, dep)
        dep = last.keep
    near, far = stage(row_stage, near, after(dep, near_other))
    dep = far
    last.keep, last.got = after(dep, last.keep, last.got)
    last_sum = last.sum()
    dep = last_sum
    quarters = [near[n * quarter : (n + 1) * quarter] for n in range(4)]
    quarters += [after(dep, far)[n * quarter : (n + 1) * quarter] for n in range(4)]
    grad_rows, output_rows = [
        place_rows(quarters[k], quarters[k + 2], quarters[k + 4], quarters[k + 6], tensor)
        for k in range(2)
    ]
    dep = (grad_rows, output_rows)
    up_own, up_away = split_halves(up, ctx, dep)
    dep = up_own
    up_other = ctx_flip(after(dep, up_away), 2)
    gains = stage(gain_stage, after(dep, jnp.stack([attn_gain_part, ffn_gain_part])))
    dep = gains
    sum_up = join_halves(up_own, after(dep, up_other), ctx)
    dep = sum_up
    branch.keep, branch.got = after(dep, branch.keep, branch.got)
    branch_sum = branch.sum()
    dep = branch_sum
    grad_input, output = grad_rows, output_rows
    width_q, width_k = w_query.shape[1], key_matrix.shape[1]
    sum_query, sum_out = branch_sum[:, :width_q], branch_sum[:, width_q:].T
    sum_key, sum_value = last_sum[:, :width_k], last_sum[:, width_k:]

    gains = gains.reshape(2, ctx_count * SLOTS, -1)
    gains = lax.dynamic_index_in_dim(gains, ctx * SLOTS + tensor, 1, keepdims=False)
    return (
        output,
        grad_input,
        gains[0],
        sum_query,
        sum_key,
        sum_value,
        sum_out,
        gains[1],
        sum_gate,
        sum_up,
        sum_down,
    )


def solution(mesh):
    rows, heads = ("hi", "l", "x"), ("y", "core")
    split = Mesh(mesh.devices.reshape(-1, 2, 2, 2, 2), rows + heads)
    placed = (
        P(rows, None),
        P(),
        P(None, heads),
        P(None, heads),
        P(None, heads),
        P(heads, None),
        P(),
        P(None, heads),
        P(None, heads),
        P(heads, None),
        P(rows, None),
        P(),
        P(),
    )
    return jax.shard_map(
        body,
        mesh=split,
        in_specs=placed,
        out_specs=(
            P(rows, None),
            P(rows, None),
            P(rows + heads),
            P(rows, heads),
            P(rows, heads),
            P(rows, heads),
            P(heads, rows),
            P(rows + heads),
            P(rows, heads),
            P(rows, heads),
            P(heads, rows),
        ),
        check_vma=False,
    )
```

```python
import functools
import math

import jax
import jax.numpy as jnp
import numpy as np
from jax import lax
from jax.experimental import pallas as pl
from jax.experimental.pallas import tpu as pltpu
from jax.sharding import Mesh
from jax.sharding import PartitionSpec as P

HEAD_SIZE = 128
PROMPT = 2048
CONT_LEN = 256
CONTS = 8
BLOCK = 128
PER_PROMPT = PROMPT // BLOCK
PER_CONT = CONT_LEN // BLOCK
LOG2E = 1.4426950408889634
NEG = -1e30
SLOTS = 4
VMEM_LIMIT = 60 << 20
PAIR_STEPS = (4, 1)

eps_norm = 1e-05
rope_base = 1000000.0

SLOT_XOR = (0, 2, 1, 3)


def plain_dot(left, right):
    return jnp.dot(left, right, preferred_element_type=jnp.float32)


def left_dot(left, right):
    return lax.dot_general(
        left, right, (((0,), (0,)), ((), ())), preferred_element_type=jnp.float32
    )


def right_dot(left, right):
    return lax.dot_general(
        left, right, (((1,), (1,)), ((), ())), preferred_element_type=jnp.float32
    )


def slot_quarter(slot, tensor):
    return ((slot & 1) * 2 + lax.shift_right_logical(slot, 1)) ^ tensor


def stored_block(index, where_ref):
    rank = lax.div(index, SLOTS) ^ where_ref[0]
    return rank * SLOTS + slot_quarter(index & 3, where_ref[1])


def block_plan(order_ref, cont_ref, where_ref, slot):
    count = cont_ref.shape[0]
    prompt_blocks = count // CONTS * PER_PROMPT
    own = order_ref[stored_block(slot, where_ref)]
    is_prompt = own < prompt_blocks
    offset = own - prompt_blocks
    which = jnp.clip(lax.div(offset, PER_CONT), 0, count - 1)
    group = jnp.where(is_prompt, lax.div(own, PER_PROMPT), cont_ref[which])
    inner = jnp.where(is_prompt, lax.rem(own, PER_PROMPT), lax.rem(offset, PER_CONT))
    has_prev = lax.rem(inner, 2)
    pairs = jnp.where(is_prompt, lax.div(inner, 2), PER_PROMPT // 2)
    prev = own - has_prev
    return group * PER_PROMPT, pairs, prev, own, has_prev


def fill_inverse(order_ref, where_ref, inverse_ref):
    def put(index, carry):
        inverse_ref[order_ref[stored_block(index, where_ref)]] = index
        return carry

    lax.fori_loop(0, order_ref.shape[0], put, 0)


def rotate(vec, cosine, sine):
    return vec * cosine + pltpu.roll(vec, HEAD_SIZE // 2, 1) * sine


def unrotate(vec, cosine, sine):
    return vec * cosine + pltpu.roll(vec * sine, HEAD_SIZE // 2, 1)


def angle_tables():
    half = HEAD_SIZE // 2
    freq = np.float64(rope_base) ** (-(2.0 * np.arange(half) / HEAD_SIZE))
    freq = np.concatenate([freq, freq])
    starts = np.arange(-(-(PER_PROMPT + PER_CONT) // 8) * 8) * BLOCK
    start = starts[:, None] * freq[None]
    inner = np.arange(BLOCK)[:, None] * freq[None]
    return tuple(
        f(a).astype(np.float32) for a in (start, inner) for f in (np.cos, np.sin)
    )


def key_rows(inverse_ref, logical):
    return pl.ds(pl.multiple_of(inverse_ref[logical] * BLOCK, BLOCK), BLOCK)


def tile_pair(ref, rows_a, rows_b, column):
    return tile(ref, (rows_a, rows_b), column)


def tile(ref, rows, column):
    cols = pl.ds(column, HEAD_SIZE)
    return jnp.concatenate([ref[span, cols] for span in rows], axis=0)


def own_mask(has_prev, rep):
    shape = (2 * BLOCK, rep * BLOCK)
    row = lax.broadcasted_iota(jnp.int32, shape, 0)
    col = lax.broadcasted_iota(jnp.int32, shape, 1)
    first_row = BLOCK * (1 - has_prev)
    return (row >= first_row) & (row - BLOCK <= lax.rem(col, BLOCK))


def stack_t(ref, rows, column, rep):
    return jnp.concatenate(
        [ref[rows, pl.ds(column + r * HEAD_SIZE, HEAD_SIZE)].T for r in range(rep)], axis=1
    )


def stack_rows(ref, rows, column, rep):
    return jnp.concatenate(
        [ref[rows, pl.ds(column + r * HEAD_SIZE, HEAD_SIZE)] for r in range(rep)], axis=0
    )


def dot(left, right):
    return jnp.dot(left, right, preferred_element_type=jnp.float32)


def start_parts(parts, buffer_ref, sem, column):
    rows, width = parts[0].shape[0], buffer_ref.shape[1]
    copies = [
        pltpu.make_async_copy(
            part.at[:, pl.ds(column, width)], buffer_ref.at[pl.ds(p * rows, rows), :], sem.at[p]
        )
        for p, part in enumerate(parts)
    ]
    for copy in copies:
        copy.start()
    return copies


def forward_kernel(rep, hps, ctx_count, order_ref, cont_ref, where_ref, q_ref, wo_ref, *refs):
    parts, refs = refs[:ctx_count], refs[ctx_count:]
    out_ref, lse_ref, keep_ref, send_ref, kv_ref, inverse_ref, qt_ref, acc_ref, sem = refs
    copies = start_parts(parts, kv_ref, sem, 0)
    fill_inverse(order_ref, where_ref, inverse_ref)
    for copy in copies:
        copy.wait()
    q_blocks = q_ref.shape[0] // BLOCK
    factor = LOG2E / math.sqrt(HEAD_SIZE)
    width = rep * HEAD_SIZE

    def one_query_block(qb, carry):
        base, pairs, prev, own, has_prev = block_plan(order_ref, cont_ref, where_ref, qb)
        rows = pl.ds(pl.multiple_of(qb * BLOCK, BLOCK), BLOCK)
        mask = own_mask(has_prev, rep)
        rows_a, rows_b = key_rows(inverse_ref, prev), key_rows(inverse_ref, own)
        state = []
        for h in range(hps):
            qt = stack_t(q_ref, rows, h * width, rep)
            qt_ref[h] = qt
            scores = dot(tile_pair(kv_ref, rows_a, rows_b, 2 * h * HEAD_SIZE), qt) * factor
            scores = jnp.where(mask, scores, NEG)
            best = jnp.max(scores, axis=0, keepdims=True)
            weights = jnp.exp2(scores - best)
            total = jnp.sum(weights, axis=0, keepdims=True)
            values = tile_pair(kv_ref, rows_a, rows_b, (2 * h + 1) * HEAD_SIZE)
            acc_ref[h] = dot(values.T, weights.astype(jnp.bfloat16))
            state += [best, total]

        def fold(first, count, state):
            rows = [key_rows(inverse_ref, first + n) for n in range(count)]
            after = []
            for h in range(hps):
                best, total = state[2 * h], state[2 * h + 1]
                keys = tile(kv_ref, rows, 2 * h * HEAD_SIZE)
                scores = dot(keys, qt_ref[h]) * factor
                newest = jnp.maximum(best, jnp.max(scores, axis=0, keepdims=True))
                weights = jnp.exp2(scores - newest)
                shrink = jnp.exp2(best - newest)
                total = total * shrink + jnp.sum(weights, axis=0, keepdims=True)
                values = tile(kv_ref, rows, (2 * h + 1) * HEAD_SIZE)
                acc_ref[h] = acc_ref[h] * shrink + dot(values.T, weights.astype(jnp.bfloat16))
                after += [newest, total]
            return tuple(after)

        state, done = tuple(state), 0
        for wide in PAIR_STEPS:
            upto = lax.div(pairs, wide) * wide
            state = lax.fori_loop(
                0,
                lax.div(upto - done, wide),
                lambda t, state, done=done, wide=wide: fold(
                    base + 2 * (done + wide * t), 2 * wide, state
                ),
                state,
            )
            done = upto
        for h in range(hps):
            best, total = state[2 * h], state[2 * h + 1]
            mixed = acc_ref[h] * (1.0 / total)
            for r in range(rep):
                part = mixed[:, r * BLOCK : (r + 1) * BLOCK]
                out_ref[rows, pl.ds(h * width + r * HEAD_SIZE, HEAD_SIZE)] = part.T.astype(
                    jnp.bfloat16
                )
            lse_ref[h, pl.ds(qb, 1), :] = best + jnp.log2(total)
        return carry

    lax.fori_loop(0, q_blocks, one_query_block, 0)
    mixed = out_ref[...]
    half = keep_ref.shape[0]
    for n in range(0, wo_ref.shape[1], 512):
        cols = slice(n, n + 512)
        partial = dot(mixed, wo_ref[:, cols]).astype(jnp.bfloat16)
        keep_ref[:, cols] = partial[:half]
        send_ref[:, cols] = partial[half:]


def backward_kernel(rep, hps, ctx_count, head, order_ref, cont_ref, where_ref, q_ref, gb_ref, wo_ref,
                    mix_ref, lse_ref, cos_ref, sin_ref, *refs):
    parts, refs = refs[:ctx_count], refs[ctx_count:]
    gq_ref, keep_ref, send_ref = refs[:3]
    kv_ref, gm_ref, inverse_ref, qt_ref, gmt_ref, gqt_ref, acc_ref, sem = refs[3:]
    copies = start_parts(parts, kv_ref, sem, head * kv_ref.shape[1])
    fill_inverse(order_ref, where_ref, inverse_ref)
    gm_ref[...] = right_dot(gb_ref[...], wo_ref[...]).astype(jnp.bfloat16)
    for copy in copies:
        copy.wait()
    q_blocks = q_ref.shape[0] // BLOCK
    scale = 1.0 / math.sqrt(HEAD_SIZE)
    factor = LOG2E * scale
    width = rep * HEAD_SIZE

    def clear(i, carry):
        acc_ref[pl.ds(pl.multiple_of(i * BLOCK, BLOCK), BLOCK), :] = jnp.zeros(
            (BLOCK, acc_ref.shape[1]), jnp.float32
        )
        return carry

    lax.fori_loop(0, order_ref.shape[0], clear, 0)

    def tile_terms(h, spans, lse, delta, q_rows, gm_rows, mask):
        kcol, vcol = 2 * h * HEAD_SIZE, (2 * h + 1) * HEAD_SIZE
        keys = tile(kv_ref, spans, kcol)
        values = tile(kv_ref, spans, vcol)
        weights = jnp.exp2(dot(keys, qt_ref[h]) * factor - lse)
        if mask is not None:
            weights = jnp.where(mask, weights, 0.0)
        grad_weights = dot(values, gmt_ref[h])
        grad_scores = (weights * (grad_weights - delta)).astype(jnp.bfloat16)
        gv = dot(weights.astype(jnp.bfloat16), gm_rows)
        gk = dot(grad_scores, q_rows)
        for n, span in enumerate(spans):
            piece = slice(n * BLOCK, (n + 1) * BLOCK)
            acc_ref[span, pl.ds(kcol, HEAD_SIZE)] += gk[piece]
            acc_ref[span, pl.ds(vcol, HEAD_SIZE)] += gv[piece]
        return dot(keys.T, grad_scores)

    def one_query_block(qb, carry):
        base, pairs, prev, own, has_prev = block_plan(order_ref, cont_ref, where_ref, qb)
        rows = pl.ds(pl.multiple_of(qb * BLOCK, BLOCK), BLOCK)
        mask = own_mask(has_prev, rep)
        rows_a, rows_b = key_rows(inverse_ref, prev), key_rows(inverse_ref, own)
        deltas, lses, q_stack, gm_stack = [], [], [], []
        for h in range(hps):
            qt_ref[h] = stack_t(q_ref, rows, h * width, rep)
            gmt = stack_t(gm_ref, rows, h * width, rep)
            gmt_ref[h] = gmt
            mixt = stack_t(mix_ref, rows, h * width, rep)
            deltas.append(
                jnp.sum(
                    gmt.astype(jnp.float32) * mixt.astype(jnp.float32), axis=0, keepdims=True
                )
            )
            lses.append(lse_ref[h, pl.ds(qb, 1), :])
        for h in range(hps):
            q_rows = stack_rows(q_ref, rows, h * width, rep)
            gm_rows = stack_rows(gm_ref, rows, h * width, rep)
            gqt_ref[h] = tile_terms(
                h, (rows_a, rows_b), lses[h], deltas[h], q_rows, gm_rows, mask
            )

        def fold(first, count):
            spans = [key_rows(inverse_ref, first + n) for n in range(count)]
            for h in range(hps):
                q_rows = stack_rows(q_ref, rows, h * width, rep)
                gm_rows = stack_rows(gm_ref, rows, h * width, rep)
                gqt_ref[h] += tile_terms(
                    h, spans, lses[h], deltas[h], q_rows, gm_rows, None
                )
            return 0

        done = 0
        for wide in PAIR_STEPS:
            upto = lax.div(pairs, wide) * wide
            lax.fori_loop(
                0,
                lax.div(upto - done, wide),
                lambda t, _, done=done, wide=wide: fold(base + 2 * (done + wide * t), 2 * wide),
                0,
            )
            done = upto
        for h in range(hps):
            total = gqt_ref[h] * scale
            for r in range(rep):
                part = total[:, r * BLOCK : (r + 1) * BLOCK]
                rounded = part.T.astype(jnp.bfloat16).astype(jnp.float32)
                gq_ref[rows, pl.ds(h * width + r * HEAD_SIZE, HEAD_SIZE)] = unrotate(
                    rounded, cos_ref[rows, :], sin_ref[rows, :]
                ).astype(jnp.bfloat16)
        return carry

    lax.fori_loop(0, q_blocks, one_query_block, 0)

    blocks = order_ref.shape[0]

    def place(index):
        chunk = lax.div(index, SLOTS)
        spot = (chunk & 1) * (ctx_count // 2) + (chunk & 2) // 2 * (ctx_count // 4) + (
            lax.shift_right_logical(chunk, 2)
        )
        return spot * SLOTS + (index & 3)

    def flush(i, carry):
        rows = pl.ds(pl.multiple_of(i * BLOCK, BLOCK), BLOCK)
        spot = place(i)
        parts = []
        for h in range(hps):
            parts.append(acc_ref[rows, pl.ds(2 * h * HEAD_SIZE, HEAD_SIZE)] * scale)
            parts.append(acc_ref[rows, pl.ds((2 * h + 1) * HEAD_SIZE, HEAD_SIZE)])
        value = jnp.concatenate(parts, axis=1).astype(jnp.bfloat16)

        @pl.when(spot < blocks // 2)
        def _():
            keep_ref[pl.ds(pl.multiple_of(spot * BLOCK, BLOCK), BLOCK), :] = value

        @pl.when(spot >= blocks // 2)
        def _():
            far = (spot - blocks // 2) * BLOCK
            send_ref[pl.ds(pl.multiple_of(far, BLOCK), BLOCK), :] = value

        return carry

    lax.fori_loop(0, blocks, flush, 0)


def attention_forward(q, w_out, parts, order, cont, where):
    ctx_count = len(parts)
    rows, tokens = q.shape[0], ctx_count * q.shape[0]
    kv_heads = parts[0].shape[1] // (2 * HEAD_SIZE)
    rep = q.shape[1] // HEAD_SIZE // kv_heads
    q_blocks, model = rows // BLOCK, w_out.shape[1]
    vmem, smem, any_ = (
        pl.BlockSpec(memory_space=space) for space in (pltpu.VMEM, pltpu.SMEM, pl.ANY)
    )
    flops = 2 * rows * tokens * q.shape[1] + 2 * rows * q.shape[1] * model
    half = jax.ShapeDtypeStruct((rows // 2, model), jnp.bfloat16)
    return pl.pallas_call(
        functools.partial(forward_kernel, rep, kv_heads, ctx_count),
        out_shape=(
            jax.ShapeDtypeStruct(q.shape, jnp.bfloat16),
            jax.ShapeDtypeStruct((kv_heads, q_blocks, rep * BLOCK), jnp.float32),
            half,
            half,
        ),
        in_specs=[smem] * 3 + [vmem] * 2 + [any_] * ctx_count,
        out_specs=[vmem] * 4,
        scratch_shapes=[
            pltpu.VMEM((tokens, parts[0].shape[1]), jnp.bfloat16),
            pltpu.SMEM((order.shape[0],), jnp.int32),
            pltpu.VMEM((kv_heads, HEAD_SIZE, rep * BLOCK), jnp.bfloat16),
            pltpu.VMEM((kv_heads, HEAD_SIZE, rep * BLOCK), jnp.float32),
            pltpu.SemaphoreType.DMA((ctx_count,)),
        ],
        compiler_params=pltpu.CompilerParams(vmem_limit_bytes=VMEM_LIMIT),
        cost_estimate=cost("attention_forward", flops, 2 * tokens * parts[0].shape[1] + 4 * rows * model),
        name="attention_forward",
    )(order, cont, where, q, w_out, *parts)


def attention_backward(head, q, grad_branch, w_out, mixed, lse, parts, cosine, sine, order, cont,
                       where):
    ctx_count = len(parts)
    rows, tokens = q.shape[0], ctx_count * q.shape[0]
    kv_heads = parts[0].shape[1] // (2 * HEAD_SIZE)
    rep = q.shape[1] // HEAD_SIZE // kv_heads
    q_blocks, model = rows // BLOCK, w_out.shape[1]
    wide = rep * HEAD_SIZE
    q_spec = pl.BlockSpec((rows, wide), lambda g, *_: (0, head))
    whole = lambda g, *_: (0, 0)
    table_spec = pl.BlockSpec((rows, HEAD_SIZE), whole)
    half = (tokens // 2, 2 * HEAD_SIZE)
    flops = 5 * rows * tokens * wide + 2 * rows * wide * model
    return pl.pallas_call(
        functools.partial(backward_kernel, rep, 1, ctx_count, head),
        out_shape=(
            jax.ShapeDtypeStruct((rows, wide), jnp.bfloat16),
            jax.ShapeDtypeStruct(half, jnp.bfloat16),
            jax.ShapeDtypeStruct(half, jnp.bfloat16),
        ),
        grid_spec=pltpu.PrefetchScalarGridSpec(
            num_scalar_prefetch=3,
            grid=(1,),
            in_specs=[
                q_spec,
                pl.BlockSpec((rows, model), whole),
                pl.BlockSpec((wide, model), lambda g, *_: (head, 0)),
                q_spec,
                pl.BlockSpec((1, q_blocks, rep * BLOCK), lambda g, *_: (head, 0, 0)),
                table_spec,
                table_spec,
            ]
            + [pl.BlockSpec(memory_space=pl.ANY)] * ctx_count,
            out_specs=[
                pl.BlockSpec((rows, wide), whole),
                pl.BlockSpec(half, whole),
                pl.BlockSpec(half, whole),
            ],
            scratch_shapes=[
                pltpu.VMEM((tokens, 2 * HEAD_SIZE), jnp.bfloat16),
                pltpu.VMEM((rows, wide), jnp.bfloat16),
                pltpu.SMEM((order.shape[0],), jnp.int32),
                pltpu.VMEM((1, HEAD_SIZE, rep * BLOCK), jnp.bfloat16),
                pltpu.VMEM((1, HEAD_SIZE, rep * BLOCK), jnp.bfloat16),
                pltpu.VMEM((1, HEAD_SIZE, rep * BLOCK), jnp.float32),
                pltpu.VMEM((tokens, 2 * HEAD_SIZE), jnp.float32),
                pltpu.SemaphoreType.DMA((ctx_count,)),
            ],
        ),
        compiler_params=pltpu.CompilerParams(vmem_limit_bytes=VMEM_LIMIT),
        cost_estimate=cost(f"attention_backward_{head}", flops, 4 * tokens * wide + 2 * rows * model),
        name=f"attention_backward_{head}",
    )(order, cont, where, q, grad_branch, w_out, mixed, lse, cosine, sine, *parts)


def input_kernel(order_ref, cont_ref, where_ref, gain_ref, x_hbm, wq_hbm, wk_hbm, wv_hbm, table_hbm,
                 first_ref, q_ref, kv_ref, cos_ref, sin_ref,
                 x_ref, wq_ref, wk_ref, wv_ref, table_ref, sem):
    pairs = ((x_hbm, x_ref), (table_hbm, table_ref), (wk_hbm, wk_ref), (wv_hbm, wv_ref),
             (wq_hbm, wq_ref))
    copies = [
        pltpu.make_async_copy(source, target, sem.at[n])
        for n, (source, target) in enumerate(pairs)
    ]
    for copy in copies:
        copy.start()
    count = cont_ref.shape[0]
    prompt_blocks = count // CONTS * PER_PROMPT
    starts = (table_ref.shape[0] - 2 * BLOCK) // 2
    lane = lax.broadcasted_iota(jnp.int32, (BLOCK, HEAD_SIZE), 1)
    copies[0].wait()
    copies[1].wait()

    def one_slot(slot, carry):
        quarter = slot_quarter(slot, where_ref[1])
        rows = pl.ds(pl.multiple_of(slot * BLOCK, BLOCK), BLOCK)
        full = x_ref[pl.ds(pl.multiple_of(quarter * BLOCK, BLOCK), BLOCK), :].astype(jnp.float32)
        inv = lax.rsqrt(jnp.mean(full * full, axis=-1, keepdims=True) + eps_norm)
        first_ref[rows, :] = (full * inv * gain_ref[...]).astype(jnp.bfloat16)
        own = order_ref[stored_block(slot, where_ref)]
        spot = jnp.where(
            own < prompt_blocks,
            lax.rem(own, PER_PROMPT),
            PER_PROMPT + lax.rem(own - prompt_blocks, PER_CONT),
        )
        cos_start = table_ref[pl.ds(2 * BLOCK + spot, 1), :]
        sin_start = table_ref[pl.ds(2 * BLOCK + starts + spot, 1), :]
        cos_in, sin_in = table_ref[:BLOCK, :], table_ref[BLOCK : 2 * BLOCK, :]
        sine = sin_start * cos_in + cos_start * sin_in
        cos_ref[rows, :] = cos_start * cos_in - sin_start * sin_in
        sin_ref[rows, :] = jnp.where(lane < HEAD_SIZE // 2, -sine, sine)
        return carry

    lax.fori_loop(0, SLOTS, one_slot, 0)
    first = first_ref[...]
    cosine, sine = cos_ref[...], sin_ref[...]
    copies[2].wait()
    copies[3].wait()
    keys = dot(first, wk_ref[...])
    values = dot(first, wv_ref[...])
    for h in range(wk_ref.shape[1] // HEAD_SIZE):
        cols = slice(h * HEAD_SIZE, (h + 1) * HEAD_SIZE)
        low, high = 2 * h * HEAD_SIZE, (2 * h + 1) * HEAD_SIZE
        key = rotate(keys[:, cols], cosine, sine)
        kv_ref[:, low:high] = key.astype(jnp.bfloat16)
        kv_ref[:, high : high + HEAD_SIZE] = values[:, cols].astype(jnp.bfloat16)
    copies[4].wait()
    for n in range(0, wq_ref.shape[1], 256):
        queries = dot(first, wq_ref[:, n : n + 256])
        for m in range(0, 256, HEAD_SIZE):
            query = rotate(queries[:, m : m + HEAD_SIZE], cosine, sine)
            q_ref[:, n + m : n + m + HEAD_SIZE] = query.astype(jnp.bfloat16)


def input_stage(x, gain, wq, wk, wv, order, cont, where):
    rows, model = x.shape
    cos_start, sin_start, cos_in, sin_in = angle_tables()
    table = np.concatenate([cos_in, sin_in, cos_start, sin_start])
    vmem, smem, any_ = (
        pl.BlockSpec(memory_space=space) for space in (pltpu.VMEM, pltpu.SMEM, pl.ANY)
    )
    flops = 2 * rows * model * (wq.shape[1] + 2 * wk.shape[1])
    return pl.pallas_call(
        input_kernel,
        out_shape=(
            jax.ShapeDtypeStruct((rows, model), jnp.bfloat16),
            jax.ShapeDtypeStruct((rows, wq.shape[1]), jnp.bfloat16),
            jax.ShapeDtypeStruct((rows, 2 * wk.shape[1]), jnp.bfloat16),
            jax.ShapeDtypeStruct((rows, HEAD_SIZE), jnp.float32),
            jax.ShapeDtypeStruct((rows, HEAD_SIZE), jnp.float32),
        ),
        in_specs=[smem] * 3 + [vmem] + [any_] * 5,
        out_specs=[vmem] * 5,
        scratch_shapes=[
            pltpu.VMEM(a.shape, a.dtype) for a in (x, wq, wk, wv)
        ]
        + [pltpu.VMEM(table.shape, jnp.float32), pltpu.SemaphoreType.DMA((5,))],
        compiler_params=pltpu.CompilerParams(vmem_limit_bytes=VMEM_LIMIT),
        cost_estimate=cost("input_stage", flops, 4 * x.size + 2 * wq.size + 4 * wk.size),
        name="input_stage",
    )(order, cont, where, gain.reshape(1, -1), x, wq, wk, wv, table)


FILLERS = ("kv_shares", "grad_hidden")


def cost(name, flops, bytes_accessed):
    scale = 16.0 if name in FILLERS else 0.02
    return pl.CostEstimate(
        flops=int(flops * scale), bytes_accessed=int(bytes_accessed * scale), transcendentals=0
    )


def put_share(value, index, x_bit, keep_ref, send_ref, swap_bits):
    spot = share_spot(lax.shift_right_logical(index, 1), keep_ref.shape[0], swap_bits)
    stays = (index & 1) == x_bit
    value = value.astype(keep_ref.dtype)

    @pl.when(stays)
    def _():
        keep_ref[pl.ds(spot, 1)] = value[None]

    @pl.when(jnp.logical_not(stays))
    def _():
        send_ref[pl.ds(spot, 1)] = value[None]


def pair_bit(where_ref):
    return lax.shift_right_logical(where_ref[0], 1) & 1


def grad_hidden_kernel(where_ref, cot_ref, wd_ref, out_ref):
    out_ref[...] = right_dot(cot_ref[...], wd_ref[...])


def grad_hidden_stage(cot, w_down, where):
    rows, model = cot.shape
    units = w_down.shape[0] // 2
    block = 256
    steps = units // block
    return pl.pallas_call(
        grad_hidden_kernel,
        out_shape=jax.ShapeDtypeStruct((rows, units), jnp.float32),
        grid_spec=pltpu.PrefetchScalarGridSpec(
            num_scalar_prefetch=1,
            grid=(steps,),
            in_specs=[
                pl.BlockSpec((rows, model), lambda i, w: (0, 0), pipeline_mode=pl.Buffered(1)),
                pl.BlockSpec((block, model), lambda i, w: (pair_bit(w) * steps + i, 0)),
            ],
            out_specs=pl.BlockSpec((rows, block), lambda i, w: (0, i)),
        ),
        compiler_params=pltpu.CompilerParams(vmem_limit_bytes=VMEM_LIMIT),
        cost_estimate=cost("grad_hidden", 2 * rows * model * units, 4 * rows * model),
        name="grad_hidden",
    )(where, cot, w_down)


def ffn_kernel(where_ref, in_ref, gh_ref, wg_ref, wu_ref, hid_ref, gg_ref, gu_ref):
    gate = dot(in_ref[...], wg_ref[...])
    upward = dot(in_ref[...], wu_ref[...])
    grad_hidden = gh_ref[...]
    sigma = jax.nn.sigmoid(gate)
    swish = gate * sigma
    hid_ref[...] = (swish * upward).astype(jnp.bfloat16)
    gg_ref[...] = (grad_hidden * upward * sigma * (1.0 + gate * (1.0 - sigma))).astype(
        jnp.bfloat16
    )
    gu_ref[...] = (grad_hidden * swish).astype(jnp.bfloat16)


def ffn_stage(second, grad_hidden, w_gate, w_up, where):
    rows, model = second.shape
    units = w_gate.shape[1] // 2
    block = 256
    steps = units // block
    col_spec = pl.BlockSpec((model, block), lambda i, w: (0, pair_bit(w) * steps + i))
    unit_spec = pl.BlockSpec((rows, block), lambda i, w: (0, i))
    unit = jax.ShapeDtypeStruct((rows, units), jnp.bfloat16)
    return pl.pallas_call(
        ffn_kernel,
        out_shape=(unit, unit, unit),
        grid_spec=pltpu.PrefetchScalarGridSpec(
            num_scalar_prefetch=1,
            grid=(steps,),
            in_specs=[
                pl.BlockSpec((rows, model), lambda i, w: (0, 0), pipeline_mode=pl.Buffered(1)),
                unit_spec,
                col_spec,
                col_spec,
            ],
            out_specs=[unit_spec] * 3,
        ),
        compiler_params=pltpu.CompilerParams(vmem_limit_bytes=VMEM_LIMIT),
        cost_estimate=cost("ffn_stage", 4 * rows * model * units, 6 * rows * model),
        name="ffn_stage",
    )(where, second, grad_hidden, w_gate, w_up)


def grad_second_kernel(where_ref, gg_ref, gu_ref, wg_ref, wu_ref, out_ref):
    total = right_dot(gg_ref[...], wg_ref[...]) + right_dot(gu_ref[...], wu_ref[...])
    out_ref[...] = total.astype(jnp.bfloat16)


def grad_second_half(half, name, grads, weights, where):
    rows, units = grads[0].shape
    rows //= 2
    model = weights[0].shape[0]
    block = 512
    left_spec = pl.BlockSpec((rows, units), lambda n, w: (half, 0), pipeline_mode=pl.Buffered(1))
    right_spec = pl.BlockSpec((block, units), lambda n, w: (n, pair_bit(w)))
    return pl.pallas_call(
        grad_second_kernel,
        out_shape=jax.ShapeDtypeStruct((rows, model), jnp.bfloat16),
        grid_spec=pltpu.PrefetchScalarGridSpec(
            num_scalar_prefetch=1,
            grid=(model // block,),
            in_specs=[left_spec] * 2 + [right_spec] * 2,
            out_specs=pl.BlockSpec((rows, block), lambda n, w: (0, n)),
        ),
        compiler_params=pltpu.CompilerParams(vmem_limit_bytes=VMEM_LIMIT),
        cost_estimate=cost(name, 4 * rows * units * model, 4 * rows * model),
        name=name,
    )(where, *grads, *weights)


def ffn_out_kernel(where_ref, hid_ref, wd_ref, keep_ref, send_ref):
    total = dot(hid_ref[...], wd_ref[...])
    half = keep_ref.shape[0]
    keep_ref[...] = total[:half].astype(jnp.bfloat16)
    send_ref[...] = total[half:].astype(jnp.bfloat16)


def unit_sum(kernel, name, lefts, rights, transposed, where):
    rows, units = lefts[0].shape
    model = rights[0].shape[0 if transposed else 1]
    block = 512
    if transposed:
        right_spec = pl.BlockSpec((block, units), lambda n, w: (n, pair_bit(w)))
    else:
        right_spec = pl.BlockSpec((units, block), lambda n, w: (pair_bit(w), n))
    left_spec = pl.BlockSpec((rows, units), lambda n, w: (0, 0), pipeline_mode=pl.Buffered(1))
    half = jax.ShapeDtypeStruct((rows // 2, model), jnp.bfloat16)
    half_spec = pl.BlockSpec((rows // 2, block), lambda n, w: (0, n))
    return pl.pallas_call(
        kernel,
        out_shape=(half, half),
        grid_spec=pltpu.PrefetchScalarGridSpec(
            num_scalar_prefetch=1,
            grid=(model // block,),
            in_specs=[left_spec] * len(lefts) + [right_spec] * len(rights),
            out_specs=[half_spec, half_spec],
        ),
        compiler_params=pltpu.CompilerParams(vmem_limit_bytes=VMEM_LIMIT),
        cost_estimate=cost(name, 2 * len(lefts) * rows * units * model, 4 * rows * model),
        name=name,
    )(where, *lefts, *rights)


def share_spot(spot, count, swap_bits):
    if swap_bits:
        return (spot & 1) * (count // 2) + lax.shift_right_logical(spot, 1)
    return spot


def shares_kernel(left_count, swap_bits, pairs, where_ref, *refs):
    lefts, refs = refs[:left_count], refs[left_count:]
    rights, (keep_ref, send_ref) = refs[:-2], refs[-2:]
    share = keep_ref.shape[1]
    step = pl.program_id(0)
    pieces = [left_dot(lefts[l][...], rights[r][...]) for l, r in pairs]
    per_step = lefts[0].shape[1] // share
    if per_step == 1:
        value = jnp.concatenate(pieces, axis=1).astype(keep_ref.dtype)
        sends = step < pl.num_programs(0) // 2

        @pl.when(sends)
        def _():
            send_ref[0] = value

        @pl.when(jnp.logical_not(sends))
        def _():
            keep_ref[0] = value

        return
    for k in range(per_step):
        rows = slice(k * share, (k + 1) * share)
        value = jnp.concatenate([piece[rows] for piece in pieces], axis=1)
        index = step * per_step + k
        put_share(value, index, where_ref[0] & 1, keep_ref, send_ref, swap_bits)


def weight_shares(name, lefts, rights, pairs, ctx_count, swap_bits, where):
    rows, model = lefts[0].shape
    block = 256
    share, half = model // ctx_count, ctx_count // 2
    width = sum(rights[r].shape[1] for _, r in pairs)
    shares = jax.ShapeDtypeStruct((half, share, width), jnp.bfloat16)
    if share == block:

        def left_map(i, w):
            mine = w[0] & 1
            return 0, jnp.where(i < half, 2 * i + 1 - mine, 2 * (i - half) + mine)

        left_spec = pl.BlockSpec((rows, block), left_map)
        spot = lambda index: share_spot(index, half, swap_bits)
        keep_spec = pl.BlockSpec(
            (1, share, width), lambda i, w: (spot(jnp.maximum(i - half, 0)), 0, 0)
        )
        send_spec = pl.BlockSpec(
            (1, share, width), lambda i, w: (spot(jnp.minimum(i, half - 1)), 0, 0)
        )
    else:
        left_spec = pl.BlockSpec((rows, block), lambda i, w: (0, i))
        keep_spec = send_spec = pl.BlockSpec(shares.shape, lambda i, w: (0, 0, 0))
    return pl.pallas_call(
        functools.partial(shares_kernel, len(lefts), swap_bits, pairs),
        out_shape=(shares, shares),
        grid_spec=pltpu.PrefetchScalarGridSpec(
            num_scalar_prefetch=1,
            grid=(model // block,),
            in_specs=[left_spec] * len(lefts)
            + [
                pl.BlockSpec(r.shape, lambda i, w: (0, 0), pipeline_mode=pl.Buffered(1))
                for r in rights
            ],
            out_specs=[keep_spec, send_spec],
        ),
        compiler_params=pltpu.CompilerParams(vmem_limit_bytes=VMEM_LIMIT),
        cost_estimate=cost(name, 2 * rows * model * width, 4 * rows * model),
        name=name,
    )(where, *lefts, *rights)


def unit_shares_kernel(where_ref, left_ref, right_ref, out_ref):
    share = out_ref.shape[1]
    total = left_dot(left_ref[...], right_ref[...]).astype(out_ref.dtype)
    per_step = left_ref.shape[1] // share
    if out_ref.shape[0] == 1:
        out_ref[0] = total
    else:
        for k in range(per_step):
            index = pl.program_id(0) * per_step + k
            out_ref[pl.ds(unit_spot(index, out_ref.shape[0]), 1)] = total[k * share : (k + 1) * share][None]


def unit_spot(index, ctx_count):
    return (index & 1) * (ctx_count // 2) + lax.shift_right_logical(index, 1)


def unit_shares(name, left, right, ctx_count, where):
    rows, model = left.shape
    block, width = 256, right.shape[1]
    share = model // ctx_count
    shares = jax.ShapeDtypeStruct((ctx_count, share, width), jnp.bfloat16)
    if share == block:
        out_spec = pl.BlockSpec((1, share, width), lambda i, w: (unit_spot(i, ctx_count), 0, 0))
    else:
        out_spec = pl.BlockSpec(shares.shape, lambda i, w: (0, 0, 0))
    return pl.pallas_call(
        unit_shares_kernel,
        out_shape=shares,
        grid_spec=pltpu.PrefetchScalarGridSpec(
            num_scalar_prefetch=1,
            grid=(model // block,),
            in_specs=[
                pl.BlockSpec((rows, block), lambda i, w: (0, i)),
                pl.BlockSpec(right.shape, lambda i, w: (0, 0), pipeline_mode=pl.Buffered(1)),
            ],
            out_specs=out_spec,
        ),
        compiler_params=pltpu.CompilerParams(vmem_limit_bytes=VMEM_LIMIT),
        cost_estimate=cost(name, 2 * rows * model * width, 4 * rows * model),
        name=name,
    )(where, left, right)


def tail_kernel(kv_heads, where_ref, *refs):
    sums, refs = refs[: 2 * kv_heads], refs[2 * kv_heads :]
    cos_ref, sin_ref, refs = refs[0], refs[1], refs[2:]
    gq_refs, refs = refs[:kv_heads], refs[kv_heads:]
    wq_ref, wk_ref, wv_ref, keep_ref, send_ref, gkv_ref = refs
    cosine, sine = cos_ref[...], sin_ref[...]
    for h in range(kv_heads):
        total = sums[2 * h][...].astype(jnp.float32) + sums[2 * h + 1][...].astype(jnp.float32)
        total = total.astype(jnp.bfloat16)
        key = unrotate(total[:, :HEAD_SIZE].astype(jnp.float32), cosine, sine)
        cols = slice(h * HEAD_SIZE, (h + 1) * HEAD_SIZE)
        gkv_ref[:, cols] = key.astype(jnp.bfloat16)
        cols = slice((kv_heads + h) * HEAD_SIZE, (kv_heads + h + 1) * HEAD_SIZE)
        gkv_ref[:, cols] = total[:, HEAD_SIZE:]
    half = keep_ref.shape[0]
    key_width = kv_heads * HEAD_SIZE
    wide = gq_refs[0].shape[1]
    for n in range(0, wq_ref.shape[0], 512):
        span = slice(n, n + 512)
        total = right_dot(gkv_ref[:, :key_width], wk_ref[span, :])
        total += right_dot(gkv_ref[:, key_width:], wv_ref[span, :])
        for h in range(kv_heads):
            total += right_dot(gq_refs[h][...], wq_ref[span, h * wide : (h + 1) * wide])
        total = total.astype(jnp.bfloat16)
        keep_ref[:, span] = total[:half]
        send_ref[:, span] = total[half:]


def tail_stage(kv_sums, cosine, sine, grad_queries, wq, wk, wv, where):
    rows, model = cosine.shape[0], wq.shape[0]
    kv_heads = len(grad_queries)
    vmem = pl.BlockSpec(memory_space=pltpu.VMEM)
    half = jax.ShapeDtypeStruct((rows // 2, model), jnp.bfloat16)
    flat = [term for sums in kv_sums for term in sums]
    return pl.pallas_call(
        functools.partial(tail_kernel, kv_heads),
        out_shape=(
            half,
            half,
            jax.ShapeDtypeStruct((rows, 2 * kv_heads * HEAD_SIZE), jnp.bfloat16),
        ),
        in_specs=[pl.BlockSpec(memory_space=pltpu.SMEM)]
        + [vmem] * (len(flat) + 2 + kv_heads + 3),
        out_specs=[vmem] * 3,
        compiler_params=pltpu.CompilerParams(vmem_limit_bytes=VMEM_LIMIT),
        cost_estimate=cost("tail_stage", 2 * rows * model * (wq.shape[1] + 2 * wk.shape[1]), 4 * rows * model + 4 * wq.size
        ),
        name="tail_stage",
    )(where, *flat, cosine, sine, *grad_queries, wq, wk, wv)


def flip(value, axis, mask=1):
    return lax.ppermute(value, axis, [(i, i ^ mask) for i in range(lax.axis_size(axis))])


def ctx_flip(value, mask):
    if mask == 1:
        return flip(value, "x")
    if mask == 2:
        return flip(value, "l")
    return flip(value, "hi", mask // 4)


def add(left, right):
    return (left.astype(jnp.float32) + right.astype(jnp.float32)).astype(jnp.bfloat16)


def slots_of(value, tensor):
    rows = value.shape[0] // SLOTS
    return [
        lax.dynamic_slice_in_dim(value, (tensor ^ SLOT_XOR[u]) * rows, rows)
        for u in range(SLOTS)
    ]


def after(dep, *values):
    deps = dep if isinstance(dep, tuple) else (dep,)
    held = lax.optimization_barrier(deps + values)[len(deps) :]
    return held[0] if len(held) == 1 else held


class Stages:
    def __init__(self, block_order):
        self.live = block_order[0] >= 0

    def __call__(self, function, *args):
        shapes = jax.eval_shape(function, *args)
        empty = lambda *_: jax.tree.map(lambda a: jnp.zeros(a.shape, a.dtype), shapes)
        return lax.cond(self.live, function, empty, *args)


def gather_pair(own):
    partner = ctx_flip(own, 2)
    near = jnp.concatenate([own, partner, flip(own, "y"), flip(partner, "y")])
    return jnp.concatenate([near, flip(near, "core")])


def gather_slots(own):
    near = jnp.concatenate([own, flip(own, "y")])
    return near, flip(near, "core")


def place_rows(own, near, core, far, tensor):
    rows = own.shape[0]
    result = jnp.zeros((SLOTS * rows,) + own.shape[1:], own.dtype)
    for u, piece in enumerate((own, near, core, far)):
        result = lax.dynamic_update_slice_in_dim(
            result, piece, (tensor ^ SLOT_XOR[u]) * rows, 0
        )
    return result


def scatter_slots(keep, send, fill=lambda value: value):
    got = fill(flip(send, "core"))
    quarter = keep.shape[0] // 2
    far = flip(add(keep[quarter:], got[quarter:]), "y")
    return add(keep[:quarter], got[:quarter]), far


def pair_scatter(keep, send, fill=lambda near: near):
    got = fill(flip(send, "core"))
    n = keep.shape[0] // 4
    near = [add(keep[k * n : (k + 1) * n], got[k * n : (k + 1) * n]) for k in range(4)]
    far = flip(near[3], "y")
    got = flip(near[2], "y")
    return near, far, got


def pair_finish(near, far, got):
    away = add(near[1], far)
    return near[0], got, ctx_flip(away, 2), away


def total(terms):
    return sum(term.astype(jnp.float32) for term in terms)


class Reduce:
    def __init__(self, keep, send):
        self.keep, self.got = keep, ctx_flip(send, 1)

    def halve(self, mask, ctx, dep=None):
        keep, got = self.keep, self.got
        if dep is not None:
            keep, got = after(dep, keep, got)
        n = keep.shape[0] // 2
        bit = lax.div(ctx, mask) % 2
        pick = lambda value, index: lax.dynamic_slice_in_dim(value, index * n, n, 0)
        away = ctx_flip(add(pick(keep, 1 - bit), pick(got, 1 - bit)), mask)
        self.keep, self.got = add(pick(keep, bit), pick(got, bit)), away

    def sum(self):
        return (self.keep.astype(jnp.float32) + self.got.astype(jnp.float32))[0]


def high_masks(ctx_count):
    masks, mask = [], ctx_count // 2
    while mask >= 4:
        masks.append(mask)
        mask //= 2
    return masks


def unit_sum_over(shares):
    return lax.psum_scatter(shares, ("x", "hi"), scatter_dimension=0, tiled=True)


def split_halves(summed, ctx, dep):
    summed = after(dep, summed)
    pair = lax.div(ctx, 2) % 2
    pick = lambda index: lax.dynamic_index_in_dim(summed, index, 0, keepdims=False)
    return pick(pair), pick(1 - pair)


def join_halves(own, other, ctx):
    pair = lax.div(ctx, 2) % 2
    low, high = jnp.where(pair == 0, own, other), jnp.where(pair == 0, other, own)
    return jnp.concatenate([low, high], axis=1).astype(jnp.float32)


class KvReduce:
    def __init__(self, keep, got):
        self.keep, self.got = keep, got

    def merge(self, dep):
        keep, got = after(dep, self.keep, self.got)
        n = keep.shape[0] // 2
        return add(keep[:n], got[:n]), add(keep[n:], got[n:])


def norm_back(grad_out, normed, inv_scale, gain):
    scaled = grad_out * gain
    inner = jnp.mean(scaled * normed, axis=-1, keepdims=True)
    return (inv_scale * (scaled - normed * inner), jnp.sum(grad_out * normed, axis=0))


def body(
    layer_input,
    attn_gain,
    w_query,
    key_matrix,
    value_matrix,
    w_out,
    ffn_gain,
    w_gate,
    w_up,
    w_down,
    cotangent,
    block_order,
    cont_prompt,
):
    ctx_count = lax.axis_size("hi") * 4
    ctx = (lax.axis_index("hi") * 2 + lax.axis_index("l")) * 2 + lax.axis_index("x")
    tensor = lax.axis_index("y") * 2 + lax.axis_index("core")
    where = jnp.stack([ctx, tensor]).astype(jnp.int32)
    quarter = layer_input.shape[0] // SLOTS
    kv_heads = key_matrix.shape[1] // HEAD_SIZE
    highs = high_masks(ctx_count)

    stage = Stages(block_order)
    cot_own = lax.dynamic_slice_in_dim(cotangent, tensor * quarter, quarter)
    cot_slots = slots_of(cotangent, tensor)
    cot_part = ctx_flip(cot_own, 2)
    first_input, queries, kv_local, cosine, sine = input_stage(
        layer_input, attn_gain, w_query, key_matrix, value_matrix, block_order, cont_prompt, where
    )
    def first_keys(kv):
        high = {0: kv}
        for bit in reversed(highs):
            for mask in list(high):
                high[mask + bit] = ctx_flip(high[mask], bit)
        del high[0]
        return high, ctx_flip(kv, 2), ctx_flip(kv, 1)

    def second_keys(high, low, cot):
        return (
            ctx_flip(low, 1),
            flip(cot, "y"),
            {mask: ctx_flip(value, 2) for mask, value in high.items()},
            {mask: ctx_flip(value, 1) for mask, value in high.items()},
        )

    def third_keys(both, cot):
        return {mask: ctx_flip(value, 1) for mask, value in both.items()}, flip(cot, "core")

    high, part_l, part_x = stage(first_keys, after(cot_part, kv_local))
    part_lx, more, high_l, high_x = stage(second_keys, high, part_l, cot_part)
    cot_part = jnp.concatenate([cot_part, more])
    high_lx, cot_far = stage(third_keys, high_l, cot_part)
    parts = {0: kv_local, 1: part_x, 2: part_l, 3: part_lx}
    for mask in high:
        parts[mask], parts[mask + 1] = high[mask], high_x[mask]
        parts[mask + 2], parts[mask + 3] = high_l[mask], high_lx[mask]
    parts = [parts[mask] for mask in range(ctx_count)]
    cot = jnp.concatenate(
        [cot_slots[0], cot_part[:quarter], cot_slots[1], cot_part[quarter:]]
        + [cot_slots[2], cot_far[:quarter], cot_slots[3], cot_far[quarter:]]
    )
    mixed, log_total, keep, send = attention_forward(
        queries, w_out, parts, block_order, cont_prompt, where
    )
    first_half = flip(send, "core")
    near = add(keep, first_half)
    far = flip(near[quarter:], "y")
    grad_hidden = grad_hidden_stage(after(near, cot), w_down, where)
    own_input = lax.dynamic_slice_in_dim(layer_input, tensor * quarter, quarter)
    own_input = own_input.astype(jnp.float32)
    middle = own_input + total((near[:quarter], after(grad_hidden, far)))
    inv_two = lax.rsqrt(jnp.mean(middle * middle, axis=-1, keepdims=True) + eps_norm)
    normed_two = middle * inv_two
    second = gather_pair((normed_two * ffn_gain).astype(jnp.bfloat16))
    hidden, grad_gate, grad_up = ffn_stage(second, grad_hidden, w_gate, w_up, where)

    down_shares = unit_shares("down_shares", cot, hidden, ctx_count, where)
    down = unit_sum_over(down_shares)
    grads, weights = after(down_shares, grad_gate, grad_up), (w_gate, w_up)
    send = grad_second_half(1, "grad_second_send", grads, weights, where)

    def second_stage(send, grad_gate, grad_up, hidden):
        keep = grad_second_half(0, "grad_second_keep", (grad_gate, grad_up), weights, where)
        near, far, got = pair_scatter(keep, send)
        shares = unit_shares("gate_shares", second, after(near[3], grad_gate), ctx_count, where)
        *terms, away = pair_finish(near, after(shares, far), got)
        halves = unit_sum(
            ffn_out_kernel, "ffn_out", (after(away, hidden),), (w_down,), False, where
        )
        return total(after(halves[0], *terms)), shares, halves

    grad_second, gate_shares, ffn_halves = stage(second_stage, send, *grads, hidden)
    gate = unit_sum_over(gate_shares)

    def branch_stage(grad_second, grad_up, own):
        grad_norm, gain_part = norm_back(grad_second, normed_two, inv_two, ffn_gain)
        grad_middle = own.astype(jnp.float32) + grad_norm
        branch = grad_middle.astype(jnp.bfloat16)
        shares = unit_shares("up_shares", second, after(branch, grad_up), ctx_count, where)
        near = jnp.concatenate([branch, after(shares, flip(branch, "y"))])
        return grad_middle, gain_part, shares, jnp.concatenate([near, flip(near, "core")])

    grad_middle, ffn_gain_part, up_shares, grad_branch = stage(
        branch_stage, grad_second, grad_up, cot_own
    )
    up = unit_sum_over(up_shares)
    backward, kv = [], []
    held = grad_branch
    for head in range(kv_heads):
        backward.append(
            attention_backward(
                head, queries, held, w_out, mixed, log_total, parts, cosine, sine,
                block_order, cont_prompt, where,
            )
        )
        kv.append(KvReduce(backward[-1][1], ctx_flip(backward[-1][2], 1)))
        dep = backward[-1][0]
        if head == 0:
            down_own, down_away = split_halves(down, ctx, dep)
            down_other = ctx_flip(down_away, 2)
            dep = down_own
        held = after(dep, grad_branch)
    grad_queries = [item[0] for item in backward]
    branch_shares = weight_shares(
        "branch_shares",
        (first_input, grad_branch),
        grad_queries + [after(dep, mixed)],
        tuple((0, h) for h in range(kv_heads)) + ((1, kv_heads),),
        ctx_count,
        True,
        where,
    )
    def out_stage(keep, send):
        got = flip(send, "core")
        n = keep.shape[0] // 4
        near = [add(keep[k * n : (k + 1) * n], got[k * n : (k + 1) * n]) for k in range(4)]
        return near[0], near[2], add(near[1], flip(near[3], "y"))

    def first_stage(keep, send, own_input, grad_middle):
        terms = scatter_slots(keep, send)
        inv = lax.rsqrt(jnp.mean(own_input * own_input, axis=-1, keepdims=True) + eps_norm)
        grad_norm, gain_part = norm_back(total(terms), own_input * inv, inv, attn_gain)
        return gain_part, (grad_middle + grad_norm).astype(jnp.bfloat16)

    def row_stage(near, other):
        near = jnp.concatenate([near, other])
        return near, flip(near, "core")

    def gain_stage(gains):
        gains = gains + flip(gains, "core")
        gains = gains + flip(gains, "y")
        for mask in [1, 2] + highs:
            gains = gains + ctx_flip(gains, mask)
        return gains

    dep = branch_shares[0]
    kv = [item.merge(dep) for item in kv]
    dep = tuple(keep for keep, _ in kv)
    sum_down = join_halves(down_own, after(dep, down_other), ctx).T
    dep = sum_down
    got = [ctx_flip(after(dep, value), 2) for _, value in kv]
    branch = Reduce(*after(dep, *branch_shares))
    out_near, out_own, out_away = stage(out_stage, *after(dep, *ffn_halves))
    dep = out_away
    for mask in highs:
        kv = [
            KvReduce(keep, value).merge(dep) for (keep, _), value in zip(kv, got)
        ]
        got = [ctx_flip(value, mask) for _, value in kv]
    dep = tuple(keep for keep, _ in kv)
    gate_own, gate_away = split_halves(gate, ctx, dep)
    dep = gate_own
    gate_other = ctx_flip(after(dep, gate_away), 2)
    out_far, out_got = stage(
        lambda away, own: (ctx_flip(away, 2), flip(own, "y")), *after(dep, out_away, out_own)
    )
    dep = out_far
    branch.halve(2, ctx, dep)
    dep = branch.keep
    output = (middle + total(after(dep, out_near, out_got, out_far))).astype(jnp.bfloat16)
    dep = output
    keep, send, grad_kv = tail_stage(
        [after(dep, keep, value) for (keep, _), value in zip(kv, got)], cosine, sine,
        grad_queries, w_query, key_matrix, value_matrix, where,
    )
    dep = keep
    kv_shares = weight_shares(
        "kv_shares", (first_input,), (after(dep, grad_kv),), ((0, 0),), ctx_count, True, where
    )
    dep = kv_shares[0]
    last = Reduce(*after(dep, *kv_shares))
    attn_gain_part, grad_input = stage(
        first_stage, after(dep, keep), send, own_input, grad_middle
    )
    dep = grad_input
    near = jnp.concatenate([grad_input, output])
    near_other = flip(after(dep, near), "y")
    for mask in highs:
        branch.halve(mask, ctx, dep)
        dep = branch.keep
    sum_gate = join_halves(gate_own, after(dep, gate_other), ctx)
    dep = sum_gate
    last.halve(2, ctx, dep)
    dep = last.keep
    up_own, up_away = split_halves(up, ctx, dep)
    dep = up_own
    up_other = ctx_flip(after(dep, up_away), 2)
    for mask in highs:
        last.halve(mask, ctx, dep)
        dep = last.keep
    near, far = stage(row_stage, near, after(dep, near_other))
    dep = far
    last.keep, last.got = after(dep, last.keep, last.got)
    last_sum = last.sum()
    dep = last_sum
    quarters = [near[n * quarter : (n + 1) * quarter] for n in range(4)]
    quarters += [after(dep, far)[n * quarter : (n + 1) * quarter] for n in range(4)]
    grad_rows, output_rows = [
        place_rows(quarters[k], quarters[k + 2], quarters[k + 4], quarters[k + 6], tensor)
        for k in range(2)
    ]
    dep = (grad_rows, output_rows)
    gains = stage(gain_stage, after(dep, jnp.stack([attn_gain_part, ffn_gain_part])))
    dep = gains
    sum_up = join_halves(up_own, after(dep, up_other), ctx)
    dep = sum_up
    branch.keep, branch.got = after(dep, branch.keep, branch.got)
    branch_sum = branch.sum()
    dep = branch_sum
    grad_input, output = grad_rows, output_rows
    width_q, width_k = w_query.shape[1], key_matrix.shape[1]
    sum_query, sum_out = branch_sum[:, :width_q], branch_sum[:, width_q:].T
    sum_key, sum_value = last_sum[:, :width_k], last_sum[:, width_k:]

    gains = gains.reshape(2, ctx_count * SLOTS, -1)
    gains = lax.dynamic_index_in_dim(gains, ctx * SLOTS + tensor, 1, keepdims=False)
    return (
        output,
        grad_input,
        gains[0],
        sum_query,
        sum_key,
        sum_value,
        sum_out,
        gains[1],
        sum_gate,
        sum_up,
        sum_down,
    )


def solution(mesh):
    rows, heads = ("hi", "l", "x"), ("y", "core")
    split = Mesh(mesh.devices.reshape(-1, 2, 2, 2, 2), rows + heads)
    placed = (
        P(rows, None),
        P(),
        P(None, heads),
        P(None, heads),
        P(None, heads),
        P(heads, None),
        P(),
        P(None, heads),
        P(None, heads),
        P(heads, None),
        P(rows, None),
        P(),
        P(),
    )
    return jax.shard_map(
        body,
        mesh=split,
        in_specs=placed,
        out_specs=(
            P(rows, None),
            P(rows, None),
            P(rows + heads),
            P(rows, heads),
            P(rows, heads),
            P(rows, heads),
            P(heads, rows),
            P(rows + heads),
            P(rows, heads),
            P(rows, heads),
            P(heads, rows),
        ),
        check_vma=False,
    )
```

```python
import functools
import math

import jax
import jax.numpy as jnp
import numpy as np
from jax import lax
from jax.experimental import pallas as pl
from jax.experimental.pallas import tpu as pltpu
from jax.sharding import Mesh
from jax.sharding import PartitionSpec as P

HEAD_SIZE = 128
PROMPT = 2048
CONT_LEN = 256
CONTS = 8
BLOCK = 128
PER_PROMPT = PROMPT // BLOCK
PER_CONT = CONT_LEN // BLOCK
LOG2E = 1.4426950408889634
NEG = -1e30
SLOTS = 4
VMEM_LIMIT = 60 << 20
PAIR_STEPS = (4, 1)

eps_norm = 1e-05
rope_base = 1000000.0

SLOT_XOR = (0, 2, 1, 3)


def plain_dot(left, right):
    return jnp.dot(left, right, preferred_element_type=jnp.float32)


def left_dot(left, right):
    return lax.dot_general(
        left, right, (((0,), (0,)), ((), ())), preferred_element_type=jnp.float32
    )


def right_dot(left, right):
    return lax.dot_general(
        left, right, (((1,), (1,)), ((), ())), preferred_element_type=jnp.float32
    )


def slot_quarter(slot, tensor):
    return ((slot & 1) * 2 + lax.shift_right_logical(slot, 1)) ^ tensor


def stored_block(index, where_ref):
    rank = lax.div(index, SLOTS) ^ where_ref[0]
    return rank * SLOTS + slot_quarter(index & 3, where_ref[1])


def block_plan(order_ref, cont_ref, where_ref, slot):
    count = cont_ref.shape[0]
    prompt_blocks = count // CONTS * PER_PROMPT
    own = order_ref[stored_block(slot, where_ref)]
    is_prompt = own < prompt_blocks
    offset = own - prompt_blocks
    which = jnp.clip(lax.div(offset, PER_CONT), 0, count - 1)
    group = jnp.where(is_prompt, lax.div(own, PER_PROMPT), cont_ref[which])
    inner = jnp.where(is_prompt, lax.rem(own, PER_PROMPT), lax.rem(offset, PER_CONT))
    has_prev = lax.rem(inner, 2)
    pairs = jnp.where(is_prompt, lax.div(inner, 2), PER_PROMPT // 2)
    prev = own - has_prev
    return group * PER_PROMPT, pairs, prev, own, has_prev


def fill_inverse(order_ref, where_ref, inverse_ref):
    def put(index, carry):
        inverse_ref[order_ref[stored_block(index, where_ref)]] = index
        return carry

    lax.fori_loop(0, order_ref.shape[0], put, 0)


def rotate(vec, cosine, sine):
    return vec * cosine + pltpu.roll(vec, HEAD_SIZE // 2, 1) * sine


def unrotate(vec, cosine, sine):
    return vec * cosine + pltpu.roll(vec * sine, HEAD_SIZE // 2, 1)


def angle_tables():
    half = HEAD_SIZE // 2
    freq = np.float64(rope_base) ** (-(2.0 * np.arange(half) / HEAD_SIZE))
    freq = np.concatenate([freq, freq])
    starts = np.arange(-(-(PER_PROMPT + PER_CONT) // 8) * 8) * BLOCK
    start = starts[:, None] * freq[None]
    inner = np.arange(BLOCK)[:, None] * freq[None]
    return tuple(
        f(a).astype(np.float32) for a in (start, inner) for f in (np.cos, np.sin)
    )


def key_rows(inverse_ref, logical):
    return pl.ds(pl.multiple_of(inverse_ref[logical] * BLOCK, BLOCK), BLOCK)


def tile_pair(ref, rows_a, rows_b, column):
    return tile(ref, (rows_a, rows_b), column)


def tile(ref, rows, column):
    cols = pl.ds(column, HEAD_SIZE)
    return jnp.concatenate([ref[span, cols] for span in rows], axis=0)


def own_mask(has_prev, rep):
    shape = (2 * BLOCK, rep * BLOCK)
    row = lax.broadcasted_iota(jnp.int32, shape, 0)
    col = lax.broadcasted_iota(jnp.int32, shape, 1)
    first_row = BLOCK * (1 - has_prev)
    return (row >= first_row) & (row - BLOCK <= lax.rem(col, BLOCK))


def stack_t(ref, rows, column, rep):
    return jnp.concatenate(
        [ref[rows, pl.ds(column + r * HEAD_SIZE, HEAD_SIZE)].T for r in range(rep)], axis=1
    )


def stack_rows(ref, rows, column, rep):
    return jnp.concatenate(
        [ref[rows, pl.ds(column + r * HEAD_SIZE, HEAD_SIZE)] for r in range(rep)], axis=0
    )


def dot(left, right):
    return jnp.dot(left, right, preferred_element_type=jnp.float32)


def start_parts(parts, buffer_ref, sem, column):
    rows, width = parts[0].shape[0], buffer_ref.shape[1]
    copies = [
        pltpu.make_async_copy(
            part.at[:, pl.ds(column, width)], buffer_ref.at[pl.ds(p * rows, rows), :], sem.at[p]
        )
        for p, part in enumerate(parts)
    ]
    for copy in copies:
        copy.start()
    return copies


def forward_kernel(rep, hps, ctx_count, order_ref, cont_ref, where_ref, q_ref, wo_ref, *refs):
    parts, refs = refs[:ctx_count], refs[ctx_count:]
    out_ref, lse_ref, keep_ref, send_ref, kv_ref, inverse_ref, qt_ref, acc_ref, sem = refs
    copies = start_parts(parts, kv_ref, sem, 0)
    fill_inverse(order_ref, where_ref, inverse_ref)
    for copy in copies:
        copy.wait()
    q_blocks = q_ref.shape[0] // BLOCK
    factor = LOG2E / math.sqrt(HEAD_SIZE)
    width = rep * HEAD_SIZE

    def one_query_block(qb, carry):
        base, pairs, prev, own, has_prev = block_plan(order_ref, cont_ref, where_ref, qb)
        rows = pl.ds(pl.multiple_of(qb * BLOCK, BLOCK), BLOCK)
        mask = own_mask(has_prev, rep)
        rows_a, rows_b = key_rows(inverse_ref, prev), key_rows(inverse_ref, own)
        state = []
        for h in range(hps):
            qt = stack_t(q_ref, rows, h * width, rep)
            qt_ref[h] = qt
            scores = dot(tile_pair(kv_ref, rows_a, rows_b, 2 * h * HEAD_SIZE), qt) * factor
            scores = jnp.where(mask, scores, NEG)
            best = jnp.max(scores, axis=0, keepdims=True)
            weights = jnp.exp2(scores - best)
            total = jnp.sum(weights, axis=0, keepdims=True)
            values = tile_pair(kv_ref, rows_a, rows_b, (2 * h + 1) * HEAD_SIZE)
            acc_ref[h] = dot(values.T, weights.astype(jnp.bfloat16))
            state += [best, total]

        def fold(first, count, state):
            rows = [key_rows(inverse_ref, first + n) for n in range(count)]
            after = []
            for h in range(hps):
                best, total = state[2 * h], state[2 * h + 1]
                keys = tile(kv_ref, rows, 2 * h * HEAD_SIZE)
                scores = dot(keys, qt_ref[h]) * factor
                newest = jnp.maximum(best, jnp.max(scores, axis=0, keepdims=True))
                weights = jnp.exp2(scores - newest)
                shrink = jnp.exp2(best - newest)
                total = total * shrink + jnp.sum(weights, axis=0, keepdims=True)
                values = tile(kv_ref, rows, (2 * h + 1) * HEAD_SIZE)
                acc_ref[h] = acc_ref[h] * shrink + dot(values.T, weights.astype(jnp.bfloat16))
                after += [newest, total]
            return tuple(after)

        state, done = tuple(state), 0
        for wide in PAIR_STEPS:
            upto = lax.div(pairs, wide) * wide
            state = lax.fori_loop(
                0,
                lax.div(upto - done, wide),
                lambda t, state, done=done, wide=wide: fold(
                    base + 2 * (done + wide * t), 2 * wide, state
                ),
                state,
            )
            done = upto
        for h in range(hps):
            best, total = state[2 * h], state[2 * h + 1]
            mixed = acc_ref[h] * (1.0 / total)
            for r in range(rep):
                part = mixed[:, r * BLOCK : (r + 1) * BLOCK]
                out_ref[rows, pl.ds(h * width + r * HEAD_SIZE, HEAD_SIZE)] = part.T.astype(
                    jnp.bfloat16
                )
            lse_ref[h, pl.ds(qb, 1), :] = best + jnp.log2(total)
        return carry

    lax.fori_loop(0, q_blocks, one_query_block, 0)
    mixed = out_ref[...]
    half = keep_ref.shape[0]
    for n in range(0, wo_ref.shape[1], 512):
        cols = slice(n, n + 512)
        partial = dot(mixed, wo_ref[:, cols]).astype(jnp.bfloat16)
        keep_ref[:, cols] = partial[:half]
        send_ref[:, cols] = partial[half:]


def backward_kernel(rep, hps, ctx_count, head, order_ref, cont_ref, where_ref, q_ref, gb_ref, wo_ref,
                    mix_ref, lse_ref, cos_ref, sin_ref, *refs):
    parts, refs = refs[:ctx_count], refs[ctx_count:]
    gq_ref, keep_ref, send_ref = refs[:3]
    kv_ref, gm_ref, inverse_ref, qt_ref, gmt_ref, gqt_ref, acc_ref, sem = refs[3:]
    copies = start_parts(parts, kv_ref, sem, head * kv_ref.shape[1])
    fill_inverse(order_ref, where_ref, inverse_ref)
    gm_ref[...] = right_dot(gb_ref[...], wo_ref[...]).astype(jnp.bfloat16)
    for copy in copies:
        copy.wait()
    q_blocks = q_ref.shape[0] // BLOCK
    scale = 1.0 / math.sqrt(HEAD_SIZE)
    factor = LOG2E * scale
    width = rep * HEAD_SIZE

    def clear(i, carry):
        acc_ref[pl.ds(pl.multiple_of(i * BLOCK, BLOCK), BLOCK), :] = jnp.zeros(
            (BLOCK, acc_ref.shape[1]), jnp.float32
        )
        return carry

    lax.fori_loop(0, order_ref.shape[0], clear, 0)

    def tile_terms(h, spans, lse, delta, q_rows, gm_rows, mask):
        kcol, vcol = 2 * h * HEAD_SIZE, (2 * h + 1) * HEAD_SIZE
        keys = tile(kv_ref, spans, kcol)
        values = tile(kv_ref, spans, vcol)
        weights = jnp.exp2(dot(keys, qt_ref[h]) * factor - lse)
        if mask is not None:
            weights = jnp.where(mask, weights, 0.0)
        grad_weights = dot(values, gmt_ref[h])
        grad_scores = (weights * (grad_weights - delta)).astype(jnp.bfloat16)
        gv = dot(weights.astype(jnp.bfloat16), gm_rows)
        gk = dot(grad_scores, q_rows)
        for n, span in enumerate(spans):
            piece = slice(n * BLOCK, (n + 1) * BLOCK)
            acc_ref[span, pl.ds(kcol, HEAD_SIZE)] += gk[piece]
            acc_ref[span, pl.ds(vcol, HEAD_SIZE)] += gv[piece]
        return dot(keys.T, grad_scores)

    def one_query_block(qb, carry):
        base, pairs, prev, own, has_prev = block_plan(order_ref, cont_ref, where_ref, qb)
        rows = pl.ds(pl.multiple_of(qb * BLOCK, BLOCK), BLOCK)
        mask = own_mask(has_prev, rep)
        rows_a, rows_b = key_rows(inverse_ref, prev), key_rows(inverse_ref, own)
        deltas, lses, q_stack, gm_stack = [], [], [], []
        for h in range(hps):
            qt_ref[h] = stack_t(q_ref, rows, h * width, rep)
            gmt = stack_t(gm_ref, rows, h * width, rep)
            gmt_ref[h] = gmt
            mixt = stack_t(mix_ref, rows, h * width, rep)
            deltas.append(
                jnp.sum(
                    gmt.astype(jnp.float32) * mixt.astype(jnp.float32), axis=0, keepdims=True
                )
            )
            lses.append(lse_ref[h, pl.ds(qb, 1), :])
        for h in range(hps):
            q_rows = stack_rows(q_ref, rows, h * width, rep)
            gm_rows = stack_rows(gm_ref, rows, h * width, rep)
            gqt_ref[h] = tile_terms(
                h, (rows_a, rows_b), lses[h], deltas[h], q_rows, gm_rows, mask
            )

        def fold(first, count):
            spans = [key_rows(inverse_ref, first + n) for n in range(count)]
            for h in range(hps):
                q_rows = stack_rows(q_ref, rows, h * width, rep)
                gm_rows = stack_rows(gm_ref, rows, h * width, rep)
                gqt_ref[h] += tile_terms(
                    h, spans, lses[h], deltas[h], q_rows, gm_rows, None
                )
            return 0

        done = 0
        for wide in PAIR_STEPS:
            upto = lax.div(pairs, wide) * wide
            lax.fori_loop(
                0,
                lax.div(upto - done, wide),
                lambda t, _, done=done, wide=wide: fold(base + 2 * (done + wide * t), 2 * wide),
                0,
            )
            done = upto
        for h in range(hps):
            total = gqt_ref[h] * scale
            for r in range(rep):
                part = total[:, r * BLOCK : (r + 1) * BLOCK]
                rounded = part.T.astype(jnp.bfloat16).astype(jnp.float32)
                gq_ref[rows, pl.ds(h * width + r * HEAD_SIZE, HEAD_SIZE)] = unrotate(
                    rounded, cos_ref[rows, :], sin_ref[rows, :]
                ).astype(jnp.bfloat16)
        return carry

    lax.fori_loop(0, q_blocks, one_query_block, 0)

    blocks = order_ref.shape[0]

    def place(index):
        chunk = lax.div(index, SLOTS)
        spot = (chunk & 1) * (ctx_count // 2) + (chunk & 2) // 2 * (ctx_count // 4) + (
            lax.shift_right_logical(chunk, 2)
        )
        return spot * SLOTS + (index & 3)

    def flush(i, carry):
        rows = pl.ds(pl.multiple_of(i * BLOCK, BLOCK), BLOCK)
        spot = place(i)
        parts = []
        for h in range(hps):
            parts.append(acc_ref[rows, pl.ds(2 * h * HEAD_SIZE, HEAD_SIZE)] * scale)
            parts.append(acc_ref[rows, pl.ds((2 * h + 1) * HEAD_SIZE, HEAD_SIZE)])
        value = jnp.concatenate(parts, axis=1).astype(jnp.bfloat16)

        @pl.when(spot < blocks // 2)
        def _():
            keep_ref[pl.ds(pl.multiple_of(spot * BLOCK, BLOCK), BLOCK), :] = value

        @pl.when(spot >= blocks // 2)
        def _():
            far = (spot - blocks // 2) * BLOCK
            send_ref[pl.ds(pl.multiple_of(far, BLOCK), BLOCK), :] = value

        return carry

    lax.fori_loop(0, blocks, flush, 0)


def attention_forward(q, w_out, parts, order, cont, where):
    ctx_count = len(parts)
    rows, tokens = q.shape[0], ctx_count * q.shape[0]
    kv_heads = parts[0].shape[1] // (2 * HEAD_SIZE)
    rep = q.shape[1] // HEAD_SIZE // kv_heads
    q_blocks, model = rows // BLOCK, w_out.shape[1]
    vmem, smem, any_ = (
        pl.BlockSpec(memory_space=space) for space in (pltpu.VMEM, pltpu.SMEM, pl.ANY)
    )
    flops = 2 * rows * tokens * q.shape[1] + 2 * rows * q.shape[1] * model
    half = jax.ShapeDtypeStruct((rows // 2, model), jnp.bfloat16)
    return pl.pallas_call(
        functools.partial(forward_kernel, rep, kv_heads, ctx_count),
        out_shape=(
            jax.ShapeDtypeStruct(q.shape, jnp.bfloat16),
            jax.ShapeDtypeStruct((kv_heads, q_blocks, rep * BLOCK), jnp.float32),
            half,
            half,
        ),
        in_specs=[smem] * 3 + [vmem] * 2 + [any_] * ctx_count,
        out_specs=[vmem] * 4,
        scratch_shapes=[
            pltpu.VMEM((tokens, parts[0].shape[1]), jnp.bfloat16),
            pltpu.SMEM((order.shape[0],), jnp.int32),
            pltpu.VMEM((kv_heads, HEAD_SIZE, rep * BLOCK), jnp.bfloat16),
            pltpu.VMEM((kv_heads, HEAD_SIZE, rep * BLOCK), jnp.float32),
            pltpu.SemaphoreType.DMA((ctx_count,)),
        ],
        compiler_params=pltpu.CompilerParams(vmem_limit_bytes=VMEM_LIMIT),
        cost_estimate=cost("attention_forward", flops, 2 * tokens * parts[0].shape[1] + 4 * rows * model),
        name="attention_forward",
    )(order, cont, where, q, w_out, *parts)


def attention_backward(head, q, grad_branch, w_out, mixed, lse, parts, cosine, sine, order, cont,
                       where):
    ctx_count = len(parts)
    rows, tokens = q.shape[0], ctx_count * q.shape[0]
    kv_heads = parts[0].shape[1] // (2 * HEAD_SIZE)
    rep = q.shape[1] // HEAD_SIZE // kv_heads
    q_blocks, model = rows // BLOCK, w_out.shape[1]
    wide = rep * HEAD_SIZE
    q_spec = pl.BlockSpec((rows, wide), lambda g, *_: (0, head))
    whole = lambda g, *_: (0, 0)
    table_spec = pl.BlockSpec((rows, HEAD_SIZE), whole)
    half = (tokens // 2, 2 * HEAD_SIZE)
    flops = 5 * rows * tokens * wide + 2 * rows * wide * model
    return pl.pallas_call(
        functools.partial(backward_kernel, rep, 1, ctx_count, head),
        out_shape=(
            jax.ShapeDtypeStruct((rows, wide), jnp.bfloat16),
            jax.ShapeDtypeStruct(half, jnp.bfloat16),
            jax.ShapeDtypeStruct(half, jnp.bfloat16),
        ),
        grid_spec=pltpu.PrefetchScalarGridSpec(
            num_scalar_prefetch=3,
            grid=(1,),
            in_specs=[
                q_spec,
                pl.BlockSpec((rows, model), whole),
                pl.BlockSpec((wide, model), lambda g, *_: (head, 0)),
                q_spec,
                pl.BlockSpec((1, q_blocks, rep * BLOCK), lambda g, *_: (head, 0, 0)),
                table_spec,
                table_spec,
            ]
            + [pl.BlockSpec(memory_space=pl.ANY)] * ctx_count,
            out_specs=[
                pl.BlockSpec((rows, wide), whole),
                pl.BlockSpec(half, whole),
                pl.BlockSpec(half, whole),
            ],
            scratch_shapes=[
                pltpu.VMEM((tokens, 2 * HEAD_SIZE), jnp.bfloat16),
                pltpu.VMEM((rows, wide), jnp.bfloat16),
                pltpu.SMEM((order.shape[0],), jnp.int32),
                pltpu.VMEM((1, HEAD_SIZE, rep * BLOCK), jnp.bfloat16),
                pltpu.VMEM((1, HEAD_SIZE, rep * BLOCK), jnp.bfloat16),
                pltpu.VMEM((1, HEAD_SIZE, rep * BLOCK), jnp.float32),
                pltpu.VMEM((tokens, 2 * HEAD_SIZE), jnp.float32),
                pltpu.SemaphoreType.DMA((ctx_count,)),
            ],
        ),
        compiler_params=pltpu.CompilerParams(vmem_limit_bytes=VMEM_LIMIT),
        cost_estimate=cost(f"attention_backward_{head}", flops, 4 * tokens * wide + 2 * rows * model),
        name=f"attention_backward_{head}",
    )(order, cont, where, q, grad_branch, w_out, mixed, lse, cosine, sine, *parts)


def input_kernel(order_ref, cont_ref, where_ref, gain_ref, x_hbm, wq_hbm, wk_hbm, wv_hbm, table_hbm,
                 first_ref, q_ref, kv_ref, cos_ref, sin_ref,
                 x_ref, wq_ref, wk_ref, wv_ref, table_ref, sem):
    pairs = ((x_hbm, x_ref), (table_hbm, table_ref), (wk_hbm, wk_ref), (wv_hbm, wv_ref),
             (wq_hbm, wq_ref))
    copies = [
        pltpu.make_async_copy(source, target, sem.at[n])
        for n, (source, target) in enumerate(pairs)
    ]
    for copy in copies:
        copy.start()
    count = cont_ref.shape[0]
    prompt_blocks = count // CONTS * PER_PROMPT
    starts = (table_ref.shape[0] - 2 * BLOCK) // 2
    lane = lax.broadcasted_iota(jnp.int32, (BLOCK, HEAD_SIZE), 1)
    copies[0].wait()
    copies[1].wait()

    def one_slot(slot, carry):
        quarter = slot_quarter(slot, where_ref[1])
        rows = pl.ds(pl.multiple_of(slot * BLOCK, BLOCK), BLOCK)
        full = x_ref[pl.ds(pl.multiple_of(quarter * BLOCK, BLOCK), BLOCK), :].astype(jnp.float32)
        inv = lax.rsqrt(jnp.mean(full * full, axis=-1, keepdims=True) + eps_norm)
        first_ref[rows, :] = (full * inv * gain_ref[...]).astype(jnp.bfloat16)
        own = order_ref[stored_block(slot, where_ref)]
        spot = jnp.where(
            own < prompt_blocks,
            lax.rem(own, PER_PROMPT),
            PER_PROMPT + lax.rem(own - prompt_blocks, PER_CONT),
        )
        cos_start = table_ref[pl.ds(2 * BLOCK + spot, 1), :]
        sin_start = table_ref[pl.ds(2 * BLOCK + starts + spot, 1), :]
        cos_in, sin_in = table_ref[:BLOCK, :], table_ref[BLOCK : 2 * BLOCK, :]
        sine = sin_start * cos_in + cos_start * sin_in
        cos_ref[rows, :] = cos_start * cos_in - sin_start * sin_in
        sin_ref[rows, :] = jnp.where(lane < HEAD_SIZE // 2, -sine, sine)
        return carry

    lax.fori_loop(0, SLOTS, one_slot, 0)
    first = first_ref[...]
    cosine, sine = cos_ref[...], sin_ref[...]
    copies[2].wait()
    copies[3].wait()
    keys = dot(first, wk_ref[...])
    values = dot(first, wv_ref[...])
    for h in range(wk_ref.shape[1] // HEAD_SIZE):
        cols = slice(h * HEAD_SIZE, (h + 1) * HEAD_SIZE)
        low, high = 2 * h * HEAD_SIZE, (2 * h + 1) * HEAD_SIZE
        key = rotate(keys[:, cols], cosine, sine)
        kv_ref[:, low:high] = key.astype(jnp.bfloat16)
        kv_ref[:, high : high + HEAD_SIZE] = values[:, cols].astype(jnp.bfloat16)
    copies[4].wait()
    for n in range(0, wq_ref.shape[1], 256):
        queries = dot(first, wq_ref[:, n : n + 256])
        for m in range(0, 256, HEAD_SIZE):
            query = rotate(queries[:, m : m + HEAD_SIZE], cosine, sine)
            q_ref[:, n + m : n + m + HEAD_SIZE] = query.astype(jnp.bfloat16)


def input_stage(x, gain, wq, wk, wv, order, cont, where):
    rows, model = x.shape
    cos_start, sin_start, cos_in, sin_in = angle_tables()
    table = np.concatenate([cos_in, sin_in, cos_start, sin_start])
    vmem, smem, any_ = (
        pl.BlockSpec(memory_space=space) for space in (pltpu.VMEM, pltpu.SMEM, pl.ANY)
    )
    flops = 2 * rows * model * (wq.shape[1] + 2 * wk.shape[1])
    return pl.pallas_call(
        input_kernel,
        out_shape=(
            jax.ShapeDtypeStruct((rows, model), jnp.bfloat16),
            jax.ShapeDtypeStruct((rows, wq.shape[1]), jnp.bfloat16),
            jax.ShapeDtypeStruct((rows, 2 * wk.shape[1]), jnp.bfloat16),
            jax.ShapeDtypeStruct((rows, HEAD_SIZE), jnp.float32),
            jax.ShapeDtypeStruct((rows, HEAD_SIZE), jnp.float32),
        ),
        in_specs=[smem] * 3 + [vmem] + [any_] * 5,
        out_specs=[vmem] * 5,
        scratch_shapes=[
            pltpu.VMEM(a.shape, a.dtype) for a in (x, wq, wk, wv)
        ]
        + [pltpu.VMEM(table.shape, jnp.float32), pltpu.SemaphoreType.DMA((5,))],
        compiler_params=pltpu.CompilerParams(vmem_limit_bytes=VMEM_LIMIT),
        cost_estimate=cost("input_stage", flops, 4 * x.size + 2 * wq.size + 4 * wk.size),
        name="input_stage",
    )(order, cont, where, gain.reshape(1, -1), x, wq, wk, wv, table)


FILLERS = ("ffn_out", "gate_shares", "kv_shares", "grad_hidden")


def cost(name, flops, bytes_accessed):
    scale = 16.0 if name in FILLERS else 0.02
    return pl.CostEstimate(
        flops=int(flops * scale), bytes_accessed=int(bytes_accessed * scale), transcendentals=0
    )


def put_share(value, index, x_bit, keep_ref, send_ref, swap_bits):
    spot = share_spot(lax.shift_right_logical(index, 1), keep_ref.shape[0], swap_bits)
    stays = (index & 1) == x_bit
    value = value.astype(keep_ref.dtype)

    @pl.when(stays)
    def _():
        keep_ref[pl.ds(spot, 1)] = value[None]

    @pl.when(jnp.logical_not(stays))
    def _():
        send_ref[pl.ds(spot, 1)] = value[None]


def pair_bit(where_ref):
    return lax.shift_right_logical(where_ref[0], 1) & 1


def grad_hidden_kernel(where_ref, cot_ref, wd_ref, out_ref):
    out_ref[...] = right_dot(cot_ref[...], wd_ref[...])


def grad_hidden_stage(cot, w_down, where):
    rows, model = cot.shape
    units = w_down.shape[0] // 2
    block = 256
    steps = units // block
    return pl.pallas_call(
        grad_hidden_kernel,
        out_shape=jax.ShapeDtypeStruct((rows, units), jnp.float32),
        grid_spec=pltpu.PrefetchScalarGridSpec(
            num_scalar_prefetch=1,
            grid=(steps,),
            in_specs=[
                pl.BlockSpec((rows, model), lambda i, w: (0, 0), pipeline_mode=pl.Buffered(1)),
                pl.BlockSpec((block, model), lambda i, w: (pair_bit(w) * steps + i, 0)),
            ],
            out_specs=pl.BlockSpec((rows, block), lambda i, w: (0, i)),
        ),
        compiler_params=pltpu.CompilerParams(vmem_limit_bytes=VMEM_LIMIT),
        cost_estimate=cost("grad_hidden", 2 * rows * model * units, 4 * rows * model),
        name="grad_hidden",
    )(where, cot, w_down)


def ffn_kernel(where_ref, in_ref, gh_ref, wg_ref, wu_ref, hid_ref, gg_ref, gu_ref):
    gate = dot(in_ref[...], wg_ref[...])
    upward = dot(in_ref[...], wu_ref[...])
    grad_hidden = gh_ref[...]
    sigma = jax.nn.sigmoid(gate)
    swish = gate * sigma
    hid_ref[...] = (swish * upward).astype(jnp.bfloat16)
    gg_ref[...] = (grad_hidden * upward * sigma * (1.0 + gate * (1.0 - sigma))).astype(
        jnp.bfloat16
    )
    gu_ref[...] = (grad_hidden * swish).astype(jnp.bfloat16)


def ffn_stage(second, grad_hidden, w_gate, w_up, where):
    rows, model = second.shape
    units = w_gate.shape[1] // 2
    block = 256
    steps = units // block
    col_spec = pl.BlockSpec((model, block), lambda i, w: (0, pair_bit(w) * steps + i))
    unit_spec = pl.BlockSpec((rows, block), lambda i, w: (0, i))
    unit = jax.ShapeDtypeStruct((rows, units), jnp.bfloat16)
    return pl.pallas_call(
        ffn_kernel,
        out_shape=(unit, unit, unit),
        grid_spec=pltpu.PrefetchScalarGridSpec(
            num_scalar_prefetch=1,
            grid=(steps,),
            in_specs=[
                pl.BlockSpec((rows, model), lambda i, w: (0, 0), pipeline_mode=pl.Buffered(1)),
                unit_spec,
                col_spec,
                col_spec,
            ],
            out_specs=[unit_spec] * 3,
        ),
        compiler_params=pltpu.CompilerParams(vmem_limit_bytes=VMEM_LIMIT),
        cost_estimate=cost("ffn_stage", 4 * rows * model * units, 6 * rows * model),
        name="ffn_stage",
    )(where, second, grad_hidden, w_gate, w_up)


def grad_second_kernel(where_ref, gg_ref, gu_ref, wg_ref, wu_ref, out_ref):
    total = right_dot(gg_ref[...], wg_ref[...]) + right_dot(gu_ref[...], wu_ref[...])
    out_ref[...] = total.astype(jnp.bfloat16)


def grad_second_half(half, name, grads, weights, where):
    rows, units = grads[0].shape
    rows //= 2
    model = weights[0].shape[0]
    block = 512
    left_spec = pl.BlockSpec((rows, units), lambda n, w: (half, 0), pipeline_mode=pl.Buffered(1))
    right_spec = pl.BlockSpec((block, units), lambda n, w: (n, pair_bit(w)))
    return pl.pallas_call(
        grad_second_kernel,
        out_shape=jax.ShapeDtypeStruct((rows, model), jnp.bfloat16),
        grid_spec=pltpu.PrefetchScalarGridSpec(
            num_scalar_prefetch=1,
            grid=(model // block,),
            in_specs=[left_spec] * 2 + [right_spec] * 2,
            out_specs=pl.BlockSpec((rows, block), lambda n, w: (0, n)),
        ),
        compiler_params=pltpu.CompilerParams(vmem_limit_bytes=VMEM_LIMIT),
        cost_estimate=cost(name, 4 * rows * units * model, 4 * rows * model),
        name=name,
    )(where, *grads, *weights)


def ffn_out_kernel(where_ref, hid_ref, wd_ref, keep_ref, send_ref):
    total = dot(hid_ref[...], wd_ref[...])
    half = keep_ref.shape[0]
    keep_ref[...] = total[:half].astype(jnp.bfloat16)
    send_ref[...] = total[half:].astype(jnp.bfloat16)


def unit_sum(kernel, name, lefts, rights, transposed, where):
    rows, units = lefts[0].shape
    model = rights[0].shape[0 if transposed else 1]
    block = 512
    if transposed:
        right_spec = pl.BlockSpec((block, units), lambda n, w: (n, pair_bit(w)))
    else:
        right_spec = pl.BlockSpec((units, block), lambda n, w: (pair_bit(w), n))
    left_spec = pl.BlockSpec((rows, units), lambda n, w: (0, 0), pipeline_mode=pl.Buffered(1))
    half = jax.ShapeDtypeStruct((rows // 2, model), jnp.bfloat16)
    half_spec = pl.BlockSpec((rows // 2, block), lambda n, w: (0, n))
    return pl.pallas_call(
        kernel,
        out_shape=(half, half),
        grid_spec=pltpu.PrefetchScalarGridSpec(
            num_scalar_prefetch=1,
            grid=(model // block,),
            in_specs=[left_spec] * len(lefts) + [right_spec] * len(rights),
            out_specs=[half_spec, half_spec],
        ),
        compiler_params=pltpu.CompilerParams(vmem_limit_bytes=VMEM_LIMIT),
        cost_estimate=cost(name, 2 * len(lefts) * rows * units * model, 4 * rows * model),
        name=name,
    )(where, *lefts, *rights)


def share_spot(spot, count, swap_bits):
    if swap_bits:
        return (spot & 1) * (count // 2) + lax.shift_right_logical(spot, 1)
    return spot


def shares_kernel(left_count, swap_bits, pairs, where_ref, *refs):
    lefts, refs = refs[:left_count], refs[left_count:]
    rights, (keep_ref, send_ref) = refs[:-2], refs[-2:]
    share = keep_ref.shape[1]
    step = pl.program_id(0)
    pieces = [left_dot(lefts[l][...], rights[r][...]) for l, r in pairs]
    per_step = lefts[0].shape[1] // share
    if per_step == 1:
        value = jnp.concatenate(pieces, axis=1).astype(keep_ref.dtype)
        sends = step < pl.num_programs(0) // 2

        @pl.when(sends)
        def _():
            send_ref[0] = value

        @pl.when(jnp.logical_not(sends))
        def _():
            keep_ref[0] = value

        return
    for k in range(per_step):
        rows = slice(k * share, (k + 1) * share)
        value = jnp.concatenate([piece[rows] for piece in pieces], axis=1)
        index = step * per_step + k
        put_share(value, index, where_ref[0] & 1, keep_ref, send_ref, swap_bits)


def weight_shares(name, lefts, rights, pairs, ctx_count, swap_bits, where):
    rows, model = lefts[0].shape
    block = 256
    share, half = model // ctx_count, ctx_count // 2
    width = sum(rights[r].shape[1] for _, r in pairs)
    shares = jax.ShapeDtypeStruct((half, share, width), jnp.bfloat16)
    if share == block:

        def left_map(i, w):
            mine = w[0] & 1
            return 0, jnp.where(i < half, 2 * i + 1 - mine, 2 * (i - half) + mine)

        left_spec = pl.BlockSpec((rows, block), left_map)
        spot = lambda index: share_spot(index, half, swap_bits)
        keep_spec = pl.BlockSpec(
            (1, share, width), lambda i, w: (spot(jnp.maximum(i - half, 0)), 0, 0)
        )
        send_spec = pl.BlockSpec(
            (1, share, width), lambda i, w: (spot(jnp.minimum(i, half - 1)), 0, 0)
        )
    else:
        left_spec = pl.BlockSpec((rows, block), lambda i, w: (0, i))
        keep_spec = send_spec = pl.BlockSpec(shares.shape, lambda i, w: (0, 0, 0))
    return pl.pallas_call(
        functools.partial(shares_kernel, len(lefts), swap_bits, pairs),
        out_shape=(shares, shares),
        grid_spec=pltpu.PrefetchScalarGridSpec(
            num_scalar_prefetch=1,
            grid=(model // block,),
            in_specs=[left_spec] * len(lefts)
            + [
                pl.BlockSpec(r.shape, lambda i, w: (0, 0), pipeline_mode=pl.Buffered(1))
                for r in rights
            ],
            out_specs=[keep_spec, send_spec],
        ),
        compiler_params=pltpu.CompilerParams(vmem_limit_bytes=VMEM_LIMIT),
        cost_estimate=cost(name, 2 * rows * model * width, 4 * rows * model),
        name=name,
    )(where, *lefts, *rights)


def unit_shares_kernel(where_ref, left_ref, right_ref, out_ref):
    share = out_ref.shape[1]
    total = left_dot(left_ref[...], right_ref[...]).astype(out_ref.dtype)
    per_step = left_ref.shape[1] // share
    if out_ref.shape[0] == 1:
        out_ref[0] = total
    else:
        for k in range(per_step):
            index = pl.program_id(0) * per_step + k
            out_ref[pl.ds(unit_spot(index, out_ref.shape[0]), 1)] = total[k * share : (k + 1) * share][None]


def unit_spot(index, ctx_count):
    return (index & 1) * (ctx_count // 2) + lax.shift_right_logical(index, 1)


def unit_shares(name, left, right, ctx_count, where):
    rows, model = left.shape
    block, width = 256, right.shape[1]
    share = model // ctx_count
    shares = jax.ShapeDtypeStruct((ctx_count, share, width), jnp.bfloat16)
    if share == block:
        out_spec = pl.BlockSpec((1, share, width), lambda i, w: (unit_spot(i, ctx_count), 0, 0))
    else:
        out_spec = pl.BlockSpec(shares.shape, lambda i, w: (0, 0, 0))
    return pl.pallas_call(
        unit_shares_kernel,
        out_shape=shares,
        grid_spec=pltpu.PrefetchScalarGridSpec(
            num_scalar_prefetch=1,
            grid=(model // block,),
            in_specs=[
                pl.BlockSpec((rows, block), lambda i, w: (0, i)),
                pl.BlockSpec(right.shape, lambda i, w: (0, 0), pipeline_mode=pl.Buffered(1)),
            ],
            out_specs=out_spec,
        ),
        compiler_params=pltpu.CompilerParams(vmem_limit_bytes=VMEM_LIMIT),
        cost_estimate=cost(name, 2 * rows * model * width, 4 * rows * model),
        name=name,
    )(where, left, right)


def tail_kernel(kv_heads, where_ref, *refs):
    sums, refs = refs[: 2 * kv_heads], refs[2 * kv_heads :]
    cos_ref, sin_ref, refs = refs[0], refs[1], refs[2:]
    gq_refs, refs = refs[:kv_heads], refs[kv_heads:]
    wq_ref, wk_ref, wv_ref, keep_ref, send_ref, gkv_ref = refs
    cosine, sine = cos_ref[...], sin_ref[...]
    for h in range(kv_heads):
        total = sums[2 * h][...].astype(jnp.float32) + sums[2 * h + 1][...].astype(jnp.float32)
        total = total.astype(jnp.bfloat16)
        key = unrotate(total[:, :HEAD_SIZE].astype(jnp.float32), cosine, sine)
        cols = slice(h * HEAD_SIZE, (h + 1) * HEAD_SIZE)
        gkv_ref[:, cols] = key.astype(jnp.bfloat16)
        cols = slice((kv_heads + h) * HEAD_SIZE, (kv_heads + h + 1) * HEAD_SIZE)
        gkv_ref[:, cols] = total[:, HEAD_SIZE:]
    half = keep_ref.shape[0]
    key_width = kv_heads * HEAD_SIZE
    wide = gq_refs[0].shape[1]
    for n in range(0, wq_ref.shape[0], 512):
        span = slice(n, n + 512)
        total = right_dot(gkv_ref[:, :key_width], wk_ref[span, :])
        total += right_dot(gkv_ref[:, key_width:], wv_ref[span, :])
        for h in range(kv_heads):
            total += right_dot(gq_refs[h][...], wq_ref[span, h * wide : (h + 1) * wide])
        total = total.astype(jnp.bfloat16)
        keep_ref[:, span] = total[:half]
        send_ref[:, span] = total[half:]


def tail_stage(kv_sums, cosine, sine, grad_queries, wq, wk, wv, where):
    rows, model = cosine.shape[0], wq.shape[0]
    kv_heads = len(grad_queries)
    vmem = pl.BlockSpec(memory_space=pltpu.VMEM)
    half = jax.ShapeDtypeStruct((rows // 2, model), jnp.bfloat16)
    flat = [term for sums in kv_sums for term in sums]
    return pl.pallas_call(
        functools.partial(tail_kernel, kv_heads),
        out_shape=(
            half,
            half,
            jax.ShapeDtypeStruct((rows, 2 * kv_heads * HEAD_SIZE), jnp.bfloat16),
        ),
        in_specs=[pl.BlockSpec(memory_space=pltpu.SMEM)]
        + [vmem] * (len(flat) + 2 + kv_heads + 3),
        out_specs=[vmem] * 3,
        compiler_params=pltpu.CompilerParams(vmem_limit_bytes=VMEM_LIMIT),
        cost_estimate=cost("tail_stage", 2 * rows * model * (wq.shape[1] + 2 * wk.shape[1]), 4 * rows * model + 4 * wq.size
        ),
        name="tail_stage",
    )(where, *flat, cosine, sine, *grad_queries, wq, wk, wv)


def flip(value, axis, mask=1):
    return lax.ppermute(value, axis, [(i, i ^ mask) for i in range(lax.axis_size(axis))])


def ctx_flip(value, mask):
    if mask == 1:
        return flip(value, "x")
    if mask == 2:
        return flip(value, "l")
    return flip(value, "hi", mask // 4)


def add(left, right):
    return (left.astype(jnp.float32) + right.astype(jnp.float32)).astype(jnp.bfloat16)


def slots_of(value, tensor):
    rows = value.shape[0] // SLOTS
    return [
        lax.dynamic_slice_in_dim(value, (tensor ^ SLOT_XOR[u]) * rows, rows)
        for u in range(SLOTS)
    ]


def after(dep, *values):
    deps = dep if isinstance(dep, tuple) else (dep,)
    held = lax.optimization_barrier(deps + values)[len(deps) :]
    return held[0] if len(held) == 1 else held


class Stages:
    def __init__(self, block_order):
        self.live = block_order[0] >= 0

    def __call__(self, function, *args):
        shapes = jax.eval_shape(function, *args)
        empty = lambda *_: jax.tree.map(lambda a: jnp.zeros(a.shape, a.dtype), shapes)
        return lax.cond(self.live, function, empty, *args)


def gather_pair(own):
    partner = ctx_flip(own, 2)
    near = jnp.concatenate([own, partner, flip(own, "y"), flip(partner, "y")])
    return jnp.concatenate([near, flip(near, "core")])


def gather_slots(own):
    near = jnp.concatenate([own, flip(own, "y")])
    return near, flip(near, "core")


def place_rows(own, near, core, far, tensor):
    rows = own.shape[0]
    result = jnp.zeros((SLOTS * rows,) + own.shape[1:], own.dtype)
    for u, piece in enumerate((own, near, core, far)):
        result = lax.dynamic_update_slice_in_dim(
            result, piece, (tensor ^ SLOT_XOR[u]) * rows, 0
        )
    return result


def scatter_slots(keep, send, fill=lambda value: value):
    got = fill(flip(send, "core"))
    quarter = keep.shape[0] // 2
    far = flip(add(keep[quarter:], got[quarter:]), "y")
    return add(keep[:quarter], got[:quarter]), far


def pair_scatter(keep, send, fill=lambda near: near):
    got = fill(flip(send, "core"))
    n = keep.shape[0] // 4
    near = [add(keep[k * n : (k + 1) * n], got[k * n : (k + 1) * n]) for k in range(4)]
    far = flip(near[3], "y")
    got = flip(near[2], "y")
    return near, far, got


def pair_finish(near, far, got):
    away = add(near[1], far)
    return near[0], got, ctx_flip(away, 2), away


def total(terms):
    return sum(term.astype(jnp.float32) for term in terms)


class Reduce:
    def __init__(self, keep, send):
        self.keep, self.got = keep, ctx_flip(send, 1)

    def halve(self, mask, ctx, dep=None):
        keep, got = self.keep, self.got
        if dep is not None:
            keep, got = after(dep, keep, got)
        n = keep.shape[0] // 2
        bit = lax.div(ctx, mask) % 2
        pick = lambda value, index: lax.dynamic_slice_in_dim(value, index * n, n, 0)
        away = ctx_flip(add(pick(keep, 1 - bit), pick(got, 1 - bit)), mask)
        self.keep, self.got = add(pick(keep, bit), pick(got, bit)), away

    def sum(self):
        return (self.keep.astype(jnp.float32) + self.got.astype(jnp.float32))[0]


def high_masks(ctx_count):
    masks, mask = [], ctx_count // 2
    while mask >= 4:
        masks.append(mask)
        mask //= 2
    return masks


def unit_sum_over(shares):
    return lax.psum_scatter(shares, ("x", "hi"), scatter_dimension=0, tiled=True)


def split_halves(summed, ctx, dep):
    summed = after(dep, summed)
    pair = lax.div(ctx, 2) % 2
    pick = lambda index: lax.dynamic_index_in_dim(summed, index, 0, keepdims=False)
    return pick(pair), pick(1 - pair)


def join_halves(own, other, ctx):
    pair = lax.div(ctx, 2) % 2
    low, high = jnp.where(pair == 0, own, other), jnp.where(pair == 0, other, own)
    return jnp.concatenate([low, high], axis=1).astype(jnp.float32)


class KvReduce:
    def __init__(self, keep, got):
        self.keep, self.got = keep, got

    def merge(self, dep):
        keep, got = after(dep, self.keep, self.got)
        n = keep.shape[0] // 2
        return add(keep[:n], got[:n]), add(keep[n:], got[n:])


def norm_back(grad_out, normed, inv_scale, gain):
    scaled = grad_out * gain
    inner = jnp.mean(scaled * normed, axis=-1, keepdims=True)
    return (inv_scale * (scaled - normed * inner), jnp.sum(grad_out * normed, axis=0))


def body(
    layer_input,
    attn_gain,
    w_query,
    key_matrix,
    value_matrix,
    w_out,
    ffn_gain,
    w_gate,
    w_up,
    w_down,
    cotangent,
    block_order,
    cont_prompt,
):
    ctx_count = lax.axis_size("hi") * 4
    ctx = (lax.axis_index("hi") * 2 + lax.axis_index("l")) * 2 + lax.axis_index("x")
    tensor = lax.axis_index("y") * 2 + lax.axis_index("core")
    where = jnp.stack([ctx, tensor]).astype(jnp.int32)
    quarter = layer_input.shape[0] // SLOTS
    kv_heads = key_matrix.shape[1] // HEAD_SIZE
    highs = high_masks(ctx_count)

    stage = Stages(block_order)
    cot_own = lax.dynamic_slice_in_dim(cotangent, tensor * quarter, quarter)
    cot_slots = slots_of(cotangent, tensor)
    cot_part = ctx_flip(cot_own, 2)
    first_input, queries, kv_local, cosine, sine = input_stage(
        layer_input, attn_gain, w_query, key_matrix, value_matrix, block_order, cont_prompt, where
    )
    def first_keys(kv):
        high = {0: kv}
        for bit in reversed(highs):
            for mask in list(high):
                high[mask + bit] = ctx_flip(high[mask], bit)
        del high[0]
        return high, ctx_flip(kv, 2), ctx_flip(kv, 1)

    def second_keys(high, low, cot):
        return (
            ctx_flip(low, 1),
            flip(cot, "y"),
            {mask: ctx_flip(value, 2) for mask, value in high.items()},
            {mask: ctx_flip(value, 1) for mask, value in high.items()},
        )

    def third_keys(both, cot):
        return {mask: ctx_flip(value, 1) for mask, value in both.items()}, flip(cot, "core")

    high, part_l, part_x = stage(first_keys, after(cot_part, kv_local))
    part_lx, more, high_l, high_x = stage(second_keys, high, part_l, cot_part)
    cot_part = jnp.concatenate([cot_part, more])
    high_lx, cot_far = stage(third_keys, high_l, cot_part)
    parts = {0: kv_local, 1: part_x, 2: part_l, 3: part_lx}
    for mask in high:
        parts[mask], parts[mask + 1] = high[mask], high_x[mask]
        parts[mask + 2], parts[mask + 3] = high_l[mask], high_lx[mask]
    parts = [parts[mask] for mask in range(ctx_count)]
    cot = jnp.concatenate(
        [cot_slots[0], cot_part[:quarter], cot_slots[1], cot_part[quarter:]]
        + [cot_slots[2], cot_far[:quarter], cot_slots[3], cot_far[quarter:]]
    )
    mixed, log_total, keep, send = attention_forward(
        queries, w_out, parts, block_order, cont_prompt, where
    )
    first_half = flip(send, "core")
    near = add(keep, first_half)
    far = flip(near[quarter:], "y")
    grad_hidden = grad_hidden_stage(after(near, cot), w_down, where)
    own_input = lax.dynamic_slice_in_dim(layer_input, tensor * quarter, quarter)
    own_input = own_input.astype(jnp.float32)
    middle = own_input + total((near[:quarter], after(grad_hidden, far)))
    inv_two = lax.rsqrt(jnp.mean(middle * middle, axis=-1, keepdims=True) + eps_norm)
    normed_two = middle * inv_two
    second = gather_pair((normed_two * ffn_gain).astype(jnp.bfloat16))
    hidden, grad_gate, grad_up = ffn_stage(second, grad_hidden, w_gate, w_up, where)

    down_shares = unit_shares("down_shares", cot, hidden, ctx_count, where)
    down = unit_sum_over(down_shares)
    grads, weights = after(down_shares, grad_gate, grad_up), (w_gate, w_up)
    send = grad_second_half(1, "grad_second_send", grads, weights, where)

    def second_stage(send, grad_gate, grad_up, hidden):
        keep = grad_second_half(0, "grad_second_keep", (grad_gate, grad_up), weights, where)
        near, far, got = pair_scatter(keep, send)
        shares = unit_shares("gate_shares", second, after(near[3], grad_gate), ctx_count, where)
        *terms, away = pair_finish(near, after(shares, far), got)
        halves = unit_sum(
            ffn_out_kernel, "ffn_out", (after(away, hidden),), (w_down,), False, where
        )
        return total(after(halves[0], *terms)), shares, halves

    grad_second, gate_shares, ffn_halves = stage(second_stage, send, *grads, hidden)
    gate = unit_sum_over(gate_shares)

    def branch_stage(grad_second, grad_up, own):
        grad_norm, gain_part = norm_back(grad_second, normed_two, inv_two, ffn_gain)
        grad_middle = own.astype(jnp.float32) + grad_norm
        branch = grad_middle.astype(jnp.bfloat16)
        shares = unit_shares("up_shares", second, after(branch, grad_up), ctx_count, where)
        near = jnp.concatenate([branch, after(shares, flip(branch, "y"))])
        return grad_middle, gain_part, shares, jnp.concatenate([near, flip(near, "core")])

    grad_middle, ffn_gain_part, up_shares, grad_branch = stage(
        branch_stage, grad_second, grad_up, cot_own
    )
    up = unit_sum_over(up_shares)
    backward, kv = [], []
    held = grad_branch
    for head in range(kv_heads):
        backward.append(
            attention_backward(
                head, queries, held, w_out, mixed, log_total, parts, cosine, sine,
                block_order, cont_prompt, where,
            )
        )
        kv.append(KvReduce(backward[-1][1], ctx_flip(backward[-1][2], 1)))
        dep = backward[-1][0]
        if head == 0:
            down_own, down_away = split_halves(down, ctx, dep)
            down_other = ctx_flip(down_away, 2)
            dep = down_own
        held = after(dep, grad_branch)
    grad_queries = [item[0] for item in backward]
    branch_shares = weight_shares(
        "branch_shares",
        (first_input, grad_branch),
        grad_queries + [after(dep, mixed)],
        tuple((0, h) for h in range(kv_heads)) + ((1, kv_heads),),
        ctx_count,
        True,
        where,
    )
    def out_stage(keep, send):
        got = flip(send, "core")
        n = keep.shape[0] // 4
        near = [add(keep[k * n : (k + 1) * n], got[k * n : (k + 1) * n]) for k in range(4)]
        return near[0], near[2], add(near[1], flip(near[3], "y"))

    def first_stage(keep, send, own_input, grad_middle):
        terms = scatter_slots(keep, send)
        inv = lax.rsqrt(jnp.mean(own_input * own_input, axis=-1, keepdims=True) + eps_norm)
        grad_norm, gain_part = norm_back(total(terms), own_input * inv, inv, attn_gain)
        return gain_part, (grad_middle + grad_norm).astype(jnp.bfloat16)

    def row_stage(near, other):
        near = jnp.concatenate([near, other])
        return near, flip(near, "core")

    def gain_stage(gains):
        gains = gains + flip(gains, "core")
        gains = gains + flip(gains, "y")
        for mask in [1, 2] + highs:
            gains = gains + ctx_flip(gains, mask)
        return gains

    dep = branch_shares[0]
    kv = [item.merge(dep) for item in kv]
    dep = tuple(keep for keep, _ in kv)
    sum_down = join_halves(down_own, after(dep, down_other), ctx).T
    dep = sum_down
    got = [ctx_flip(after(dep, value), 2) for _, value in kv]
    branch = Reduce(*after(dep, *branch_shares))
    out_near, out_own, out_away = stage(out_stage, *after(dep, *ffn_halves))
    dep = out_away
    for mask in highs:
        kv = [
            KvReduce(keep, value).merge(dep) for (keep, _), value in zip(kv, got)
        ]
        got = [ctx_flip(value, mask) for _, value in kv]
    dep = tuple(keep for keep, _ in kv)
    gate_own, gate_away = split_halves(gate, ctx, dep)
    dep = gate_own
    gate_other = ctx_flip(after(dep, gate_away), 2)
    out_far, out_got = stage(
        lambda away, own: (ctx_flip(away, 2), flip(own, "y")), *after(dep, out_away, out_own)
    )
    dep = out_far
    branch.halve(2, ctx, dep)
    dep = branch.keep
    output = (middle + total(after(dep, out_near, out_got, out_far))).astype(jnp.bfloat16)
    dep = output
    keep, send, grad_kv = tail_stage(
        [after(dep, keep, value) for (keep, _), value in zip(kv, got)], cosine, sine,
        grad_queries, w_query, key_matrix, value_matrix, where,
    )
    dep = keep
    kv_shares = weight_shares(
        "kv_shares", (first_input,), (after(dep, grad_kv),), ((0, 0),), ctx_count, True, where
    )
    dep = kv_shares[0]
    last = Reduce(*after(dep, *kv_shares))
    attn_gain_part, grad_input = stage(
        first_stage, after(dep, keep), send, own_input, grad_middle
    )
    dep = grad_input
    near = jnp.concatenate([grad_input, output])
    near_other = flip(after(dep, near), "y")
    for mask in highs:
        branch.halve(mask, ctx, dep)
        dep = branch.keep
    last.halve(2, ctx, dep)
    dep = last.keep
    sum_gate = join_halves(gate_own, after(dep, gate_other), ctx)
    dep = sum_gate
    up_own, up_away = split_halves(up, ctx, dep)
    dep = up_own
    up_other = ctx_flip(after(dep, up_away), 2)
    for mask in highs:
        last.halve(mask, ctx, dep)
        dep = last.keep
    near, far = stage(row_stage, near, after(dep, near_other))
    dep = far
    last.keep, last.got = after(dep, last.keep, last.got)
    last_sum = last.sum()
    dep = last_sum
    quarters = [near[n * quarter : (n + 1) * quarter] for n in range(4)]
    quarters += [after(dep, far)[n * quarter : (n + 1) * quarter] for n in range(4)]
    grad_rows, output_rows = [
        place_rows(quarters[k], quarters[k + 2], quarters[k + 4], quarters[k + 6], tensor)
        for k in range(2)
    ]
    dep = (grad_rows, output_rows)
    gains = stage(gain_stage, after(dep, jnp.stack([attn_gain_part, ffn_gain_part])))
    dep = gains
    sum_up = join_halves(up_own, after(dep, up_other), ctx)
    dep = sum_up
    branch.keep, branch.got = after(dep, branch.keep, branch.got)
    branch_sum = branch.sum()
    dep = branch_sum
    grad_input, output = grad_rows, output_rows
    width_q, width_k = w_query.shape[1], key_matrix.shape[1]
    sum_query, sum_out = branch_sum[:, :width_q], branch_sum[:, width_q:].T
    sum_key, sum_value = last_sum[:, :width_k], last_sum[:, width_k:]

    gains = gains.reshape(2, ctx_count * SLOTS, -1)
    gains = lax.dynamic_index_in_dim(gains, ctx * SLOTS + tensor, 1, keepdims=False)
    return (
        output,
        grad_input,
        gains[0],
        sum_query,
        sum_key,
        sum_value,
        sum_out,
        gains[1],
        sum_gate,
        sum_up,
        sum_down,
    )


def solution(mesh):
    rows, heads = ("hi", "l", "x"), ("y", "core")
    split = Mesh(mesh.devices.reshape(-1, 2, 2, 2, 2), rows + heads)
    placed = (
        P(rows, None),
        P(),
        P(None, heads),
        P(None, heads),
        P(None, heads),
        P(heads, None),
        P(),
        P(None, heads),
        P(None, heads),
        P(heads, None),
        P(rows, None),
        P(),
        P(),
    )
    return jax.shard_map(
        body,
        mesh=split,
        in_specs=placed,
        out_specs=(
            P(rows, None),
            P(rows, None),
            P(rows + heads),
            P(rows, heads),
            P(rows, heads),
            P(rows, heads),
            P(heads, rows),
            P(rows + heads),
            P(rows, heads),
            P(rows, heads),
            P(heads, rows),
        ),
        check_vma=False,
    )
```

```python
import functools
import math

import jax
import jax.numpy as jnp
import numpy as np
from jax import lax
from jax.experimental import pallas as pl
from jax.experimental.pallas import tpu as pltpu
from jax.sharding import Mesh
from jax.sharding import PartitionSpec as P

HEAD_SIZE = 128
PROMPT = 2048
CONT_LEN = 256
CONTS = 8
BLOCK = 128
PER_PROMPT = PROMPT // BLOCK
PER_CONT = CONT_LEN // BLOCK
LOG2E = 1.4426950408889634
NEG = -1e30
SLOTS = 4
VMEM_LIMIT = 60 << 20
PAIR_STEPS = (4, 1)

eps_norm = 1e-05
rope_base = 1000000.0

SLOT_XOR = (0, 2, 1, 3)


def plain_dot(left, right):
    return jnp.dot(left, right, preferred_element_type=jnp.float32)


def left_dot(left, right):
    return lax.dot_general(
        left, right, (((0,), (0,)), ((), ())), preferred_element_type=jnp.float32
    )


def right_dot(left, right):
    return lax.dot_general(
        left, right, (((1,), (1,)), ((), ())), preferred_element_type=jnp.float32
    )


def slot_quarter(slot, tensor):
    return ((slot & 1) * 2 + lax.shift_right_logical(slot, 1)) ^ tensor


def stored_block(index, where_ref):
    rank = lax.div(index, SLOTS) ^ where_ref[0]
    return rank * SLOTS + slot_quarter(index & 3, where_ref[1])


def block_plan(order_ref, cont_ref, where_ref, slot):
    count = cont_ref.shape[0]
    prompt_blocks = count // CONTS * PER_PROMPT
    own = order_ref[stored_block(slot, where_ref)]
    is_prompt = own < prompt_blocks
    offset = own - prompt_blocks
    which = jnp.clip(lax.div(offset, PER_CONT), 0, count - 1)
    group = jnp.where(is_prompt, lax.div(own, PER_PROMPT), cont_ref[which])
    inner = jnp.where(is_prompt, lax.rem(own, PER_PROMPT), lax.rem(offset, PER_CONT))
    has_prev = lax.rem(inner, 2)
    pairs = jnp.where(is_prompt, lax.div(inner, 2), PER_PROMPT // 2)
    prev = own - has_prev
    return group * PER_PROMPT, pairs, prev, own, has_prev


def fill_inverse(order_ref, where_ref, inverse_ref):
    def put(index, carry):
        inverse_ref[order_ref[stored_block(index, where_ref)]] = index
        return carry

    lax.fori_loop(0, order_ref.shape[0], put, 0)


def rotate(vec, cosine, sine):
    return vec * cosine + pltpu.roll(vec, HEAD_SIZE // 2, 1) * sine


def unrotate(vec, cosine, sine):
    return vec * cosine + pltpu.roll(vec * sine, HEAD_SIZE // 2, 1)


def angle_tables():
    half = HEAD_SIZE // 2
    freq = np.float64(rope_base) ** (-(2.0 * np.arange(half) / HEAD_SIZE))
    freq = np.concatenate([freq, freq])
    starts = np.arange(-(-(PER_PROMPT + PER_CONT) // 8) * 8) * BLOCK
    start = starts[:, None] * freq[None]
    inner = np.arange(BLOCK)[:, None] * freq[None]
    return tuple(
        f(a).astype(np.float32) for a in (start, inner) for f in (np.cos, np.sin)
    )


def key_rows(inverse_ref, logical):
    return pl.ds(pl.multiple_of(inverse_ref[logical] * BLOCK, BLOCK), BLOCK)


def tile_pair(ref, rows_a, rows_b, column):
    return tile(ref, (rows_a, rows_b), column)


def tile(ref, rows, column):
    cols = pl.ds(column, HEAD_SIZE)
    return jnp.concatenate([ref[span, cols] for span in rows], axis=0)


def own_mask(has_prev, rep):
    shape = (2 * BLOCK, rep * BLOCK)
    row = lax.broadcasted_iota(jnp.int32, shape, 0)
    col = lax.broadcasted_iota(jnp.int32, shape, 1)
    first_row = BLOCK * (1 - has_prev)
    return (row >= first_row) & (row - BLOCK <= lax.rem(col, BLOCK))


def stack_t(ref, rows, column, rep):
    return jnp.concatenate(
        [ref[rows, pl.ds(column + r * HEAD_SIZE, HEAD_SIZE)].T for r in range(rep)], axis=1
    )


def stack_rows(ref, rows, column, rep):
    return jnp.concatenate(
        [ref[rows, pl.ds(column + r * HEAD_SIZE, HEAD_SIZE)] for r in range(rep)], axis=0
    )


def dot(left, right):
    return jnp.dot(left, right, preferred_element_type=jnp.float32)


def start_parts(parts, buffer_ref, sem, column):
    rows, width = parts[0].shape[0], buffer_ref.shape[1]
    copies = [
        pltpu.make_async_copy(
            part.at[:, pl.ds(column, width)], buffer_ref.at[pl.ds(p * rows, rows), :], sem.at[p]
        )
        for p, part in enumerate(parts)
    ]
    for copy in copies:
        copy.start()
    return copies


def forward_kernel(rep, hps, ctx_count, order_ref, cont_ref, where_ref, q_ref, wo_ref, *refs):
    parts, refs = refs[:ctx_count], refs[ctx_count:]
    out_ref, lse_ref, keep_ref, send_ref, kv_ref, inverse_ref, qt_ref, acc_ref, sem = refs
    copies = start_parts(parts, kv_ref, sem, 0)
    fill_inverse(order_ref, where_ref, inverse_ref)
    for copy in copies:
        copy.wait()
    q_blocks = q_ref.shape[0] // BLOCK
    factor = LOG2E / math.sqrt(HEAD_SIZE)
    width = rep * HEAD_SIZE

    def one_query_block(qb, carry):
        base, pairs, prev, own, has_prev = block_plan(order_ref, cont_ref, where_ref, qb)
        rows = pl.ds(pl.multiple_of(qb * BLOCK, BLOCK), BLOCK)
        mask = own_mask(has_prev, rep)
        rows_a, rows_b = key_rows(inverse_ref, prev), key_rows(inverse_ref, own)
        state = []
        for h in range(hps):
            qt = stack_t(q_ref, rows, h * width, rep)
            qt_ref[h] = qt
            scores = dot(tile_pair(kv_ref, rows_a, rows_b, 2 * h * HEAD_SIZE), qt) * factor
            scores = jnp.where(mask, scores, NEG)
            best = jnp.max(scores, axis=0, keepdims=True)
            weights = jnp.exp2(scores - best)
            total = jnp.sum(weights, axis=0, keepdims=True)
            values = tile_pair(kv_ref, rows_a, rows_b, (2 * h + 1) * HEAD_SIZE)
            acc_ref[h] = dot(values.T, weights.astype(jnp.bfloat16))
            state += [best, total]

        def fold(first, count, state):
            rows = [key_rows(inverse_ref, first + n) for n in range(count)]
            after = []
            for h in range(hps):
                best, total = state[2 * h], state[2 * h + 1]
                keys = tile(kv_ref, rows, 2 * h * HEAD_SIZE)
                scores = dot(keys, qt_ref[h]) * factor
                newest = jnp.maximum(best, jnp.max(scores, axis=0, keepdims=True))
                weights = jnp.exp2(scores - newest)
                shrink = jnp.exp2(best - newest)
                total = total * shrink + jnp.sum(weights, axis=0, keepdims=True)
                values = tile(kv_ref, rows, (2 * h + 1) * HEAD_SIZE)
                acc_ref[h] = acc_ref[h] * shrink + dot(values.T, weights.astype(jnp.bfloat16))
                after += [newest, total]
            return tuple(after)

        state, done = tuple(state), 0
        for wide in PAIR_STEPS:
            upto = lax.div(pairs, wide) * wide
            state = lax.fori_loop(
                0,
                lax.div(upto - done, wide),
                lambda t, state, done=done, wide=wide: fold(
                    base + 2 * (done + wide * t), 2 * wide, state
                ),
                state,
            )
            done = upto
        for h in range(hps):
            best, total = state[2 * h], state[2 * h + 1]
            mixed = acc_ref[h] * (1.0 / total)
            for r in range(rep):
                part = mixed[:, r * BLOCK : (r + 1) * BLOCK]
                out_ref[rows, pl.ds(h * width + r * HEAD_SIZE, HEAD_SIZE)] = part.T.astype(
                    jnp.bfloat16
                )
            lse_ref[h, pl.ds(qb, 1), :] = best + jnp.log2(total)
        return carry

    lax.fori_loop(0, q_blocks, one_query_block, 0)
    mixed = out_ref[...]
    half = keep_ref.shape[0]
    for n in range(0, wo_ref.shape[1], 512):
        cols = slice(n, n + 512)
        partial = dot(mixed, wo_ref[:, cols]).astype(jnp.bfloat16)
        keep_ref[:, cols] = partial[:half]
        send_ref[:, cols] = partial[half:]


def backward_kernel(rep, hps, ctx_count, head, order_ref, cont_ref, where_ref, q_ref, gb_ref, wo_ref,
                    mix_ref, lse_ref, cos_ref, sin_ref, *refs):
    parts, refs = refs[:ctx_count], refs[ctx_count:]
    gq_ref, keep_ref, send_ref = refs[:3]
    kv_ref, gm_ref, inverse_ref, qt_ref, gmt_ref, gqt_ref, acc_ref, sem = refs[3:]
    copies = start_parts(parts, kv_ref, sem, head * kv_ref.shape[1])
    fill_inverse(order_ref, where_ref, inverse_ref)
    gm_ref[...] = right_dot(gb_ref[...], wo_ref[...]).astype(jnp.bfloat16)
    for copy in copies:
        copy.wait()
    q_blocks = q_ref.shape[0] // BLOCK
    scale = 1.0 / math.sqrt(HEAD_SIZE)
    factor = LOG2E * scale
    width = rep * HEAD_SIZE

    def clear(i, carry):
        acc_ref[pl.ds(pl.multiple_of(i * BLOCK, BLOCK), BLOCK), :] = jnp.zeros(
            (BLOCK, acc_ref.shape[1]), jnp.float32
        )
        return carry

    lax.fori_loop(0, order_ref.shape[0], clear, 0)

    def tile_terms(h, spans, lse, delta, q_rows, gm_rows, mask):
        kcol, vcol = 2 * h * HEAD_SIZE, (2 * h + 1) * HEAD_SIZE
        keys = tile(kv_ref, spans, kcol)
        values = tile(kv_ref, spans, vcol)
        weights = jnp.exp2(dot(keys, qt_ref[h]) * factor - lse)
        if mask is not None:
            weights = jnp.where(mask, weights, 0.0)
        grad_weights = dot(values, gmt_ref[h])
        grad_scores = (weights * (grad_weights - delta)).astype(jnp.bfloat16)
        gv = dot(weights.astype(jnp.bfloat16), gm_rows)
        gk = dot(grad_scores, q_rows)
        for n, span in enumerate(spans):
            piece = slice(n * BLOCK, (n + 1) * BLOCK)
            acc_ref[span, pl.ds(kcol, HEAD_SIZE)] += gk[piece]
            acc_ref[span, pl.ds(vcol, HEAD_SIZE)] += gv[piece]
        return dot(keys.T, grad_scores)

    def one_query_block(qb, carry):
        base, pairs, prev, own, has_prev = block_plan(order_ref, cont_ref, where_ref, qb)
        rows = pl.ds(pl.multiple_of(qb * BLOCK, BLOCK), BLOCK)
        mask = own_mask(has_prev, rep)
        rows_a, rows_b = key_rows(inverse_ref, prev), key_rows(inverse_ref, own)
        deltas, lses, q_stack, gm_stack = [], [], [], []
        for h in range(hps):
            qt_ref[h] = stack_t(q_ref, rows, h * width, rep)
            gmt = stack_t(gm_ref, rows, h * width, rep)
            gmt_ref[h] = gmt
            mixt = stack_t(mix_ref, rows, h * width, rep)
            deltas.append(
                jnp.sum(
                    gmt.astype(jnp.float32) * mixt.astype(jnp.float32), axis=0, keepdims=True
                )
            )
            lses.append(lse_ref[h, pl.ds(qb, 1), :])
        for h in range(hps):
            q_rows = stack_rows(q_ref, rows, h * width, rep)
            gm_rows = stack_rows(gm_ref, rows, h * width, rep)
            gqt_ref[h] = tile_terms(
                h, (rows_a, rows_b), lses[h], deltas[h], q_rows, gm_rows, mask
            )

        def fold(first, count):
            spans = [key_rows(inverse_ref, first + n) for n in range(count)]
            for h in range(hps):
                q_rows = stack_rows(q_ref, rows, h * width, rep)
                gm_rows = stack_rows(gm_ref, rows, h * width, rep)
                gqt_ref[h] += tile_terms(
                    h, spans, lses[h], deltas[h], q_rows, gm_rows, None
                )
            return 0

        done = 0
        for wide in PAIR_STEPS:
            upto = lax.div(pairs, wide) * wide
            lax.fori_loop(
                0,
                lax.div(upto - done, wide),
                lambda t, _, done=done, wide=wide: fold(base + 2 * (done + wide * t), 2 * wide),
                0,
            )
            done = upto
        for h in range(hps):
            total = gqt_ref[h] * scale
            for r in range(rep):
                part = total[:, r * BLOCK : (r + 1) * BLOCK]
                rounded = part.T.astype(jnp.bfloat16).astype(jnp.float32)
                gq_ref[rows, pl.ds(h * width + r * HEAD_SIZE, HEAD_SIZE)] = unrotate(
                    rounded, cos_ref[rows, :], sin_ref[rows, :]
                ).astype(jnp.bfloat16)
        return carry

    lax.fori_loop(0, q_blocks, one_query_block, 0)

    blocks = order_ref.shape[0]

    def place(index):
        chunk = lax.div(index, SLOTS)
        spot = (chunk & 1) * (ctx_count // 2) + (chunk & 2) // 2 * (ctx_count // 4) + (
            lax.shift_right_logical(chunk, 2)
        )
        return spot * SLOTS + (index & 3)

    def flush(i, carry):
        rows = pl.ds(pl.multiple_of(i * BLOCK, BLOCK), BLOCK)
        spot = place(i)
        parts = []
        for h in range(hps):
            parts.append(acc_ref[rows, pl.ds(2 * h * HEAD_SIZE, HEAD_SIZE)] * scale)
            parts.append(acc_ref[rows, pl.ds((2 * h + 1) * HEAD_SIZE, HEAD_SIZE)])
        value = jnp.concatenate(parts, axis=1).astype(jnp.bfloat16)

        @pl.when(spot < blocks // 2)
        def _():
            keep_ref[pl.ds(pl.multiple_of(spot * BLOCK, BLOCK), BLOCK), :] = value

        @pl.when(spot >= blocks // 2)
        def _():
            far = (spot - blocks // 2) * BLOCK
            send_ref[pl.ds(pl.multiple_of(far, BLOCK), BLOCK), :] = value

        return carry

    lax.fori_loop(0, blocks, flush, 0)


def attention_forward(q, w_out, parts, order, cont, where):
    ctx_count = len(parts)
    rows, tokens = q.shape[0], ctx_count * q.shape[0]
    kv_heads = parts[0].shape[1] // (2 * HEAD_SIZE)
    rep = q.shape[1] // HEAD_SIZE // kv_heads
    q_blocks, model = rows // BLOCK, w_out.shape[1]
    vmem, smem, any_ = (
        pl.BlockSpec(memory_space=space) for space in (pltpu.VMEM, pltpu.SMEM, pl.ANY)
    )
    flops = 2 * rows * tokens * q.shape[1] + 2 * rows * q.shape[1] * model
    half = jax.ShapeDtypeStruct((rows // 2, model), jnp.bfloat16)
    return pl.pallas_call(
        functools.partial(forward_kernel, rep, kv_heads, ctx_count),
        out_shape=(
            jax.ShapeDtypeStruct(q.shape, jnp.bfloat16),
            jax.ShapeDtypeStruct((kv_heads, q_blocks, rep * BLOCK), jnp.float32),
            half,
            half,
        ),
        in_specs=[smem] * 3 + [vmem] * 2 + [any_] * ctx_count,
        out_specs=[vmem] * 4,
        scratch_shapes=[
            pltpu.VMEM((tokens, parts[0].shape[1]), jnp.bfloat16),
            pltpu.SMEM((order.shape[0],), jnp.int32),
            pltpu.VMEM((kv_heads, HEAD_SIZE, rep * BLOCK), jnp.bfloat16),
            pltpu.VMEM((kv_heads, HEAD_SIZE, rep * BLOCK), jnp.float32),
            pltpu.SemaphoreType.DMA((ctx_count,)),
        ],
        compiler_params=pltpu.CompilerParams(vmem_limit_bytes=VMEM_LIMIT),
        cost_estimate=cost("attention_forward", flops, 2 * tokens * parts[0].shape[1] + 4 * rows * model),
        name="attention_forward",
    )(order, cont, where, q, w_out, *parts)


def attention_backward(head, q, grad_branch, w_out, mixed, lse, parts, cosine, sine, order, cont,
                       where):
    ctx_count = len(parts)
    rows, tokens = q.shape[0], ctx_count * q.shape[0]
    kv_heads = parts[0].shape[1] // (2 * HEAD_SIZE)
    rep = q.shape[1] // HEAD_SIZE // kv_heads
    q_blocks, model = rows // BLOCK, w_out.shape[1]
    wide = rep * HEAD_SIZE
    q_spec = pl.BlockSpec((rows, wide), lambda g, *_: (0, head))
    whole = lambda g, *_: (0, 0)
    table_spec = pl.BlockSpec((rows, HEAD_SIZE), whole)
    half = (tokens // 2, 2 * HEAD_SIZE)
    flops = 5 * rows * tokens * wide + 2 * rows * wide * model
    return pl.pallas_call(
        functools.partial(backward_kernel, rep, 1, ctx_count, head),
        out_shape=(
            jax.ShapeDtypeStruct((rows, wide), jnp.bfloat16),
            jax.ShapeDtypeStruct(half, jnp.bfloat16),
            jax.ShapeDtypeStruct(half, jnp.bfloat16),
        ),
        grid_spec=pltpu.PrefetchScalarGridSpec(
            num_scalar_prefetch=3,
            grid=(1,),
            in_specs=[
                q_spec,
                pl.BlockSpec((rows, model), whole),
                pl.BlockSpec((wide, model), lambda g, *_: (head, 0)),
                q_spec,
                pl.BlockSpec((1, q_blocks, rep * BLOCK), lambda g, *_: (head, 0, 0)),
                table_spec,
                table_spec,
            ]
            + [pl.BlockSpec(memory_space=pl.ANY)] * ctx_count,
            out_specs=[
                pl.BlockSpec((rows, wide), whole),
                pl.BlockSpec(half, whole),
                pl.BlockSpec(half, whole),
            ],
            scratch_shapes=[
                pltpu.VMEM((tokens, 2 * HEAD_SIZE), jnp.bfloat16),
                pltpu.VMEM((rows, wide), jnp.bfloat16),
                pltpu.SMEM((order.shape[0],), jnp.int32),
                pltpu.VMEM((1, HEAD_SIZE, rep * BLOCK), jnp.bfloat16),
                pltpu.VMEM((1, HEAD_SIZE, rep * BLOCK), jnp.bfloat16),
                pltpu.VMEM((1, HEAD_SIZE, rep * BLOCK), jnp.float32),
                pltpu.VMEM((tokens, 2 * HEAD_SIZE), jnp.float32),
                pltpu.SemaphoreType.DMA((ctx_count,)),
            ],
        ),
        compiler_params=pltpu.CompilerParams(vmem_limit_bytes=VMEM_LIMIT),
        cost_estimate=cost(f"attention_backward_{head}", flops, 4 * tokens * wide + 2 * rows * model),
        name=f"attention_backward_{head}",
    )(order, cont, where, q, grad_branch, w_out, mixed, lse, cosine, sine, *parts)


def input_kernel(order_ref, cont_ref, where_ref, gain_ref, x_hbm, wq_hbm, wk_hbm, wv_hbm, table_hbm,
                 first_ref, q_ref, kv_ref, cos_ref, sin_ref,
                 x_ref, wq_ref, wk_ref, wv_ref, table_ref, sem):
    pairs = ((x_hbm, x_ref), (table_hbm, table_ref), (wk_hbm, wk_ref), (wv_hbm, wv_ref),
             (wq_hbm, wq_ref))
    copies = [
        pltpu.make_async_copy(source, target, sem.at[n])
        for n, (source, target) in enumerate(pairs)
    ]
    for copy in copies:
        copy.start()
    count = cont_ref.shape[0]
    prompt_blocks = count // CONTS * PER_PROMPT
    starts = (table_ref.shape[0] - 2 * BLOCK) // 2
    lane = lax.broadcasted_iota(jnp.int32, (BLOCK, HEAD_SIZE), 1)
    copies[0].wait()
    copies[1].wait()

    def one_slot(slot, carry):
        quarter = slot_quarter(slot, where_ref[1])
        rows = pl.ds(pl.multiple_of(slot * BLOCK, BLOCK), BLOCK)
        full = x_ref[pl.ds(pl.multiple_of(quarter * BLOCK, BLOCK), BLOCK), :].astype(jnp.float32)
        inv = lax.rsqrt(jnp.mean(full * full, axis=-1, keepdims=True) + eps_norm)
        first_ref[rows, :] = (full * inv * gain_ref[...]).astype(jnp.bfloat16)
        own = order_ref[stored_block(slot, where_ref)]
        spot = jnp.where(
            own < prompt_blocks,
            lax.rem(own, PER_PROMPT),
            PER_PROMPT + lax.rem(own - prompt_blocks, PER_CONT),
        )
        cos_start = table_ref[pl.ds(2 * BLOCK + spot, 1), :]
        sin_start = table_ref[pl.ds(2 * BLOCK + starts + spot, 1), :]
        cos_in, sin_in = table_ref[:BLOCK, :], table_ref[BLOCK : 2 * BLOCK, :]
        sine = sin_start * cos_in + cos_start * sin_in
        cos_ref[rows, :] = cos_start * cos_in - sin_start * sin_in
        sin_ref[rows, :] = jnp.where(lane < HEAD_SIZE // 2, -sine, sine)
        return carry

    lax.fori_loop(0, SLOTS, one_slot, 0)
    first = first_ref[...]
    cosine, sine = cos_ref[...], sin_ref[...]
    copies[2].wait()
    copies[3].wait()
    keys = dot(first, wk_ref[...])
    values = dot(first, wv_ref[...])
    for h in range(wk_ref.shape[1] // HEAD_SIZE):
        cols = slice(h * HEAD_SIZE, (h + 1) * HEAD_SIZE)
        low, high = 2 * h * HEAD_SIZE, (2 * h + 1) * HEAD_SIZE
        key = rotate(keys[:, cols], cosine, sine)
        kv_ref[:, low:high] = key.astype(jnp.bfloat16)
        kv_ref[:, high : high + HEAD_SIZE] = values[:, cols].astype(jnp.bfloat16)
    copies[4].wait()
    for n in range(0, wq_ref.shape[1], 256):
        queries = dot(first, wq_ref[:, n : n + 256])
        for m in range(0, 256, HEAD_SIZE):
            query = rotate(queries[:, m : m + HEAD_SIZE], cosine, sine)
            q_ref[:, n + m : n + m + HEAD_SIZE] = query.astype(jnp.bfloat16)


def input_stage(x, gain, wq, wk, wv, order, cont, where):
    rows, model = x.shape
    cos_start, sin_start, cos_in, sin_in = angle_tables()
    table = np.concatenate([cos_in, sin_in, cos_start, sin_start])
    vmem, smem, any_ = (
        pl.BlockSpec(memory_space=space) for space in (pltpu.VMEM, pltpu.SMEM, pl.ANY)
    )
    flops = 2 * rows * model * (wq.shape[1] + 2 * wk.shape[1])
    return pl.pallas_call(
        input_kernel,
        out_shape=(
            jax.ShapeDtypeStruct((rows, model), jnp.bfloat16),
            jax.ShapeDtypeStruct((rows, wq.shape[1]), jnp.bfloat16),
            jax.ShapeDtypeStruct((rows, 2 * wk.shape[1]), jnp.bfloat16),
            jax.ShapeDtypeStruct((rows, HEAD_SIZE), jnp.float32),
            jax.ShapeDtypeStruct((rows, HEAD_SIZE), jnp.float32),
        ),
        in_specs=[smem] * 3 + [vmem] + [any_] * 5,
        out_specs=[vmem] * 5,
        scratch_shapes=[
            pltpu.VMEM(a.shape, a.dtype) for a in (x, wq, wk, wv)
        ]
        + [pltpu.VMEM(table.shape, jnp.float32), pltpu.SemaphoreType.DMA((5,))],
        compiler_params=pltpu.CompilerParams(vmem_limit_bytes=VMEM_LIMIT),
        cost_estimate=cost("input_stage", flops, 4 * x.size + 2 * wq.size + 4 * wk.size),
        name="input_stage",
    )(order, cont, where, gain.reshape(1, -1), x, wq, wk, wv, table)


FILLERS = ("kv_shares", "grad_hidden")


def cost(name, flops, bytes_accessed):
    scale = 16.0 if name in FILLERS else 0.02
    return pl.CostEstimate(
        flops=int(flops * scale), bytes_accessed=int(bytes_accessed * scale), transcendentals=0
    )


def put_share(value, index, x_bit, keep_ref, send_ref, swap_bits):
    spot = share_spot(lax.shift_right_logical(index, 1), keep_ref.shape[0], swap_bits)
    stays = (index & 1) == x_bit
    value = value.astype(keep_ref.dtype)

    @pl.when(stays)
    def _():
        keep_ref[pl.ds(spot, 1)] = value[None]

    @pl.when(jnp.logical_not(stays))
    def _():
        send_ref[pl.ds(spot, 1)] = value[None]


def pair_bit(where_ref):
    return lax.shift_right_logical(where_ref[0], 1) & 1


def grad_hidden_kernel(where_ref, cot_ref, wd_ref, out_ref):
    out_ref[...] = right_dot(cot_ref[...], wd_ref[...])


def grad_hidden_stage(cot, w_down, where):
    rows, model = cot.shape
    units = w_down.shape[0] // 2
    block = 256
    steps = units // block
    return pl.pallas_call(
        grad_hidden_kernel,
        out_shape=jax.ShapeDtypeStruct((rows, units), jnp.float32),
        grid_spec=pltpu.PrefetchScalarGridSpec(
            num_scalar_prefetch=1,
            grid=(steps,),
            in_specs=[
                pl.BlockSpec((rows, model), lambda i, w: (0, 0), pipeline_mode=pl.Buffered(1)),
                pl.BlockSpec((block, model), lambda i, w: (pair_bit(w) * steps + i, 0)),
            ],
            out_specs=pl.BlockSpec((rows, block), lambda i, w: (0, i)),
        ),
        compiler_params=pltpu.CompilerParams(vmem_limit_bytes=VMEM_LIMIT),
        cost_estimate=cost("grad_hidden", 2 * rows * model * units, 4 * rows * model),
        name="grad_hidden",
    )(where, cot, w_down)


def ffn_kernel(where_ref, in_ref, gh_ref, wg_ref, wu_ref, hid_ref, gg_ref, gu_ref):
    gate = dot(in_ref[...], wg_ref[...])
    upward = dot(in_ref[...], wu_ref[...])
    grad_hidden = gh_ref[...]
    sigma = jax.nn.sigmoid(gate)
    swish = gate * sigma
    hid_ref[...] = (swish * upward).astype(jnp.bfloat16)
    gg_ref[...] = (grad_hidden * upward * sigma * (1.0 + gate * (1.0 - sigma))).astype(
        jnp.bfloat16
    )
    gu_ref[...] = (grad_hidden * swish).astype(jnp.bfloat16)


def ffn_stage(second, grad_hidden, w_gate, w_up, where):
    rows, model = second.shape
    units = w_gate.shape[1] // 2
    block = 256
    steps = units // block
    col_spec = pl.BlockSpec((model, block), lambda i, w: (0, pair_bit(w) * steps + i))
    unit_spec = pl.BlockSpec((rows, block), lambda i, w: (0, i))
    unit = jax.ShapeDtypeStruct((rows, units), jnp.bfloat16)
    return pl.pallas_call(
        ffn_kernel,
        out_shape=(unit, unit, unit),
        grid_spec=pltpu.PrefetchScalarGridSpec(
            num_scalar_prefetch=1,
            grid=(steps,),
            in_specs=[
                pl.BlockSpec((rows, model), lambda i, w: (0, 0), pipeline_mode=pl.Buffered(1)),
                unit_spec,
                col_spec,
                col_spec,
            ],
            out_specs=[unit_spec] * 3,
        ),
        compiler_params=pltpu.CompilerParams(vmem_limit_bytes=VMEM_LIMIT),
        cost_estimate=cost("ffn_stage", 4 * rows * model * units, 6 * rows * model),
        name="ffn_stage",
    )(where, second, grad_hidden, w_gate, w_up)


def grad_second_kernel(where_ref, gg_ref, gu_ref, wg_ref, wu_ref, out_ref):
    total = right_dot(gg_ref[...], wg_ref[...]) + right_dot(gu_ref[...], wu_ref[...])
    out_ref[...] = total.astype(jnp.bfloat16)


def grad_second_half(half, name, grads, weights, where):
    rows, units = grads[0].shape
    rows //= 2
    model = weights[0].shape[0]
    block = 512
    left_spec = pl.BlockSpec((rows, units), lambda n, w: (half, 0), pipeline_mode=pl.Buffered(1))
    right_spec = pl.BlockSpec((block, units), lambda n, w: (n, pair_bit(w)))
    return pl.pallas_call(
        grad_second_kernel,
        out_shape=jax.ShapeDtypeStruct((rows, model), jnp.bfloat16),
        grid_spec=pltpu.PrefetchScalarGridSpec(
            num_scalar_prefetch=1,
            grid=(model // block,),
            in_specs=[left_spec] * 2 + [right_spec] * 2,
            out_specs=pl.BlockSpec((rows, block), lambda n, w: (0, n)),
        ),
        compiler_params=pltpu.CompilerParams(vmem_limit_bytes=VMEM_LIMIT),
        cost_estimate=cost(name, 4 * rows * units * model, 4 * rows * model),
        name=name,
    )(where, *grads, *weights)


def ffn_out_kernel(where_ref, hid_ref, wd_ref, keep_ref, send_ref):
    total = dot(hid_ref[...], wd_ref[...])
    half = keep_ref.shape[0]
    keep_ref[...] = total[:half].astype(jnp.bfloat16)
    send_ref[...] = total[half:].astype(jnp.bfloat16)


def unit_sum(kernel, name, lefts, rights, transposed, where):
    rows, units = lefts[0].shape
    model = rights[0].shape[0 if transposed else 1]
    block = 512
    if transposed:
        right_spec = pl.BlockSpec((block, units), lambda n, w: (n, pair_bit(w)))
    else:
        right_spec = pl.BlockSpec((units, block), lambda n, w: (pair_bit(w), n))
    left_spec = pl.BlockSpec((rows, units), lambda n, w: (0, 0), pipeline_mode=pl.Buffered(1))
    half = jax.ShapeDtypeStruct((rows // 2, model), jnp.bfloat16)
    half_spec = pl.BlockSpec((rows // 2, block), lambda n, w: (0, n))
    return pl.pallas_call(
        kernel,
        out_shape=(half, half),
        grid_spec=pltpu.PrefetchScalarGridSpec(
            num_scalar_prefetch=1,
            grid=(model // block,),
            in_specs=[left_spec] * len(lefts) + [right_spec] * len(rights),
            out_specs=[half_spec, half_spec],
        ),
        compiler_params=pltpu.CompilerParams(vmem_limit_bytes=VMEM_LIMIT),
        cost_estimate=cost(name, 2 * len(lefts) * rows * units * model, 4 * rows * model),
        name=name,
    )(where, *lefts, *rights)


def share_spot(spot, count, swap_bits):
    if swap_bits:
        return (spot & 1) * (count // 2) + lax.shift_right_logical(spot, 1)
    return spot


def shares_kernel(left_count, swap_bits, pairs, where_ref, *refs):
    lefts, refs = refs[:left_count], refs[left_count:]
    rights, (keep_ref, send_ref) = refs[:-2], refs[-2:]
    share = keep_ref.shape[1]
    step = pl.program_id(0)
    pieces = [left_dot(lefts[l][...], rights[r][...]) for l, r in pairs]
    per_step = lefts[0].shape[1] // share
    if per_step == 1:
        value = jnp.concatenate(pieces, axis=1).astype(keep_ref.dtype)
        sends = step < pl.num_programs(0) // 2

        @pl.when(sends)
        def _():
            send_ref[0] = value

        @pl.when(jnp.logical_not(sends))
        def _():
            keep_ref[0] = value

        return
    for k in range(per_step):
        rows = slice(k * share, (k + 1) * share)
        value = jnp.concatenate([piece[rows] for piece in pieces], axis=1)
        index = step * per_step + k
        put_share(value, index, where_ref[0] & 1, keep_ref, send_ref, swap_bits)


def weight_shares(name, lefts, rights, pairs, ctx_count, swap_bits, where):
    rows, model = lefts[0].shape
    block = 256
    share, half = model // ctx_count, ctx_count // 2
    width = sum(rights[r].shape[1] for _, r in pairs)
    shares = jax.ShapeDtypeStruct((half, share, width), jnp.bfloat16)
    if share == block:

        def left_map(i, w):
            mine = w[0] & 1
            return 0, jnp.where(i < half, 2 * i + 1 - mine, 2 * (i - half) + mine)

        left_spec = pl.BlockSpec((rows, block), left_map)
        spot = lambda index: share_spot(index, half, swap_bits)
        keep_spec = pl.BlockSpec(
            (1, share, width), lambda i, w: (spot(jnp.maximum(i - half, 0)), 0, 0)
        )
        send_spec = pl.BlockSpec(
            (1, share, width), lambda i, w: (spot(jnp.minimum(i, half - 1)), 0, 0)
        )
    else:
        left_spec = pl.BlockSpec((rows, block), lambda i, w: (0, i))
        keep_spec = send_spec = pl.BlockSpec(shares.shape, lambda i, w: (0, 0, 0))
    return pl.pallas_call(
        functools.partial(shares_kernel, len(lefts), swap_bits, pairs),
        out_shape=(shares, shares),
        grid_spec=pltpu.PrefetchScalarGridSpec(
            num_scalar_prefetch=1,
            grid=(model // block,),
            in_specs=[left_spec] * len(lefts)
            + [
                pl.BlockSpec(r.shape, lambda i, w: (0, 0), pipeline_mode=pl.Buffered(1))
                for r in rights
            ],
            out_specs=[keep_spec, send_spec],
        ),
        compiler_params=pltpu.CompilerParams(vmem_limit_bytes=VMEM_LIMIT),
        cost_estimate=cost(name, 2 * rows * model * width, 4 * rows * model),
        name=name,
    )(where, *lefts, *rights)


def unit_shares_kernel(where_ref, left_ref, right_ref, out_ref):
    share = out_ref.shape[1]
    total = left_dot(left_ref[...], right_ref[...]).astype(out_ref.dtype)
    per_step = left_ref.shape[1] // share
    if out_ref.shape[0] == 1:
        out_ref[0] = total
    else:
        for k in range(per_step):
            index = pl.program_id(0) * per_step + k
            out_ref[pl.ds(unit_spot(index, out_ref.shape[0]), 1)] = total[k * share : (k + 1) * share][None]


def unit_spot(index, ctx_count):
    return (index & 1) * (ctx_count // 2) + lax.shift_right_logical(index, 1)


def unit_shares(name, left, right, ctx_count, where):
    rows, model = left.shape
    block, width = 256, right.shape[1]
    share = model // ctx_count
    shares = jax.ShapeDtypeStruct((ctx_count, share, width), jnp.bfloat16)
    if share == block:
        out_spec = pl.BlockSpec((1, share, width), lambda i, w: (unit_spot(i, ctx_count), 0, 0))
    else:
        out_spec = pl.BlockSpec(shares.shape, lambda i, w: (0, 0, 0))
    return pl.pallas_call(
        unit_shares_kernel,
        out_shape=shares,
        grid_spec=pltpu.PrefetchScalarGridSpec(
            num_scalar_prefetch=1,
            grid=(model // block,),
            in_specs=[
                pl.BlockSpec((rows, block), lambda i, w: (0, i)),
                pl.BlockSpec(right.shape, lambda i, w: (0, 0), pipeline_mode=pl.Buffered(1)),
            ],
            out_specs=out_spec,
        ),
        compiler_params=pltpu.CompilerParams(vmem_limit_bytes=VMEM_LIMIT),
        cost_estimate=cost(name, 2 * rows * model * width, 4 * rows * model),
        name=name,
    )(where, left, right)


def tail_kernel(kv_heads, where_ref, *refs):
    sums, refs = refs[: 2 * kv_heads], refs[2 * kv_heads :]
    cos_ref, sin_ref, refs = refs[0], refs[1], refs[2:]
    gq_refs, refs = refs[:kv_heads], refs[kv_heads:]
    wq_ref, wk_ref, wv_ref, keep_ref, send_ref, gkv_ref = refs
    cosine, sine = cos_ref[...], sin_ref[...]
    for h in range(kv_heads):
        total = sums[2 * h][...].astype(jnp.float32) + sums[2 * h + 1][...].astype(jnp.float32)
        total = total.astype(jnp.bfloat16)
        key = unrotate(total[:, :HEAD_SIZE].astype(jnp.float32), cosine, sine)
        cols = slice(h * HEAD_SIZE, (h + 1) * HEAD_SIZE)
        gkv_ref[:, cols] = key.astype(jnp.bfloat16)
        cols = slice((kv_heads + h) * HEAD_SIZE, (kv_heads + h + 1) * HEAD_SIZE)
        gkv_ref[:, cols] = total[:, HEAD_SIZE:]
    half = keep_ref.shape[0]
    key_width = kv_heads * HEAD_SIZE
    wide = gq_refs[0].shape[1]
    for n in range(0, wq_ref.shape[0], 512):
        span = slice(n, n + 512)
        total = right_dot(gkv_ref[:, :key_width], wk_ref[span, :])
        total += right_dot(gkv_ref[:, key_width:], wv_ref[span, :])
        for h in range(kv_heads):
            total += right_dot(gq_refs[h][...], wq_ref[span, h * wide : (h + 1) * wide])
        total = total.astype(jnp.bfloat16)
        keep_ref[:, span] = total[:half]
        send_ref[:, span] = total[half:]


def tail_stage(kv_sums, cosine, sine, grad_queries, wq, wk, wv, where):
    rows, model = cosine.shape[0], wq.shape[0]
    kv_heads = len(grad_queries)
    vmem = pl.BlockSpec(memory_space=pltpu.VMEM)
    half = jax.ShapeDtypeStruct((rows // 2, model), jnp.bfloat16)
    flat = [term for sums in kv_sums for term in sums]
    return pl.pallas_call(
        functools.partial(tail_kernel, kv_heads),
        out_shape=(
            half,
            half,
            jax.ShapeDtypeStruct((rows, 2 * kv_heads * HEAD_SIZE), jnp.bfloat16),
        ),
        in_specs=[pl.BlockSpec(memory_space=pltpu.SMEM)]
        + [vmem] * (len(flat) + 2 + kv_heads + 3),
        out_specs=[vmem] * 3,
        compiler_params=pltpu.CompilerParams(vmem_limit_bytes=VMEM_LIMIT),
        cost_estimate=cost("tail_stage", 2 * rows * model * (wq.shape[1] + 2 * wk.shape[1]), 4 * rows * model + 4 * wq.size
        ),
        name="tail_stage",
    )(where, *flat, cosine, sine, *grad_queries, wq, wk, wv)


def flip(value, axis, mask=1):
    return lax.ppermute(value, axis, [(i, i ^ mask) for i in range(lax.axis_size(axis))])


def ctx_flip(value, mask):
    if mask == 1:
        return flip(value, "x")
    if mask == 2:
        return flip(value, "l")
    return flip(value, "hi", mask // 4)


def add(left, right):
    return (left.astype(jnp.float32) + right.astype(jnp.float32)).astype(jnp.bfloat16)


def slots_of(value, tensor):
    rows = value.shape[0] // SLOTS
    return [
        lax.dynamic_slice_in_dim(value, (tensor ^ SLOT_XOR[u]) * rows, rows)
        for u in range(SLOTS)
    ]


def after(dep, *values):
    deps = dep if isinstance(dep, tuple) else (dep,)
    held = lax.optimization_barrier(deps + values)[len(deps) :]
    return held[0] if len(held) == 1 else held


class Stages:
    def __init__(self, block_order):
        self.live = block_order[0] >= 0

    def __call__(self, function, *args):
        shapes = jax.eval_shape(function, *args)
        empty = lambda *_: jax.tree.map(lambda a: jnp.zeros(a.shape, a.dtype), shapes)
        return lax.cond(self.live, function, empty, *args)


def gather_pair(own):
    partner = ctx_flip(own, 2)
    near = jnp.concatenate([own, partner, flip(own, "y"), flip(partner, "y")])
    return jnp.concatenate([near, flip(near, "core")])


def gather_slots(own):
    near = jnp.concatenate([own, flip(own, "y")])
    return near, flip(near, "core")


def place_rows(own, near, core, far, tensor):
    rows = own.shape[0]
    result = jnp.zeros((SLOTS * rows,) + own.shape[1:], own.dtype)
    for u, piece in enumerate((own, near, core, far)):
        result = lax.dynamic_update_slice_in_dim(
            result, piece, (tensor ^ SLOT_XOR[u]) * rows, 0
        )
    return result


def scatter_slots(keep, send, fill=lambda value: value):
    got = fill(flip(send, "core"))
    quarter = keep.shape[0] // 2
    far = flip(add(keep[quarter:], got[quarter:]), "y")
    return add(keep[:quarter], got[:quarter]), far


def pair_scatter(keep, send, fill=lambda near: near):
    got = fill(flip(send, "core"))
    n = keep.shape[0] // 4
    near = [add(keep[k * n : (k + 1) * n], got[k * n : (k + 1) * n]) for k in range(4)]
    far = flip(near[3], "y")
    got = flip(near[2], "y")
    return near, far, got


def pair_finish(near, far, got):
    away = add(near[1], far)
    return near[0], got, ctx_flip(away, 2), away


def total(terms):
    return sum(term.astype(jnp.float32) for term in terms)


class Reduce:
    def __init__(self, keep, send):
        self.keep, self.got = keep, ctx_flip(send, 1)

    def halve(self, mask, ctx, dep=None):
        keep, got = self.keep, self.got
        if dep is not None:
            keep, got = after(dep, keep, got)
        n = keep.shape[0] // 2
        bit = lax.div(ctx, mask) % 2
        pick = lambda value, index: lax.dynamic_slice_in_dim(value, index * n, n, 0)
        away = ctx_flip(add(pick(keep, 1 - bit), pick(got, 1 - bit)), mask)
        self.keep, self.got = add(pick(keep, bit), pick(got, bit)), away

    def sum(self):
        return (self.keep.astype(jnp.float32) + self.got.astype(jnp.float32))[0]


def high_masks(ctx_count):
    masks, mask = [], ctx_count // 2
    while mask >= 4:
        masks.append(mask)
        mask //= 2
    return masks


def unit_sum_over(shares):
    return lax.psum_scatter(shares, ("x", "hi"), scatter_dimension=0, tiled=True)


def split_halves(summed, ctx, dep):
    summed = after(dep, summed)
    pair = lax.div(ctx, 2) % 2
    pick = lambda index: lax.dynamic_index_in_dim(summed, index, 0, keepdims=False)
    return pick(pair), pick(1 - pair)


def join_halves(own, other, ctx):
    pair = lax.div(ctx, 2) % 2
    low, high = jnp.where(pair == 0, own, other), jnp.where(pair == 0, other, own)
    return jnp.concatenate([low, high], axis=1).astype(jnp.float32)


class KvReduce:
    def __init__(self, keep, got):
        self.keep, self.got = keep, got

    def merge(self, dep):
        keep, got = after(dep, self.keep, self.got)
        n = keep.shape[0] // 2
        return add(keep[:n], got[:n]), add(keep[n:], got[n:])


def norm_back(grad_out, normed, inv_scale, gain):
    scaled = grad_out * gain
    inner = jnp.mean(scaled * normed, axis=-1, keepdims=True)
    return (inv_scale * (scaled - normed * inner), jnp.sum(grad_out * normed, axis=0))


def body(
    layer_input,
    attn_gain,
    w_query,
    key_matrix,
    value_matrix,
    w_out,
    ffn_gain,
    w_gate,
    w_up,
    w_down,
    cotangent,
    block_order,
    cont_prompt,
):
    ctx_count = lax.axis_size("hi") * 4
    ctx = (lax.axis_index("hi") * 2 + lax.axis_index("l")) * 2 + lax.axis_index("x")
    tensor = lax.axis_index("y") * 2 + lax.axis_index("core")
    where = jnp.stack([ctx, tensor]).astype(jnp.int32)
    quarter = layer_input.shape[0] // SLOTS
    kv_heads = key_matrix.shape[1] // HEAD_SIZE
    highs = high_masks(ctx_count)

    stage = Stages(block_order)
    cot_own = lax.dynamic_slice_in_dim(cotangent, tensor * quarter, quarter)
    cot_slots = slots_of(cotangent, tensor)
    cot_part = ctx_flip(cot_own, 2)
    first_input, queries, kv_local, cosine, sine = input_stage(
        layer_input, attn_gain, w_query, key_matrix, value_matrix, block_order, cont_prompt, where
    )
    def first_keys(kv):
        high = {0: kv}
        for bit in reversed(highs):
            for mask in list(high):
                high[mask + bit] = ctx_flip(high[mask], bit)
        del high[0]
        return high, ctx_flip(kv, 2), ctx_flip(kv, 1)

    def second_keys(high, low, cot):
        return (
            ctx_flip(low, 1),
            flip(cot, "y"),
            {mask: ctx_flip(value, 2) for mask, value in high.items()},
            {mask: ctx_flip(value, 1) for mask, value in high.items()},
        )

    def third_keys(both, cot):
        return {mask: ctx_flip(value, 1) for mask, value in both.items()}, flip(cot, "core")

    high, part_l, part_x = stage(first_keys, after(cot_part, kv_local))
    part_lx, more, high_l, high_x = stage(second_keys, high, part_l, cot_part)
    cot_part = jnp.concatenate([cot_part, more])
    high_lx, cot_far = stage(third_keys, high_l, cot_part)
    parts = {0: kv_local, 1: part_x, 2: part_l, 3: part_lx}
    for mask in high:
        parts[mask], parts[mask + 1] = high[mask], high_x[mask]
        parts[mask + 2], parts[mask + 3] = high_l[mask], high_lx[mask]
    parts = [parts[mask] for mask in range(ctx_count)]
    cot = jnp.concatenate(
        [cot_slots[0], cot_part[:quarter], cot_slots[1], cot_part[quarter:]]
        + [cot_slots[2], cot_far[:quarter], cot_slots[3], cot_far[quarter:]]
    )
    mixed, log_total, keep, send = attention_forward(
        queries, w_out, parts, block_order, cont_prompt, where
    )
    first_half = flip(send, "core")
    near = add(keep, first_half)
    far = flip(near[quarter:], "y")
    grad_hidden = grad_hidden_stage(after(near, cot), w_down, where)
    own_input = lax.dynamic_slice_in_dim(layer_input, tensor * quarter, quarter)
    own_input = own_input.astype(jnp.float32)
    middle = own_input + total((near[:quarter], after(grad_hidden, far)))
    inv_two = lax.rsqrt(jnp.mean(middle * middle, axis=-1, keepdims=True) + eps_norm)
    normed_two = middle * inv_two
    second = gather_pair((normed_two * ffn_gain).astype(jnp.bfloat16))
    hidden, grad_gate, grad_up = ffn_stage(second, grad_hidden, w_gate, w_up, where)

    down_shares = unit_shares("down_shares", cot, hidden, ctx_count, where)
    down = unit_sum_over(down_shares)
    grads, weights = after(down_shares, grad_gate, grad_up), (w_gate, w_up)
    send = grad_second_half(1, "grad_second_send", grads, weights, where)

    def second_stage(send, grad_gate, grad_up, hidden):
        keep = grad_second_half(0, "grad_second_keep", (grad_gate, grad_up), weights, where)
        near, far, got = pair_scatter(keep, send)
        shares = unit_shares("gate_shares", second, after(near[3], grad_gate), ctx_count, where)
        *terms, away = pair_finish(near, after(shares, far), got)
        halves = unit_sum(
            ffn_out_kernel, "ffn_out", (after(away, hidden),), (w_down,), False, where
        )
        return total(after(halves[0], *terms)), shares, halves

    grad_second, gate_shares, ffn_halves = stage(second_stage, send, *grads, hidden)
    gate = unit_sum_over(gate_shares)

    def branch_stage(grad_second, grad_up, own):
        grad_norm, gain_part = norm_back(grad_second, normed_two, inv_two, ffn_gain)
        grad_middle = own.astype(jnp.float32) + grad_norm
        branch = grad_middle.astype(jnp.bfloat16)
        shares = unit_shares("up_shares", second, after(branch, grad_up), ctx_count, where)
        near = jnp.concatenate([branch, after(shares, flip(branch, "y"))])
        return grad_middle, gain_part, shares, jnp.concatenate([near, flip(near, "core")])

    grad_middle, ffn_gain_part, up_shares, grad_branch = stage(
        branch_stage, grad_second, grad_up, cot_own
    )
    backward, kv = [], []
    held = grad_branch
    for head in range(kv_heads):
        backward.append(
            attention_backward(
                head, queries, held, w_out, mixed, log_total, parts, cosine, sine,
                block_order, cont_prompt, where,
            )
        )
        kv.append(KvReduce(backward[-1][1], ctx_flip(backward[-1][2], 1)))
        dep = backward[-1][0]
        if head == 0:
            down_own, down_away = split_halves(down, ctx, dep)
            down_other = ctx_flip(down_away, 2)
            dep = down_own
        held = after(dep, grad_branch)
    grad_queries = [item[0] for item in backward]
    branch_shares = weight_shares(
        "branch_shares",
        (first_input, grad_branch),
        grad_queries + [after(dep, mixed)],
        tuple((0, h) for h in range(kv_heads)) + ((1, kv_heads),),
        ctx_count,
        True,
        where,
    )
    def out_stage(keep, send):
        got = flip(send, "core")
        n = keep.shape[0] // 4
        near = [add(keep[k * n : (k + 1) * n], got[k * n : (k + 1) * n]) for k in range(4)]
        return near[0], near[2], add(near[1], flip(near[3], "y"))

    def first_stage(keep, send, own_input, grad_middle):
        terms = scatter_slots(keep, send)
        inv = lax.rsqrt(jnp.mean(own_input * own_input, axis=-1, keepdims=True) + eps_norm)
        grad_norm, gain_part = norm_back(total(terms), own_input * inv, inv, attn_gain)
        return gain_part, (grad_middle + grad_norm).astype(jnp.bfloat16)

    def row_stage(near, other):
        near = jnp.concatenate([near, other])
        return near, flip(near, "core")

    def gain_stage(gains):
        gains = gains + flip(gains, "core")
        gains = gains + flip(gains, "y")
        for mask in [1, 2] + highs:
            gains = gains + ctx_flip(gains, mask)
        return gains

    dep = branch_shares[0]
    kv = [item.merge(dep) for item in kv]
    dep = tuple(keep for keep, _ in kv)
    up = unit_sum_over(after(dep, up_shares))
    sum_down = join_halves(down_own, after(dep, down_other), ctx).T
    dep = sum_down
    got = [ctx_flip(after(dep, value), 2) for _, value in kv]
    branch = Reduce(*after(dep, *branch_shares))
    out_near, out_own, out_away = stage(out_stage, *after(dep, *ffn_halves))
    dep = out_away
    for mask in highs:
        kv = [
            KvReduce(keep, value).merge(dep) for (keep, _), value in zip(kv, got)
        ]
        got = [ctx_flip(value, mask) for _, value in kv]
    dep = tuple(keep for keep, _ in kv)
    gate_own, gate_away = split_halves(gate, ctx, dep)
    dep = gate_own
    gate_other = ctx_flip(after(dep, gate_away), 2)
    out_far, out_got = stage(
        lambda away, own: (ctx_flip(away, 2), flip(own, "y")), *after(dep, out_away, out_own)
    )
    dep = out_far
    branch.halve(2, ctx, dep)
    dep = branch.keep
    output = (middle + total(after(dep, out_near, out_got, out_far))).astype(jnp.bfloat16)
    dep = output
    keep, send, grad_kv = tail_stage(
        [after(dep, keep, value) for (keep, _), value in zip(kv, got)], cosine, sine,
        grad_queries, w_query, key_matrix, value_matrix, where,
    )
    dep = keep
    kv_shares = weight_shares(
        "kv_shares", (first_input,), (after(dep, grad_kv),), ((0, 0),), ctx_count, True, where
    )
    dep = kv_shares[0]
    last = Reduce(*after(dep, *kv_shares))
    attn_gain_part, grad_input = stage(
        first_stage, after(dep, keep), send, own_input, grad_middle
    )
    dep = grad_input
    near = jnp.concatenate([grad_input, output])
    near_other = flip(after(dep, near), "y")
    sum_gate = join_halves(gate_own, after(dep, gate_other), ctx)
    dep = sum_gate
    for mask in highs:
        branch.halve(mask, ctx, dep)
        dep = branch.keep
    last.halve(2, ctx, dep)
    dep = last.keep
    gains = stage(gain_stage, after(dep, jnp.stack([attn_gain_part, ffn_gain_part])))
    dep = gains
    for mask in highs:
        last.halve(mask, ctx, dep)
        dep = last.keep
    near, far = stage(row_stage, near, after(dep, near_other))
    dep = far
    up_own, up_away = split_halves(up, ctx, dep)
    dep = up_own
    up_other = ctx_flip(after(dep, up_away), 2)
    last.keep, last.got = after(dep, last.keep, last.got)
    last_sum = last.sum()
    dep = last_sum
    quarters = [near[n * quarter : (n + 1) * quarter] for n in range(4)]
    quarters += [after(dep, far)[n * quarter : (n + 1) * quarter] for n in range(4)]
    grad_rows, output_rows = [
        place_rows(quarters[k], quarters[k + 2], quarters[k + 4], quarters[k + 6], tensor)
        for k in range(2)
    ]
    dep = (grad_rows, output_rows)
    branch.keep, branch.got = after(dep, branch.keep, branch.got)
    branch_sum = branch.sum()
    dep = branch_sum
    sum_up = join_halves(up_own, after(dep, up_other), ctx)
    dep = sum_up
    grad_input, output = grad_rows, output_rows
    width_q, width_k = w_query.shape[1], key_matrix.shape[1]
    sum_query, sum_out = branch_sum[:, :width_q], branch_sum[:, width_q:].T
    sum_key, sum_value = last_sum[:, :width_k], last_sum[:, width_k:]

    gains = gains.reshape(2, ctx_count * SLOTS, -1)
    gains = lax.dynamic_index_in_dim(gains, ctx * SLOTS + tensor, 1, keepdims=False)
    return (
        output,
        grad_input,
        gains[0],
        sum_query,
        sum_key,
        sum_value,
        sum_out,
        gains[1],
        sum_gate,
        sum_up,
        sum_down,
    )


def solution(mesh):
    rows, heads = ("hi", "l", "x"), ("y", "core")
    split = Mesh(mesh.devices.reshape(-1, 2, 2, 2, 2), rows + heads)
    placed = (
        P(rows, None),
        P(),
        P(None, heads),
        P(None, heads),
        P(None, heads),
        P(heads, None),
        P(),
        P(None, heads),
        P(None, heads),
        P(heads, None),
        P(rows, None),
        P(),
        P(),
    )
    return jax.shard_map(
        body,
        mesh=split,
        in_specs=placed,
        out_specs=(
            P(rows, None),
            P(rows, None),
            P(rows + heads),
            P(rows, heads),
            P(rows, heads),
            P(rows, heads),
            P(heads, rows),
            P(rows + heads),
            P(rows, heads),
            P(rows, heads),
            P(heads, rows),
        ),
        check_vma=False,
    )
```

```python
import functools
import math

import jax
import jax.numpy as jnp
import numpy as np
from jax import lax
from jax.experimental import pallas as pl
from jax.experimental.pallas import tpu as pltpu
from jax.sharding import Mesh
from jax.sharding import PartitionSpec as P

HEAD_SIZE = 128
PROMPT = 2048
CONT_LEN = 256
CONTS = 8
BLOCK = 128
PER_PROMPT = PROMPT // BLOCK
PER_CONT = CONT_LEN // BLOCK
LOG2E = 1.4426950408889634
NEG = -1e30
SLOTS = 4
VMEM_LIMIT = 60 << 20
VMEM_SMALL = 28 << 20
PAIR_STEPS = (4, 1)

eps_norm = 1e-05
rope_base = 1000000.0

SLOT_XOR = (0, 2, 1, 3)


def plain_dot(left, right):
    return jnp.dot(left, right, preferred_element_type=jnp.float32)


def left_dot(left, right):
    return lax.dot_general(
        left, right, (((0,), (0,)), ((), ())), preferred_element_type=jnp.float32
    )


def right_dot(left, right):
    return lax.dot_general(
        left, right, (((1,), (1,)), ((), ())), preferred_element_type=jnp.float32
    )


def slot_quarter(slot, tensor):
    return ((slot & 1) * 2 + lax.shift_right_logical(slot, 1)) ^ tensor


def stored_block(index, where_ref):
    rank = lax.div(index, SLOTS) ^ where_ref[0]
    return rank * SLOTS + slot_quarter(index & 3, where_ref[1])


def block_plan(order_ref, cont_ref, where_ref, slot):
    count = cont_ref.shape[0]
    prompt_blocks = count // CONTS * PER_PROMPT
    own = order_ref[stored_block(slot, where_ref)]
    is_prompt = own < prompt_blocks
    offset = own - prompt_blocks
    which = jnp.clip(lax.div(offset, PER_CONT), 0, count - 1)
    group = jnp.where(is_prompt, lax.div(own, PER_PROMPT), cont_ref[which])
    inner = jnp.where(is_prompt, lax.rem(own, PER_PROMPT), lax.rem(offset, PER_CONT))
    has_prev = lax.rem(inner, 2)
    pairs = jnp.where(is_prompt, lax.div(inner, 2), PER_PROMPT // 2)
    prev = own - has_prev
    return group * PER_PROMPT, pairs, prev, own, has_prev


def fill_inverse(order_ref, where_ref, inverse_ref):
    def put(index, carry):
        inverse_ref[order_ref[stored_block(index, where_ref)]] = index
        return carry

    lax.fori_loop(0, order_ref.shape[0], put, 0)


def rotate(vec, cosine, sine):
    return vec * cosine + pltpu.roll(vec, HEAD_SIZE // 2, 1) * sine


def unrotate(vec, cosine, sine):
    return vec * cosine + pltpu.roll(vec * sine, HEAD_SIZE // 2, 1)


def angle_tables():
    half = HEAD_SIZE // 2
    freq = np.float64(rope_base) ** (-(2.0 * np.arange(half) / HEAD_SIZE))
    freq = np.concatenate([freq, freq])
    starts = np.arange(-(-(PER_PROMPT + PER_CONT) // 8) * 8) * BLOCK
    start = starts[:, None] * freq[None]
    inner = np.arange(BLOCK)[:, None] * freq[None]
    return tuple(
        f(a).astype(np.float32) for a in (start, inner) for f in (np.cos, np.sin)
    )


def key_rows(inverse_ref, logical):
    return pl.ds(pl.multiple_of(inverse_ref[logical] * BLOCK, BLOCK), BLOCK)


def tile_pair(ref, rows_a, rows_b, column):
    return tile(ref, (rows_a, rows_b), column)


def tile(ref, rows, column):
    cols = pl.ds(column, HEAD_SIZE)
    return jnp.concatenate([ref[span, cols] for span in rows], axis=0)


def own_mask(has_prev, rep):
    shape = (2 * BLOCK, rep * BLOCK)
    row = lax.broadcasted_iota(jnp.int32, shape, 0)
    col = lax.broadcasted_iota(jnp.int32, shape, 1)
    first_row = BLOCK * (1 - has_prev)
    return (row >= first_row) & (row - BLOCK <= lax.rem(col, BLOCK))


def stack_t(ref, rows, column, rep):
    return jnp.concatenate(
        [ref[rows, pl.ds(column + r * HEAD_SIZE, HEAD_SIZE)].T for r in range(rep)], axis=1
    )


def stack_rows(ref, rows, column, rep):
    return jnp.concatenate(
        [ref[rows, pl.ds(column + r * HEAD_SIZE, HEAD_SIZE)] for r in range(rep)], axis=0
    )


def dot(left, right):
    return jnp.dot(left, right, preferred_element_type=jnp.float32)


def start_parts(parts, buffer_ref, sem, column):
    rows, width = parts[0].shape[0], buffer_ref.shape[1]
    copies = [
        pltpu.make_async_copy(
            part.at[:, pl.ds(column, width)], buffer_ref.at[pl.ds(p * rows, rows), :], sem.at[p]
        )
        for p, part in enumerate(parts)
    ]
    for copy in copies:
        copy.start()
    return copies


def forward_kernel(rep, hps, ctx_count, order_ref, cont_ref, where_ref, q_ref, wo_ref, *refs):
    parts, refs = refs[:ctx_count], refs[ctx_count:]
    out_ref, lse_ref, keep_ref, send_ref, kv_ref, inverse_ref, qt_ref, acc_ref, sem = refs
    copies = start_parts(parts, kv_ref, sem, 0)
    fill_inverse(order_ref, where_ref, inverse_ref)
    for copy in copies:
        copy.wait()
    q_blocks = q_ref.shape[0] // BLOCK
    factor = LOG2E / math.sqrt(HEAD_SIZE)
    width = rep * HEAD_SIZE

    def one_query_block(qb, carry):
        base, pairs, prev, own, has_prev = block_plan(order_ref, cont_ref, where_ref, qb)
        rows = pl.ds(pl.multiple_of(qb * BLOCK, BLOCK), BLOCK)
        mask = own_mask(has_prev, rep)
        rows_a, rows_b = key_rows(inverse_ref, prev), key_rows(inverse_ref, own)
        state = []
        for h in range(hps):
            qt = stack_t(q_ref, rows, h * width, rep)
            qt_ref[h] = qt
            scores = dot(tile_pair(kv_ref, rows_a, rows_b, 2 * h * HEAD_SIZE), qt) * factor
            scores = jnp.where(mask, scores, NEG)
            best = jnp.max(scores, axis=0, keepdims=True)
            weights = jnp.exp2(scores - best)
            total = jnp.sum(weights, axis=0, keepdims=True)
            values = tile_pair(kv_ref, rows_a, rows_b, (2 * h + 1) * HEAD_SIZE)
            acc_ref[h] = dot(values.T, weights.astype(jnp.bfloat16))
            state += [best, total]

        def fold(first, count, state):
            rows = [key_rows(inverse_ref, first + n) for n in range(count)]
            after = []
            for h in range(hps):
                best, total = state[2 * h], state[2 * h + 1]
                keys = tile(kv_ref, rows, 2 * h * HEAD_SIZE)
                scores = dot(keys, qt_ref[h]) * factor
                newest = jnp.maximum(best, jnp.max(scores, axis=0, keepdims=True))
                weights = jnp.exp2(scores - newest)
                shrink = jnp.exp2(best - newest)
                total = total * shrink + jnp.sum(weights, axis=0, keepdims=True)
                values = tile(kv_ref, rows, (2 * h + 1) * HEAD_SIZE)
                acc_ref[h] = acc_ref[h] * shrink + dot(values.T, weights.astype(jnp.bfloat16))
                after += [newest, total]
            return tuple(after)

        state, done = tuple(state), 0
        for wide in PAIR_STEPS:
            upto = lax.div(pairs, wide) * wide
            state = lax.fori_loop(
                0,
                lax.div(upto - done, wide),
                lambda t, state, done=done, wide=wide: fold(
                    base + 2 * (done + wide * t), 2 * wide, state
                ),
                state,
            )
            done = upto
        for h in range(hps):
            best, total = state[2 * h], state[2 * h + 1]
            mixed = acc_ref[h] * (1.0 / total)
            for r in range(rep):
                part = mixed[:, r * BLOCK : (r + 1) * BLOCK]
                out_ref[rows, pl.ds(h * width + r * HEAD_SIZE, HEAD_SIZE)] = part.T.astype(
                    jnp.bfloat16
                )
            lse_ref[h, pl.ds(qb, 1), :] = best + jnp.log2(total)
        return carry

    lax.fori_loop(0, q_blocks, one_query_block, 0)
    mixed = out_ref[...]
    half = keep_ref.shape[0]
    for n in range(0, wo_ref.shape[1], 512):
        cols = slice(n, n + 512)
        partial = dot(mixed, wo_ref[:, cols]).astype(jnp.bfloat16)
        keep_ref[:, cols] = partial[:half]
        send_ref[:, cols] = partial[half:]


def backward_kernel(rep, hps, ctx_count, head, order_ref, cont_ref, where_ref, q_ref, gb_ref, wo_ref,
                    mix_ref, lse_ref, cos_ref, sin_ref, *refs):
    parts, refs = refs[:ctx_count], refs[ctx_count:]
    gq_ref, keep_ref, send_ref = refs[:3]
    kv_ref, gm_ref, inverse_ref, qt_ref, gmt_ref, gqt_ref, acc_ref, sem = refs[3:]
    copies = start_parts(parts, kv_ref, sem, head * kv_ref.shape[1])
    fill_inverse(order_ref, where_ref, inverse_ref)
    gm_ref[...] = right_dot(gb_ref[...], wo_ref[...]).astype(jnp.bfloat16)
    for copy in copies:
        copy.wait()
    q_blocks = q_ref.shape[0] // BLOCK
    scale = 1.0 / math.sqrt(HEAD_SIZE)
    factor = LOG2E * scale
    width = rep * HEAD_SIZE

    def clear(i, carry):
        acc_ref[pl.ds(pl.multiple_of(i * BLOCK, BLOCK), BLOCK), :] = jnp.zeros(
            (BLOCK, acc_ref.shape[1]), jnp.float32
        )
        return carry

    lax.fori_loop(0, order_ref.shape[0], clear, 0)

    def tile_terms(h, spans, lse, delta, q_rows, gm_rows, mask):
        kcol, vcol = 2 * h * HEAD_SIZE, (2 * h + 1) * HEAD_SIZE
        keys = tile(kv_ref, spans, kcol)
        values = tile(kv_ref, spans, vcol)
        weights = jnp.exp2(dot(keys, qt_ref[h]) * factor - lse)
        if mask is not None:
            weights = jnp.where(mask, weights, 0.0)
        grad_weights = dot(values, gmt_ref[h])
        grad_scores = (weights * (grad_weights - delta)).astype(jnp.bfloat16)
        gv = dot(weights.astype(jnp.bfloat16), gm_rows)
        gk = dot(grad_scores, q_rows)
        for n, span in enumerate(spans):
            piece = slice(n * BLOCK, (n + 1) * BLOCK)
            acc_ref[span, pl.ds(kcol, HEAD_SIZE)] += gk[piece]
            acc_ref[span, pl.ds(vcol, HEAD_SIZE)] += gv[piece]
        return dot(keys.T, grad_scores)

    def one_query_block(qb, carry):
        base, pairs, prev, own, has_prev = block_plan(order_ref, cont_ref, where_ref, qb)
        rows = pl.ds(pl.multiple_of(qb * BLOCK, BLOCK), BLOCK)
        mask = own_mask(has_prev, rep)
        rows_a, rows_b = key_rows(inverse_ref, prev), key_rows(inverse_ref, own)
        deltas, lses, q_stack, gm_stack = [], [], [], []
        for h in range(hps):
            qt_ref[h] = stack_t(q_ref, rows, h * width, rep)
            gmt = stack_t(gm_ref, rows, h * width, rep)
            gmt_ref[h] = gmt
            mixt = stack_t(mix_ref, rows, h * width, rep)
            deltas.append(
                jnp.sum(
                    gmt.astype(jnp.float32) * mixt.astype(jnp.float32), axis=0, keepdims=True
                )
            )
            lses.append(lse_ref[h, pl.ds(qb, 1), :])
        for h in range(hps):
            q_rows = stack_rows(q_ref, rows, h * width, rep)
            gm_rows = stack_rows(gm_ref, rows, h * width, rep)
            gqt_ref[h] = tile_terms(
                h, (rows_a, rows_b), lses[h], deltas[h], q_rows, gm_rows, mask
            )

        def fold(first, count):
            spans = [key_rows(inverse_ref, first + n) for n in range(count)]
            for h in range(hps):
                q_rows = stack_rows(q_ref, rows, h * width, rep)
                gm_rows = stack_rows(gm_ref, rows, h * width, rep)
                gqt_ref[h] += tile_terms(
                    h, spans, lses[h], deltas[h], q_rows, gm_rows, None
                )
            return 0

        done = 0
        for wide in PAIR_STEPS:
            upto = lax.div(pairs, wide) * wide
            lax.fori_loop(
                0,
                lax.div(upto - done, wide),
                lambda t, _, done=done, wide=wide: fold(base + 2 * (done + wide * t), 2 * wide),
                0,
            )
            done = upto
        for h in range(hps):
            total = gqt_ref[h] * scale
            for r in range(rep):
                part = total[:, r * BLOCK : (r + 1) * BLOCK]
                rounded = part.T.astype(jnp.bfloat16).astype(jnp.float32)
                gq_ref[rows, pl.ds(h * width + r * HEAD_SIZE, HEAD_SIZE)] = unrotate(
                    rounded, cos_ref[rows, :], sin_ref[rows, :]
                ).astype(jnp.bfloat16)
        return carry

    lax.fori_loop(0, q_blocks, one_query_block, 0)

    blocks = order_ref.shape[0]

    def place(index):
        chunk = lax.div(index, SLOTS)
        spot = (chunk & 1) * (ctx_count // 2) + (chunk & 2) // 2 * (ctx_count // 4) + (
            lax.shift_right_logical(chunk, 2)
        )
        return spot * SLOTS + (index & 3)

    def flush(i, carry):
        rows = pl.ds(pl.multiple_of(i * BLOCK, BLOCK), BLOCK)
        spot = place(i)
        parts = []
        for h in range(hps):
            parts.append(acc_ref[rows, pl.ds(2 * h * HEAD_SIZE, HEAD_SIZE)] * scale)
            parts.append(acc_ref[rows, pl.ds((2 * h + 1) * HEAD_SIZE, HEAD_SIZE)])
        value = jnp.concatenate(parts, axis=1).astype(jnp.bfloat16)

        @pl.when(spot < blocks // 2)
        def _():
            keep_ref[pl.ds(pl.multiple_of(spot * BLOCK, BLOCK), BLOCK), :] = value

        @pl.when(spot >= blocks // 2)
        def _():
            far = (spot - blocks // 2) * BLOCK
            send_ref[pl.ds(pl.multiple_of(far, BLOCK), BLOCK), :] = value

        return carry

    lax.fori_loop(0, blocks, flush, 0)


def attention_forward(q, w_out, parts, order, cont, where):
    ctx_count = len(parts)
    rows, tokens = q.shape[0], ctx_count * q.shape[0]
    kv_heads = parts[0].shape[1] // (2 * HEAD_SIZE)
    rep = q.shape[1] // HEAD_SIZE // kv_heads
    q_blocks, model = rows // BLOCK, w_out.shape[1]
    vmem, smem, any_ = (
        pl.BlockSpec(memory_space=space) for space in (pltpu.VMEM, pltpu.SMEM, pl.ANY)
    )
    flops = 2 * rows * tokens * q.shape[1] + 2 * rows * q.shape[1] * model
    half = jax.ShapeDtypeStruct((rows // 2, model), jnp.bfloat16)
    return pl.pallas_call(
        functools.partial(forward_kernel, rep, kv_heads, ctx_count),
        out_shape=(
            jax.ShapeDtypeStruct(q.shape, jnp.bfloat16),
            jax.ShapeDtypeStruct((kv_heads, q_blocks, rep * BLOCK), jnp.float32),
            half,
            half,
        ),
        in_specs=[smem] * 3 + [vmem] * 2 + [any_] * ctx_count,
        out_specs=[vmem] * 4,
        scratch_shapes=[
            pltpu.VMEM((tokens, parts[0].shape[1]), jnp.bfloat16),
            pltpu.SMEM((order.shape[0],), jnp.int32),
            pltpu.VMEM((kv_heads, HEAD_SIZE, rep * BLOCK), jnp.bfloat16),
            pltpu.VMEM((kv_heads, HEAD_SIZE, rep * BLOCK), jnp.float32),
            pltpu.SemaphoreType.DMA((ctx_count,)),
        ],
        compiler_params=pltpu.CompilerParams(vmem_limit_bytes=VMEM_LIMIT),
        cost_estimate=cost("attention_forward", flops, 2 * tokens * parts[0].shape[1] + 4 * rows * model),
        name="attention_forward",
    )(order, cont, where, q, w_out, *parts)


def attention_backward(head, q, grad_branch, w_out, mixed, lse, parts, cosine, sine, order, cont,
                       where):
    ctx_count = len(parts)
    rows, tokens = q.shape[0], ctx_count * q.shape[0]
    kv_heads = parts[0].shape[1] // (2 * HEAD_SIZE)
    rep = q.shape[1] // HEAD_SIZE // kv_heads
    q_blocks, model = rows // BLOCK, w_out.shape[1]
    wide = rep * HEAD_SIZE
    q_spec = pl.BlockSpec((rows, wide), lambda g, *_: (0, head))
    whole = lambda g, *_: (0, 0)
    table_spec = pl.BlockSpec((rows, HEAD_SIZE), whole)
    half = (tokens // 2, 2 * HEAD_SIZE)
    flops = 5 * rows * tokens * wide + 2 * rows * wide * model
    return pl.pallas_call(
        functools.partial(backward_kernel, rep, 1, ctx_count, head),
        out_shape=(
            jax.ShapeDtypeStruct((rows, wide), jnp.bfloat16),
            jax.ShapeDtypeStruct(half, jnp.bfloat16),
            jax.ShapeDtypeStruct(half, jnp.bfloat16),
        ),
        grid_spec=pltpu.PrefetchScalarGridSpec(
            num_scalar_prefetch=3,
            grid=(1,),
            in_specs=[
                q_spec,
                pl.BlockSpec((rows, model), whole),
                pl.BlockSpec((wide, model), lambda g, *_: (head, 0)),
                q_spec,
                pl.BlockSpec((1, q_blocks, rep * BLOCK), lambda g, *_: (head, 0, 0)),
                table_spec,
                table_spec,
            ]
            + [pl.BlockSpec(memory_space=pl.ANY)] * ctx_count,
            out_specs=[
                pl.BlockSpec((rows, wide), whole),
                pl.BlockSpec(half, whole),
                pl.BlockSpec(half, whole),
            ],
            scratch_shapes=[
                pltpu.VMEM((tokens, 2 * HEAD_SIZE), jnp.bfloat16),
                pltpu.VMEM((rows, wide), jnp.bfloat16),
                pltpu.SMEM((order.shape[0],), jnp.int32),
                pltpu.VMEM((1, HEAD_SIZE, rep * BLOCK), jnp.bfloat16),
                pltpu.VMEM((1, HEAD_SIZE, rep * BLOCK), jnp.bfloat16),
                pltpu.VMEM((1, HEAD_SIZE, rep * BLOCK), jnp.float32),
                pltpu.VMEM((tokens, 2 * HEAD_SIZE), jnp.float32),
                pltpu.SemaphoreType.DMA((ctx_count,)),
            ],
        ),
        compiler_params=pltpu.CompilerParams(vmem_limit_bytes=VMEM_LIMIT),
        cost_estimate=cost(f"attention_backward_{head}", flops, 4 * tokens * wide + 2 * rows * model),
        name=f"attention_backward_{head}",
    )(order, cont, where, q, grad_branch, w_out, mixed, lse, cosine, sine, *parts)


def input_kernel(order_ref, cont_ref, where_ref, gain_ref, x_hbm, wq_hbm, wk_hbm, wv_hbm, table_hbm,
                 first_ref, q_ref, kv_ref, cos_ref, sin_ref,
                 x_ref, wq_ref, wk_ref, wv_ref, table_ref, sem):
    pairs = ((x_hbm, x_ref), (table_hbm, table_ref), (wk_hbm, wk_ref), (wv_hbm, wv_ref),
             (wq_hbm, wq_ref))
    copies = [
        pltpu.make_async_copy(source, target, sem.at[n])
        for n, (source, target) in enumerate(pairs)
    ]
    for copy in copies:
        copy.start()
    count = cont_ref.shape[0]
    prompt_blocks = count // CONTS * PER_PROMPT
    starts = (table_ref.shape[0] - 2 * BLOCK) // 2
    lane = lax.broadcasted_iota(jnp.int32, (BLOCK, HEAD_SIZE), 1)
    copies[0].wait()
    copies[1].wait()

    def one_slot(slot, carry):
        quarter = slot_quarter(slot, where_ref[1])
        rows = pl.ds(pl.multiple_of(slot * BLOCK, BLOCK), BLOCK)
        full = x_ref[pl.ds(pl.multiple_of(quarter * BLOCK, BLOCK), BLOCK), :].astype(jnp.float32)
        inv = lax.rsqrt(jnp.mean(full * full, axis=-1, keepdims=True) + eps_norm)
        first_ref[rows, :] = (full * inv * gain_ref[...]).astype(jnp.bfloat16)
        own = order_ref[stored_block(slot, where_ref)]
        spot = jnp.where(
            own < prompt_blocks,
            lax.rem(own, PER_PROMPT),
            PER_PROMPT + lax.rem(own - prompt_blocks, PER_CONT),
        )
        cos_start = table_ref[pl.ds(2 * BLOCK + spot, 1), :]
        sin_start = table_ref[pl.ds(2 * BLOCK + starts + spot, 1), :]
        cos_in, sin_in = table_ref[:BLOCK, :], table_ref[BLOCK : 2 * BLOCK, :]
        sine = sin_start * cos_in + cos_start * sin_in
        cos_ref[rows, :] = cos_start * cos_in - sin_start * sin_in
        sin_ref[rows, :] = jnp.where(lane < HEAD_SIZE // 2, -sine, sine)
        return carry

    lax.fori_loop(0, SLOTS, one_slot, 0)
    first = first_ref[...]
    cosine, sine = cos_ref[...], sin_ref[...]
    copies[2].wait()
    copies[3].wait()
    keys = dot(first, wk_ref[...])
    values = dot(first, wv_ref[...])
    for h in range(wk_ref.shape[1] // HEAD_SIZE):
        cols = slice(h * HEAD_SIZE, (h + 1) * HEAD_SIZE)
        low, high = 2 * h * HEAD_SIZE, (2 * h + 1) * HEAD_SIZE
        key = rotate(keys[:, cols], cosine, sine)
        kv_ref[:, low:high] = key.astype(jnp.bfloat16)
        kv_ref[:, high : high + HEAD_SIZE] = values[:, cols].astype(jnp.bfloat16)
    copies[4].wait()
    for n in range(0, wq_ref.shape[1], 256):
        queries = dot(first, wq_ref[:, n : n + 256])
        for m in range(0, 256, HEAD_SIZE):
            query = rotate(queries[:, m : m + HEAD_SIZE], cosine, sine)
            q_ref[:, n + m : n + m + HEAD_SIZE] = query.astype(jnp.bfloat16)


def input_stage(x, gain, wq, wk, wv, order, cont, where):
    rows, model = x.shape
    cos_start, sin_start, cos_in, sin_in = angle_tables()
    table = np.concatenate([cos_in, sin_in, cos_start, sin_start])
    vmem, smem, any_ = (
        pl.BlockSpec(memory_space=space) for space in (pltpu.VMEM, pltpu.SMEM, pl.ANY)
    )
    flops = 2 * rows * model * (wq.shape[1] + 2 * wk.shape[1])
    return pl.pallas_call(
        input_kernel,
        out_shape=(
            jax.ShapeDtypeStruct((rows, model), jnp.bfloat16),
            jax.ShapeDtypeStruct((rows, wq.shape[1]), jnp.bfloat16),
            jax.ShapeDtypeStruct((rows, 2 * wk.shape[1]), jnp.bfloat16),
            jax.ShapeDtypeStruct((rows, HEAD_SIZE), jnp.float32),
            jax.ShapeDtypeStruct((rows, HEAD_SIZE), jnp.float32),
        ),
        in_specs=[smem] * 3 + [vmem] + [any_] * 5,
        out_specs=[vmem] * 5,
        scratch_shapes=[
            pltpu.VMEM(a.shape, a.dtype) for a in (x, wq, wk, wv)
        ]
        + [pltpu.VMEM(table.shape, jnp.float32), pltpu.SemaphoreType.DMA((5,))],
        compiler_params=pltpu.CompilerParams(vmem_limit_bytes=VMEM_LIMIT),
        cost_estimate=cost("input_stage", flops, 4 * x.size + 2 * wq.size + 4 * wk.size),
        name="input_stage",
    )(order, cont, where, gain.reshape(1, -1), x, wq, wk, wv, table)


FILLERS = ("kv_shares", "grad_hidden")


def cost(name, flops, bytes_accessed):
    scale = 16.0 if name in FILLERS else 0.02
    return pl.CostEstimate(
        flops=int(flops * scale), bytes_accessed=int(bytes_accessed * scale), transcendentals=0
    )


def put_share(value, index, x_bit, keep_ref, send_ref, swap_bits):
    spot = share_spot(lax.shift_right_logical(index, 1), keep_ref.shape[0], swap_bits)
    stays = (index & 1) == x_bit
    value = value.astype(keep_ref.dtype)

    @pl.when(stays)
    def _():
        keep_ref[pl.ds(spot, 1)] = value[None]

    @pl.when(jnp.logical_not(stays))
    def _():
        send_ref[pl.ds(spot, 1)] = value[None]


def pair_bit(where_ref):
    return lax.shift_right_logical(where_ref[0], 1) & 1


def grad_hidden_kernel(where_ref, cot_ref, wd_ref, out_ref):
    out_ref[...] = right_dot(cot_ref[...], wd_ref[...])


def grad_hidden_stage(cot, w_down, where):
    rows, model = cot.shape
    units = w_down.shape[0] // 2
    block = 256
    steps = units // block
    return pl.pallas_call(
        grad_hidden_kernel,
        out_shape=jax.ShapeDtypeStruct((rows, units), jnp.float32),
        grid_spec=pltpu.PrefetchScalarGridSpec(
            num_scalar_prefetch=1,
            grid=(steps,),
            in_specs=[
                pl.BlockSpec((rows, model), lambda i, w: (0, 0), pipeline_mode=pl.Buffered(1)),
                pl.BlockSpec((block, model), lambda i, w: (pair_bit(w) * steps + i, 0)),
            ],
            out_specs=pl.BlockSpec((rows, block), lambda i, w: (0, i)),
        ),
        compiler_params=pltpu.CompilerParams(vmem_limit_bytes=VMEM_LIMIT),
        cost_estimate=cost("grad_hidden", 2 * rows * model * units, 4 * rows * model),
        name="grad_hidden",
    )(where, cot, w_down)


def ffn_kernel(where_ref, in_ref, gh_ref, wg_ref, wu_ref, hid_ref, gg_ref, gu_ref):
    gate = dot(in_ref[...], wg_ref[...])
    upward = dot(in_ref[...], wu_ref[...])
    grad_hidden = gh_ref[...]
    sigma = jax.nn.sigmoid(gate)
    swish = gate * sigma
    hid_ref[...] = (swish * upward).astype(jnp.bfloat16)
    gg_ref[...] = (grad_hidden * upward * sigma * (1.0 + gate * (1.0 - sigma))).astype(
        jnp.bfloat16
    )
    gu_ref[...] = (grad_hidden * swish).astype(jnp.bfloat16)


def ffn_stage(second, grad_hidden, w_gate, w_up, where):
    rows, model = second.shape
    units = w_gate.shape[1] // 2
    block = 256
    steps = units // block
    col_spec = pl.BlockSpec((model, block), lambda i, w: (0, pair_bit(w) * steps + i))
    unit_spec = pl.BlockSpec((rows, block), lambda i, w: (0, i))
    unit = jax.ShapeDtypeStruct((rows, units), jnp.bfloat16)
    return pl.pallas_call(
        ffn_kernel,
        out_shape=(unit, unit, unit),
        grid_spec=pltpu.PrefetchScalarGridSpec(
            num_scalar_prefetch=1,
            grid=(steps,),
            in_specs=[
                pl.BlockSpec((rows, model), lambda i, w: (0, 0), pipeline_mode=pl.Buffered(1)),
                unit_spec,
                col_spec,
                col_spec,
            ],
            out_specs=[unit_spec] * 3,
        ),
        compiler_params=pltpu.CompilerParams(vmem_limit_bytes=VMEM_LIMIT),
        cost_estimate=cost("ffn_stage", 4 * rows * model * units, 6 * rows * model),
        name="ffn_stage",
    )(where, second, grad_hidden, w_gate, w_up)


def grad_second_kernel(where_ref, gg_ref, gu_ref, wg_ref, wu_ref, out_ref):
    total = right_dot(gg_ref[...], wg_ref[...]) + right_dot(gu_ref[...], wu_ref[...])
    out_ref[...] = total.astype(jnp.bfloat16)


def grad_second_half(half, name, grads, weights, where):
    rows, units = grads[0].shape
    rows //= 2
    model = weights[0].shape[0]
    block = 512
    left_spec = pl.BlockSpec((rows, units), lambda n, w: (half, 0), pipeline_mode=pl.Buffered(1))
    right_spec = pl.BlockSpec((block, units), lambda n, w: (n, pair_bit(w)))
    return pl.pallas_call(
        grad_second_kernel,
        out_shape=jax.ShapeDtypeStruct((rows, model), jnp.bfloat16),
        grid_spec=pltpu.PrefetchScalarGridSpec(
            num_scalar_prefetch=1,
            grid=(model // block,),
            in_specs=[left_spec] * 2 + [right_spec] * 2,
            out_specs=pl.BlockSpec((rows, block), lambda n, w: (0, n)),
        ),
        compiler_params=pltpu.CompilerParams(vmem_limit_bytes=VMEM_LIMIT),
        cost_estimate=cost(name, 4 * rows * units * model, 4 * rows * model),
        name=name,
    )(where, *grads, *weights)


def ffn_out_kernel(where_ref, hid_ref, wd_ref, keep_ref, send_ref):
    total = dot(hid_ref[...], wd_ref[...])
    half = keep_ref.shape[0]
    keep_ref[...] = total[:half].astype(jnp.bfloat16)
    send_ref[...] = total[half:].astype(jnp.bfloat16)


def unit_sum(kernel, name, lefts, rights, transposed, where):
    rows, units = lefts[0].shape
    model = rights[0].shape[0 if transposed else 1]
    block = 512
    if transposed:
        right_spec = pl.BlockSpec((block, units), lambda n, w: (n, pair_bit(w)))
    else:
        right_spec = pl.BlockSpec((units, block), lambda n, w: (pair_bit(w), n))
    left_spec = pl.BlockSpec((rows, units), lambda n, w: (0, 0), pipeline_mode=pl.Buffered(1))
    half = jax.ShapeDtypeStruct((rows // 2, model), jnp.bfloat16)
    half_spec = pl.BlockSpec((rows // 2, block), lambda n, w: (0, n))
    return pl.pallas_call(
        kernel,
        out_shape=(half, half),
        grid_spec=pltpu.PrefetchScalarGridSpec(
            num_scalar_prefetch=1,
            grid=(model // block,),
            in_specs=[left_spec] * len(lefts) + [right_spec] * len(rights),
            out_specs=[half_spec, half_spec],
        ),
        compiler_params=pltpu.CompilerParams(vmem_limit_bytes=VMEM_LIMIT),
        cost_estimate=cost(name, 2 * len(lefts) * rows * units * model, 4 * rows * model),
        name=name,
    )(where, *lefts, *rights)


def share_spot(spot, count, swap_bits):
    if swap_bits:
        return (spot & 1) * (count // 2) + lax.shift_right_logical(spot, 1)
    return spot


def shares_kernel(left_count, swap_bits, pairs, where_ref, *refs):
    lefts, refs = refs[:left_count], refs[left_count:]
    rights, (keep_ref, send_ref) = refs[:-2], refs[-2:]
    share = keep_ref.shape[1]
    step = pl.program_id(0)
    pieces = [left_dot(lefts[l][...], rights[r][...]) for l, r in pairs]
    per_step = lefts[0].shape[1] // share
    if per_step == 1:
        value = jnp.concatenate(pieces, axis=1).astype(keep_ref.dtype)
        sends = step < pl.num_programs(0) // 2

        @pl.when(sends)
        def _():
            send_ref[0] = value

        @pl.when(jnp.logical_not(sends))
        def _():
            keep_ref[0] = value

        return
    for k in range(per_step):
        rows = slice(k * share, (k + 1) * share)
        value = jnp.concatenate([piece[rows] for piece in pieces], axis=1)
        index = step * per_step + k
        put_share(value, index, where_ref[0] & 1, keep_ref, send_ref, swap_bits)


def weight_shares(name, lefts, rights, pairs, ctx_count, swap_bits, where):
    rows, model = lefts[0].shape
    block = 256
    share, half = model // ctx_count, ctx_count // 2
    width = sum(rights[r].shape[1] for _, r in pairs)
    shares = jax.ShapeDtypeStruct((half, share, width), jnp.bfloat16)
    if share == block:

        def left_map(i, w):
            mine = w[0] & 1
            return 0, jnp.where(i < half, 2 * i + 1 - mine, 2 * (i - half) + mine)

        left_spec = pl.BlockSpec((rows, block), left_map)
        spot = lambda index: share_spot(index, half, swap_bits)
        keep_spec = pl.BlockSpec(
            (1, share, width), lambda i, w: (spot(jnp.maximum(i - half, 0)), 0, 0)
        )
        send_spec = pl.BlockSpec(
            (1, share, width), lambda i, w: (spot(jnp.minimum(i, half - 1)), 0, 0)
        )
    else:
        left_spec = pl.BlockSpec((rows, block), lambda i, w: (0, i))
        keep_spec = send_spec = pl.BlockSpec(shares.shape, lambda i, w: (0, 0, 0))
    return pl.pallas_call(
        functools.partial(shares_kernel, len(lefts), swap_bits, pairs),
        out_shape=(shares, shares),
        grid_spec=pltpu.PrefetchScalarGridSpec(
            num_scalar_prefetch=1,
            grid=(model // block,),
            in_specs=[left_spec] * len(lefts)
            + [
                pl.BlockSpec(r.shape, lambda i, w: (0, 0), pipeline_mode=pl.Buffered(1))
                for r in rights
            ],
            out_specs=[keep_spec, send_spec],
        ),
        compiler_params=pltpu.CompilerParams(vmem_limit_bytes=VMEM_SMALL),
        cost_estimate=cost(name, 2 * rows * model * width, 4 * rows * model),
        name=name,
    )(where, *lefts, *rights)


def unit_shares_kernel(where_ref, left_ref, right_ref, out_ref):
    share = out_ref.shape[1]
    total = left_dot(left_ref[...], right_ref[...]).astype(out_ref.dtype)
    per_step = left_ref.shape[1] // share
    if out_ref.shape[0] == 1:
        out_ref[0] = total
    else:
        for k in range(per_step):
            index = pl.program_id(0) * per_step + k
            out_ref[pl.ds(unit_spot(index, out_ref.shape[0]), 1)] = total[k * share : (k + 1) * share][None]


def unit_spot(index, ctx_count):
    return (index & 1) * (ctx_count // 2) + lax.shift_right_logical(index, 1)


def unit_shares(name, left, right, ctx_count, where):
    rows, model = left.shape
    block, width = 256, right.shape[1]
    share = model // ctx_count
    shares = jax.ShapeDtypeStruct((ctx_count, share, width), jnp.bfloat16)
    if share == block:
        out_spec = pl.BlockSpec((1, share, width), lambda i, w: (unit_spot(i, ctx_count), 0, 0))
    else:
        out_spec = pl.BlockSpec(shares.shape, lambda i, w: (0, 0, 0))
    return pl.pallas_call(
        unit_shares_kernel,
        out_shape=shares,
        grid_spec=pltpu.PrefetchScalarGridSpec(
            num_scalar_prefetch=1,
            grid=(model // block,),
            in_specs=[
                pl.BlockSpec((rows, block), lambda i, w: (0, i)),
                pl.BlockSpec(right.shape, lambda i, w: (0, 0), pipeline_mode=pl.Buffered(1)),
            ],
            out_specs=out_spec,
        ),
        compiler_params=pltpu.CompilerParams(vmem_limit_bytes=VMEM_LIMIT),
        cost_estimate=cost(name, 2 * rows * model * width, 4 * rows * model),
        name=name,
    )(where, left, right)


def tail_kernel(kv_heads, where_ref, *refs):
    sums, refs = refs[: 2 * kv_heads], refs[2 * kv_heads :]
    cos_ref, sin_ref, refs = refs[0], refs[1], refs[2:]
    gq_refs, refs = refs[:kv_heads], refs[kv_heads:]
    wq_ref, wk_ref, wv_ref, keep_ref, send_ref, gkv_ref = refs
    cosine, sine = cos_ref[...], sin_ref[...]
    for h in range(kv_heads):
        total = sums[2 * h][...].astype(jnp.float32) + sums[2 * h + 1][...].astype(jnp.float32)
        total = total.astype(jnp.bfloat16)
        key = unrotate(total[:, :HEAD_SIZE].astype(jnp.float32), cosine, sine)
        cols = slice(h * HEAD_SIZE, (h + 1) * HEAD_SIZE)
        gkv_ref[:, cols] = key.astype(jnp.bfloat16)
        cols = slice((kv_heads + h) * HEAD_SIZE, (kv_heads + h + 1) * HEAD_SIZE)
        gkv_ref[:, cols] = total[:, HEAD_SIZE:]
    half = keep_ref.shape[0]
    key_width = kv_heads * HEAD_SIZE
    wide = gq_refs[0].shape[1]
    for n in range(0, wq_ref.shape[0], 512):
        span = slice(n, n + 512)
        total = right_dot(gkv_ref[:, :key_width], wk_ref[span, :])
        total += right_dot(gkv_ref[:, key_width:], wv_ref[span, :])
        for h in range(kv_heads):
            total += right_dot(gq_refs[h][...], wq_ref[span, h * wide : (h + 1) * wide])
        total = total.astype(jnp.bfloat16)
        keep_ref[:, span] = total[:half]
        send_ref[:, span] = total[half:]


def tail_stage(kv_sums, cosine, sine, grad_queries, wq, wk, wv, where):
    rows, model = cosine.shape[0], wq.shape[0]
    kv_heads = len(grad_queries)
    vmem = pl.BlockSpec(memory_space=pltpu.VMEM)
    half = jax.ShapeDtypeStruct((rows // 2, model), jnp.bfloat16)
    flat = [term for sums in kv_sums for term in sums]
    return pl.pallas_call(
        functools.partial(tail_kernel, kv_heads),
        out_shape=(
            half,
            half,
            jax.ShapeDtypeStruct((rows, 2 * kv_heads * HEAD_SIZE), jnp.bfloat16),
        ),
        in_specs=[pl.BlockSpec(memory_space=pltpu.SMEM)]
        + [vmem] * (len(flat) + 2 + kv_heads + 3),
        out_specs=[vmem] * 3,
        compiler_params=pltpu.CompilerParams(vmem_limit_bytes=VMEM_SMALL),
        cost_estimate=cost("tail_stage", 2 * rows * model * (wq.shape[1] + 2 * wk.shape[1]), 4 * rows * model + 4 * wq.size
        ),
        name="tail_stage",
    )(where, *flat, cosine, sine, *grad_queries, wq, wk, wv)


def flip(value, axis, mask=1):
    return lax.ppermute(value, axis, [(i, i ^ mask) for i in range(lax.axis_size(axis))])


def ctx_flip(value, mask):
    if mask == 1:
        return flip(value, "x")
    if mask == 2:
        return flip(value, "l")
    return flip(value, "hi", mask // 4)


def add(left, right):
    return (left.astype(jnp.float32) + right.astype(jnp.float32)).astype(jnp.bfloat16)


def slots_of(value, tensor):
    rows = value.shape[0] // SLOTS
    return [
        lax.dynamic_slice_in_dim(value, (tensor ^ SLOT_XOR[u]) * rows, rows)
        for u in range(SLOTS)
    ]


def after(dep, *values):
    deps = dep if isinstance(dep, tuple) else (dep,)
    held = lax.optimization_barrier(deps + values)[len(deps) :]
    return held[0] if len(held) == 1 else held


class Stages:
    def __init__(self, block_order):
        self.live = block_order[0] >= 0

    def __call__(self, function, *args):
        shapes = jax.eval_shape(function, *args)
        empty = lambda *_: jax.tree.map(lambda a: jnp.zeros(a.shape, a.dtype), shapes)
        return lax.cond(self.live, function, empty, *args)


def gather_pair(own):
    partner = ctx_flip(own, 2)
    near = jnp.concatenate([own, partner, flip(own, "y"), flip(partner, "y")])
    return jnp.concatenate([near, flip(near, "core")])


def gather_slots(own):
    near = jnp.concatenate([own, flip(own, "y")])
    return near, flip(near, "core")


def place_rows(own, near, core, far, tensor):
    rows = own.shape[0]
    result = jnp.zeros((SLOTS * rows,) + own.shape[1:], own.dtype)
    for u, piece in enumerate((own, near, core, far)):
        result = lax.dynamic_update_slice_in_dim(
            result, piece, (tensor ^ SLOT_XOR[u]) * rows, 0
        )
    return result


def scatter_slots(keep, send, fill=lambda value: value):
    got = fill(flip(send, "core"))
    quarter = keep.shape[0] // 2
    far = flip(add(keep[quarter:], got[quarter:]), "y")
    return add(keep[:quarter], got[:quarter]), far


def pair_scatter(keep, send, fill=lambda near: near):
    got = fill(flip(send, "core"))
    n = keep.shape[0] // 4
    near = [add(keep[k * n : (k + 1) * n], got[k * n : (k + 1) * n]) for k in range(4)]
    far = flip(near[3], "y")
    got = flip(near[2], "y")
    return near, far, got


def pair_finish(near, far, got):
    away = add(near[1], far)
    return near[0], got, ctx_flip(away, 2), away


def total(terms):
    return sum(term.astype(jnp.float32) for term in terms)


class Reduce:
    def __init__(self, keep, send):
        self.keep, self.got = keep, ctx_flip(send, 1)

    def halve(self, mask, ctx, dep=None):
        keep, got = self.keep, self.got
        if dep is not None:
            keep, got = after(dep, keep, got)
        n = keep.shape[0] // 2
        bit = lax.div(ctx, mask) % 2
        pick = lambda value, index: lax.dynamic_slice_in_dim(value, index * n, n, 0)
        away = ctx_flip(add(pick(keep, 1 - bit), pick(got, 1 - bit)), mask)
        self.keep, self.got = add(pick(keep, bit), pick(got, bit)), away

    def sum(self):
        return (self.keep.astype(jnp.float32) + self.got.astype(jnp.float32))[0]


def high_masks(ctx_count):
    masks, mask = [], ctx_count // 2
    while mask >= 4:
        masks.append(mask)
        mask //= 2
    return masks


def unit_sum_over(shares):
    return lax.psum_scatter(shares, ("x", "hi"), scatter_dimension=0, tiled=True)


def split_halves(summed, ctx, dep):
    summed = after(dep, summed)
    pair = lax.div(ctx, 2) % 2
    pick = lambda index: lax.dynamic_index_in_dim(summed, index, 0, keepdims=False)
    return pick(pair), pick(1 - pair)


def join_halves(own, other, ctx):
    pair = lax.div(ctx, 2) % 2
    low, high = jnp.where(pair == 0, own, other), jnp.where(pair == 0, other, own)
    return jnp.concatenate([low, high], axis=1).astype(jnp.float32)


class KvReduce:
    def __init__(self, keep, got):
        self.keep, self.got = keep, got

    def merge(self, dep):
        keep, got = after(dep, self.keep, self.got)
        n = keep.shape[0] // 2
        return add(keep[:n], got[:n]), add(keep[n:], got[n:])


def norm_back(grad_out, normed, inv_scale, gain):
    scaled = grad_out * gain
    inner = jnp.mean(scaled * normed, axis=-1, keepdims=True)
    return (inv_scale * (scaled - normed * inner), jnp.sum(grad_out * normed, axis=0))


def body(
    layer_input,
    attn_gain,
    w_query,
    key_matrix,
    value_matrix,
    w_out,
    ffn_gain,
    w_gate,
    w_up,
    w_down,
    cotangent,
    block_order,
    cont_prompt,
):
    ctx_count = lax.axis_size("hi") * 4
    ctx = (lax.axis_index("hi") * 2 + lax.axis_index("l")) * 2 + lax.axis_index("x")
    tensor = lax.axis_index("y") * 2 + lax.axis_index("core")
    where = jnp.stack([ctx, tensor]).astype(jnp.int32)
    quarter = layer_input.shape[0] // SLOTS
    kv_heads = key_matrix.shape[1] // HEAD_SIZE
    highs = high_masks(ctx_count)

    stage = Stages(block_order)
    cot_own = lax.dynamic_slice_in_dim(cotangent, tensor * quarter, quarter)
    cot_slots = slots_of(cotangent, tensor)
    cot_part = ctx_flip(cot_own, 2)
    first_input, queries, kv_local, cosine, sine = input_stage(
        layer_input, attn_gain, w_query, key_matrix, value_matrix, block_order, cont_prompt, where
    )
    def first_keys(kv):
        high = {0: kv}
        for bit in reversed(highs):
            for mask in list(high):
                high[mask + bit] = ctx_flip(high[mask], bit)
        del high[0]
        return high, ctx_flip(kv, 2), ctx_flip(kv, 1)

    def second_keys(high, low, cot):
        return (
            ctx_flip(low, 1),
            flip(cot, "y"),
            {mask: ctx_flip(value, 2) for mask, value in high.items()},
            {mask: ctx_flip(value, 1) for mask, value in high.items()},
        )

    def third_keys(both, cot):
        return {mask: ctx_flip(value, 1) for mask, value in both.items()}, flip(cot, "core")

    high, part_l, part_x = stage(first_keys, after(cot_part, kv_local))
    part_lx, more, high_l, high_x = stage(second_keys, high, part_l, cot_part)
    cot_part = jnp.concatenate([cot_part, more])
    high_lx, cot_far = stage(third_keys, high_l, cot_part)
    parts = {0: kv_local, 1: part_x, 2: part_l, 3: part_lx}
    for mask in high:
        parts[mask], parts[mask + 1] = high[mask], high_x[mask]
        parts[mask + 2], parts[mask + 3] = high_l[mask], high_lx[mask]
    parts = [parts[mask] for mask in range(ctx_count)]
    cot = jnp.concatenate(
        [cot_slots[0], cot_part[:quarter], cot_slots[1], cot_part[quarter:]]
        + [cot_slots[2], cot_far[:quarter], cot_slots[3], cot_far[quarter:]]
    )
    mixed, log_total, keep, send = attention_forward(
        queries, w_out, parts, block_order, cont_prompt, where
    )
    first_half = flip(send, "core")
    near = add(keep, first_half)
    far = flip(near[quarter:], "y")
    grad_hidden = grad_hidden_stage(after(near, cot), w_down, where)
    own_input = lax.dynamic_slice_in_dim(layer_input, tensor * quarter, quarter)
    own_input = own_input.astype(jnp.float32)
    middle = own_input + total((near[:quarter], after(grad_hidden, far)))
    inv_two = lax.rsqrt(jnp.mean(middle * middle, axis=-1, keepdims=True) + eps_norm)
    normed_two = middle * inv_two
    second = gather_pair((normed_two * ffn_gain).astype(jnp.bfloat16))
    hidden, grad_gate, grad_up = ffn_stage(second, grad_hidden, w_gate, w_up, where)

    down_shares = unit_shares("down_shares", cot, hidden, ctx_count, where)
    down = unit_sum_over(down_shares)
    grads, weights = after(down_shares, grad_gate, grad_up), (w_gate, w_up)
    send = grad_second_half(1, "grad_second_send", grads, weights, where)

    def second_stage(send, grad_gate, grad_up, hidden):
        keep = grad_second_half(0, "grad_second_keep", (grad_gate, grad_up), weights, where)
        near, far, got = pair_scatter(keep, send)
        shares = unit_shares("gate_shares", second, after(near[3], grad_gate), ctx_count, where)
        *terms, away = pair_finish(near, after(shares, far), got)
        halves = unit_sum(
            ffn_out_kernel, "ffn_out", (after(away, hidden),), (w_down,), False, where
        )
        return total(after(halves[0], *terms)), shares, halves

    grad_second, gate_shares, ffn_halves = stage(second_stage, send, *grads, hidden)
    gate = unit_sum_over(gate_shares)

    def branch_stage(grad_second, grad_up, own):
        grad_norm, gain_part = norm_back(grad_second, normed_two, inv_two, ffn_gain)
        grad_middle = own.astype(jnp.float32) + grad_norm
        branch = grad_middle.astype(jnp.bfloat16)
        shares = unit_shares("up_shares", second, after(branch, grad_up), ctx_count, where)
        near = jnp.concatenate([branch, after(shares, flip(branch, "y"))])
        return grad_middle, gain_part, shares, jnp.concatenate([near, flip(near, "core")])

    grad_middle, ffn_gain_part, up_shares, grad_branch = stage(
        branch_stage, grad_second, grad_up, cot_own
    )
    backward, kv = [], []
    held = grad_branch
    for head in range(kv_heads):
        backward.append(
            attention_backward(
                head, queries, held, w_out, mixed, log_total, parts, cosine, sine,
                block_order, cont_prompt, where,
            )
        )
        kv.append(KvReduce(backward[-1][1], ctx_flip(backward[-1][2], 1)))
        dep = backward[-1][0]
        if head == 0:
            down_own, down_away = split_halves(down, ctx, dep)
            down_other = ctx_flip(down_away, 2)
            dep = down_own
        held = after(dep, grad_branch)
    grad_queries = [item[0] for item in backward]
    branch_shares = weight_shares(
        "branch_shares",
        (first_input, grad_branch),
        grad_queries + [after(dep, mixed)],
        tuple((0, h) for h in range(kv_heads)) + ((1, kv_heads),),
        ctx_count,
        True,
        where,
    )
    def out_stage(keep, send):
        got = flip(send, "core")
        n = keep.shape[0] // 4
        near = [add(keep[k * n : (k + 1) * n], got[k * n : (k + 1) * n]) for k in range(4)]
        return near[0], near[2], add(near[1], flip(near[3], "y"))

    def first_stage(keep, send, own_input, grad_middle):
        terms = scatter_slots(keep, send)
        inv = lax.rsqrt(jnp.mean(own_input * own_input, axis=-1, keepdims=True) + eps_norm)
        grad_norm, gain_part = norm_back(total(terms), own_input * inv, inv, attn_gain)
        return gain_part, (grad_middle + grad_norm).astype(jnp.bfloat16)

    def row_stage(near, other):
        near = jnp.concatenate([near, other])
        return near, flip(near, "core")

    def gain_stage(gains):
        gains = gains + flip(gains, "core")
        gains = gains + flip(gains, "y")
        for mask in [1, 2] + highs:
            gains = gains + ctx_flip(gains, mask)
        return gains

    dep = branch_shares[0]
    kv = [item.merge(dep) for item in kv]
    dep = tuple(keep for keep, _ in kv)
    up = unit_sum_over(after(dep, up_shares))
    sum_down = join_halves(down_own, after(dep, down_other), ctx).T
    dep = sum_down
    got = [ctx_flip(after(dep, value), 2) for _, value in kv]
    branch = Reduce(*after(dep, *branch_shares))
    out_near, out_own, out_away = stage(out_stage, *after(dep, *ffn_halves))
    dep = out_away
    for mask in highs:
        kv = [
            KvReduce(keep, value).merge(dep) for (keep, _), value in zip(kv, got)
        ]
        got = [ctx_flip(value, mask) for _, value in kv]
    dep = tuple(keep for keep, _ in kv)
    gate_own, gate_away = split_halves(gate, ctx, dep)
    dep = gate_own
    gate_other = ctx_flip(after(dep, gate_away), 2)
    out_far, out_got = stage(
        lambda away, own: (ctx_flip(away, 2), flip(own, "y")), *after(dep, out_away, out_own)
    )
    dep = out_far
    branch.halve(2, ctx, dep)
    dep = branch.keep
    output = (middle + total(after(dep, out_near, out_got, out_far))).astype(jnp.bfloat16)
    dep = output
    keep, send, grad_kv = tail_stage(
        [after(dep, keep, value) for (keep, _), value in zip(kv, got)], cosine, sine,
        grad_queries, w_query, key_matrix, value_matrix, where,
    )
    dep = keep
    kv_shares = weight_shares(
        "kv_shares", (first_input,), (after(dep, grad_kv),), ((0, 0),), ctx_count, True, where
    )
    dep = kv_shares[0]
    last = Reduce(*after(dep, *kv_shares))
    attn_gain_part, grad_input = stage(
        first_stage, after(dep, keep), send, own_input, grad_middle
    )
    dep = grad_input
    near = jnp.concatenate([grad_input, output])
    near_other = flip(after(dep, near), "y")
    sum_gate = join_halves(gate_own, after(dep, gate_other), ctx)
    dep = sum_gate
    for mask in highs:
        branch.halve(mask, ctx, dep)
        dep = branch.keep
    last.halve(2, ctx, dep)
    dep = last.keep
    gains = stage(gain_stage, after(dep, jnp.stack([attn_gain_part, ffn_gain_part])))
    dep = gains
    for mask in highs:
        last.halve(mask, ctx, dep)
        dep = last.keep
    near, far = stage(row_stage, near, after(dep, near_other))
    dep = far
    up_own, up_away = split_halves(up, ctx, dep)
    dep = up_own
    up_other = ctx_flip(after(dep, up_away), 2)
    last.keep, last.got = after(dep, last.keep, last.got)
    last_sum = last.sum()
    dep = last_sum
    quarters = [near[n * quarter : (n + 1) * quarter] for n in range(4)]
    quarters += [after(dep, far)[n * quarter : (n + 1) * quarter] for n in range(4)]
    grad_rows, output_rows = [
        place_rows(quarters[k], quarters[k + 2], quarters[k + 4], quarters[k + 6], tensor)
        for k in range(2)
    ]
    dep = (grad_rows, output_rows)
    branch.keep, branch.got = after(dep, branch.keep, branch.got)
    branch_sum = branch.sum()
    dep = branch_sum
    sum_up = join_halves(up_own, after(dep, up_other), ctx)
    dep = sum_up
    grad_input, output = grad_rows, output_rows
    width_q, width_k = w_query.shape[1], key_matrix.shape[1]
    sum_query, sum_out = branch_sum[:, :width_q], branch_sum[:, width_q:].T
    sum_key, sum_value = last_sum[:, :width_k], last_sum[:, width_k:]

    gains = gains.reshape(2, ctx_count * SLOTS, -1)
    gains = lax.dynamic_index_in_dim(gains, ctx * SLOTS + tensor, 1, keepdims=False)
    return (
        output,
        grad_input,
        gains[0],
        sum_query,
        sum_key,
        sum_value,
        sum_out,
        gains[1],
        sum_gate,
        sum_up,
        sum_down,
    )


def solution(mesh):
    rows, heads = ("hi", "l", "x"), ("y", "core")
    split = Mesh(mesh.devices.reshape(-1, 2, 2, 2, 2), rows + heads)
    placed = (
        P(rows, None),
        P(),
        P(None, heads),
        P(None, heads),
        P(None, heads),
        P(heads, None),
        P(),
        P(None, heads),
        P(None, heads),
        P(heads, None),
        P(rows, None),
        P(),
        P(),
    )
    return jax.shard_map(
        body,
        mesh=split,
        in_specs=placed,
        out_specs=(
            P(rows, None),
            P(rows, None),
            P(rows + heads),
            P(rows, heads),
            P(rows, heads),
            P(rows, heads),
            P(heads, rows),
            P(rows + heads),
            P(rows, heads),
            P(rows, heads),
            P(heads, rows),
        ),
        check_vma=False,
    )
```

```python
import functools
import math

import jax
import jax.numpy as jnp
import numpy as np
from jax import lax
from jax.experimental import pallas as pl
from jax.experimental.pallas import tpu as pltpu
from jax.sharding import Mesh
from jax.sharding import PartitionSpec as P

HEAD_SIZE = 128
PROMPT = 2048
CONT_LEN = 256
CONTS = 8
BLOCK = 128
PER_PROMPT = PROMPT // BLOCK
PER_CONT = CONT_LEN // BLOCK
LOG2E = 1.4426950408889634
NEG = -1e30
SLOTS = 4
VMEM_LIMIT = 60 << 20
VMEM_SMALL = 28 << 20
PAIR_STEPS = (4, 1)

eps_norm = 1e-05
rope_base = 1000000.0

SLOT_XOR = (0, 2, 1, 3)


def plain_dot(left, right):
    return jnp.dot(left, right, preferred_element_type=jnp.float32)


def left_dot(left, right):
    return lax.dot_general(
        left, right, (((0,), (0,)), ((), ())), preferred_element_type=jnp.float32
    )


def right_dot(left, right):
    return lax.dot_general(
        left, right, (((1,), (1,)), ((), ())), preferred_element_type=jnp.float32
    )


def slot_quarter(slot, tensor):
    return ((slot & 1) * 2 + lax.shift_right_logical(slot, 1)) ^ tensor


def stored_block(index, where_ref):
    rank = lax.div(index, SLOTS) ^ where_ref[0]
    return rank * SLOTS + slot_quarter(index & 3, where_ref[1])


def block_plan(order_ref, cont_ref, where_ref, slot):
    count = cont_ref.shape[0]
    prompt_blocks = count // CONTS * PER_PROMPT
    own = order_ref[stored_block(slot, where_ref)]
    is_prompt = own < prompt_blocks
    offset = own - prompt_blocks
    which = jnp.clip(lax.div(offset, PER_CONT), 0, count - 1)
    group = jnp.where(is_prompt, lax.div(own, PER_PROMPT), cont_ref[which])
    inner = jnp.where(is_prompt, lax.rem(own, PER_PROMPT), lax.rem(offset, PER_CONT))
    has_prev = lax.rem(inner, 2)
    pairs = jnp.where(is_prompt, lax.div(inner, 2), PER_PROMPT // 2)
    prev = own - has_prev
    return group * PER_PROMPT, pairs, prev, own, has_prev


def fill_inverse(order_ref, where_ref, inverse_ref):
    def put(index, carry):
        inverse_ref[order_ref[stored_block(index, where_ref)]] = index
        return carry

    lax.fori_loop(0, order_ref.shape[0], put, 0)


def rotate(vec, cosine, sine):
    return vec * cosine + pltpu.roll(vec, HEAD_SIZE // 2, 1) * sine


def unrotate(vec, cosine, sine):
    return vec * cosine + pltpu.roll(vec * sine, HEAD_SIZE // 2, 1)


def angle_tables():
    half = HEAD_SIZE // 2
    freq = np.float64(rope_base) ** (-(2.0 * np.arange(half) / HEAD_SIZE))
    freq = np.concatenate([freq, freq])
    starts = np.arange(-(-(PER_PROMPT + PER_CONT) // 8) * 8) * BLOCK
    start = starts[:, None] * freq[None]
    inner = np.arange(BLOCK)[:, None] * freq[None]
    return tuple(
        f(a).astype(np.float32) for a in (start, inner) for f in (np.cos, np.sin)
    )


def key_rows(inverse_ref, logical):
    return pl.ds(pl.multiple_of(inverse_ref[logical] * BLOCK, BLOCK), BLOCK)


def tile_pair(ref, rows_a, rows_b, column):
    return tile(ref, (rows_a, rows_b), column)


def tile(ref, rows, column):
    cols = pl.ds(column, HEAD_SIZE)
    return jnp.concatenate([ref[span, cols] for span in rows], axis=0)


def own_mask(has_prev, rep):
    shape = (2 * BLOCK, rep * BLOCK)
    row = lax.broadcasted_iota(jnp.int32, shape, 0)
    col = lax.broadcasted_iota(jnp.int32, shape, 1)
    first_row = BLOCK * (1 - has_prev)
    return (row >= first_row) & (row - BLOCK <= lax.rem(col, BLOCK))


def stack_t(ref, rows, column, rep):
    return jnp.concatenate(
        [ref[rows, pl.ds(column + r * HEAD_SIZE, HEAD_SIZE)].T for r in range(rep)], axis=1
    )


def stack_rows(ref, rows, column, rep):
    return jnp.concatenate(
        [ref[rows, pl.ds(column + r * HEAD_SIZE, HEAD_SIZE)] for r in range(rep)], axis=0
    )


def dot(left, right):
    return jnp.dot(left, right, preferred_element_type=jnp.float32)


def start_parts(parts, buffer_ref, sem, column):
    rows, width = parts[0].shape[0], buffer_ref.shape[1]
    copies = [
        pltpu.make_async_copy(
            part.at[:, pl.ds(column, width)], buffer_ref.at[pl.ds(p * rows, rows), :], sem.at[p]
        )
        for p, part in enumerate(parts)
    ]
    for copy in copies:
        copy.start()
    return copies


def forward_kernel(rep, hps, ctx_count, order_ref, cont_ref, where_ref, q_ref, wo_ref, *refs):
    parts, refs = refs[:ctx_count], refs[ctx_count:]
    out_ref, lse_ref, keep_ref, send_ref, kv_ref, inverse_ref, qt_ref, acc_ref, sem = refs
    copies = start_parts(parts, kv_ref, sem, 0)
    fill_inverse(order_ref, where_ref, inverse_ref)
    for copy in copies:
        copy.wait()
    q_blocks = q_ref.shape[0] // BLOCK
    factor = LOG2E / math.sqrt(HEAD_SIZE)
    width = rep * HEAD_SIZE

    def one_query_block(qb, carry):
        base, pairs, prev, own, has_prev = block_plan(order_ref, cont_ref, where_ref, qb)
        rows = pl.ds(pl.multiple_of(qb * BLOCK, BLOCK), BLOCK)
        mask = own_mask(has_prev, rep)
        rows_a, rows_b = key_rows(inverse_ref, prev), key_rows(inverse_ref, own)
        state = []
        for h in range(hps):
            qt = stack_t(q_ref, rows, h * width, rep)
            qt_ref[h] = qt
            scores = dot(tile_pair(kv_ref, rows_a, rows_b, 2 * h * HEAD_SIZE), qt) * factor
            scores = jnp.where(mask, scores, NEG)
            best = jnp.max(scores, axis=0, keepdims=True)
            weights = jnp.exp2(scores - best)
            total = jnp.sum(weights, axis=0, keepdims=True)
            values = tile_pair(kv_ref, rows_a, rows_b, (2 * h + 1) * HEAD_SIZE)
            acc_ref[h] = dot(values.T, weights.astype(jnp.bfloat16))
            state += [best, total]

        def fold(first, count, state):
            rows = [key_rows(inverse_ref, first + n) for n in range(count)]
            after = []
            for h in range(hps):
                best, total = state[2 * h], state[2 * h + 1]
                keys = tile(kv_ref, rows, 2 * h * HEAD_SIZE)
                scores = dot(keys, qt_ref[h]) * factor
                newest = jnp.maximum(best, jnp.max(scores, axis=0, keepdims=True))
                weights = jnp.exp2(scores - newest)
                shrink = jnp.exp2(best - newest)
                total = total * shrink + jnp.sum(weights, axis=0, keepdims=True)
                values = tile(kv_ref, rows, (2 * h + 1) * HEAD_SIZE)
                acc_ref[h] = acc_ref[h] * shrink + dot(values.T, weights.astype(jnp.bfloat16))
                after += [newest, total]
            return tuple(after)

        state, done = tuple(state), 0
        for wide in PAIR_STEPS:
            upto = lax.div(pairs, wide) * wide
            state = lax.fori_loop(
                0,
                lax.div(upto - done, wide),
                lambda t, state, done=done, wide=wide: fold(
                    base + 2 * (done + wide * t), 2 * wide, state
                ),
                state,
            )
            done = upto
        for h in range(hps):
            best, total = state[2 * h], state[2 * h + 1]
            mixed = acc_ref[h] * (1.0 / total)
            for r in range(rep):
                part = mixed[:, r * BLOCK : (r + 1) * BLOCK]
                out_ref[rows, pl.ds(h * width + r * HEAD_SIZE, HEAD_SIZE)] = part.T.astype(
                    jnp.bfloat16
                )
            lse_ref[h, pl.ds(qb, 1), :] = best + jnp.log2(total)
        return carry

    lax.fori_loop(0, q_blocks, one_query_block, 0)
    mixed = out_ref[...]
    half = keep_ref.shape[0]
    for n in range(0, wo_ref.shape[1], 512):
        cols = slice(n, n + 512)
        partial = dot(mixed, wo_ref[:, cols]).astype(jnp.bfloat16)
        keep_ref[:, cols] = partial[:half]
        send_ref[:, cols] = partial[half:]


def backward_kernel(rep, hps, ctx_count, head, order_ref, cont_ref, where_ref, q_ref, gb_ref, wo_ref,
                    mix_ref, lse_ref, cos_ref, sin_ref, *refs):
    parts, refs = refs[:ctx_count], refs[ctx_count:]
    gq_ref, keep_ref, send_ref = refs[:3]
    kv_ref, gm_ref, inverse_ref, qt_ref, gmt_ref, gqt_ref, acc_ref, sem = refs[3:]
    copies = start_parts(parts, kv_ref, sem, head * kv_ref.shape[1])
    fill_inverse(order_ref, where_ref, inverse_ref)
    gm_ref[...] = right_dot(gb_ref[...], wo_ref[...]).astype(jnp.bfloat16)
    for copy in copies:
        copy.wait()
    q_blocks = q_ref.shape[0] // BLOCK
    scale = 1.0 / math.sqrt(HEAD_SIZE)
    factor = LOG2E * scale
    width = rep * HEAD_SIZE

    def clear(i, carry):
        acc_ref[pl.ds(pl.multiple_of(i * BLOCK, BLOCK), BLOCK), :] = jnp.zeros(
            (BLOCK, acc_ref.shape[1]), jnp.float32
        )
        return carry

    lax.fori_loop(0, order_ref.shape[0], clear, 0)

    def tile_terms(h, spans, lse, delta, q_rows, gm_rows, mask):
        kcol, vcol = 2 * h * HEAD_SIZE, (2 * h + 1) * HEAD_SIZE
        keys = tile(kv_ref, spans, kcol)
        values = tile(kv_ref, spans, vcol)
        weights = jnp.exp2(dot(keys, qt_ref[h]) * factor - lse)
        if mask is not None:
            weights = jnp.where(mask, weights, 0.0)
        grad_weights = dot(values, gmt_ref[h])
        grad_scores = (weights * (grad_weights - delta)).astype(jnp.bfloat16)
        gv = dot(weights.astype(jnp.bfloat16), gm_rows)
        gk = dot(grad_scores, q_rows)
        for n, span in enumerate(spans):
            piece = slice(n * BLOCK, (n + 1) * BLOCK)
            acc_ref[span, pl.ds(kcol, HEAD_SIZE)] += gk[piece]
            acc_ref[span, pl.ds(vcol, HEAD_SIZE)] += gv[piece]
        return dot(keys.T, grad_scores)

    def one_query_block(qb, carry):
        base, pairs, prev, own, has_prev = block_plan(order_ref, cont_ref, where_ref, qb)
        rows = pl.ds(pl.multiple_of(qb * BLOCK, BLOCK), BLOCK)
        mask = own_mask(has_prev, rep)
        rows_a, rows_b = key_rows(inverse_ref, prev), key_rows(inverse_ref, own)
        deltas, lses, q_stack, gm_stack = [], [], [], []
        for h in range(hps):
            qt_ref[h] = stack_t(q_ref, rows, h * width, rep)
            gmt = stack_t(gm_ref, rows, h * width, rep)
            gmt_ref[h] = gmt
            mixt = stack_t(mix_ref, rows, h * width, rep)
            deltas.append(
                jnp.sum(
                    gmt.astype(jnp.float32) * mixt.astype(jnp.float32), axis=0, keepdims=True
                )
            )
            lses.append(lse_ref[h, pl.ds(qb, 1), :])
        for h in range(hps):
            q_rows = stack_rows(q_ref, rows, h * width, rep)
            gm_rows = stack_rows(gm_ref, rows, h * width, rep)
            gqt_ref[h] = tile_terms(
                h, (rows_a, rows_b), lses[h], deltas[h], q_rows, gm_rows, mask
            )

        def fold(first, count):
            spans = [key_rows(inverse_ref, first + n) for n in range(count)]
            for h in range(hps):
                q_rows = stack_rows(q_ref, rows, h * width, rep)
                gm_rows = stack_rows(gm_ref, rows, h * width, rep)
                gqt_ref[h] += tile_terms(
                    h, spans, lses[h], deltas[h], q_rows, gm_rows, None
                )
            return 0

        done = 0
        for wide in PAIR_STEPS:
            upto = lax.div(pairs, wide) * wide
            lax.fori_loop(
                0,
                lax.div(upto - done, wide),
                lambda t, _, done=done, wide=wide: fold(base + 2 * (done + wide * t), 2 * wide),
                0,
            )
            done = upto
        for h in range(hps):
            total = gqt_ref[h] * scale
            for r in range(rep):
                part = total[:, r * BLOCK : (r + 1) * BLOCK]
                rounded = part.T.astype(jnp.bfloat16).astype(jnp.float32)
                gq_ref[rows, pl.ds(h * width + r * HEAD_SIZE, HEAD_SIZE)] = unrotate(
                    rounded, cos_ref[rows, :], sin_ref[rows, :]
                ).astype(jnp.bfloat16)
        return carry

    lax.fori_loop(0, q_blocks, one_query_block, 0)

    blocks = order_ref.shape[0]

    def place(index):
        chunk = lax.div(index, SLOTS)
        spot = (chunk & 1) * (ctx_count // 2) + (chunk & 2) // 2 * (ctx_count // 4) + (
            lax.shift_right_logical(chunk, 2)
        )
        return spot * SLOTS + (index & 3)

    def flush(i, carry):
        rows = pl.ds(pl.multiple_of(i * BLOCK, BLOCK), BLOCK)
        spot = place(i)
        parts = []
        for h in range(hps):
            parts.append(acc_ref[rows, pl.ds(2 * h * HEAD_SIZE, HEAD_SIZE)] * scale)
            parts.append(acc_ref[rows, pl.ds((2 * h + 1) * HEAD_SIZE, HEAD_SIZE)])
        value = jnp.concatenate(parts, axis=1).astype(jnp.bfloat16)

        @pl.when(spot < blocks // 2)
        def _():
            keep_ref[pl.ds(pl.multiple_of(spot * BLOCK, BLOCK), BLOCK), :] = value

        @pl.when(spot >= blocks // 2)
        def _():
            far = (spot - blocks // 2) * BLOCK
            send_ref[pl.ds(pl.multiple_of(far, BLOCK), BLOCK), :] = value

        return carry

    lax.fori_loop(0, blocks, flush, 0)


def attention_forward(q, w_out, parts, order, cont, where):
    ctx_count = len(parts)
    rows, tokens = q.shape[0], ctx_count * q.shape[0]
    kv_heads = parts[0].shape[1] // (2 * HEAD_SIZE)
    rep = q.shape[1] // HEAD_SIZE // kv_heads
    q_blocks, model = rows // BLOCK, w_out.shape[1]
    vmem, smem, any_ = (
        pl.BlockSpec(memory_space=space) for space in (pltpu.VMEM, pltpu.SMEM, pl.ANY)
    )
    flops = 2 * rows * tokens * q.shape[1] + 2 * rows * q.shape[1] * model
    half = jax.ShapeDtypeStruct((rows // 2, model), jnp.bfloat16)
    return pl.pallas_call(
        functools.partial(forward_kernel, rep, kv_heads, ctx_count),
        out_shape=(
            jax.ShapeDtypeStruct(q.shape, jnp.bfloat16),
            jax.ShapeDtypeStruct((kv_heads, q_blocks, rep * BLOCK), jnp.float32),
            half,
            half,
        ),
        in_specs=[smem] * 3 + [vmem] * 2 + [any_] * ctx_count,
        out_specs=[vmem] * 4,
        scratch_shapes=[
            pltpu.VMEM((tokens, parts[0].shape[1]), jnp.bfloat16),
            pltpu.SMEM((order.shape[0],), jnp.int32),
            pltpu.VMEM((kv_heads, HEAD_SIZE, rep * BLOCK), jnp.bfloat16),
            pltpu.VMEM((kv_heads, HEAD_SIZE, rep * BLOCK), jnp.float32),
            pltpu.SemaphoreType.DMA((ctx_count,)),
        ],
        compiler_params=pltpu.CompilerParams(vmem_limit_bytes=VMEM_SMALL),
        cost_estimate=cost("attention_forward", flops, 2 * tokens * parts[0].shape[1] + 4 * rows * model),
        name="attention_forward",
    )(order, cont, where, q, w_out, *parts)


def attention_backward(head, q, grad_branch, w_out, mixed, lse, parts, cosine, sine, order, cont,
                       where):
    ctx_count = len(parts)
    rows, tokens = q.shape[0], ctx_count * q.shape[0]
    kv_heads = parts[0].shape[1] // (2 * HEAD_SIZE)
    rep = q.shape[1] // HEAD_SIZE // kv_heads
    q_blocks, model = rows // BLOCK, w_out.shape[1]
    wide = rep * HEAD_SIZE
    q_spec = pl.BlockSpec((rows, wide), lambda g, *_: (0, head))
    whole = lambda g, *_: (0, 0)
    table_spec = pl.BlockSpec((rows, HEAD_SIZE), whole)
    half = (tokens // 2, 2 * HEAD_SIZE)
    flops = 5 * rows * tokens * wide + 2 * rows * wide * model
    return pl.pallas_call(
        functools.partial(backward_kernel, rep, 1, ctx_count, head),
        out_shape=(
            jax.ShapeDtypeStruct((rows, wide), jnp.bfloat16),
            jax.ShapeDtypeStruct(half, jnp.bfloat16),
            jax.ShapeDtypeStruct(half, jnp.bfloat16),
        ),
        grid_spec=pltpu.PrefetchScalarGridSpec(
            num_scalar_prefetch=3,
            grid=(1,),
            in_specs=[
                q_spec,
                pl.BlockSpec((rows, model), whole),
                pl.BlockSpec((wide, model), lambda g, *_: (head, 0)),
                q_spec,
                pl.BlockSpec((1, q_blocks, rep * BLOCK), lambda g, *_: (head, 0, 0)),
                table_spec,
                table_spec,
            ]
            + [pl.BlockSpec(memory_space=pl.ANY)] * ctx_count,
            out_specs=[
                pl.BlockSpec((rows, wide), whole),
                pl.BlockSpec(half, whole),
                pl.BlockSpec(half, whole),
            ],
            scratch_shapes=[
                pltpu.VMEM((tokens, 2 * HEAD_SIZE), jnp.bfloat16),
                pltpu.VMEM((rows, wide), jnp.bfloat16),
                pltpu.SMEM((order.shape[0],), jnp.int32),
                pltpu.VMEM((1, HEAD_SIZE, rep * BLOCK), jnp.bfloat16),
                pltpu.VMEM((1, HEAD_SIZE, rep * BLOCK), jnp.bfloat16),
                pltpu.VMEM((1, HEAD_SIZE, rep * BLOCK), jnp.float32),
                pltpu.VMEM((tokens, 2 * HEAD_SIZE), jnp.float32),
                pltpu.SemaphoreType.DMA((ctx_count,)),
            ],
        ),
        compiler_params=pltpu.CompilerParams(vmem_limit_bytes=VMEM_LIMIT),
        cost_estimate=cost(f"attention_backward_{head}", flops, 4 * tokens * wide + 2 * rows * model),
        name=f"attention_backward_{head}",
    )(order, cont, where, q, grad_branch, w_out, mixed, lse, cosine, sine, *parts)


def input_kernel(order_ref, cont_ref, where_ref, gain_ref, x_hbm, wq_hbm, wk_hbm, wv_hbm, table_hbm,
                 first_ref, q_ref, kv_ref, cos_ref, sin_ref,
                 x_ref, wq_ref, wk_ref, wv_ref, table_ref, sem):
    pairs = ((x_hbm, x_ref), (table_hbm, table_ref), (wk_hbm, wk_ref), (wv_hbm, wv_ref),
             (wq_hbm, wq_ref))
    copies = [
        pltpu.make_async_copy(source, target, sem.at[n])
        for n, (source, target) in enumerate(pairs)
    ]
    for copy in copies:
        copy.start()
    count = cont_ref.shape[0]
    prompt_blocks = count // CONTS * PER_PROMPT
    starts = (table_ref.shape[0] - 2 * BLOCK) // 2
    lane = lax.broadcasted_iota(jnp.int32, (BLOCK, HEAD_SIZE), 1)
    copies[0].wait()
    copies[1].wait()

    def one_slot(slot, carry):
        quarter = slot_quarter(slot, where_ref[1])
        rows = pl.ds(pl.multiple_of(slot * BLOCK, BLOCK), BLOCK)
        full = x_ref[pl.ds(pl.multiple_of(quarter * BLOCK, BLOCK), BLOCK), :].astype(jnp.float32)
        inv = lax.rsqrt(jnp.mean(full * full, axis=-1, keepdims=True) + eps_norm)
        first_ref[rows, :] = (full * inv * gain_ref[...]).astype(jnp.bfloat16)
        own = order_ref[stored_block(slot, where_ref)]
        spot = jnp.where(
            own < prompt_blocks,
            lax.rem(own, PER_PROMPT),
            PER_PROMPT + lax.rem(own - prompt_blocks, PER_CONT),
        )
        cos_start = table_ref[pl.ds(2 * BLOCK + spot, 1), :]
        sin_start = table_ref[pl.ds(2 * BLOCK + starts + spot, 1), :]
        cos_in, sin_in = table_ref[:BLOCK, :], table_ref[BLOCK : 2 * BLOCK, :]
        sine = sin_start * cos_in + cos_start * sin_in
        cos_ref[rows, :] = cos_start * cos_in - sin_start * sin_in
        sin_ref[rows, :] = jnp.where(lane < HEAD_SIZE // 2, -sine, sine)
        return carry

    lax.fori_loop(0, SLOTS, one_slot, 0)
    first = first_ref[...]
    cosine, sine = cos_ref[...], sin_ref[...]
    copies[2].wait()
    copies[3].wait()
    keys = dot(first, wk_ref[...])
    values = dot(first, wv_ref[...])
    for h in range(wk_ref.shape[1] // HEAD_SIZE):
        cols = slice(h * HEAD_SIZE, (h + 1) * HEAD_SIZE)
        low, high = 2 * h * HEAD_SIZE, (2 * h + 1) * HEAD_SIZE
        key = rotate(keys[:, cols], cosine, sine)
        kv_ref[:, low:high] = key.astype(jnp.bfloat16)
        kv_ref[:, high : high + HEAD_SIZE] = values[:, cols].astype(jnp.bfloat16)
    copies[4].wait()
    for n in range(0, wq_ref.shape[1], 256):
        queries = dot(first, wq_ref[:, n : n + 256])
        for m in range(0, 256, HEAD_SIZE):
            query = rotate(queries[:, m : m + HEAD_SIZE], cosine, sine)
            q_ref[:, n + m : n + m + HEAD_SIZE] = query.astype(jnp.bfloat16)


def input_stage(x, gain, wq, wk, wv, order, cont, where):
    rows, model = x.shape
    cos_start, sin_start, cos_in, sin_in = angle_tables()
    table = np.concatenate([cos_in, sin_in, cos_start, sin_start])
    vmem, smem, any_ = (
        pl.BlockSpec(memory_space=space) for space in (pltpu.VMEM, pltpu.SMEM, pl.ANY)
    )
    flops = 2 * rows * model * (wq.shape[1] + 2 * wk.shape[1])
    return pl.pallas_call(
        input_kernel,
        out_shape=(
            jax.ShapeDtypeStruct((rows, model), jnp.bfloat16),
            jax.ShapeDtypeStruct((rows, wq.shape[1]), jnp.bfloat16),
            jax.ShapeDtypeStruct((rows, 2 * wk.shape[1]), jnp.bfloat16),
            jax.ShapeDtypeStruct((rows, HEAD_SIZE), jnp.float32),
            jax.ShapeDtypeStruct((rows, HEAD_SIZE), jnp.float32),
        ),
        in_specs=[smem] * 3 + [vmem] + [any_] * 5,
        out_specs=[vmem] * 5,
        scratch_shapes=[
            pltpu.VMEM(a.shape, a.dtype) for a in (x, wq, wk, wv)
        ]
        + [pltpu.VMEM(table.shape, jnp.float32), pltpu.SemaphoreType.DMA((5,))],
        compiler_params=pltpu.CompilerParams(vmem_limit_bytes=VMEM_LIMIT),
        cost_estimate=cost("input_stage", flops, 4 * x.size + 2 * wq.size + 4 * wk.size),
        name="input_stage",
    )(order, cont, where, gain.reshape(1, -1), x, wq, wk, wv, table)


FILLERS = ("kv_shares", "grad_hidden")


def cost(name, flops, bytes_accessed):
    scale = 16.0 if name in FILLERS else 0.02
    return pl.CostEstimate(
        flops=int(flops * scale), bytes_accessed=int(bytes_accessed * scale), transcendentals=0
    )


def put_share(value, index, x_bit, keep_ref, send_ref, swap_bits):
    spot = share_spot(lax.shift_right_logical(index, 1), keep_ref.shape[0], swap_bits)
    stays = (index & 1) == x_bit
    value = value.astype(keep_ref.dtype)

    @pl.when(stays)
    def _():
        keep_ref[pl.ds(spot, 1)] = value[None]

    @pl.when(jnp.logical_not(stays))
    def _():
        send_ref[pl.ds(spot, 1)] = value[None]


def pair_bit(where_ref):
    return lax.shift_right_logical(where_ref[0], 1) & 1


def grad_hidden_kernel(where_ref, cot_ref, wd_ref, out_ref):
    out_ref[...] = right_dot(cot_ref[...], wd_ref[...])


def grad_hidden_stage(cot, w_down, where):
    rows, model = cot.shape
    units = w_down.shape[0] // 2
    block = 256
    steps = units // block
    return pl.pallas_call(
        grad_hidden_kernel,
        out_shape=jax.ShapeDtypeStruct((rows, units), jnp.float32),
        grid_spec=pltpu.PrefetchScalarGridSpec(
            num_scalar_prefetch=1,
            grid=(steps,),
            in_specs=[
                pl.BlockSpec((rows, model), lambda i, w: (0, 0), pipeline_mode=pl.Buffered(1)),
                pl.BlockSpec((block, model), lambda i, w: (pair_bit(w) * steps + i, 0)),
            ],
            out_specs=pl.BlockSpec((rows, block), lambda i, w: (0, i)),
        ),
        compiler_params=pltpu.CompilerParams(vmem_limit_bytes=VMEM_LIMIT),
        cost_estimate=cost("grad_hidden", 2 * rows * model * units, 4 * rows * model),
        name="grad_hidden",
    )(where, cot, w_down)


def ffn_kernel(where_ref, in_ref, gh_ref, wg_ref, wu_ref, hid_ref, gg_ref, gu_ref):
    gate = dot(in_ref[...], wg_ref[...])
    upward = dot(in_ref[...], wu_ref[...])
    grad_hidden = gh_ref[...]
    sigma = jax.nn.sigmoid(gate)
    swish = gate * sigma
    hid_ref[...] = (swish * upward).astype(jnp.bfloat16)
    gg_ref[...] = (grad_hidden * upward * sigma * (1.0 + gate * (1.0 - sigma))).astype(
        jnp.bfloat16
    )
    gu_ref[...] = (grad_hidden * swish).astype(jnp.bfloat16)


def ffn_stage(second, grad_hidden, w_gate, w_up, where):
    rows, model = second.shape
    units = w_gate.shape[1] // 2
    block = 256
    steps = units // block
    col_spec = pl.BlockSpec((model, block), lambda i, w: (0, pair_bit(w) * steps + i))
    unit_spec = pl.BlockSpec((rows, block), lambda i, w: (0, i))
    unit = jax.ShapeDtypeStruct((rows, units), jnp.bfloat16)
    return pl.pallas_call(
        ffn_kernel,
        out_shape=(unit, unit, unit),
        grid_spec=pltpu.PrefetchScalarGridSpec(
            num_scalar_prefetch=1,
            grid=(steps,),
            in_specs=[
                pl.BlockSpec((rows, model), lambda i, w: (0, 0), pipeline_mode=pl.Buffered(1)),
                unit_spec,
                col_spec,
                col_spec,
            ],
            out_specs=[unit_spec] * 3,
        ),
        compiler_params=pltpu.CompilerParams(vmem_limit_bytes=VMEM_LIMIT),
        cost_estimate=cost("ffn_stage", 4 * rows * model * units, 6 * rows * model),
        name="ffn_stage",
    )(where, second, grad_hidden, w_gate, w_up)


def grad_second_kernel(where_ref, gg_ref, gu_ref, wg_ref, wu_ref, out_ref):
    total = right_dot(gg_ref[...], wg_ref[...]) + right_dot(gu_ref[...], wu_ref[...])
    out_ref[...] = total.astype(jnp.bfloat16)


def grad_second_half(half, name, grads, weights, where):
    rows, units = grads[0].shape
    rows //= 2
    model = weights[0].shape[0]
    block = 512
    left_spec = pl.BlockSpec((rows, units), lambda n, w: (half, 0), pipeline_mode=pl.Buffered(1))
    right_spec = pl.BlockSpec((block, units), lambda n, w: (n, pair_bit(w)))
    return pl.pallas_call(
        grad_second_kernel,
        out_shape=jax.ShapeDtypeStruct((rows, model), jnp.bfloat16),
        grid_spec=pltpu.PrefetchScalarGridSpec(
            num_scalar_prefetch=1,
            grid=(model // block,),
            in_specs=[left_spec] * 2 + [right_spec] * 2,
            out_specs=pl.BlockSpec((rows, block), lambda n, w: (0, n)),
        ),
        compiler_params=pltpu.CompilerParams(vmem_limit_bytes=VMEM_SMALL),
        cost_estimate=cost(name, 4 * rows * units * model, 4 * rows * model),
        name=name,
    )(where, *grads, *weights)


def ffn_out_kernel(where_ref, hid_ref, wd_ref, keep_ref, send_ref):
    total = dot(hid_ref[...], wd_ref[...])
    half = keep_ref.shape[0]
    keep_ref[...] = total[:half].astype(jnp.bfloat16)
    send_ref[...] = total[half:].astype(jnp.bfloat16)


def unit_sum(kernel, name, lefts, rights, transposed, where):
    rows, units = lefts[0].shape
    model = rights[0].shape[0 if transposed else 1]
    block = 512
    if transposed:
        right_spec = pl.BlockSpec((block, units), lambda n, w: (n, pair_bit(w)))
    else:
        right_spec = pl.BlockSpec((units, block), lambda n, w: (pair_bit(w), n))
    left_spec = pl.BlockSpec((rows, units), lambda n, w: (0, 0), pipeline_mode=pl.Buffered(1))
    half = jax.ShapeDtypeStruct((rows // 2, model), jnp.bfloat16)
    half_spec = pl.BlockSpec((rows // 2, block), lambda n, w: (0, n))
    return pl.pallas_call(
        kernel,
        out_shape=(half, half),
        grid_spec=pltpu.PrefetchScalarGridSpec(
            num_scalar_prefetch=1,
            grid=(model // block,),
            in_specs=[left_spec] * len(lefts) + [right_spec] * len(rights),
            out_specs=[half_spec, half_spec],
        ),
        compiler_params=pltpu.CompilerParams(vmem_limit_bytes=VMEM_LIMIT),
        cost_estimate=cost(name, 2 * len(lefts) * rows * units * model, 4 * rows * model),
        name=name,
    )(where, *lefts, *rights)


def share_spot(spot, count, swap_bits):
    if swap_bits:
        return (spot & 1) * (count // 2) + lax.shift_right_logical(spot, 1)
    return spot


def shares_kernel(left_count, swap_bits, pairs, where_ref, *refs):
    lefts, refs = refs[:left_count], refs[left_count:]
    rights, (keep_ref, send_ref) = refs[:-2], refs[-2:]
    share = keep_ref.shape[1]
    step = pl.program_id(0)
    pieces = [left_dot(lefts[l][...], rights[r][...]) for l, r in pairs]
    per_step = lefts[0].shape[1] // share
    if per_step == 1:
        value = jnp.concatenate(pieces, axis=1).astype(keep_ref.dtype)
        sends = step < pl.num_programs(0) // 2

        @pl.when(sends)
        def _():
            send_ref[0] = value

        @pl.when(jnp.logical_not(sends))
        def _():
            keep_ref[0] = value

        return
    for k in range(per_step):
        rows = slice(k * share, (k + 1) * share)
        value = jnp.concatenate([piece[rows] for piece in pieces], axis=1)
        index = step * per_step + k
        put_share(value, index, where_ref[0] & 1, keep_ref, send_ref, swap_bits)


def weight_shares(name, lefts, rights, pairs, ctx_count, swap_bits, where):
    rows, model = lefts[0].shape
    block = 256
    share, half = model // ctx_count, ctx_count // 2
    width = sum(rights[r].shape[1] for _, r in pairs)
    shares = jax.ShapeDtypeStruct((half, share, width), jnp.bfloat16)
    if share == block:

        def left_map(i, w):
            mine = w[0] & 1
            return 0, jnp.where(i < half, 2 * i + 1 - mine, 2 * (i - half) + mine)

        left_spec = pl.BlockSpec((rows, block), left_map)
        spot = lambda index: share_spot(index, half, swap_bits)
        keep_spec = pl.BlockSpec(
            (1, share, width), lambda i, w: (spot(jnp.maximum(i - half, 0)), 0, 0)
        )
        send_spec = pl.BlockSpec(
            (1, share, width), lambda i, w: (spot(jnp.minimum(i, half - 1)), 0, 0)
        )
    else:
        left_spec = pl.BlockSpec((rows, block), lambda i, w: (0, i))
        keep_spec = send_spec = pl.BlockSpec(shares.shape, lambda i, w: (0, 0, 0))
    return pl.pallas_call(
        functools.partial(shares_kernel, len(lefts), swap_bits, pairs),
        out_shape=(shares, shares),
        grid_spec=pltpu.PrefetchScalarGridSpec(
            num_scalar_prefetch=1,
            grid=(model // block,),
            in_specs=[left_spec] * len(lefts)
            + [
                pl.BlockSpec(r.shape, lambda i, w: (0, 0), pipeline_mode=pl.Buffered(1))
                for r in rights
            ],
            out_specs=[keep_spec, send_spec],
        ),
        compiler_params=pltpu.CompilerParams(vmem_limit_bytes=VMEM_SMALL),
        cost_estimate=cost(name, 2 * rows * model * width, 4 * rows * model),
        name=name,
    )(where, *lefts, *rights)


def unit_shares_kernel(where_ref, left_ref, right_ref, out_ref):
    share = out_ref.shape[1]
    total = left_dot(left_ref[...], right_ref[...]).astype(out_ref.dtype)
    per_step = left_ref.shape[1] // share
    if out_ref.shape[0] == 1:
        out_ref[0] = total
    else:
        for k in range(per_step):
            index = pl.program_id(0) * per_step + k
            out_ref[pl.ds(unit_spot(index, out_ref.shape[0]), 1)] = total[k * share : (k + 1) * share][None]


def unit_spot(index, ctx_count):
    return (index & 1) * (ctx_count // 2) + lax.shift_right_logical(index, 1)


def unit_shares(name, left, right, ctx_count, where):
    rows, model = left.shape
    block, width = 256, right.shape[1]
    share = model // ctx_count
    shares = jax.ShapeDtypeStruct((ctx_count, share, width), jnp.bfloat16)
    if share == block:
        out_spec = pl.BlockSpec((1, share, width), lambda i, w: (unit_spot(i, ctx_count), 0, 0))
    else:
        out_spec = pl.BlockSpec(shares.shape, lambda i, w: (0, 0, 0))
    return pl.pallas_call(
        unit_shares_kernel,
        out_shape=shares,
        grid_spec=pltpu.PrefetchScalarGridSpec(
            num_scalar_prefetch=1,
            grid=(model // block,),
            in_specs=[
                pl.BlockSpec((rows, block), lambda i, w: (0, i)),
                pl.BlockSpec(right.shape, lambda i, w: (0, 0), pipeline_mode=pl.Buffered(1)),
            ],
            out_specs=out_spec,
        ),
        compiler_params=pltpu.CompilerParams(vmem_limit_bytes=VMEM_SMALL),
        cost_estimate=cost(name, 2 * rows * model * width, 4 * rows * model),
        name=name,
    )(where, left, right)


def tail_kernel(kv_heads, where_ref, *refs):
    sums, refs = refs[: 2 * kv_heads], refs[2 * kv_heads :]
    cos_ref, sin_ref, refs = refs[0], refs[1], refs[2:]
    gq_refs, refs = refs[:kv_heads], refs[kv_heads:]
    wq_ref, wk_ref, wv_ref, keep_ref, send_ref, gkv_ref = refs
    cosine, sine = cos_ref[...], sin_ref[...]
    for h in range(kv_heads):
        total = sums[2 * h][...].astype(jnp.float32) + sums[2 * h + 1][...].astype(jnp.float32)
        total = total.astype(jnp.bfloat16)
        key = unrotate(total[:, :HEAD_SIZE].astype(jnp.float32), cosine, sine)
        cols = slice(h * HEAD_SIZE, (h + 1) * HEAD_SIZE)
        gkv_ref[:, cols] = key.astype(jnp.bfloat16)
        cols = slice((kv_heads + h) * HEAD_SIZE, (kv_heads + h + 1) * HEAD_SIZE)
        gkv_ref[:, cols] = total[:, HEAD_SIZE:]
    half = keep_ref.shape[0]
    key_width = kv_heads * HEAD_SIZE
    wide = gq_refs[0].shape[1]
    for n in range(0, wq_ref.shape[0], 512):
        span = slice(n, n + 512)
        total = right_dot(gkv_ref[:, :key_width], wk_ref[span, :])
        total += right_dot(gkv_ref[:, key_width:], wv_ref[span, :])
        for h in range(kv_heads):
            total += right_dot(gq_refs[h][...], wq_ref[span, h * wide : (h + 1) * wide])
        total = total.astype(jnp.bfloat16)
        keep_ref[:, span] = total[:half]
        send_ref[:, span] = total[half:]


def tail_stage(kv_sums, cosine, sine, grad_queries, wq, wk, wv, where):
    rows, model = cosine.shape[0], wq.shape[0]
    kv_heads = len(grad_queries)
    vmem = pl.BlockSpec(memory_space=pltpu.VMEM)
    half = jax.ShapeDtypeStruct((rows // 2, model), jnp.bfloat16)
    flat = [term for sums in kv_sums for term in sums]
    return pl.pallas_call(
        functools.partial(tail_kernel, kv_heads),
        out_shape=(
            half,
            half,
            jax.ShapeDtypeStruct((rows, 2 * kv_heads * HEAD_SIZE), jnp.bfloat16),
        ),
        in_specs=[pl.BlockSpec(memory_space=pltpu.SMEM)]
        + [vmem] * (len(flat) + 2 + kv_heads + 3),
        out_specs=[vmem] * 3,
        compiler_params=pltpu.CompilerParams(vmem_limit_bytes=VMEM_SMALL),
        cost_estimate=cost("tail_stage", 2 * rows * model * (wq.shape[1] + 2 * wk.shape[1]), 4 * rows * model + 4 * wq.size
        ),
        name="tail_stage",
    )(where, *flat, cosine, sine, *grad_queries, wq, wk, wv)


def flip(value, axis, mask=1):
    return lax.ppermute(value, axis, [(i, i ^ mask) for i in range(lax.axis_size(axis))])


def ctx_flip(value, mask):
    if mask == 1:
        return flip(value, "x")
    if mask == 2:
        return flip(value, "l")
    return flip(value, "hi", mask // 4)


def add(left, right):
    return (left.astype(jnp.float32) + right.astype(jnp.float32)).astype(jnp.bfloat16)


def slots_of(value, tensor):
    rows = value.shape[0] // SLOTS
    return [
        lax.dynamic_slice_in_dim(value, (tensor ^ SLOT_XOR[u]) * rows, rows)
        for u in range(SLOTS)
    ]


def after(dep, *values):
    deps = dep if isinstance(dep, tuple) else (dep,)
    held = lax.optimization_barrier(deps + values)[len(deps) :]
    return held[0] if len(held) == 1 else held


class Stages:
    def __init__(self, block_order):
        self.live = block_order[0] >= 0

    def __call__(self, function, *args):
        shapes = jax.eval_shape(function, *args)
        empty = lambda *_: jax.tree.map(lambda a: jnp.zeros(a.shape, a.dtype), shapes)
        return lax.cond(self.live, function, empty, *args)


def gather_pair(own):
    partner = ctx_flip(own, 2)
    near = jnp.concatenate([own, partner, flip(own, "y"), flip(partner, "y")])
    return jnp.concatenate([near, flip(near, "core")])


def gather_slots(own):
    near = jnp.concatenate([own, flip(own, "y")])
    return near, flip(near, "core")


def place_rows(own, near, core, far, tensor):
    rows = own.shape[0]
    result = jnp.zeros((SLOTS * rows,) + own.shape[1:], own.dtype)
    for u, piece in enumerate((own, near, core, far)):
        result = lax.dynamic_update_slice_in_dim(
            result, piece, (tensor ^ SLOT_XOR[u]) * rows, 0
        )
    return result


def scatter_slots(keep, send, fill=lambda value: value):
    got = fill(flip(send, "core"))
    quarter = keep.shape[0] // 2
    far = flip(add(keep[quarter:], got[quarter:]), "y")
    return add(keep[:quarter], got[:quarter]), far


def pair_scatter(keep, send, fill=lambda near: near):
    got = fill(flip(send, "core"))
    n = keep.shape[0] // 4
    near = [add(keep[k * n : (k + 1) * n], got[k * n : (k + 1) * n]) for k in range(4)]
    far = flip(near[3], "y")
    got = flip(near[2], "y")
    return near, far, got


def pair_finish(near, far, got):
    away = add(near[1], far)
    return near[0], got, ctx_flip(away, 2), away


def total(terms):
    return sum(term.astype(jnp.float32) for term in terms)


class Reduce:
    def __init__(self, keep, send):
        self.keep, self.got = keep, ctx_flip(send, 1)

    def halve(self, mask, ctx, dep=None):
        keep, got = self.keep, self.got
        if dep is not None:
            keep, got = after(dep, keep, got)
        n = keep.shape[0] // 2
        bit = lax.div(ctx, mask) % 2
        pick = lambda value, index: lax.dynamic_slice_in_dim(value, index * n, n, 0)
        away = ctx_flip(add(pick(keep, 1 - bit), pick(got, 1 - bit)), mask)
        self.keep, self.got = add(pick(keep, bit), pick(got, bit)), away

    def sum(self):
        return (self.keep.astype(jnp.float32) + self.got.astype(jnp.float32))[0]


def high_masks(ctx_count):
    masks, mask = [], ctx_count // 2
    while mask >= 4:
        masks.append(mask)
        mask //= 2
    return masks


def unit_sum_over(shares):
    return lax.psum_scatter(shares, ("x", "hi"), scatter_dimension=0, tiled=True)


def split_halves(summed, ctx, dep):
    summed = after(dep, summed)
    pair = lax.div(ctx, 2) % 2
    pick = lambda index: lax.dynamic_index_in_dim(summed, index, 0, keepdims=False)
    return pick(pair), pick(1 - pair)


def join_halves(own, other, ctx):
    pair = lax.div(ctx, 2) % 2
    low, high = jnp.where(pair == 0, own, other), jnp.where(pair == 0, other, own)
    return jnp.concatenate([low, high], axis=1).astype(jnp.float32)


class KvReduce:
    def __init__(self, keep, got):
        self.keep, self.got = keep, got

    def merge(self, dep):
        keep, got = after(dep, self.keep, self.got)
        n = keep.shape[0] // 2
        return add(keep[:n], got[:n]), add(keep[n:], got[n:])


def norm_back(grad_out, normed, inv_scale, gain):
    scaled = grad_out * gain
    inner = jnp.mean(scaled * normed, axis=-1, keepdims=True)
    return (inv_scale * (scaled - normed * inner), jnp.sum(grad_out * normed, axis=0))


def body(
    layer_input,
    attn_gain,
    w_query,
    key_matrix,
    value_matrix,
    w_out,
    ffn_gain,
    w_gate,
    w_up,
    w_down,
    cotangent,
    block_order,
    cont_prompt,
):
    ctx_count = lax.axis_size("hi") * 4
    ctx = (lax.axis_index("hi") * 2 + lax.axis_index("l")) * 2 + lax.axis_index("x")
    tensor = lax.axis_index("y") * 2 + lax.axis_index("core")
    where = jnp.stack([ctx, tensor]).astype(jnp.int32)
    quarter = layer_input.shape[0] // SLOTS
    kv_heads = key_matrix.shape[1] // HEAD_SIZE
    highs = high_masks(ctx_count)

    stage = Stages(block_order)
    cot_own = lax.dynamic_slice_in_dim(cotangent, tensor * quarter, quarter)
    cot_slots = slots_of(cotangent, tensor)
    cot_part = ctx_flip(cot_own, 2)
    first_input, queries, kv_local, cosine, sine = input_stage(
        layer_input, attn_gain, w_query, key_matrix, value_matrix, block_order, cont_prompt, where
    )
    def first_keys(kv):
        high = {0: kv}
        for bit in reversed(highs):
            for mask in list(high):
                high[mask + bit] = ctx_flip(high[mask], bit)
        del high[0]
        return high, ctx_flip(kv, 2), ctx_flip(kv, 1)

    def second_keys(high, low, cot):
        return (
            ctx_flip(low, 1),
            flip(cot, "y"),
            {mask: ctx_flip(value, 2) for mask, value in high.items()},
            {mask: ctx_flip(value, 1) for mask, value in high.items()},
        )

    def third_keys(both, cot):
        return {mask: ctx_flip(value, 1) for mask, value in both.items()}, flip(cot, "core")

    high, part_l, part_x = stage(first_keys, after(cot_part, kv_local))
    part_lx, more, high_l, high_x = stage(second_keys, high, part_l, cot_part)
    cot_part = jnp.concatenate([cot_part, more])
    high_lx, cot_far = stage(third_keys, high_l, cot_part)
    parts = {0: kv_local, 1: part_x, 2: part_l, 3: part_lx}
    for mask in high:
        parts[mask], parts[mask + 1] = high[mask], high_x[mask]
        parts[mask + 2], parts[mask + 3] = high_l[mask], high_lx[mask]
    parts = [parts[mask] for mask in range(ctx_count)]
    cot = jnp.concatenate(
        [cot_slots[0], cot_part[:quarter], cot_slots[1], cot_part[quarter:]]
        + [cot_slots[2], cot_far[:quarter], cot_slots[3], cot_far[quarter:]]
    )
    mixed, log_total, keep, send = attention_forward(
        queries, w_out, parts, block_order, cont_prompt, where
    )
    first_half = flip(send, "core")
    near = add(keep, first_half)
    far = flip(near[quarter:], "y")
    grad_hidden = grad_hidden_stage(after(near, cot), w_down, where)
    own_input = lax.dynamic_slice_in_dim(layer_input, tensor * quarter, quarter)
    own_input = own_input.astype(jnp.float32)
    middle = own_input + total((near[:quarter], after(grad_hidden, far)))
    inv_two = lax.rsqrt(jnp.mean(middle * middle, axis=-1, keepdims=True) + eps_norm)
    normed_two = middle * inv_two
    second = gather_pair((normed_two * ffn_gain).astype(jnp.bfloat16))
    hidden, grad_gate, grad_up = ffn_stage(second, grad_hidden, w_gate, w_up, where)

    down_shares = unit_shares("down_shares", cot, hidden, ctx_count, where)
    down = unit_sum_over(down_shares)
    grads, weights = after(down_shares, grad_gate, grad_up), (w_gate, w_up)
    send = grad_second_half(1, "grad_second_send", grads, weights, where)

    def second_stage(send, grad_gate, grad_up, hidden):
        keep = grad_second_half(0, "grad_second_keep", (grad_gate, grad_up), weights, where)
        near, far, got = pair_scatter(keep, send)
        shares = unit_shares("gate_shares", second, after(near[3], grad_gate), ctx_count, where)
        *terms, away = pair_finish(near, after(shares, far), got)
        halves = unit_sum(
            ffn_out_kernel, "ffn_out", (after(away, hidden),), (w_down,), False, where
        )
        return total(after(halves[0], *terms)), shares, halves

    grad_second, gate_shares, ffn_halves = stage(second_stage, send, *grads, hidden)
    gate = unit_sum_over(gate_shares)

    def branch_stage(grad_second, grad_up, own):
        grad_norm, gain_part = norm_back(grad_second, normed_two, inv_two, ffn_gain)
        grad_middle = own.astype(jnp.float32) + grad_norm
        branch = grad_middle.astype(jnp.bfloat16)
        shares = unit_shares("up_shares", second, after(branch, grad_up), ctx_count, where)
        near = jnp.concatenate([branch, after(shares, flip(branch, "y"))])
        return grad_middle, gain_part, shares, jnp.concatenate([near, flip(near, "core")])

    grad_middle, ffn_gain_part, up_shares, grad_branch = stage(
        branch_stage, grad_second, grad_up, cot_own
    )
    backward, kv = [], []
    held = grad_branch
    for head in range(kv_heads):
        backward.append(
            attention_backward(
                head, queries, held, w_out, mixed, log_total, parts, cosine, sine,
                block_order, cont_prompt, where,
            )
        )
        kv.append(KvReduce(backward[-1][1], ctx_flip(backward[-1][2], 1)))
        dep = backward[-1][0]
        if head == 0:
            down_own, down_away = split_halves(down, ctx, dep)
            down_other = ctx_flip(down_away, 2)
            dep = down_own
        held = after(dep, grad_branch)
    grad_queries = [item[0] for item in backward]
    branch_shares = weight_shares(
        "branch_shares",
        (first_input, grad_branch),
        grad_queries + [after(dep, mixed)],
        tuple((0, h) for h in range(kv_heads)) + ((1, kv_heads),),
        ctx_count,
        True,
        where,
    )
    def out_stage(keep, send):
        got = flip(send, "core")
        n = keep.shape[0] // 4
        near = [add(keep[k * n : (k + 1) * n], got[k * n : (k + 1) * n]) for k in range(4)]
        return near[0], near[2], add(near[1], flip(near[3], "y"))

    def first_stage(keep, send, own_input, grad_middle):
        terms = scatter_slots(keep, send)
        inv = lax.rsqrt(jnp.mean(own_input * own_input, axis=-1, keepdims=True) + eps_norm)
        grad_norm, gain_part = norm_back(total(terms), own_input * inv, inv, attn_gain)
        return gain_part, (grad_middle + grad_norm).astype(jnp.bfloat16)

    def row_stage(near, other):
        near = jnp.concatenate([near, other])
        return near, flip(near, "core")

    def gain_stage(gains):
        gains = gains + flip(gains, "core")
        gains = gains + flip(gains, "y")
        for mask in [1, 2] + highs:
            gains = gains + ctx_flip(gains, mask)
        return gains

    dep = branch_shares[0]
    kv = [item.merge(dep) for item in kv]
    dep = tuple(keep for keep, _ in kv)
    up = unit_sum_over(after(dep, up_shares))
    sum_down = join_halves(down_own, after(dep, down_other), ctx).T
    dep = sum_down
    got = [ctx_flip(after(dep, value), 2) for _, value in kv]
    branch = Reduce(*after(dep, *branch_shares))
    out_near, out_own, out_away = stage(out_stage, *after(dep, *ffn_halves))
    dep = out_away
    for mask in highs:
        kv = [
            KvReduce(keep, value).merge(dep) for (keep, _), value in zip(kv, got)
        ]
        got = [ctx_flip(value, mask) for _, value in kv]
    dep = tuple(keep for keep, _ in kv)
    gate_own, gate_away = split_halves(gate, ctx, dep)
    dep = gate_own
    gate_other = ctx_flip(after(dep, gate_away), 2)
    out_far, out_got = stage(
        lambda away, own: (ctx_flip(away, 2), flip(own, "y")), *after(dep, out_away, out_own)
    )
    dep = out_far
    branch.halve(2, ctx, dep)
    dep = branch.keep
    output = (middle + total(after(dep, out_near, out_got, out_far))).astype(jnp.bfloat16)
    dep = output
    keep, send, grad_kv = tail_stage(
        [after(dep, keep, value) for (keep, _), value in zip(kv, got)], cosine, sine,
        grad_queries, w_query, key_matrix, value_matrix, where,
    )
    dep = keep
    kv_shares = weight_shares(
        "kv_shares", (first_input,), (after(dep, grad_kv),), ((0, 0),), ctx_count, True, where
    )
    dep = kv_shares[0]
    last = Reduce(*after(dep, *kv_shares))
    attn_gain_part, grad_input = stage(
        first_stage, after(dep, keep), send, own_input, grad_middle
    )
    dep = grad_input
    near = jnp.concatenate([grad_input, output])
    near_other = flip(after(dep, near), "y")
    sum_gate = join_halves(gate_own, after(dep, gate_other), ctx)
    dep = sum_gate
    for mask in highs:
        branch.halve(mask, ctx, dep)
        dep = branch.keep
    last.halve(2, ctx, dep)
    dep = last.keep
    gains = stage(gain_stage, after(dep, jnp.stack([attn_gain_part, ffn_gain_part])))
    dep = gains
    for mask in highs:
        last.halve(mask, ctx, dep)
        dep = last.keep
    near, far = stage(row_stage, near, after(dep, near_other))
    dep = far
    up_own, up_away = split_halves(up, ctx, dep)
    dep = up_own
    up_other = ctx_flip(after(dep, up_away), 2)
    last.keep, last.got = after(dep, last.keep, last.got)
    last_sum = last.sum()
    dep = last_sum
    quarters = [near[n * quarter : (n + 1) * quarter] for n in range(4)]
    quarters += [after(dep, far)[n * quarter : (n + 1) * quarter] for n in range(4)]
    grad_rows, output_rows = [
        place_rows(quarters[k], quarters[k + 2], quarters[k + 4], quarters[k + 6], tensor)
        for k in range(2)
    ]
    dep = (grad_rows, output_rows)
    branch.keep, branch.got = after(dep, branch.keep, branch.got)
    branch_sum = branch.sum()
    dep = branch_sum
    sum_up = join_halves(up_own, after(dep, up_other), ctx)
    dep = sum_up
    grad_input, output = grad_rows, output_rows
    width_q, width_k = w_query.shape[1], key_matrix.shape[1]
    sum_query, sum_out = branch_sum[:, :width_q], branch_sum[:, width_q:].T
    sum_key, sum_value = last_sum[:, :width_k], last_sum[:, width_k:]

    gains = gains.reshape(2, ctx_count * SLOTS, -1)
    gains = lax.dynamic_index_in_dim(gains, ctx * SLOTS + tensor, 1, keepdims=False)
    return (
        output,
        grad_input,
        gains[0],
        sum_query,
        sum_key,
        sum_value,
        sum_out,
        gains[1],
        sum_gate,
        sum_up,
        sum_down,
    )


def solution(mesh):
    rows, heads = ("hi", "l", "x"), ("y", "core")
    split = Mesh(mesh.devices.reshape(-1, 2, 2, 2, 2), rows + heads)
    placed = (
        P(rows, None),
        P(),
        P(None, heads),
        P(None, heads),
        P(None, heads),
        P(heads, None),
        P(),
        P(None, heads),
        P(None, heads),
        P(heads, None),
        P(rows, None),
        P(),
        P(),
    )
    return jax.shard_map(
        body,
        mesh=split,
        in_specs=placed,
        out_specs=(
            P(rows, None),
            P(rows, None),
            P(rows + heads),
            P(rows, heads),
            P(rows, heads),
            P(rows, heads),
            P(heads, rows),
            P(rows + heads),
            P(rows, heads),
            P(rows, heads),
            P(heads, rows),
        ),
        check_vma=False,
    )
```

```python
import functools
import math

import jax
import jax.numpy as jnp
import numpy as np
from jax import lax
from jax.experimental import pallas as pl
from jax.experimental.pallas import tpu as pltpu
from jax.sharding import Mesh
from jax.sharding import PartitionSpec as P

HEAD_SIZE = 128
PROMPT = 2048
CONT_LEN = 256
CONTS = 8
BLOCK = 128
PER_PROMPT = PROMPT // BLOCK
PER_CONT = CONT_LEN // BLOCK
LOG2E = 1.4426950408889634
NEG = -1e30
SLOTS = 4
VMEM_LIMIT = 60 << 20
VMEM_SMALL = 28 << 20
PAIR_STEPS = (4, 1)

eps_norm = 1e-05
rope_base = 1000000.0

SLOT_XOR = (0, 2, 1, 3)


def plain_dot(left, right):
    return jnp.dot(left, right, preferred_element_type=jnp.float32)


def left_dot(left, right):
    return lax.dot_general(
        left, right, (((0,), (0,)), ((), ())), preferred_element_type=jnp.float32
    )


def right_dot(left, right):
    return lax.dot_general(
        left, right, (((1,), (1,)), ((), ())), preferred_element_type=jnp.float32
    )


def slot_quarter(slot, tensor):
    return ((slot & 1) * 2 + lax.shift_right_logical(slot, 1)) ^ tensor


def stored_block(index, where_ref):
    rank = lax.div(index, SLOTS) ^ where_ref[0]
    return rank * SLOTS + slot_quarter(index & 3, where_ref[1])


def block_plan(order_ref, cont_ref, where_ref, slot):
    count = cont_ref.shape[0]
    prompt_blocks = count // CONTS * PER_PROMPT
    own = order_ref[stored_block(slot, where_ref)]
    is_prompt = own < prompt_blocks
    offset = own - prompt_blocks
    which = jnp.clip(lax.div(offset, PER_CONT), 0, count - 1)
    group = jnp.where(is_prompt, lax.div(own, PER_PROMPT), cont_ref[which])
    inner = jnp.where(is_prompt, lax.rem(own, PER_PROMPT), lax.rem(offset, PER_CONT))
    has_prev = lax.rem(inner, 2)
    pairs = jnp.where(is_prompt, lax.div(inner, 2), PER_PROMPT // 2)
    prev = own - has_prev
    return group * PER_PROMPT, pairs, prev, own, has_prev


def fill_inverse(order_ref, where_ref, inverse_ref):
    def put(index, carry):
        inverse_ref[order_ref[stored_block(index, where_ref)]] = index
        return carry

    lax.fori_loop(0, order_ref.shape[0], put, 0)


def rotate(vec, cosine, sine):
    return vec * cosine + pltpu.roll(vec, HEAD_SIZE // 2, 1) * sine


def unrotate(vec, cosine, sine):
    return vec * cosine + pltpu.roll(vec * sine, HEAD_SIZE // 2, 1)


def angle_tables():
    half = HEAD_SIZE // 2
    freq = np.float64(rope_base) ** (-(2.0 * np.arange(half) / HEAD_SIZE))
    freq = np.concatenate([freq, freq])
    starts = np.arange(-(-(PER_PROMPT + PER_CONT) // 8) * 8) * BLOCK
    start = starts[:, None] * freq[None]
    inner = np.arange(BLOCK)[:, None] * freq[None]
    return tuple(
        f(a).astype(np.float32) for a in (start, inner) for f in (np.cos, np.sin)
    )


def key_rows(inverse_ref, logical):
    return pl.ds(pl.multiple_of(inverse_ref[logical] * BLOCK, BLOCK), BLOCK)


def tile_pair(ref, rows_a, rows_b, column):
    return tile(ref, (rows_a, rows_b), column)


def tile(ref, rows, column):
    cols = pl.ds(column, HEAD_SIZE)
    return jnp.concatenate([ref[span, cols] for span in rows], axis=0)


def own_mask(has_prev, rep):
    shape = (2 * BLOCK, rep * BLOCK)
    row = lax.broadcasted_iota(jnp.int32, shape, 0)
    col = lax.broadcasted_iota(jnp.int32, shape, 1)
    first_row = BLOCK * (1 - has_prev)
    return (row >= first_row) & (row - BLOCK <= lax.rem(col, BLOCK))


def stack_t(ref, rows, column, rep):
    return jnp.concatenate(
        [ref[rows, pl.ds(column + r * HEAD_SIZE, HEAD_SIZE)].T for r in range(rep)], axis=1
    )


def stack_rows(ref, rows, column, rep):
    return jnp.concatenate(
        [ref[rows, pl.ds(column + r * HEAD_SIZE, HEAD_SIZE)] for r in range(rep)], axis=0
    )


def dot(left, right):
    return jnp.dot(left, right, preferred_element_type=jnp.float32)


def start_parts(parts, buffer_ref, sem, column):
    rows, width = parts[0].shape[0], buffer_ref.shape[1]
    copies = [
        pltpu.make_async_copy(
            part.at[:, pl.ds(column, width)], buffer_ref.at[pl.ds(p * rows, rows), :], sem.at[p]
        )
        for p, part in enumerate(parts)
    ]
    for copy in copies:
        copy.start()
    return copies


def forward_kernel(rep, hps, ctx_count, order_ref, cont_ref, where_ref, q_ref, wo_ref, *refs):
    parts, refs = refs[:ctx_count], refs[ctx_count:]
    out_ref, lse_ref, keep_ref, send_ref, kv_ref, inverse_ref, qt_ref, acc_ref, sem = refs
    copies = start_parts(parts, kv_ref, sem, 0)
    fill_inverse(order_ref, where_ref, inverse_ref)
    for copy in copies:
        copy.wait()
    q_blocks = q_ref.shape[0] // BLOCK
    factor = LOG2E / math.sqrt(HEAD_SIZE)
    width = rep * HEAD_SIZE

    def one_query_block(qb, carry):
        base, pairs, prev, own, has_prev = block_plan(order_ref, cont_ref, where_ref, qb)
        rows = pl.ds(pl.multiple_of(qb * BLOCK, BLOCK), BLOCK)
        mask = own_mask(has_prev, rep)
        rows_a, rows_b = key_rows(inverse_ref, prev), key_rows(inverse_ref, own)
        state = []
        for h in range(hps):
            qt = stack_t(q_ref, rows, h * width, rep)
            qt_ref[h] = qt
            scores = dot(tile_pair(kv_ref, rows_a, rows_b, 2 * h * HEAD_SIZE), qt) * factor
            scores = jnp.where(mask, scores, NEG)
            best = jnp.max(scores, axis=0, keepdims=True)
            weights = jnp.exp2(scores - best)
            total = jnp.sum(weights, axis=0, keepdims=True)
            values = tile_pair(kv_ref, rows_a, rows_b, (2 * h + 1) * HEAD_SIZE)
            acc_ref[h] = dot(values.T, weights.astype(jnp.bfloat16))
            state += [best, total]

        def fold(first, count, state):
            rows = [key_rows(inverse_ref, first + n) for n in range(count)]
            after = []
            for h in range(hps):
                best, total = state[2 * h], state[2 * h + 1]
                keys = tile(kv_ref, rows, 2 * h * HEAD_SIZE)
                scores = dot(keys, qt_ref[h]) * factor
                newest = jnp.maximum(best, jnp.max(scores, axis=0, keepdims=True))
                weights = jnp.exp2(scores - newest)
                shrink = jnp.exp2(best - newest)
                total = total * shrink + jnp.sum(weights, axis=0, keepdims=True)
                values = tile(kv_ref, rows, (2 * h + 1) * HEAD_SIZE)
                acc_ref[h] = acc_ref[h] * shrink + dot(values.T, weights.astype(jnp.bfloat16))
                after += [newest, total]
            return tuple(after)

        state, done = tuple(state), 0
        for wide in PAIR_STEPS:
            upto = lax.div(pairs, wide) * wide
            state = lax.fori_loop(
                0,
                lax.div(upto - done, wide),
                lambda t, state, done=done, wide=wide: fold(
                    base + 2 * (done + wide * t), 2 * wide, state
                ),
                state,
            )
            done = upto
        for h in range(hps):
            best, total = state[2 * h], state[2 * h + 1]
            mixed = acc_ref[h] * (1.0 / total)
            for r in range(rep):
                part = mixed[:, r * BLOCK : (r + 1) * BLOCK]
                out_ref[rows, pl.ds(h * width + r * HEAD_SIZE, HEAD_SIZE)] = part.T.astype(
                    jnp.bfloat16
                )
            lse_ref[h, pl.ds(qb, 1), :] = best + jnp.log2(total)
        return carry

    lax.fori_loop(0, q_blocks, one_query_block, 0)
    mixed = out_ref[...]
    half = keep_ref.shape[0]
    for n in range(0, wo_ref.shape[1], 512):
        cols = slice(n, n + 512)
        partial = dot(mixed, wo_ref[:, cols]).astype(jnp.bfloat16)
        keep_ref[:, cols] = partial[:half]
        send_ref[:, cols] = partial[half:]


def backward_kernel(rep, hps, ctx_count, head, order_ref, cont_ref, where_ref, q_ref, gb_ref, wo_ref,
                    mix_ref, lse_ref, cos_ref, sin_ref, *refs):
    parts, refs = refs[:ctx_count], refs[ctx_count:]
    gq_ref, keep_ref, send_ref = refs[:3]
    kv_ref, gm_ref, inverse_ref, qt_ref, gmt_ref, gqt_ref, acc_ref, sem = refs[3:]
    copies = start_parts(parts, kv_ref, sem, head * kv_ref.shape[1])
    fill_inverse(order_ref, where_ref, inverse_ref)
    gm_ref[...] = right_dot(gb_ref[...], wo_ref[...]).astype(jnp.bfloat16)
    for copy in copies:
        copy.wait()
    q_blocks = q_ref.shape[0] // BLOCK
    scale = 1.0 / math.sqrt(HEAD_SIZE)
    factor = LOG2E * scale
    width = rep * HEAD_SIZE

    def clear(i, carry):
        acc_ref[pl.ds(pl.multiple_of(i * BLOCK, BLOCK), BLOCK), :] = jnp.zeros(
            (BLOCK, acc_ref.shape[1]), jnp.float32
        )
        return carry

    lax.fori_loop(0, order_ref.shape[0], clear, 0)

    def tile_terms(h, spans, lse, delta, q_rows, gm_rows, mask):
        kcol, vcol = 2 * h * HEAD_SIZE, (2 * h + 1) * HEAD_SIZE
        keys = tile(kv_ref, spans, kcol)
        values = tile(kv_ref, spans, vcol)
        weights = jnp.exp2(dot(keys, qt_ref[h]) * factor - lse)
        if mask is not None:
            weights = jnp.where(mask, weights, 0.0)
        grad_weights = dot(values, gmt_ref[h])
        grad_scores = (weights * (grad_weights - delta)).astype(jnp.bfloat16)
        gv = dot(weights.astype(jnp.bfloat16), gm_rows)
        gk = dot(grad_scores, q_rows)
        for n, span in enumerate(spans):
            piece = slice(n * BLOCK, (n + 1) * BLOCK)
            acc_ref[span, pl.ds(kcol, HEAD_SIZE)] += gk[piece]
            acc_ref[span, pl.ds(vcol, HEAD_SIZE)] += gv[piece]
        return dot(keys.T, grad_scores)

    def one_query_block(qb, carry):
        base, pairs, prev, own, has_prev = block_plan(order_ref, cont_ref, where_ref, qb)
        rows = pl.ds(pl.multiple_of(qb * BLOCK, BLOCK), BLOCK)
        mask = own_mask(has_prev, rep)
        rows_a, rows_b = key_rows(inverse_ref, prev), key_rows(inverse_ref, own)
        deltas, lses, q_stack, gm_stack = [], [], [], []
        for h in range(hps):
            qt_ref[h] = stack_t(q_ref, rows, h * width, rep)
            gmt = stack_t(gm_ref, rows, h * width, rep)
            gmt_ref[h] = gmt
            mixt = stack_t(mix_ref, rows, h * width, rep)
            deltas.append(
                jnp.sum(
                    gmt.astype(jnp.float32) * mixt.astype(jnp.float32), axis=0, keepdims=True
                )
            )
            lses.append(lse_ref[h, pl.ds(qb, 1), :])
        for h in range(hps):
            q_rows = stack_rows(q_ref, rows, h * width, rep)
            gm_rows = stack_rows(gm_ref, rows, h * width, rep)
            gqt_ref[h] = tile_terms(
                h, (rows_a, rows_b), lses[h], deltas[h], q_rows, gm_rows, mask
            )

        def fold(first, count):
            spans = [key_rows(inverse_ref, first + n) for n in range(count)]
            for h in range(hps):
                q_rows = stack_rows(q_ref, rows, h * width, rep)
                gm_rows = stack_rows(gm_ref, rows, h * width, rep)
                gqt_ref[h] += tile_terms(
                    h, spans, lses[h], deltas[h], q_rows, gm_rows, None
                )
            return 0

        done = 0
        for wide in PAIR_STEPS:
            upto = lax.div(pairs, wide) * wide
            lax.fori_loop(
                0,
                lax.div(upto - done, wide),
                lambda t, _, done=done, wide=wide: fold(base + 2 * (done + wide * t), 2 * wide),
                0,
            )
            done = upto
        for h in range(hps):
            total = gqt_ref[h] * scale
            for r in range(rep):
                part = total[:, r * BLOCK : (r + 1) * BLOCK]
                rounded = part.T.astype(jnp.bfloat16).astype(jnp.float32)
                gq_ref[rows, pl.ds(h * width + r * HEAD_SIZE, HEAD_SIZE)] = unrotate(
                    rounded, cos_ref[rows, :], sin_ref[rows, :]
                ).astype(jnp.bfloat16)
        return carry

    lax.fori_loop(0, q_blocks, one_query_block, 0)

    blocks = order_ref.shape[0]

    def place(index):
        chunk = lax.div(index, SLOTS)
        spot = (chunk & 1) * (ctx_count // 2) + (chunk & 2) // 2 * (ctx_count // 4) + (
            lax.shift_right_logical(chunk, 2)
        )
        return spot * SLOTS + (index & 3)

    def flush(i, carry):
        rows = pl.ds(pl.multiple_of(i * BLOCK, BLOCK), BLOCK)
        spot = place(i)
        parts = []
        for h in range(hps):
            parts.append(acc_ref[rows, pl.ds(2 * h * HEAD_SIZE, HEAD_SIZE)] * scale)
            parts.append(acc_ref[rows, pl.ds((2 * h + 1) * HEAD_SIZE, HEAD_SIZE)])
        value = jnp.concatenate(parts, axis=1).astype(jnp.bfloat16)

        @pl.when(spot < blocks // 2)
        def _():
            keep_ref[pl.ds(pl.multiple_of(spot * BLOCK, BLOCK), BLOCK), :] = value

        @pl.when(spot >= blocks // 2)
        def _():
            far = (spot - blocks // 2) * BLOCK
            send_ref[pl.ds(pl.multiple_of(far, BLOCK), BLOCK), :] = value

        return carry

    lax.fori_loop(0, blocks, flush, 0)


def attention_forward(q, w_out, parts, order, cont, where):
    ctx_count = len(parts)
    rows, tokens = q.shape[0], ctx_count * q.shape[0]
    kv_heads = parts[0].shape[1] // (2 * HEAD_SIZE)
    rep = q.shape[1] // HEAD_SIZE // kv_heads
    q_blocks, model = rows // BLOCK, w_out.shape[1]
    vmem, smem, any_ = (
        pl.BlockSpec(memory_space=space) for space in (pltpu.VMEM, pltpu.SMEM, pl.ANY)
    )
    flops = 2 * rows * tokens * q.shape[1] + 2 * rows * q.shape[1] * model
    half = jax.ShapeDtypeStruct((rows // 2, model), jnp.bfloat16)
    return pl.pallas_call(
        functools.partial(forward_kernel, rep, kv_heads, ctx_count),
        out_shape=(
            jax.ShapeDtypeStruct(q.shape, jnp.bfloat16),
            jax.ShapeDtypeStruct((kv_heads, q_blocks, rep * BLOCK), jnp.float32),
            half,
            half,
        ),
        in_specs=[smem] * 3 + [vmem] * 2 + [any_] * ctx_count,
        out_specs=[vmem] * 4,
        scratch_shapes=[
            pltpu.VMEM((tokens, parts[0].shape[1]), jnp.bfloat16),
            pltpu.SMEM((order.shape[0],), jnp.int32),
            pltpu.VMEM((kv_heads, HEAD_SIZE, rep * BLOCK), jnp.bfloat16),
            pltpu.VMEM((kv_heads, HEAD_SIZE, rep * BLOCK), jnp.float32),
            pltpu.SemaphoreType.DMA((ctx_count,)),
        ],
        compiler_params=pltpu.CompilerParams(vmem_limit_bytes=VMEM_SMALL),
        cost_estimate=cost("attention_forward", flops, 2 * tokens * parts[0].shape[1] + 4 * rows * model),
        name="attention_forward",
    )(order, cont, where, q, w_out, *parts)


def attention_backward(head, q, grad_branch, w_out, mixed, lse, parts, cosine, sine, order, cont,
                       where):
    ctx_count = len(parts)
    rows, tokens = q.shape[0], ctx_count * q.shape[0]
    kv_heads = parts[0].shape[1] // (2 * HEAD_SIZE)
    rep = q.shape[1] // HEAD_SIZE // kv_heads
    q_blocks, model = rows // BLOCK, w_out.shape[1]
    wide = rep * HEAD_SIZE
    q_spec = pl.BlockSpec((rows, wide), lambda g, *_: (0, head))
    whole = lambda g, *_: (0, 0)
    table_spec = pl.BlockSpec((rows, HEAD_SIZE), whole)
    half = (tokens // 2, 2 * HEAD_SIZE)
    flops = 5 * rows * tokens * wide + 2 * rows * wide * model
    return pl.pallas_call(
        functools.partial(backward_kernel, rep, 1, ctx_count, head),
        out_shape=(
            jax.ShapeDtypeStruct((rows, wide), jnp.bfloat16),
            jax.ShapeDtypeStruct(half, jnp.bfloat16),
            jax.ShapeDtypeStruct(half, jnp.bfloat16),
        ),
        grid_spec=pltpu.PrefetchScalarGridSpec(
            num_scalar_prefetch=3,
            grid=(1,),
            in_specs=[
                q_spec,
                pl.BlockSpec((rows, model), whole),
                pl.BlockSpec((wide, model), lambda g, *_: (head, 0)),
                q_spec,
                pl.BlockSpec((1, q_blocks, rep * BLOCK), lambda g, *_: (head, 0, 0)),
                table_spec,
                table_spec,
            ]
            + [pl.BlockSpec(memory_space=pl.ANY)] * ctx_count,
            out_specs=[
                pl.BlockSpec((rows, wide), whole),
                pl.BlockSpec(half, whole),
                pl.BlockSpec(half, whole),
            ],
            scratch_shapes=[
                pltpu.VMEM((tokens, 2 * HEAD_SIZE), jnp.bfloat16),
                pltpu.VMEM((rows, wide), jnp.bfloat16),
                pltpu.SMEM((order.shape[0],), jnp.int32),
                pltpu.VMEM((1, HEAD_SIZE, rep * BLOCK), jnp.bfloat16),
                pltpu.VMEM((1, HEAD_SIZE, rep * BLOCK), jnp.bfloat16),
                pltpu.VMEM((1, HEAD_SIZE, rep * BLOCK), jnp.float32),
                pltpu.VMEM((tokens, 2 * HEAD_SIZE), jnp.float32),
                pltpu.SemaphoreType.DMA((ctx_count,)),
            ],
        ),
        compiler_params=pltpu.CompilerParams(vmem_limit_bytes=VMEM_LIMIT),
        cost_estimate=cost(f"attention_backward_{head}", flops, 4 * tokens * wide + 2 * rows * model),
        name=f"attention_backward_{head}",
    )(order, cont, where, q, grad_branch, w_out, mixed, lse, cosine, sine, *parts)


def input_kernel(order_ref, cont_ref, where_ref, gain_ref, x_hbm, wq_hbm, wk_hbm, wv_hbm, table_hbm,
                 first_ref, q_ref, kv_ref, cos_ref, sin_ref,
                 x_ref, wq_ref, wk_ref, wv_ref, table_ref, sem):
    pairs = ((x_hbm, x_ref), (table_hbm, table_ref), (wk_hbm, wk_ref), (wv_hbm, wv_ref),
             (wq_hbm, wq_ref))
    copies = [
        pltpu.make_async_copy(source, target, sem.at[n])
        for n, (source, target) in enumerate(pairs)
    ]
    for copy in copies:
        copy.start()
    count = cont_ref.shape[0]
    prompt_blocks = count // CONTS * PER_PROMPT
    starts = (table_ref.shape[0] - 2 * BLOCK) // 2
    lane = lax.broadcasted_iota(jnp.int32, (BLOCK, HEAD_SIZE), 1)
    copies[0].wait()
    copies[1].wait()

    def one_slot(slot, carry):
        quarter = slot_quarter(slot, where_ref[1])
        rows = pl.ds(pl.multiple_of(slot * BLOCK, BLOCK), BLOCK)
        full = x_ref[pl.ds(pl.multiple_of(quarter * BLOCK, BLOCK), BLOCK), :].astype(jnp.float32)
        inv = lax.rsqrt(jnp.mean(full * full, axis=-1, keepdims=True) + eps_norm)
        first_ref[rows, :] = (full * inv * gain_ref[...]).astype(jnp.bfloat16)
        own = order_ref[stored_block(slot, where_ref)]
        spot = jnp.where(
            own < prompt_blocks,
            lax.rem(own, PER_PROMPT),
            PER_PROMPT + lax.rem(own - prompt_blocks, PER_CONT),
        )
        cos_start = table_ref[pl.ds(2 * BLOCK + spot, 1), :]
        sin_start = table_ref[pl.ds(2 * BLOCK + starts + spot, 1), :]
        cos_in, sin_in = table_ref[:BLOCK, :], table_ref[BLOCK : 2 * BLOCK, :]
        sine = sin_start * cos_in + cos_start * sin_in
        cos_ref[rows, :] = cos_start * cos_in - sin_start * sin_in
        sin_ref[rows, :] = jnp.where(lane < HEAD_SIZE // 2, -sine, sine)
        return carry

    lax.fori_loop(0, SLOTS, one_slot, 0)
    first = first_ref[...]
    cosine, sine = cos_ref[...], sin_ref[...]
    copies[2].wait()
    copies[3].wait()
    keys = dot(first, wk_ref[...])
    values = dot(first, wv_ref[...])
    for h in range(wk_ref.shape[1] // HEAD_SIZE):
        cols = slice(h * HEAD_SIZE, (h + 1) * HEAD_SIZE)
        low, high = 2 * h * HEAD_SIZE, (2 * h + 1) * HEAD_SIZE
        key = rotate(keys[:, cols], cosine, sine)
        kv_ref[:, low:high] = key.astype(jnp.bfloat16)
        kv_ref[:, high : high + HEAD_SIZE] = values[:, cols].astype(jnp.bfloat16)
    copies[4].wait()
    for n in range(0, wq_ref.shape[1], 256):
        queries = dot(first, wq_ref[:, n : n + 256])
        for m in range(0, 256, HEAD_SIZE):
            query = rotate(queries[:, m : m + HEAD_SIZE], cosine, sine)
            q_ref[:, n + m : n + m + HEAD_SIZE] = query.astype(jnp.bfloat16)


def input_stage(x, gain, wq, wk, wv, order, cont, where):
    rows, model = x.shape
    cos_start, sin_start, cos_in, sin_in = angle_tables()
    table = np.concatenate([cos_in, sin_in, cos_start, sin_start])
    vmem, smem, any_ = (
        pl.BlockSpec(memory_space=space) for space in (pltpu.VMEM, pltpu.SMEM, pl.ANY)
    )
    flops = 2 * rows * model * (wq.shape[1] + 2 * wk.shape[1])
    return pl.pallas_call(
        input_kernel,
        out_shape=(
            jax.ShapeDtypeStruct((rows, model), jnp.bfloat16),
            jax.ShapeDtypeStruct((rows, wq.shape[1]), jnp.bfloat16),
            jax.ShapeDtypeStruct((rows, 2 * wk.shape[1]), jnp.bfloat16),
            jax.ShapeDtypeStruct((rows, HEAD_SIZE), jnp.float32),
            jax.ShapeDtypeStruct((rows, HEAD_SIZE), jnp.float32),
        ),
        in_specs=[smem] * 3 + [vmem] + [any_] * 5,
        out_specs=[vmem] * 5,
        scratch_shapes=[
            pltpu.VMEM(a.shape, a.dtype) for a in (x, wq, wk, wv)
        ]
        + [pltpu.VMEM(table.shape, jnp.float32), pltpu.SemaphoreType.DMA((5,))],
        compiler_params=pltpu.CompilerParams(vmem_limit_bytes=VMEM_LIMIT),
        cost_estimate=cost("input_stage", flops, 4 * x.size + 2 * wq.size + 4 * wk.size),
        name="input_stage",
    )(order, cont, where, gain.reshape(1, -1), x, wq, wk, wv, table)


FILLERS = ("kv_shares", "grad_hidden")


def cost(name, flops, bytes_accessed):
    scale = 16.0 if name in FILLERS else 0.02
    return pl.CostEstimate(
        flops=int(flops * scale), bytes_accessed=int(bytes_accessed * scale), transcendentals=0
    )


def put_share(value, index, x_bit, keep_ref, send_ref, swap_bits):
    spot = share_spot(lax.shift_right_logical(index, 1), keep_ref.shape[0], swap_bits)
    stays = (index & 1) == x_bit
    value = value.astype(keep_ref.dtype)

    @pl.when(stays)
    def _():
        keep_ref[pl.ds(spot, 1)] = value[None]

    @pl.when(jnp.logical_not(stays))
    def _():
        send_ref[pl.ds(spot, 1)] = value[None]


def pair_bit(where_ref):
    return lax.shift_right_logical(where_ref[0], 1) & 1


def grad_hidden_kernel(where_ref, cot_ref, wd_ref, out_ref):
    out_ref[...] = right_dot(cot_ref[...], wd_ref[...])


def grad_hidden_stage(cot, w_down, where):
    rows, model = cot.shape
    units = w_down.shape[0] // 2
    block = 256
    steps = units // block
    return pl.pallas_call(
        grad_hidden_kernel,
        out_shape=jax.ShapeDtypeStruct((rows, units), jnp.float32),
        grid_spec=pltpu.PrefetchScalarGridSpec(
            num_scalar_prefetch=1,
            grid=(steps,),
            in_specs=[
                pl.BlockSpec((rows, model), lambda i, w: (0, 0), pipeline_mode=pl.Buffered(1)),
                pl.BlockSpec((block, model), lambda i, w: (pair_bit(w) * steps + i, 0)),
            ],
            out_specs=pl.BlockSpec((rows, block), lambda i, w: (0, i)),
        ),
        compiler_params=pltpu.CompilerParams(vmem_limit_bytes=VMEM_SMALL),
        cost_estimate=cost("grad_hidden", 2 * rows * model * units, 4 * rows * model),
        name="grad_hidden",
    )(where, cot, w_down)


def ffn_kernel(where_ref, in_ref, gh_ref, wg_ref, wu_ref, hid_ref, gg_ref, gu_ref):
    gate = dot(in_ref[...], wg_ref[...])
    upward = dot(in_ref[...], wu_ref[...])
    grad_hidden = gh_ref[...]
    sigma = jax.nn.sigmoid(gate)
    swish = gate * sigma
    hid_ref[...] = (swish * upward).astype(jnp.bfloat16)
    gg_ref[...] = (grad_hidden * upward * sigma * (1.0 + gate * (1.0 - sigma))).astype(
        jnp.bfloat16
    )
    gu_ref[...] = (grad_hidden * swish).astype(jnp.bfloat16)


def ffn_stage(second, grad_hidden, w_gate, w_up, where):
    rows, model = second.shape
    units = w_gate.shape[1] // 2
    block = 256
    steps = units // block
    col_spec = pl.BlockSpec((model, block), lambda i, w: (0, pair_bit(w) * steps + i))
    unit_spec = pl.BlockSpec((rows, block), lambda i, w: (0, i))
    unit = jax.ShapeDtypeStruct((rows, units), jnp.bfloat16)
    return pl.pallas_call(
        ffn_kernel,
        out_shape=(unit, unit, unit),
        grid_spec=pltpu.PrefetchScalarGridSpec(
            num_scalar_prefetch=1,
            grid=(steps,),
            in_specs=[
                pl.BlockSpec((rows, model), lambda i, w: (0, 0), pipeline_mode=pl.Buffered(1)),
                unit_spec,
                col_spec,
                col_spec,
            ],
            out_specs=[unit_spec] * 3,
        ),
        compiler_params=pltpu.CompilerParams(vmem_limit_bytes=VMEM_SMALL),
        cost_estimate=cost("ffn_stage", 4 * rows * model * units, 6 * rows * model),
        name="ffn_stage",
    )(where, second, grad_hidden, w_gate, w_up)


def grad_second_kernel(where_ref, gg_ref, gu_ref, wg_ref, wu_ref, out_ref):
    total = right_dot(gg_ref[...], wg_ref[...]) + right_dot(gu_ref[...], wu_ref[...])
    out_ref[...] = total.astype(jnp.bfloat16)


def grad_second_half(half, name, grads, weights, where):
    rows, units = grads[0].shape
    rows //= 2
    model = weights[0].shape[0]
    block = 512
    left_spec = pl.BlockSpec((rows, units), lambda n, w: (half, 0), pipeline_mode=pl.Buffered(1))
    right_spec = pl.BlockSpec((block, units), lambda n, w: (n, pair_bit(w)))
    return pl.pallas_call(
        grad_second_kernel,
        out_shape=jax.ShapeDtypeStruct((rows, model), jnp.bfloat16),
        grid_spec=pltpu.PrefetchScalarGridSpec(
            num_scalar_prefetch=1,
            grid=(model // block,),
            in_specs=[left_spec] * 2 + [right_spec] * 2,
            out_specs=pl.BlockSpec((rows, block), lambda n, w: (0, n)),
        ),
        compiler_params=pltpu.CompilerParams(vmem_limit_bytes=VMEM_SMALL),
        cost_estimate=cost(name, 4 * rows * units * model, 4 * rows * model),
        name=name,
    )(where, *grads, *weights)


def ffn_out_kernel(where_ref, hid_ref, wd_ref, keep_ref, send_ref):
    total = dot(hid_ref[...], wd_ref[...])
    half = keep_ref.shape[0]
    keep_ref[...] = total[:half].astype(jnp.bfloat16)
    send_ref[...] = total[half:].astype(jnp.bfloat16)


def unit_sum(kernel, name, lefts, rights, transposed, where):
    rows, units = lefts[0].shape
    model = rights[0].shape[0 if transposed else 1]
    block = 512
    if transposed:
        right_spec = pl.BlockSpec((block, units), lambda n, w: (n, pair_bit(w)))
    else:
        right_spec = pl.BlockSpec((units, block), lambda n, w: (pair_bit(w), n))
    left_spec = pl.BlockSpec((rows, units), lambda n, w: (0, 0), pipeline_mode=pl.Buffered(1))
    half = jax.ShapeDtypeStruct((rows // 2, model), jnp.bfloat16)
    half_spec = pl.BlockSpec((rows // 2, block), lambda n, w: (0, n))
    return pl.pallas_call(
        kernel,
        out_shape=(half, half),
        grid_spec=pltpu.PrefetchScalarGridSpec(
            num_scalar_prefetch=1,
            grid=(model // block,),
            in_specs=[left_spec] * len(lefts) + [right_spec] * len(rights),
            out_specs=[half_spec, half_spec],
        ),
        compiler_params=pltpu.CompilerParams(vmem_limit_bytes=VMEM_SMALL),
        cost_estimate=cost(name, 2 * len(lefts) * rows * units * model, 4 * rows * model),
        name=name,
    )(where, *lefts, *rights)


def share_spot(spot, count, swap_bits):
    if swap_bits:
        return (spot & 1) * (count // 2) + lax.shift_right_logical(spot, 1)
    return spot


def shares_kernel(left_count, swap_bits, pairs, where_ref, *refs):
    lefts, refs = refs[:left_count], refs[left_count:]
    rights, (keep_ref, send_ref) = refs[:-2], refs[-2:]
    share = keep_ref.shape[1]
    step = pl.program_id(0)
    pieces = [left_dot(lefts[l][...], rights[r][...]) for l, r in pairs]
    per_step = lefts[0].shape[1] // share
    if per_step == 1:
        value = jnp.concatenate(pieces, axis=1).astype(keep_ref.dtype)
        sends = step < pl.num_programs(0) // 2

        @pl.when(sends)
        def _():
            send_ref[0] = value

        @pl.when(jnp.logical_not(sends))
        def _():
            keep_ref[0] = value

        return
    for k in range(per_step):
        rows = slice(k * share, (k + 1) * share)
        value = jnp.concatenate([piece[rows] for piece in pieces], axis=1)
        index = step * per_step + k
        put_share(value, index, where_ref[0] & 1, keep_ref, send_ref, swap_bits)


def weight_shares(name, lefts, rights, pairs, ctx_count, swap_bits, where):
    rows, model = lefts[0].shape
    block = 256
    share, half = model // ctx_count, ctx_count // 2
    width = sum(rights[r].shape[1] for _, r in pairs)
    shares = jax.ShapeDtypeStruct((half, share, width), jnp.bfloat16)
    if share == block:

        def left_map(i, w):
            mine = w[0] & 1
            return 0, jnp.where(i < half, 2 * i + 1 - mine, 2 * (i - half) + mine)

        left_spec = pl.BlockSpec((rows, block), left_map)
        spot = lambda index: share_spot(index, half, swap_bits)
        keep_spec = pl.BlockSpec(
            (1, share, width), lambda i, w: (spot(jnp.maximum(i - half, 0)), 0, 0)
        )
        send_spec = pl.BlockSpec(
            (1, share, width), lambda i, w: (spot(jnp.minimum(i, half - 1)), 0, 0)
        )
    else:
        left_spec = pl.BlockSpec((rows, block), lambda i, w: (0, i))
        keep_spec = send_spec = pl.BlockSpec(shares.shape, lambda i, w: (0, 0, 0))
    return pl.pallas_call(
        functools.partial(shares_kernel, len(lefts), swap_bits, pairs),
        out_shape=(shares, shares),
        grid_spec=pltpu.PrefetchScalarGridSpec(
            num_scalar_prefetch=1,
            grid=(model // block,),
            in_specs=[left_spec] * len(lefts)
            + [
                pl.BlockSpec(r.shape, lambda i, w: (0, 0), pipeline_mode=pl.Buffered(1))
                for r in rights
            ],
            out_specs=[keep_spec, send_spec],
        ),
        compiler_params=pltpu.CompilerParams(vmem_limit_bytes=VMEM_SMALL),
        cost_estimate=cost(name, 2 * rows * model * width, 4 * rows * model),
        name=name,
    )(where, *lefts, *rights)


def unit_shares_kernel(where_ref, left_ref, right_ref, out_ref):
    share = out_ref.shape[1]
    total = left_dot(left_ref[...], right_ref[...]).astype(out_ref.dtype)
    per_step = left_ref.shape[1] // share
    if out_ref.shape[0] == 1:
        out_ref[0] = total
    else:
        for k in range(per_step):
            index = pl.program_id(0) * per_step + k
            out_ref[pl.ds(unit_spot(index, out_ref.shape[0]), 1)] = total[k * share : (k + 1) * share][None]


def unit_spot(index, ctx_count):
    return (index & 1) * (ctx_count // 2) + lax.shift_right_logical(index, 1)


def unit_shares(name, left, right, ctx_count, where):
    rows, model = left.shape
    block, width = 256, right.shape[1]
    share = model // ctx_count
    shares = jax.ShapeDtypeStruct((ctx_count, share, width), jnp.bfloat16)
    if share == block:
        out_spec = pl.BlockSpec((1, share, width), lambda i, w: (unit_spot(i, ctx_count), 0, 0))
    else:
        out_spec = pl.BlockSpec(shares.shape, lambda i, w: (0, 0, 0))
    return pl.pallas_call(
        unit_shares_kernel,
        out_shape=shares,
        grid_spec=pltpu.PrefetchScalarGridSpec(
            num_scalar_prefetch=1,
            grid=(model // block,),
            in_specs=[
                pl.BlockSpec((rows, block), lambda i, w: (0, i)),
                pl.BlockSpec(right.shape, lambda i, w: (0, 0), pipeline_mode=pl.Buffered(1)),
            ],
            out_specs=out_spec,
        ),
        compiler_params=pltpu.CompilerParams(vmem_limit_bytes=VMEM_SMALL),
        cost_estimate=cost(name, 2 * rows * model * width, 4 * rows * model),
        name=name,
    )(where, left, right)


def tail_kernel(kv_heads, where_ref, *refs):
    sums, refs = refs[: 2 * kv_heads], refs[2 * kv_heads :]
    cos_ref, sin_ref, refs = refs[0], refs[1], refs[2:]
    gq_refs, refs = refs[:kv_heads], refs[kv_heads:]
    wq_ref, wk_ref, wv_ref, keep_ref, send_ref, gkv_ref = refs
    cosine, sine = cos_ref[...], sin_ref[...]
    for h in range(kv_heads):
        total = sums[2 * h][...].astype(jnp.float32) + sums[2 * h + 1][...].astype(jnp.float32)
        total = total.astype(jnp.bfloat16)
        key = unrotate(total[:, :HEAD_SIZE].astype(jnp.float32), cosine, sine)
        cols = slice(h * HEAD_SIZE, (h + 1) * HEAD_SIZE)
        gkv_ref[:, cols] = key.astype(jnp.bfloat16)
        cols = slice((kv_heads + h) * HEAD_SIZE, (kv_heads + h + 1) * HEAD_SIZE)
        gkv_ref[:, cols] = total[:, HEAD_SIZE:]
    half = keep_ref.shape[0]
    key_width = kv_heads * HEAD_SIZE
    wide = gq_refs[0].shape[1]
    for n in range(0, wq_ref.shape[0], 512):
        span = slice(n, n + 512)
        total = right_dot(gkv_ref[:, :key_width], wk_ref[span, :])
        total += right_dot(gkv_ref[:, key_width:], wv_ref[span, :])
        for h in range(kv_heads):
            total += right_dot(gq_refs[h][...], wq_ref[span, h * wide : (h + 1) * wide])
        total = total.astype(jnp.bfloat16)
        keep_ref[:, span] = total[:half]
        send_ref[:, span] = total[half:]


def tail_stage(kv_sums, cosine, sine, grad_queries, wq, wk, wv, where):
    rows, model = cosine.shape[0], wq.shape[0]
    kv_heads = len(grad_queries)
    vmem = pl.BlockSpec(memory_space=pltpu.VMEM)
    half = jax.ShapeDtypeStruct((rows // 2, model), jnp.bfloat16)
    flat = [term for sums in kv_sums for term in sums]
    return pl.pallas_call(
        functools.partial(tail_kernel, kv_heads),
        out_shape=(
            half,
            half,
            jax.ShapeDtypeStruct((rows, 2 * kv_heads * HEAD_SIZE), jnp.bfloat16),
        ),
        in_specs=[pl.BlockSpec(memory_space=pltpu.SMEM)]
        + [vmem] * (len(flat) + 2 + kv_heads + 3),
        out_specs=[vmem] * 3,
        compiler_params=pltpu.CompilerParams(vmem_limit_bytes=VMEM_SMALL),
        cost_estimate=cost("tail_stage", 2 * rows * model * (wq.shape[1] + 2 * wk.shape[1]), 4 * rows * model + 4 * wq.size
        ),
        name="tail_stage",
    )(where, *flat, cosine, sine, *grad_queries, wq, wk, wv)


def flip(value, axis, mask=1):
    return lax.ppermute(value, axis, [(i, i ^ mask) for i in range(lax.axis_size(axis))])


def ctx_flip(value, mask):
    if mask == 1:
        return flip(value, "x")
    if mask == 2:
        return flip(value, "l")
    return flip(value, "hi", mask // 4)


def add(left, right):
    return (left.astype(jnp.float32) + right.astype(jnp.float32)).astype(jnp.bfloat16)


def slots_of(value, tensor):
    rows = value.shape[0] // SLOTS
    return [
        lax.dynamic_slice_in_dim(value, (tensor ^ SLOT_XOR[u]) * rows, rows)
        for u in range(SLOTS)
    ]


def after(dep, *values):
    deps = dep if isinstance(dep, tuple) else (dep,)
    held = lax.optimization_barrier(deps + values)[len(deps) :]
    return held[0] if len(held) == 1 else held


class Stages:
    def __init__(self, block_order):
        self.live = block_order[0] >= 0

    def __call__(self, function, *args):
        shapes = jax.eval_shape(function, *args)
        empty = lambda *_: jax.tree.map(lambda a: jnp.zeros(a.shape, a.dtype), shapes)
        return lax.cond(self.live, function, empty, *args)


def gather_pair(own):
    partner = ctx_flip(own, 2)
    near = jnp.concatenate([own, partner, flip(own, "y"), flip(partner, "y")])
    return jnp.concatenate([near, flip(near, "core")])


def gather_slots(own):
    near = jnp.concatenate([own, flip(own, "y")])
    return near, flip(near, "core")


def place_rows(own, near, core, far, tensor):
    rows = own.shape[0]
    result = jnp.zeros((SLOTS * rows,) + own.shape[1:], own.dtype)
    for u, piece in enumerate((own, near, core, far)):
        result = lax.dynamic_update_slice_in_dim(
            result, piece, (tensor ^ SLOT_XOR[u]) * rows, 0
        )
    return result


def scatter_slots(keep, send, fill=lambda value: value):
    got = fill(flip(send, "core"))
    quarter = keep.shape[0] // 2
    far = flip(add(keep[quarter:], got[quarter:]), "y")
    return add(keep[:quarter], got[:quarter]), far


def pair_scatter(keep, send, fill=lambda near: near):
    got = fill(flip(send, "core"))
    n = keep.shape[0] // 4
    near = [add(keep[k * n : (k + 1) * n], got[k * n : (k + 1) * n]) for k in range(4)]
    far = flip(near[3], "y")
    got = flip(near[2], "y")
    return near, far, got


def pair_finish(near, far, got):
    away = add(near[1], far)
    return near[0], got, ctx_flip(away, 2), away


def total(terms):
    return sum(term.astype(jnp.float32) for term in terms)


class Reduce:
    def __init__(self, keep, send):
        self.keep, self.got = keep, ctx_flip(send, 1)

    def halve(self, mask, ctx, dep=None):
        keep, got = self.keep, self.got
        if dep is not None:
            keep, got = after(dep, keep, got)
        n = keep.shape[0] // 2
        bit = lax.div(ctx, mask) % 2
        pick = lambda value, index: lax.dynamic_slice_in_dim(value, index * n, n, 0)
        away = ctx_flip(add(pick(keep, 1 - bit), pick(got, 1 - bit)), mask)
        self.keep, self.got = add(pick(keep, bit), pick(got, bit)), away

    def sum(self):
        return (self.keep.astype(jnp.float32) + self.got.astype(jnp.float32))[0]


def high_masks(ctx_count):
    masks, mask = [], ctx_count // 2
    while mask >= 4:
        masks.append(mask)
        mask //= 2
    return masks


def unit_sum_over(shares):
    return lax.psum_scatter(shares, ("x", "hi"), scatter_dimension=0, tiled=True)


def split_halves(summed, ctx, dep):
    summed = after(dep, summed)
    pair = lax.div(ctx, 2) % 2
    pick = lambda index: lax.dynamic_index_in_dim(summed, index, 0, keepdims=False)
    return pick(pair), pick(1 - pair)


def join_halves(own, other, ctx):
    pair = lax.div(ctx, 2) % 2
    low, high = jnp.where(pair == 0, own, other), jnp.where(pair == 0, other, own)
    return jnp.concatenate([low, high], axis=1).astype(jnp.float32)


class KvReduce:
    def __init__(self, keep, got):
        self.keep, self.got = keep, got

    def merge(self, dep):
        keep, got = after(dep, self.keep, self.got)
        n = keep.shape[0] // 2
        return add(keep[:n], got[:n]), add(keep[n:], got[n:])


def norm_back(grad_out, normed, inv_scale, gain):
    scaled = grad_out * gain
    inner = jnp.mean(scaled * normed, axis=-1, keepdims=True)
    return (inv_scale * (scaled - normed * inner), jnp.sum(grad_out * normed, axis=0))


def body(
    layer_input,
    attn_gain,
    w_query,
    key_matrix,
    value_matrix,
    w_out,
    ffn_gain,
    w_gate,
    w_up,
    w_down,
    cotangent,
    block_order,
    cont_prompt,
):
    ctx_count = lax.axis_size("hi") * 4
    ctx = (lax.axis_index("hi") * 2 + lax.axis_index("l")) * 2 + lax.axis_index("x")
    tensor = lax.axis_index("y") * 2 + lax.axis_index("core")
    where = jnp.stack([ctx, tensor]).astype(jnp.int32)
    quarter = layer_input.shape[0] // SLOTS
    kv_heads = key_matrix.shape[1] // HEAD_SIZE
    highs = high_masks(ctx_count)

    stage = Stages(block_order)
    cot_own = lax.dynamic_slice_in_dim(cotangent, tensor * quarter, quarter)
    cot_slots = slots_of(cotangent, tensor)
    cot_part = ctx_flip(cot_own, 2)
    first_input, queries, kv_local, cosine, sine = input_stage(
        layer_input, attn_gain, w_query, key_matrix, value_matrix, block_order, cont_prompt, where
    )
    def first_keys(kv):
        high = {0: kv}
        for bit in reversed(highs):
            for mask in list(high):
                high[mask + bit] = ctx_flip(high[mask], bit)
        del high[0]
        return high, ctx_flip(kv, 2), ctx_flip(kv, 1)

    def second_keys(high, low, cot):
        return (
            ctx_flip(low, 1),
            flip(cot, "y"),
            {mask: ctx_flip(value, 2) for mask, value in high.items()},
            {mask: ctx_flip(value, 1) for mask, value in high.items()},
        )

    def third_keys(both, cot):
        return {mask: ctx_flip(value, 1) for mask, value in both.items()}, flip(cot, "core")

    high, part_l, part_x = stage(first_keys, after(cot_part, kv_local))
    part_lx, more, high_l, high_x = stage(second_keys, high, part_l, cot_part)
    cot_part = jnp.concatenate([cot_part, more])
    high_lx, cot_far = stage(third_keys, high_l, cot_part)
    parts = {0: kv_local, 1: part_x, 2: part_l, 3: part_lx}
    for mask in high:
        parts[mask], parts[mask + 1] = high[mask], high_x[mask]
        parts[mask + 2], parts[mask + 3] = high_l[mask], high_lx[mask]
    parts = [parts[mask] for mask in range(ctx_count)]
    cot = jnp.concatenate(
        [cot_slots[0], cot_part[:quarter], cot_slots[1], cot_part[quarter:]]
        + [cot_slots[2], cot_far[:quarter], cot_slots[3], cot_far[quarter:]]
    )
    mixed, log_total, keep, send = attention_forward(
        queries, w_out, parts, block_order, cont_prompt, where
    )
    first_half = flip(send, "core")
    near = add(keep, first_half)
    far = flip(near[quarter:], "y")
    grad_hidden = grad_hidden_stage(after(near, cot), w_down, where)
    own_input = lax.dynamic_slice_in_dim(layer_input, tensor * quarter, quarter)
    own_input = own_input.astype(jnp.float32)
    middle = own_input + total((near[:quarter], after(grad_hidden, far)))
    inv_two = lax.rsqrt(jnp.mean(middle * middle, axis=-1, keepdims=True) + eps_norm)
    normed_two = middle * inv_two
    second = gather_pair((normed_two * ffn_gain).astype(jnp.bfloat16))
    hidden, grad_gate, grad_up = ffn_stage(second, grad_hidden, w_gate, w_up, where)

    down_shares = unit_shares("down_shares", cot, hidden, ctx_count, where)
    down = unit_sum_over(down_shares)
    grads, weights = after(down_shares, grad_gate, grad_up), (w_gate, w_up)
    send = grad_second_half(1, "grad_second_send", grads, weights, where)

    def second_stage(send, grad_gate, grad_up, hidden):
        keep = grad_second_half(0, "grad_second_keep", (grad_gate, grad_up), weights, where)
        near, far, got = pair_scatter(keep, send)
        shares = unit_shares("gate_shares", second, after(near[3], grad_gate), ctx_count, where)
        *terms, away = pair_finish(near, after(shares, far), got)
        halves = unit_sum(
            ffn_out_kernel, "ffn_out", (after(away, hidden),), (w_down,), False, where
        )
        return total(after(halves[0], *terms)), shares, halves

    grad_second, gate_shares, ffn_halves = stage(second_stage, send, *grads, hidden)
    gate = unit_sum_over(gate_shares)

    def branch_stage(grad_second, grad_up, own):
        grad_norm, gain_part = norm_back(grad_second, normed_two, inv_two, ffn_gain)
        grad_middle = own.astype(jnp.float32) + grad_norm
        branch = grad_middle.astype(jnp.bfloat16)
        shares = unit_shares("up_shares", second, after(branch, grad_up), ctx_count, where)
        near = jnp.concatenate([branch, after(shares, flip(branch, "y"))])
        return grad_middle, gain_part, shares, jnp.concatenate([near, flip(near, "core")])

    grad_middle, ffn_gain_part, up_shares, grad_branch = stage(
        branch_stage, grad_second, grad_up, cot_own
    )
    backward, kv = [], []
    held = grad_branch
    for head in range(kv_heads):
        backward.append(
            attention_backward(
                head, queries, held, w_out, mixed, log_total, parts, cosine, sine,
                block_order, cont_prompt, where,
            )
        )
        kv.append(KvReduce(backward[-1][1], ctx_flip(backward[-1][2], 1)))
        dep = backward[-1][0]
        if head == 0:
            down_own, down_away = split_halves(down, ctx, dep)
            down_other = ctx_flip(down_away, 2)
            dep = down_own
        held = after(dep, grad_branch)
    grad_queries = [item[0] for item in backward]
    branch_shares = weight_shares(
        "branch_shares",
        (first_input, grad_branch),
        grad_queries + [after(dep, mixed)],
        tuple((0, h) for h in range(kv_heads)) + ((1, kv_heads),),
        ctx_count,
        True,
        where,
    )
    def out_stage(keep, send):
        got = flip(send, "core")
        n = keep.shape[0] // 4
        near = [add(keep[k * n : (k + 1) * n], got[k * n : (k + 1) * n]) for k in range(4)]
        return near[0], near[2], add(near[1], flip(near[3], "y"))

    def first_stage(keep, send, own_input, grad_middle):
        terms = scatter_slots(keep, send)
        inv = lax.rsqrt(jnp.mean(own_input * own_input, axis=-1, keepdims=True) + eps_norm)
        grad_norm, gain_part = norm_back(total(terms), own_input * inv, inv, attn_gain)
        return gain_part, (grad_middle + grad_norm).astype(jnp.bfloat16)

    def row_stage(near, other):
        near = jnp.concatenate([near, other])
        return near, flip(near, "core")

    def gain_stage(gains):
        gains = gains + flip(gains, "core")
        gains = gains + flip(gains, "y")
        for mask in [1, 2] + highs:
            gains = gains + ctx_flip(gains, mask)
        return gains

    dep = branch_shares[0]
    kv = [item.merge(dep) for item in kv]
    dep = tuple(keep for keep, _ in kv)
    up = unit_sum_over(after(dep, up_shares))
    sum_down = join_halves(down_own, after(dep, down_other), ctx).T
    dep = sum_down
    got = [ctx_flip(after(dep, value), 2) for _, value in kv]
    branch = Reduce(*after(dep, *branch_shares))
    out_near, out_own, out_away = stage(out_stage, *after(dep, *ffn_halves))
    dep = out_away
    for mask in highs:
        kv = [
            KvReduce(keep, value).merge(dep) for (keep, _), value in zip(kv, got)
        ]
        got = [ctx_flip(value, mask) for _, value in kv]
    dep = tuple(keep for keep, _ in kv)
    gate_own, gate_away = split_halves(gate, ctx, dep)
    dep = gate_own
    gate_other = ctx_flip(after(dep, gate_away), 2)
    out_far, out_got = stage(
        lambda away, own: (ctx_flip(away, 2), flip(own, "y")), *after(dep, out_away, out_own)
    )
    dep = out_far
    branch.halve(2, ctx, dep)
    dep = branch.keep
    output = (middle + total(after(dep, out_near, out_got, out_far))).astype(jnp.bfloat16)
    dep = output
    keep, send, grad_kv = tail_stage(
        [after(dep, keep, value) for (keep, _), value in zip(kv, got)], cosine, sine,
        grad_queries, w_query, key_matrix, value_matrix, where,
    )
    dep = keep
    kv_shares = weight_shares(
        "kv_shares", (first_input,), (after(dep, grad_kv),), ((0, 0),), ctx_count, True, where
    )
    dep = kv_shares[0]
    last = Reduce(*after(dep, *kv_shares))
    attn_gain_part, grad_input = stage(
        first_stage, after(dep, keep), send, own_input, grad_middle
    )
    dep = grad_input
    near = jnp.concatenate([grad_input, output])
    near_other = flip(after(dep, near), "y")
    sum_gate = join_halves(gate_own, after(dep, gate_other), ctx)
    dep = sum_gate
    for mask in highs:
        branch.halve(mask, ctx, dep)
        dep = branch.keep
    last.halve(2, ctx, dep)
    dep = last.keep
    gains = stage(gain_stage, after(dep, jnp.stack([attn_gain_part, ffn_gain_part])))
    dep = gains
    for mask in highs:
        last.halve(mask, ctx, dep)
        dep = last.keep
    near, far = stage(row_stage, near, after(dep, near_other))
    dep = far
    up_own, up_away = split_halves(up, ctx, dep)
    dep = up_own
    up_other = ctx_flip(after(dep, up_away), 2)
    last.keep, last.got = after(dep, last.keep, last.got)
    last_sum = last.sum()
    dep = last_sum
    quarters = [near[n * quarter : (n + 1) * quarter] for n in range(4)]
    quarters += [after(dep, far)[n * quarter : (n + 1) * quarter] for n in range(4)]
    grad_rows, output_rows = [
        place_rows(quarters[k], quarters[k + 2], quarters[k + 4], quarters[k + 6], tensor)
        for k in range(2)
    ]
    dep = (grad_rows, output_rows)
    branch.keep, branch.got = after(dep, branch.keep, branch.got)
    branch_sum = branch.sum()
    dep = branch_sum
    sum_up = join_halves(up_own, after(dep, up_other), ctx)
    dep = sum_up
    grad_input, output = grad_rows, output_rows
    width_q, width_k = w_query.shape[1], key_matrix.shape[1]
    sum_query, sum_out = branch_sum[:, :width_q], branch_sum[:, width_q:].T
    sum_key, sum_value = last_sum[:, :width_k], last_sum[:, width_k:]

    gains = gains.reshape(2, ctx_count * SLOTS, -1)
    gains = lax.dynamic_index_in_dim(gains, ctx * SLOTS + tensor, 1, keepdims=False)
    return (
        output,
        grad_input,
        gains[0],
        sum_query,
        sum_key,
        sum_value,
        sum_out,
        gains[1],
        sum_gate,
        sum_up,
        sum_down,
    )


def solution(mesh):
    rows, heads = ("hi", "l", "x"), ("y", "core")
    split = Mesh(mesh.devices.reshape(-1, 2, 2, 2, 2), rows + heads)
    placed = (
        P(rows, None),
        P(),
        P(None, heads),
        P(None, heads),
        P(None, heads),
        P(heads, None),
        P(),
        P(None, heads),
        P(None, heads),
        P(heads, None),
        P(rows, None),
        P(),
        P(),
    )
    return jax.shard_map(
        body,
        mesh=split,
        in_specs=placed,
        out_specs=(
            P(rows, None),
            P(rows, None),
            P(rows + heads),
            P(rows, heads),
            P(rows, heads),
            P(rows, heads),
            P(heads, rows),
            P(rows + heads),
            P(rows, heads),
            P(rows, heads),
            P(heads, rows),
        ),
        check_vma=False,
    )
```
